32 devices in a mesh: groups: 2 (over y), dom: 4 (over z), cls: 4 (over x, core).
Axes of the slice: x: 2, y: 2, z: 4, core: 2. Of those that a mesh axis runs over, the one named last changes fastest.
Arguments:
- particle_spectra: bfloat16 [512, 2304], P(('groups', 'dom', 'cls')), parts along dimension 0, may hold values from -10 to 10
- class_spectra: bfloat16 [512, 2304], P(('groups', 'cls')), parts along dimension 0, may hold values from -0.25 to 0.25
- shift_index: int32 [512, 16], P(('groups', 'dom', 'cls')), parts along dimension 0, may hold values from 0 to 120
- prior_rotation: int32 [512], P(('groups', 'dom', 'cls')), parts along dimension 0, may hold values from 0 to 7
- particle_group: int32 [512], P(('groups', 'dom', 'cls')), parts along dimension 0, may hold values from 0 to 63
- group_scale: float32 [128], P('groups'), parts along dimension 0, may hold values from 0.6 to 1.6
Outputs:
- class_sums: float32 [512, 2304], P(('groups', 'cls'), 'dom'), parts along dimension 0
- class_weights: float32 [512], P(('groups', 'cls')), parts along dimension 0
The draws below stay inside these ranges and needn't reach their ends.
There are 2 independent parts, one for each index of `groups`. The reference program is written for one: setup_inputs(seed, part) draws one part's arguments, and reference() takes and returns one part's arrays. A program takes and returns all parts, laid end to end along the dimension named above; each array names one. Nothing has to cross between parts.
All inputs are finite; a program needn't handle non-finite values.
Results may differ from the reference program's by a relative error of at most 0.0067.
Values may be sent and summed in bfloat16 or wider, within the bound.
No kernel may reach another device: no remote copies, remote signals or barrier semaphores. Data moves between devices by JAX's collectives and lax.ppermute only.
A program may use at most 64 MiB of HBM per device.

```python
import math
import jax
import jax.numpy as jnp
from jax import lax

CYCLES = 18
ANG = 64
IMG = 64
K = 256
ANG_STEP = 1
ROTS = 8
NT = 16
SHIFT_R = 5
NGROUPS = 64
PD = 16
SHIFTW = 11
F2 = 2304
P_SIZE = 256


def draw_shift_index(key, part):
    return jax.random.randint(jax.random.fold_in(key, 101), (P_SIZE, NT), 0, SHIFTW * SHIFTW, dtype=jnp.int32)


def draw_class_spectra(key, part):
    keys_all = jax.random.split(jax.random.fold_in(key, 202), 2)
    class_scale = jnp.exp(jax.random.uniform(keys_all[0], (K, 1), jnp.float32, math.log(0.6), math.log(1.7)))
    values = jnp.clip(jax.random.normal(keys_all[1], (K, F2), jnp.float32), -4.0, 4.0) * 0.03 * class_scale
    return values.astype(jnp.bfloat16)


def draw_particle_spectra(key, part):
    keys_all = jax.random.split(jax.random.fold_in(key, 303), 2)
    values = jnp.clip(jax.random.normal(keys_all[1], (P_SIZE, F2), jnp.float32), -6.0, 6.0)
    return values.astype(jnp.bfloat16)


def touch_ends(drawn, own_key, smallest, top_value):
    dims = drawn.shape
    index_at = [jax.random.randint(jax.random.fold_in(own_key, axis), (), 0, dims[axis]) for axis in range(len(dims))]
    drawn = drawn.at[tuple(index_at)].set(smallest)
    longest = dims.index(max(dims))
    index_at[longest] = (index_at[longest] + 1) % dims[longest]
    return drawn.at[tuple(index_at)].set(top_value)


def setup_inputs(seed: int = 0, part: int = 0) -> dict:
    key_of = jax.random.split(jax.random.key(seed), 7)
    part_splits = jax.random.split(jax.random.fold_in(key_of[6], part), 7)
    particle_spectra = draw_particle_spectra(jax.random.fold_in(jax.random.fold_in(key_of[6], part), 71), part)
    class_spectra = draw_class_spectra(jax.random.fold_in(jax.random.fold_in(key_of[6], part), 71), part)
    shift_index = draw_shift_index(jax.random.fold_in(jax.random.fold_in(key_of[6], part), 71), part)
    prior_rotation = touch_ends(jax.random.randint(part_splits[3], (P_SIZE,), 0, ROTS), jax.random.fold_in(part_splits[3], 1), 0, ROTS - 1).astype(jnp.int32)
    particle_group = touch_ends(jax.random.randint(part_splits[4], (P_SIZE,), 0, NGROUPS), jax.random.fold_in(part_splits[4], 1), 0, NGROUPS - 1).astype(jnp.int32)
    group_scale = jnp.clip(jnp.exp(jax.random.uniform(part_splits[5], (NGROUPS,), jnp.float32, math.log(0.6), math.log(1.6))), 0.6, 1.6)
    return dict(particle_spectra=particle_spectra, class_spectra=class_spectra, shift_index=shift_index, prior_rotation=prior_rotation, particle_group=particle_group, group_scale=group_scale)


rot_prior_weight = 0.5


def frequency_grid():
    radius = jnp.arange(CYCLES).astype(jnp.float32) + 1.0
    angles = jnp.arange(ANG).astype(jnp.float32) * (2.0 * math.pi / ANG)
    freq_x = (radius[:, None] * jnp.cos(angles)[None, :]).reshape(-1)
    freq_y = (radius[:, None] * jnp.sin(angles)[None, :]).reshape(-1)
    return freq_x, freq_y


def shifted_rows(spectra, shifts):
    half_width = spectra.shape[1] // 2
    freq_x, freq_y = frequency_grid()
    offset_x = (shifts % SHIFTW - SHIFT_R).astype(jnp.float32)
    offset_y = (shifts // SHIFTW - SHIFT_R).astype(jnp.float32)
    phase_angle = (2.0 * math.pi / IMG) * (offset_x[:, :, None] * freq_x[None, None, :] + offset_y[:, :, None] * freq_y[None, None, :])
    real_in = spectra[:, None, :half_width].astype(jnp.float32)
    imag_in = spectra[:, None, half_width:].astype(jnp.float32)
    cosine = jnp.cos(phase_angle)
    sine_part = jnp.sin(phase_angle)
    real_out = real_in * cosine - imag_in * sine_part
    imag_out = real_in * sine_part + imag_in * cosine
    joined = jnp.concatenate([real_out, imag_out], axis=2).astype(jnp.bfloat16)
    return joined.reshape(spectra.shape[0] * shifts.shape[1], 2 * half_width)


def turned_rows(shifted, rotation):
    reshaped = shifted.reshape(shifted.shape[0], -1, ANG)
    return jnp.roll(reshaped, -ANG_STEP * rotation, axis=2).reshape(shifted.shape)


def block_terms(spectra, shifts, priors, groups, group_scale, class_spectra, ref_norms):
    candidates = shifts.shape[1]
    shifted = shifted_rows(spectra, shifts)
    row_scales = jnp.repeat(group_scale[groups], candidates)
    prior_rows = jnp.repeat(priors, candidates)
    hypotheses = []
    for rotation in range(ROTS):
        intersection = jnp.dot(turned_rows(shifted, rotation), class_spectra.T, preferred_element_type=jnp.float32)
        distance = jnp.abs(rotation - prior_rows).astype(jnp.float32)
        hypotheses.append(row_scales[:, None] * intersection - 0.5 * (row_scales * row_scales)[:, None] * ref_norms[None, :] - rot_prior_weight * (distance * distance)[:, None])
    reshaped = jnp.stack(hypotheses).reshape(ROTS, spectra.shape[0], candidates, -1)
    highest = jnp.max(reshaped, axis=(0, 2, 3))
    exponent = jnp.exp(reshaped - highest[None, :, None, None])
    normalizer = jnp.sum(exponent, axis=(0, 2, 3))
    posterior = (exponent / normalizer[None, :, None, None]).reshape(ROTS, shifted.shape[0], -1)
    class_total = jnp.zeros((class_spectra.shape[0], class_spectra.shape[1]), jnp.float32)
    for rotation in range(ROTS):
        weight = (posterior[rotation] * row_scales[:, None]).astype(jnp.bfloat16)
        class_total = class_total + jnp.dot(weight.T, turned_rows(shifted, rotation), preferred_element_type=jnp.float32)
    weight_sums = jnp.sum(posterior * (row_scales * row_scales)[None, :, None], axis=(0, 1))
    return class_total, weight_sums


def reference(particle_spectra, class_spectra, shift_index, prior_rotation, particle_group, group_scale):
    ref_norms = jnp.sum(jnp.square(class_spectra.astype(jnp.float32)), axis=1)
    block_count = particle_spectra.shape[0] // PD
    block_inputs = (particle_spectra.reshape(block_count, PD, -1), shift_index.reshape(block_count, PD, -1), prior_rotation.reshape(block_count, PD), particle_group.reshape(block_count, PD))

    def accumulate(running, block_data):
        class_total, weight_sums = block_terms(block_data[0], block_data[1], block_data[2], block_data[3], group_scale, class_spectra, ref_norms)
        return (running[0] + class_total, running[1] + weight_sums), None

    starting = (jnp.zeros((K, F2), jnp.float32), jnp.zeros((K,), jnp.float32))
    (class_sums, class_weights), _ = lax.scan(accumulate, starting, block_inputs)
    return class_sums, class_weights
```

```python
import functools
import math

import jax
import jax.numpy as jnp
import ml_dtypes
import numpy as np
from jax import lax
from jax.experimental import pallas as pl
from jax.experimental.pallas import tpu as pltpu
from jax.sharding import PartitionSpec as P

CYCLES = 18
ANG = 64
IMG = 64
ANG_STEP = 1
ROTS = 8
SHIFT_R = 5
SHIFTW = 11
HALF = CYCLES * ANG
COLS = 2 * HALF
LANES = 128
META = LANES
ROT_PRIOR = 0.5
VMEM_LIMIT = 56 * 1024 * 1024


def phase_table():
    angles = np.arange(ANG) * (2.0 * math.pi / ANG)
    radius = np.arange(CYCLES) + 1.0
    fx = (radius[:, None] * np.cos(angles)[None, :]).reshape(-1)
    fy = (radius[:, None] * np.sin(angles)[None, :]).reshape(-1)
    offsets = np.arange(SHIFTW * SHIFTW)
    dx = offsets % SHIFTW - SHIFT_R
    dy = offsets // SHIFTW - SHIFT_R
    phase = (2.0 * math.pi / IMG) * (dx[:, None] * fx[None, :] + dy[:, None] * fy[None, :])
    values = np.zeros((LANES, COLS), np.float32)
    values[: SHIFTW * SHIFTW] = np.concatenate([np.cos(phase), np.sin(phase)], axis=1)
    high = values.astype(ml_dtypes.bfloat16)
    low = (values - high.astype(np.float32)).astype(ml_dtypes.bfloat16)
    return np.concatenate([high, low], axis=0)


def exchange(array, axis, distance):
    return lax.ppermute(array, axis, [(i, i ^ distance) for i in range(lax.axis_size(axis))])


def lane_index(shape):
    return lax.broadcasted_iota(jnp.int32, shape, len(shape) - 1)


def rotate_classes(class_ref, rotated_ref, norm_ref):
    classes = class_ref.shape[0]
    total = jnp.zeros((classes, LANES), jnp.float32)
    lane = lane_index((classes, LANES)) % ANG
    for tile in range(COLS // LANES):
        columns = slice(tile * LANES, (tile + 1) * LANES)
        value = class_ref[:, columns].astype(jnp.float32)
        total = total + value * value
        other = pltpu.roll(value, ANG, 1)
        for rotation in range(ROTS):
            offset = ANG_STEP * rotation % ANG
            turned = value
            if offset:
                turned = pltpu.roll(jnp.where(lane < ANG - offset, value, other), offset, 1)
            rotated_ref[rotation * classes : (rotation + 1) * classes, columns] = turned.astype(
                jnp.bfloat16
            )
    norm_ref[...] = jnp.broadcast_to(jnp.sum(total, axis=1, keepdims=True), (classes, LANES))


def to_lanes(column, width):
    n = column.shape[0]
    row = lax.broadcasted_iota(jnp.int32, (n, width), 0)
    return jnp.sum(
        jnp.where(lane_index((n, width)) % n == row, column, 0.0), axis=0, keepdims=True
    )


def fold_lanes(row, period, combine):
    result = row[:, :LANES]
    for part in range(1, row.shape[1] // LANES):
        result = combine(result, row[:, part * LANES : (part + 1) * LANES])
    step = LANES // 2
    while step >= period:
        result = combine(result, pltpu.roll(result, step, 1))
        step //= 2
    return result


def score_block(block_ref, table_ref, scale_ref, rotated_ref, norm_ref, shifted_ref, out):
    particles = block_ref.shape[0]
    classes = norm_ref.shape[0]
    candidates = shifted_ref.shape[0] // particles
    rows = particles * candidates
    repeat = rows // LANES
    meta = block_ref[:, COLS : COLS + META].astype(jnp.float32)
    index = meta[:, :candidates].astype(jnp.int32)
    lane = lane_index((particles, LANES))
    hot = jnp.concatenate(
        [
            jnp.where(index[:, t : t + 1] == lane, 1.0, 0.0).astype(jnp.bfloat16)
            for t in range(candidates)
        ],
        axis=0,
    )
    hot = jnp.concatenate([hot, hot], axis=1)
    groups = scale_ref.shape[1]
    group = meta[:, candidates + 1 : candidates + 2].astype(jnp.int32)
    scale_column = jnp.sum(
        jnp.where(group == lane_index((particles, groups)), scale_ref[...], 0.0),
        axis=1,
        keepdims=True,
    )
    scale = to_lanes(scale_column, rows)
    prior = to_lanes(meta[:, candidates : candidates + 1], rows)
    width = 3 * LANES
    for start in range(0, HALF, width):
        real_columns = slice(start, start + width)
        imag_columns = slice(HALF + start, HALF + start + width)
        cosine = jnp.dot(hot, table_ref[:, real_columns], preferred_element_type=jnp.float32)
        sine = jnp.dot(hot, table_ref[:, imag_columns], preferred_element_type=jnp.float32)
        real = block_ref[:, real_columns].astype(jnp.float32)
        imag = block_ref[:, imag_columns].astype(jnp.float32)
        for t in range(candidates):
            part = slice(t * particles, (t + 1) * particles)
            c, s = cosine[part], sine[part]
            shifted_ref[part, real_columns] = (real * c - imag * s).astype(jnp.bfloat16)
            shifted_ref[part, imag_columns] = (real * s + imag * c).astype(jnp.bfloat16)
    product = lax.dot_general(
        rotated_ref[...],
        shifted_ref[...],
        (((1,), (1,)), ((), ())),
        preferred_element_type=jnp.float32,
    )
    norm = jnp.concatenate([norm_ref[...]] * repeat, axis=1)
    half_square = 0.5 * scale * scale
    scores = []
    highest = None
    for rotation in range(ROTS):
        distance = jnp.abs(rotation - prior)
        score = (
            scale * product[rotation * classes : (rotation + 1) * classes]
            - half_square * norm
            - ROT_PRIOR * (distance * distance)
        )
        scores.append(score)
        peak = jnp.max(score, axis=0, keepdims=True)
        highest = peak if highest is None else jnp.maximum(highest, peak)
    highest = fold_lanes(highest, particles, jnp.maximum)
    wide = jnp.concatenate([highest] * repeat, axis=1)
    total = None
    for rotation in range(ROTS):
        value = jnp.exp(scores[rotation] - wide)
        out(rotation, value)
        added = jnp.sum(value, axis=0, keepdims=True)
        total = added if total is None else total + added
    total = fold_lanes(total, particles, jnp.add)
    return highest, total, scale[:, :LANES]


def own_kernel(
    block_ref, class_ref, table_ref, scale_ref,
    shifted_ref, exp_ref, stats_ref, rotated_ref, norm_ref,
):
    rotate_classes(class_ref, rotated_ref, norm_ref)
    classes = norm_ref.shape[0]

    def out(rotation, value):
        exp_ref[rotation * classes : (rotation + 1) * classes, :] = value

    highest, total, scale = score_block(
        block_ref, table_ref, scale_ref, rotated_ref, norm_ref, shifted_ref, out
    )
    stats_ref[0:1, :] = highest
    stats_ref[1:2, :] = total
    stats_ref[2:3, :] = scale
    stats_ref[3:8, :] = jnp.zeros((5, LANES), jnp.float32)


def rest_kernel(count, *refs):
    blocks = refs[: count - 1]
    table_ref, scale_ref, rotated_ref, norm_ref, own_ref = refs[count - 1 : count + 4]
    shifted_ref, exp_ref, stats_ref, scales_ref = refs[count + 4 :]
    classes = norm_ref.shape[0]
    rows = shifted_ref.shape[0] // (count - 1)
    stats_ref[0:2, :] = own_ref[0:2, :]
    scales_ref[...] = jnp.zeros_like(scales_ref)
    scales_ref[0:1, :] = own_ref[2:3, :]
    for block in range(count - 1):
        part = slice(block * rows, (block + 1) * rows)

        def out(rotation, value):
            exp_ref[rotation * classes : (rotation + 1) * classes, part] = value

        highest, total, scale = score_block(
            blocks[block], table_ref, scale_ref, rotated_ref, norm_ref, shifted_ref.at[part, :], out
        )
        stats_ref[2 * block + 2 : 2 * block + 3, :] = highest
        stats_ref[2 * block + 3 : 2 * block + 4, :] = total
        scales_ref[block + 1 : block + 2, :] = scale


def sums_kernel(count, doms, width, *refs):
    stats = refs[:count]
    place_ref, scales_ref, exp_own, exp_rest, shifted_own, shifted_rest = refs[count : count + 6]
    own_out = refs[count + 6]
    sends = refs[count + 7 : count + 6 + doms]
    weight_ref, sums_ref, parts_ref = refs[count + 6 + doms :]
    rows = shifted_own.shape[0]
    repeat = rows // LANES
    classes = exp_own.shape[0] // ROTS
    mass = jnp.zeros((classes, rows), jnp.float32)
    for block in range(count):
        highs = [stats[c][2 * (c ^ block) : 2 * (c ^ block) + 1, :] for c in range(count)]
        lows = [stats[c][2 * (c ^ block) + 1 : 2 * (c ^ block) + 2, :] for c in range(count)]
        top = functools.reduce(jnp.maximum, highs)
        total = functools.reduce(jnp.add, [l * jnp.exp(h - top) for h, l in zip(highs, lows)])
        factor = jnp.exp(highs[0] - top) / total
        scale = scales_ref[block : block + 1, :]
        factor = jnp.concatenate([factor] * repeat, axis=1)
        scale = jnp.concatenate([scale] * repeat, axis=1)
        for rotation in range(ROTS):
            rotated = slice(rotation * classes, (rotation + 1) * classes)
            value = (
                exp_own[rotated, :]
                if block == 0
                else exp_rest[rotated, (block - 1) * rows : block * rows]
            )
            weight = value * factor * scale
            mass = mass + weight * scale
            weight_ref[rotated, block * rows : (block + 1) * rows] = weight.astype(jnp.bfloat16)
    mass = jnp.sum(mass, axis=1, keepdims=True)
    wide = 2 * LANES
    lane = lane_index((classes, wide)) % ANG
    for start in range(0, COLS, wide):
        columns = slice(start, start + wide)
        product = jnp.dot(
            weight_ref[:, :rows], shifted_own[:, columns], preferred_element_type=jnp.float32
        ) + jnp.dot(
            weight_ref[:, rows:], shifted_rest[:, columns], preferred_element_type=jnp.float32
        )
        inside = product[:classes]
        wrapped = None
        for rotation in range(1, ROTS):
            offset = ANG_STEP * rotation % ANG
            turned = jnp.concatenate(
                [
                    pltpu.roll(
                        product[rotation * classes : (rotation + 1) * classes, s : s + LANES],
                        LANES - offset,
                        1,
                    )
                    for s in range(0, wide, LANES)
                ],
                axis=1,
            )
            within = lane < ANG - offset
            inside = inside + jnp.where(within, turned, 0.0)
            over = jnp.where(within, 0.0, turned)
            wrapped = over if wrapped is None else wrapped + over
        wrapped = jnp.concatenate(
            [pltpu.roll(wrapped[:, s : s + LANES], ANG, 1) for s in range(0, wide, LANES)], axis=1
        )
        sums_ref[:, columns] = inside + wrapped
    padded = own_out.shape[1]
    lane = lane_index((classes, padded))
    high = mass.astype(jnp.bfloat16).astype(jnp.float32)
    middle = (mass - high).astype(jnp.bfloat16).astype(jnp.float32)
    low = (mass - high - middle).astype(jnp.bfloat16).astype(jnp.float32)
    tail = jnp.where(
        lane == width, high, jnp.where(lane == width + 1, middle, jnp.where(lane == width + 2, low, 0.0))
    )
    for dom in range(doms):
        first = width * dom
        base = first // LANES * LANES
        span = -(-(first - base + width) // LANES) * LANES
        part = sums_ref[:, base : base + span]
        if first > base:
            part = pltpu.roll(part, span - (first - base), 1)
        if span < padded:
            part = jnp.concatenate([part, jnp.zeros((classes, padded - span), jnp.float32)], axis=1)
        parts_ref[dom] = jnp.where(lane < width, part[:, :padded], tail)
    place = place_ref[0]
    own_out[...] = parts_ref[place]
    for distance in range(1, doms):
        sends[distance - 1][...] = parts_ref[place ^ distance].astype(jnp.bfloat16)


def final_kernel(width, own_ref, *refs):
    received, sums_ref, weights_ref = refs[:-2], refs[-2], refs[-1]
    total = own_ref[...]
    for ref in received:
        total = total + ref[...].astype(jnp.float32)
    sums_ref[...] = total[:, :width]
    lane = lane_index(total.shape)
    mass = jnp.sum(
        jnp.where((lane >= width) & (lane < width + 3), total, 0.0), axis=1, keepdims=True
    )
    weights_ref[...] = to_lanes(mass, total.shape[0])


def call(kernel, shapes, scratch, flops, moved, *args, smem=()):
    vmem = pl.BlockSpec(memory_space=pltpu.VMEM)
    scalar = pl.BlockSpec(memory_space=pltpu.SMEM)
    return pl.pallas_call(
        kernel,
        out_shape=shapes,
        in_specs=[scalar if i in smem else vmem for i in range(len(args))],
        out_specs=[vmem] * len(shapes),
        scratch_shapes=scratch,
        compiler_params=pltpu.CompilerParams(vmem_limit_bytes=VMEM_LIMIT),
        cost_estimate=pl.CostEstimate(flops=flops, bytes_accessed=moved, transcendentals=0),
    )(*args)


def body(particle_spectra, class_spectra, shift_index, prior_rotation, particle_group, group_scale):
    count = lax.axis_size("cls")
    doms = lax.axis_size("dom")
    particles, candidates = shift_index.shape
    classes = class_spectra.shape[0]
    rows = particles * candidates
    width = COLS // doms
    padded = -(-(width + 3) // LANES) * LANES
    f32, bf16 = jnp.float32, jnp.bfloat16
    shape = jax.ShapeDtypeStruct

    meta = jnp.concatenate(
        [
            shift_index,
            prior_rotation[:, None],
            particle_group[:, None],
            jnp.zeros((particles, META - candidates - 2), jnp.int32),
        ],
        axis=1,
    ).astype(bf16)
    packed = jnp.concatenate([particle_spectra, meta], axis=1)
    others = [exchange(packed, "cls", distance) for distance in range(1, count)]
    table = jnp.asarray(phase_table())
    scales = group_scale[None, :]
    stat_rows = -(-2 * count // 8) * 8
    work = 2 * rows * COLS * (ROTS * classes + 256)
    shifted_own, exp_own, stats_own, rotated, norm = call(
        own_kernel,
        [
            shape((rows, COLS), bf16),
            shape((ROTS * classes, rows), f32),
            shape((8, LANES), f32),
            shape((ROTS * classes, COLS), bf16),
            shape((classes, LANES), f32),
        ],
        [],
        work,
        4 * rows * COLS,
        packed, class_spectra, table, scales,
    )
    rest = (count - 1) * rows
    shifted_rest, exp_rest, stats, scale_rows = call(
        functools.partial(rest_kernel, count),
        [
            shape((rest, COLS), bf16),
            shape((ROTS * classes, rest), f32),
            shape((stat_rows, LANES), f32),
            shape((-(-count // 8) * 8, LANES), f32),
        ],
        [],
        work * (count - 1),
        4 * rest * COLS,
        *others, table, scales, rotated, norm, stats_own,
    )
    all_stats = [stats] + [exchange(stats, "cls", distance) for distance in range(1, count)]
    place = lax.axis_index("dom").astype(jnp.int32).reshape(1)
    own, *sends = call(
        functools.partial(sums_kernel, count, doms, width),
        [shape((classes, padded), f32)] + [shape((classes, padded), bf16)] * (doms - 1),
        [
            pltpu.VMEM((ROTS * classes, count * rows), bf16),
            pltpu.VMEM((classes, COLS), f32),
            pltpu.VMEM((doms, classes, padded), f32),
        ],
        2 * count * rows * COLS * ROTS * classes,
        4 * count * rows * COLS,
        *all_stats, place, scale_rows, exp_own, exp_rest, shifted_own, shifted_rest,
        smem=(count,),
    )
    received = [exchange(sends[distance - 1], "dom", distance) for distance in range(1, doms)]
    class_sums, class_weights = call(
        functools.partial(final_kernel, width),
        [shape((classes, width), f32), shape((1, classes), f32)],
        [],
        doms * classes * padded,
        4 * doms * classes * padded,
        own, *received,
    )
    return class_sums, class_weights.reshape(classes)


def solution(mesh):
    placed = (
        P(("groups", "dom", "cls"), None),
        P(("groups", "cls"), None),
        P(("groups", "dom", "cls"), None),
        P(("groups", "dom", "cls")),
        P(("groups", "dom", "cls")),
        P("groups"),
    )
    return jax.shard_map(
        body,
        mesh=mesh,
        in_specs=placed,
        out_specs=(P(("groups", "cls"), "dom"), P(("groups", "cls"))),
        check_vma=False,
    )
```

```python
import functools
import math

import jax
import jax.numpy as jnp
import ml_dtypes
import numpy as np
from jax import lax
from jax.experimental import pallas as pl
from jax.experimental.pallas import tpu as pltpu
from jax.sharding import PartitionSpec as P

CYCLES = 18
ANG = 64
IMG = 64
ANG_STEP = 1
ROTS = 8
SHIFT_R = 5
SHIFTW = 11
HALF = CYCLES * ANG
COLS = 2 * HALF
LANES = 128
META = LANES
ROT_PRIOR = 0.5
VMEM_LIMIT = 20 * 1024 * 1024


def phase_table():
    angles = np.arange(ANG) * (2.0 * math.pi / ANG)
    radius = np.arange(CYCLES) + 1.0
    fx = (radius[:, None] * np.cos(angles)[None, :]).reshape(-1)
    fy = (radius[:, None] * np.sin(angles)[None, :]).reshape(-1)
    offsets = np.arange(SHIFTW * SHIFTW)
    dx = offsets % SHIFTW - SHIFT_R
    dy = offsets // SHIFTW - SHIFT_R
    phase = (2.0 * math.pi / IMG) * (dx[:, None] * fx[None, :] + dy[:, None] * fy[None, :])
    values = np.zeros((LANES, COLS), np.float32)
    values[: SHIFTW * SHIFTW] = np.concatenate([np.cos(phase), np.sin(phase)], axis=1)
    high = values.astype(ml_dtypes.bfloat16)
    low = (values - high.astype(np.float32)).astype(ml_dtypes.bfloat16)
    return np.concatenate([high, low], axis=0)


def exchange(array, axis, distance):
    return lax.ppermute(array, axis, [(i, i ^ distance) for i in range(lax.axis_size(axis))])


def lane_index(shape):
    return lax.broadcasted_iota(jnp.int32, shape, len(shape) - 1)


def rotate_classes(class_ref, rotated_ref, norm_ref):
    classes = class_ref.shape[0]
    total = jnp.zeros((classes, LANES), jnp.float32)
    lane = lane_index((classes, LANES)) % ANG
    for tile in range(COLS // LANES):
        columns = slice(tile * LANES, (tile + 1) * LANES)
        value = class_ref[:, columns].astype(jnp.float32)
        total = total + value * value
        other = pltpu.roll(value, ANG, 1)
        for rotation in range(ROTS):
            offset = ANG_STEP * rotation % ANG
            turned = value
            if offset:
                turned = pltpu.roll(jnp.where(lane < ANG - offset, value, other), offset, 1)
            rotated_ref[rotation * classes : (rotation + 1) * classes, columns] = turned.astype(
                jnp.bfloat16
            )
    norm_ref[...] = jnp.broadcast_to(jnp.sum(total, axis=1, keepdims=True), (classes, LANES))


def to_lanes(column, width):
    n = column.shape[0]
    row = lax.broadcasted_iota(jnp.int32, (n, width), 0)
    return jnp.sum(
        jnp.where(lane_index((n, width)) % n == row, column, 0.0), axis=0, keepdims=True
    )


def fold_lanes(row, period, combine):
    result = row[:, :LANES]
    for part in range(1, row.shape[1] // LANES):
        result = combine(result, row[:, part * LANES : (part + 1) * LANES])
    step = LANES // 2
    while step >= period:
        result = combine(result, pltpu.roll(result, step, 1))
        step //= 2
    return result


def to_column(row):
    n = row.shape[1]
    diagonal = lax.broadcasted_iota(jnp.int32, (n, n), 0) == lane_index((n, n))
    return jnp.sum(jnp.where(diagonal, row, 0.0), axis=1, keepdims=True)


def pack_kernel(particle_ref, index_ref, prior_ref, group_ref, packed_ref):
    particles, candidates = index_ref.shape
    packed_ref[:, :COLS] = particle_ref[...]
    lane = lane_index((particles, META))
    index = jnp.concatenate(
        [index_ref[...].astype(jnp.float32), jnp.zeros((particles, META - candidates), jnp.float32)],
        axis=1,
    )
    prior = to_column(prior_ref[...].astype(jnp.float32))
    group = to_column(group_ref[...].astype(jnp.float32))
    meta = jnp.where(lane == candidates, prior, jnp.where(lane == candidates + 1, group, index))
    packed_ref[:, COLS:] = meta.astype(jnp.bfloat16)


def score_block(block_ref, table_ref, scale_ref, rotated_ref, norm_ref, shifted_ref, out):
    particles = block_ref.shape[0]
    classes = norm_ref.shape[0]
    candidates = shifted_ref.shape[0] // particles
    rows = particles * candidates
    repeat = rows // LANES
    meta = block_ref[:, COLS : COLS + META].astype(jnp.float32)
    index = meta[:, :candidates].astype(jnp.int32)
    lane = lane_index((particles, LANES))
    hot = jnp.concatenate(
        [
            jnp.where(index[:, t : t + 1] == lane, 1.0, 0.0).astype(jnp.bfloat16)
            for t in range(candidates)
        ],
        axis=0,
    )
    hot = jnp.concatenate([hot, hot], axis=1)
    groups = scale_ref.shape[1]
    group = meta[:, candidates + 1 : candidates + 2].astype(jnp.int32)
    scale_column = jnp.sum(
        jnp.where(group == lane_index((particles, groups)), scale_ref[...], 0.0),
        axis=1,
        keepdims=True,
    )
    scale = to_lanes(scale_column, rows)
    prior = to_lanes(meta[:, candidates : candidates + 1], rows)
    width = 3 * LANES
    for start in range(0, HALF, width):
        real_columns = slice(start, start + width)
        imag_columns = slice(HALF + start, HALF + start + width)
        cosine = jnp.dot(hot, table_ref[:, real_columns], preferred_element_type=jnp.float32)
        sine = jnp.dot(hot, table_ref[:, imag_columns], preferred_element_type=jnp.float32)
        real = block_ref[:, real_columns].astype(jnp.float32)
        imag = block_ref[:, imag_columns].astype(jnp.float32)
        for t in range(candidates):
            part = slice(t * particles, (t + 1) * particles)
            c, s = cosine[part], sine[part]
            shifted_ref[part, real_columns] = (real * c - imag * s).astype(jnp.bfloat16)
            shifted_ref[part, imag_columns] = (real * s + imag * c).astype(jnp.bfloat16)
    product = lax.dot_general(
        rotated_ref[...],
        shifted_ref[...],
        (((1,), (1,)), ((), ())),
        preferred_element_type=jnp.float32,
    )
    norm = jnp.concatenate([norm_ref[...]] * repeat, axis=1)
    half_square = 0.5 * scale * scale
    scores = []
    highest = None
    for rotation in range(ROTS):
        distance = jnp.abs(rotation - prior)
        score = (
            scale * product[rotation * classes : (rotation + 1) * classes]
            - half_square * norm
            - ROT_PRIOR * (distance * distance)
        )
        scores.append(score)
        peak = jnp.max(score, axis=0, keepdims=True)
        highest = peak if highest is None else jnp.maximum(highest, peak)
    highest = fold_lanes(highest, particles, jnp.maximum)
    wide = jnp.concatenate([highest] * repeat, axis=1)
    total = None
    for rotation in range(ROTS):
        value = jnp.exp(scores[rotation] - wide)
        out(rotation, value)
        added = jnp.sum(value, axis=0, keepdims=True)
        total = added if total is None else total + added
    total = fold_lanes(total, particles, jnp.add)
    return highest, total, scale[:, :LANES]


def own_kernel(
    block_ref, class_ref, table_ref, scale_ref,
    shifted_ref, exp_ref, stats_ref, rotated_ref, norm_ref,
):
    rotate_classes(class_ref, rotated_ref, norm_ref)
    classes = norm_ref.shape[0]

    def out(rotation, value):
        exp_ref[rotation * classes : (rotation + 1) * classes, :] = value

    highest, total, scale = score_block(
        block_ref, table_ref, scale_ref, rotated_ref, norm_ref, shifted_ref, out
    )
    stats_ref[0:1, :] = highest
    stats_ref[1:2, :] = total
    stats_ref[2:3, :] = scale
    stats_ref[3:8, :] = jnp.zeros((5, LANES), jnp.float32)


def rest_kernel(count, *refs):
    blocks = refs[: count - 1]
    table_ref, scale_ref, rotated_ref, norm_ref, own_ref = refs[count - 1 : count + 4]
    shifted_ref, exp_ref, stats_ref, scales_ref = refs[count + 4 :]
    classes = norm_ref.shape[0]
    rows = shifted_ref.shape[0] // (count - 1)
    stats_ref[0:2, :] = own_ref[0:2, :]
    scales_ref[...] = jnp.zeros_like(scales_ref)
    scales_ref[0:1, :] = own_ref[2:3, :]
    for block in range(count - 1):
        part = slice(block * rows, (block + 1) * rows)

        def out(rotation, value):
            exp_ref[rotation * classes : (rotation + 1) * classes, part] = value

        highest, total, scale = score_block(
            blocks[block], table_ref, scale_ref, rotated_ref, norm_ref, shifted_ref.at[part, :], out
        )
        stats_ref[2 * block + 2 : 2 * block + 3, :] = highest
        stats_ref[2 * block + 3 : 2 * block + 4, :] = total
        scales_ref[block + 1 : block + 2, :] = scale


def sums_kernel(count, doms, width, *refs):
    stats = refs[:count]
    place_ref, scales_ref, exp_own, exp_rest, shifted_own, shifted_rest = refs[count : count + 6]
    own_out = refs[count + 6]
    sends = refs[count + 7 : count + 6 + doms]
    weight_ref, sums_ref, parts_ref = refs[count + 6 + doms :]
    rows = shifted_own.shape[0]
    repeat = rows // LANES
    classes = exp_own.shape[0] // ROTS
    mass = jnp.zeros((classes, rows), jnp.float32)
    for block in range(count):
        highs = [stats[c][2 * (c ^ block) : 2 * (c ^ block) + 1, :] for c in range(count)]
        lows = [stats[c][2 * (c ^ block) + 1 : 2 * (c ^ block) + 2, :] for c in range(count)]
        top = functools.reduce(jnp.maximum, highs)
        total = functools.reduce(jnp.add, [l * jnp.exp(h - top) for h, l in zip(highs, lows)])
        factor = jnp.exp(highs[0] - top) / total
        scale = scales_ref[block : block + 1, :]
        factor = jnp.concatenate([factor] * repeat, axis=1)
        scale = jnp.concatenate([scale] * repeat, axis=1)
        for rotation in range(ROTS):
            rotated = slice(rotation * classes, (rotation + 1) * classes)
            value = (
                exp_own[rotated, :]
                if block == 0
                else exp_rest[rotated, (block - 1) * rows : block * rows]
            )
            weight = value * factor * scale
            mass = mass + weight * scale
            weight_ref[rotated, block * rows : (block + 1) * rows] = weight.astype(jnp.bfloat16)
    mass = jnp.sum(mass, axis=1, keepdims=True)
    wide = 2 * LANES
    lane = lane_index((classes, wide)) % ANG
    for start in range(0, COLS, wide):
        columns = slice(start, start + wide)
        product = jnp.dot(
            weight_ref[:, :rows], shifted_own[:, columns], preferred_element_type=jnp.float32
        ) + jnp.dot(
            weight_ref[:, rows:], shifted_rest[:, columns], preferred_element_type=jnp.float32
        )
        inside = product[:classes]
        wrapped = None
        for rotation in range(1, ROTS):
            offset = ANG_STEP * rotation % ANG
            turned = jnp.concatenate(
                [
                    pltpu.roll(
                        product[rotation * classes : (rotation + 1) * classes, s : s + LANES],
                        LANES - offset,
                        1,
                    )
                    for s in range(0, wide, LANES)
                ],
                axis=1,
            )
            within = lane < ANG - offset
            inside = inside + jnp.where(within, turned, 0.0)
            over = jnp.where(within, 0.0, turned)
            wrapped = over if wrapped is None else wrapped + over
        wrapped = jnp.concatenate(
            [pltpu.roll(wrapped[:, s : s + LANES], ANG, 1) for s in range(0, wide, LANES)], axis=1
        )
        sums_ref[:, columns] = inside + wrapped
    padded = own_out.shape[1]
    lane = lane_index((classes, padded))
    high = mass.astype(jnp.bfloat16).astype(jnp.float32)
    middle = (mass - high).astype(jnp.bfloat16).astype(jnp.float32)
    low = (mass - high - middle).astype(jnp.bfloat16).astype(jnp.float32)
    tail = jnp.where(
        lane == width, high, jnp.where(lane == width + 1, middle, jnp.where(lane == width + 2, low, 0.0))
    )
    for dom in range(doms):
        first = width * dom
        base = first // LANES * LANES
        span = -(-(first - base + width) // LANES) * LANES
        part = sums_ref[:, base : base + span]
        if first > base:
            part = pltpu.roll(part, span - (first - base), 1)
        if span < padded:
            part = jnp.concatenate([part, jnp.zeros((classes, padded - span), jnp.float32)], axis=1)
        parts_ref[dom] = jnp.where(lane < width, part[:, :padded], tail)
    place = place_ref[0]
    own_out[...] = parts_ref[place]
    for distance in range(1, doms):
        sends[distance - 1][...] = parts_ref[place ^ distance].astype(jnp.bfloat16)


def final_kernel(width, own_ref, *refs):
    received, sums_ref, weights_ref = refs[:-2], refs[-2], refs[-1]
    total = own_ref[...]
    for ref in received:
        total = total + ref[...].astype(jnp.float32)
    sums_ref[...] = total[:, :width]
    lane = lane_index(total.shape)
    mass = jnp.sum(
        jnp.where((lane >= width) & (lane < width + 3), total, 0.0), axis=1, keepdims=True
    )
    weights_ref[...] = to_lanes(mass, total.shape[0])


def call(kernel, shapes, scratch, flops, moved, *args, smem=()):
    vmem = pl.BlockSpec(memory_space=pltpu.VMEM)
    scalar = pl.BlockSpec(memory_space=pltpu.SMEM)
    return pl.pallas_call(
        kernel,
        out_shape=shapes,
        in_specs=[scalar if i in smem else vmem for i in range(len(args))],
        out_specs=[vmem] * len(shapes),
        scratch_shapes=scratch,
        compiler_params=pltpu.CompilerParams(vmem_limit_bytes=VMEM_LIMIT),
        cost_estimate=pl.CostEstimate(flops=flops, bytes_accessed=moved, transcendentals=0),
    )(*args)


def body(particle_spectra, class_spectra, shift_index, prior_rotation, particle_group, group_scale):
    count = lax.axis_size("cls")
    doms = lax.axis_size("dom")
    particles, candidates = shift_index.shape
    classes = class_spectra.shape[0]
    rows = particles * candidates
    width = COLS // doms
    padded = -(-(width + 3) // LANES) * LANES
    f32, bf16 = jnp.float32, jnp.bfloat16
    shape = jax.ShapeDtypeStruct

    (packed,) = call(
        pack_kernel,
        [shape((particles, COLS + META), bf16)],
        [],
        particles * COLS,
        4 * particles * COLS,
        particle_spectra, shift_index, prior_rotation[None, :], particle_group[None, :],
    )
    others = [exchange(packed, "cls", distance) for distance in range(1, count)]
    table = jnp.asarray(phase_table())
    scales = group_scale[None, :]
    stat_rows = -(-2 * count // 8) * 8
    work = 2 * rows * COLS * (ROTS * classes + 256)
    shifted_own, exp_own, stats_own, rotated, norm = call(
        own_kernel,
        [
            shape((rows, COLS), bf16),
            shape((ROTS * classes, rows), f32),
            shape((8, LANES), f32),
            shape((ROTS * classes, COLS), bf16),
            shape((classes, LANES), f32),
        ],
        [],
        work,
        4 * rows * COLS,
        packed, class_spectra, table, scales,
    )
    rest = (count - 1) * rows
    shifted_rest, exp_rest, stats, scale_rows = call(
        functools.partial(rest_kernel, count),
        [
            shape((rest, COLS), bf16),
            shape((ROTS * classes, rest), f32),
            shape((stat_rows, LANES), f32),
            shape((-(-count // 8) * 8, LANES), f32),
        ],
        [],
        work * (count - 1),
        4 * rest * COLS,
        *others, table, scales, rotated, norm, stats_own,
    )
    all_stats = [stats] + [exchange(stats, "cls", distance) for distance in range(1, count)]
    place = lax.axis_index("dom").astype(jnp.int32).reshape(1)
    own, *sends = call(
        functools.partial(sums_kernel, count, doms, width),
        [shape((classes, padded), f32)] + [shape((classes, padded), bf16)] * (doms - 1),
        [
            pltpu.VMEM((ROTS * classes, count * rows), bf16),
            pltpu.VMEM((classes, COLS), f32),
            pltpu.VMEM((doms, classes, padded), f32),
        ],
        2 * count * rows * COLS * ROTS * classes,
        4 * count * rows * COLS,
        *all_stats, place, scale_rows, exp_own, exp_rest, shifted_own, shifted_rest,
        smem=(count,),
    )
    received = [exchange(sends[distance - 1], "dom", distance) for distance in range(1, doms)]
    class_sums, class_weights = call(
        functools.partial(final_kernel, width),
        [shape((classes, width), f32), shape((1, classes), f32)],
        [],
        doms * classes * padded,
        4 * doms * classes * padded,
        own, *received,
    )
    return class_sums, class_weights.reshape(classes)


def solution(mesh):
    placed = (
        P(("groups", "dom", "cls"), None),
        P(("groups", "cls"), None),
        P(("groups", "dom", "cls"), None),
        P(("groups", "dom", "cls")),
        P(("groups", "dom", "cls")),
        P("groups"),
    )
    return jax.shard_map(
        body,
        mesh=mesh,
        in_specs=placed,
        out_specs=(P(("groups", "cls"), "dom"), P(("groups", "cls"))),
        check_vma=False,
    )
```

```python
import functools
import math

import jax
import jax.numpy as jnp
import ml_dtypes
import numpy as np
from jax import lax
from jax.experimental import pallas as pl
from jax.experimental.pallas import tpu as pltpu
from jax.sharding import PartitionSpec as P

CYCLES = 18
ANG = 64
IMG = 64
ANG_STEP = 1
ROTS = 8
SHIFT_R = 5
SHIFTW = 11
HALF = CYCLES * ANG
COLS = 2 * HALF
LANES = 128
META = LANES
ROT_PRIOR = 0.5
VMEM_LIMIT = 20 * 1024 * 1024


def phase_table():
    angles = np.arange(ANG) * (2.0 * math.pi / ANG)
    radius = np.arange(CYCLES) + 1.0
    fx = (radius[:, None] * np.cos(angles)[None, :]).reshape(-1)
    fy = (radius[:, None] * np.sin(angles)[None, :]).reshape(-1)
    offsets = np.arange(SHIFTW * SHIFTW)
    dx = offsets % SHIFTW - SHIFT_R
    dy = offsets // SHIFTW - SHIFT_R
    phase = (2.0 * math.pi / IMG) * (dx[:, None] * fx[None, :] + dy[:, None] * fy[None, :])
    values = np.zeros((LANES, COLS), np.float32)
    values[: SHIFTW * SHIFTW] = np.concatenate([np.cos(phase), np.sin(phase)], axis=1)
    high = values.astype(ml_dtypes.bfloat16)
    low = (values - high.astype(np.float32)).astype(ml_dtypes.bfloat16)
    return np.concatenate([high, low], axis=0)


def exchange(array, axis, distance):
    return lax.ppermute(array, axis, [(i, i ^ distance) for i in range(lax.axis_size(axis))])


def lane_index(shape):
    return lax.broadcasted_iota(jnp.int32, shape, len(shape) - 1)


def rotate_classes(class_ref, rotated_ref, norm_ref):
    classes = class_ref.shape[0]
    total = jnp.zeros((classes, LANES), jnp.float32)
    lane = lane_index((classes, LANES)) % ANG
    for tile in range(COLS // LANES):
        columns = slice(tile * LANES, (tile + 1) * LANES)
        value = class_ref[:, columns].astype(jnp.float32)
        total = total + value * value
        other = pltpu.roll(value, ANG, 1)
        for rotation in range(ROTS):
            offset = ANG_STEP * rotation % ANG
            turned = value
            if offset:
                turned = pltpu.roll(jnp.where(lane < ANG - offset, value, other), offset, 1)
            rotated_ref[rotation * classes : (rotation + 1) * classes, columns] = turned.astype(
                jnp.bfloat16
            )
    norm_ref[...] = jnp.broadcast_to(jnp.sum(total, axis=1, keepdims=True), (classes, LANES))


def to_lanes(column, width):
    n = column.shape[0]
    row = lax.broadcasted_iota(jnp.int32, (n, width), 0)
    return jnp.sum(
        jnp.where(lane_index((n, width)) % n == row, column, 0.0), axis=0, keepdims=True
    )


def fold_lanes(row, period, combine):
    result = row[:, :LANES]
    for part in range(1, row.shape[1] // LANES):
        result = combine(result, row[:, part * LANES : (part + 1) * LANES])
    step = LANES // 2
    while step >= period:
        result = combine(result, pltpu.roll(result, step, 1))
        step //= 2
    return result


def to_column(row):
    n = row.shape[1]
    diagonal = lax.broadcasted_iota(jnp.int32, (n, n), 0) == lane_index((n, n))
    return jnp.sum(jnp.where(diagonal, row, 0.0), axis=1, keepdims=True)


def pack_kernel(particle_hbm, index_hbm, prior_hbm, group_hbm, packed_ref, index_ref, prior_ref, group_ref, sems):
    particles, candidates = index_ref.shape
    copies = [
        pltpu.make_async_copy(source, target, sems.at[i])
        for i, (source, target) in enumerate(
            [
                (index_hbm, index_ref),
                (prior_hbm, prior_ref),
                (group_hbm, group_ref),
                (particle_hbm, packed_ref.at[:, pl.ds(0, COLS)]),
            ]
        )
    ]
    for copy in copies:
        copy.start()
    for copy in copies[:3]:
        copy.wait()
    lane = lane_index((particles, META))
    index = jnp.concatenate(
        [index_ref[...].astype(jnp.float32), jnp.zeros((particles, META - candidates), jnp.float32)],
        axis=1,
    )
    prior = to_column(prior_ref[...].astype(jnp.float32))
    group = to_column(group_ref[...].astype(jnp.float32))
    meta = jnp.where(lane == candidates, prior, jnp.where(lane == candidates + 1, group, index))
    packed_ref[:, COLS:] = meta.astype(jnp.bfloat16)
    copies[3].wait()


def score_block(block_ref, table_ref, scale_ref, rotated_ref, norm_ref, shifted_ref, out):
    particles = block_ref.shape[0]
    classes = norm_ref.shape[0]
    candidates = shifted_ref.shape[0] // particles
    rows = particles * candidates
    repeat = rows // LANES
    meta = block_ref[:, COLS : COLS + META].astype(jnp.float32)
    index = meta[:, :candidates].astype(jnp.int32)
    lane = lane_index((particles, LANES))
    hot = jnp.concatenate(
        [
            jnp.where(index[:, t : t + 1] == lane, 1.0, 0.0).astype(jnp.bfloat16)
            for t in range(candidates)
        ],
        axis=0,
    )
    hot = jnp.concatenate([hot, hot], axis=1)
    groups = scale_ref.shape[1]
    group = meta[:, candidates + 1 : candidates + 2].astype(jnp.int32)
    scale_column = jnp.sum(
        jnp.where(group == lane_index((particles, groups)), scale_ref[...], 0.0),
        axis=1,
        keepdims=True,
    )
    scale = to_lanes(scale_column, rows)
    prior = to_lanes(meta[:, candidates : candidates + 1], rows)
    width = 3 * LANES
    for start in range(0, HALF, width):
        real_columns = slice(start, start + width)
        imag_columns = slice(HALF + start, HALF + start + width)
        cosine = jnp.dot(hot, table_ref[:, real_columns], preferred_element_type=jnp.float32)
        sine = jnp.dot(hot, table_ref[:, imag_columns], preferred_element_type=jnp.float32)
        real = block_ref[:, real_columns].astype(jnp.float32)
        imag = block_ref[:, imag_columns].astype(jnp.float32)
        for t in range(candidates):
            part = slice(t * particles, (t + 1) * particles)
            c, s = cosine[part], sine[part]
            shifted_ref[part, real_columns] = (real * c - imag * s).astype(jnp.bfloat16)
            shifted_ref[part, imag_columns] = (real * s + imag * c).astype(jnp.bfloat16)
    product = lax.dot_general(
        rotated_ref[...],
        shifted_ref[...],
        (((1,), (1,)), ((), ())),
        preferred_element_type=jnp.float32,
    )
    norm = jnp.concatenate([norm_ref[...]] * repeat, axis=1)
    half_square = 0.5 * scale * scale
    scores = []
    highest = None
    for rotation in range(ROTS):
        distance = jnp.abs(rotation - prior)
        score = (
            scale * product[rotation * classes : (rotation + 1) * classes]
            - half_square * norm
            - ROT_PRIOR * (distance * distance)
        )
        scores.append(score)
        peak = jnp.max(score, axis=0, keepdims=True)
        highest = peak if highest is None else jnp.maximum(highest, peak)
    highest = fold_lanes(highest, particles, jnp.maximum)
    wide = jnp.concatenate([highest] * repeat, axis=1)
    total = None
    for rotation in range(ROTS):
        value = jnp.exp(scores[rotation] - wide)
        out(rotation, value)
        added = jnp.sum(value, axis=0, keepdims=True)
        total = added if total is None else total + added
    total = fold_lanes(total, particles, jnp.add)
    return highest, total, scale[:, :LANES]


def own_kernel(
    count, block_ref, class_hbm, table_hbm, scale_hbm,
    shifted_ref, exp_ref, stats_ref, rotated_ref, norm_ref, table_ref, scale_ref,
    class_ref, sems,
):
    copies = [
        pltpu.make_async_copy(source, target, sems.at[i])
        for i, (source, target) in enumerate(
            [(class_hbm, class_ref), (scale_hbm, scale_ref), (table_hbm, table_ref)]
        )
    ]
    for copy in copies:
        copy.start()
    copies[0].wait()
    rotate_classes(class_ref, rotated_ref, norm_ref)
    copies[1].wait()
    copies[2].wait()
    classes = norm_ref.shape[0]

    rows = exp_ref.shape[1] // count

    def out(rotation, value):
        exp_ref[rotation * classes : (rotation + 1) * classes, 0:rows] = value

    highest, total, scale = score_block(
        block_ref, table_ref, scale_ref, rotated_ref, norm_ref, shifted_ref.at[0:rows, :], out
    )
    stats_ref[...] = jnp.zeros_like(stats_ref)
    stats_ref[0:1, :] = highest
    stats_ref[1:2, :] = total
    stats_ref[2 * count : 2 * count + 1, :] = scale


def rest_kernel(count, *refs):
    blocks = refs[: count - 1]
    table_ref, scale_ref, rotated_ref, norm_ref, own_ref = refs[count - 1 : count + 4]
    shifted_ref, exp_ref, stats_ref = refs[count + 6 :]
    classes = norm_ref.shape[0]
    rows = exp_ref.shape[1] // count
    stats_ref[...] = own_ref[...]
    for block in range(1, count):
        part = slice(block * rows, (block + 1) * rows)

        def out(rotation, value):
            exp_ref[rotation * classes : (rotation + 1) * classes, part] = value

        highest, total, scale = score_block(
            blocks[block - 1], table_ref, scale_ref, rotated_ref, norm_ref,
            shifted_ref.at[part, :], out,
        )
        stats_ref[2 * block : 2 * block + 1, :] = highest
        stats_ref[2 * block + 1 : 2 * block + 2, :] = total
        stats_ref[2 * count + block : 2 * count + block + 1, :] = scale


def sums_kernel(count, doms, width, *refs):
    stats = refs[:count]
    exp_ref, shifted_ref = refs[count : count + 2]
    own_out = refs[count + 2]
    sends = refs[count + 3 : count + 2 + doms]
    weight_ref, sums_ref, parts_ref = refs[count + 2 + doms :]
    rows = exp_ref.shape[1] // count
    repeat = rows // LANES
    classes = weight_ref.shape[0] // ROTS
    mass = jnp.zeros((classes, rows), jnp.float32)
    for block in range(count):
        highs = [stats[c][2 * (c ^ block) : 2 * (c ^ block) + 1, :] for c in range(count)]
        lows = [stats[c][2 * (c ^ block) + 1 : 2 * (c ^ block) + 2, :] for c in range(count)]
        top = functools.reduce(jnp.maximum, highs)
        total = functools.reduce(jnp.add, [l * jnp.exp(h - top) for h, l in zip(highs, lows)])
        factor = jnp.exp(highs[0] - top) / total
        scale = stats[0][2 * count + block : 2 * count + block + 1, :]
        factor = jnp.concatenate([factor] * repeat, axis=1)
        scale = jnp.concatenate([scale] * repeat, axis=1)
        for rotation in range(ROTS):
            rotated = slice(rotation * classes, (rotation + 1) * classes)
            value = exp_ref[rotated, block * rows : (block + 1) * rows]
            weight = value * factor * scale
            mass = mass + weight * scale
            weight_ref[rotated, block * rows : (block + 1) * rows] = weight.astype(jnp.bfloat16)
    mass = jnp.sum(mass, axis=1, keepdims=True)
    wide = 2 * LANES
    lane = lane_index((classes, wide)) % ANG
    for start in range(0, COLS, wide):
        columns = slice(start, start + wide)
        product = jnp.dot(
            weight_ref[...], shifted_ref[:, columns], preferred_element_type=jnp.float32
        )
        inside = product[:classes]
        wrapped = None
        for rotation in range(1, ROTS):
            offset = ANG_STEP * rotation % ANG
            turned = jnp.concatenate(
                [
                    pltpu.roll(
                        product[rotation * classes : (rotation + 1) * classes, s : s + LANES],
                        LANES - offset,
                        1,
                    )
                    for s in range(0, wide, LANES)
                ],
                axis=1,
            )
            within = lane < ANG - offset
            inside = inside + jnp.where(within, turned, 0.0)
            over = jnp.where(within, 0.0, turned)
            wrapped = over if wrapped is None else wrapped + over
        wrapped = jnp.concatenate(
            [pltpu.roll(wrapped[:, s : s + LANES], ANG, 1) for s in range(0, wide, LANES)], axis=1
        )
        sums_ref[:, columns] = inside + wrapped
    padded = own_out.shape[1]
    lane = lane_index((classes, padded))
    high = mass.astype(jnp.bfloat16).astype(jnp.float32)
    middle = (mass - high).astype(jnp.bfloat16).astype(jnp.float32)
    low = (mass - high - middle).astype(jnp.bfloat16).astype(jnp.float32)
    tail = jnp.where(
        lane == width, high, jnp.where(lane == width + 1, middle, jnp.where(lane == width + 2, low, 0.0))
    )
    for dom in range(doms):
        first = width * dom
        base = first // LANES * LANES
        span = -(-(first - base + width) // LANES) * LANES
        part = sums_ref[:, base : base + span]
        if first > base:
            part = pltpu.roll(part, span - (first - base), 1)
        if span < padded:
            part = jnp.concatenate([part, jnp.zeros((classes, padded - span), jnp.float32)], axis=1)
        parts_ref[dom] = jnp.where(lane < width, part[:, :padded], tail)
    place = lax.axis_index("dom")
    own_out[...] = parts_ref[place]
    for distance in range(1, doms):
        sends[distance - 1][...] = parts_ref[place ^ distance].astype(jnp.bfloat16)


def final_kernel(width, own_ref, *refs):
    received, sums_ref, weights_ref = refs[:-2], refs[-2], refs[-1]
    total = own_ref[...]
    for ref in received:
        total = total + ref[...].astype(jnp.float32)
    sums_ref[...] = total[:, :width]
    lane = lane_index(total.shape)
    mass = jnp.sum(
        jnp.where((lane >= width) & (lane < width + 3), total, 0.0), axis=1, keepdims=True
    )
    weights_ref[...] = to_lanes(mass, total.shape[0])


def call(kernel, shapes, scratch, flops, moved, *args, smem=(), hbm=(), chip=(), pinned=True, aliases=None):
    vmem = pl.BlockSpec(memory_space=pltpu.VMEM)
    scalar = pl.BlockSpec(memory_space=pltpu.SMEM)
    place = pl.BlockSpec(memory_space=pltpu.HBM)
    args = [
        pltpu.with_memory_space_constraint(a, pltpu.HBM) if i in hbm
        else pltpu.with_memory_space_constraint(a, pltpu.VMEM) if i in chip
        else a
        for i, a in enumerate(args)
    ]
    return pl.pallas_call(
        kernel,
        out_shape=[pltpu.VMEM(s.shape, s.dtype) if pinned else s for s in shapes],
        in_specs=[scalar if i in smem else place if i in hbm else vmem for i in range(len(args))],
        out_specs=[vmem] * len(shapes),
        scratch_shapes=scratch,
        input_output_aliases=aliases or {},
        compiler_params=pltpu.CompilerParams(vmem_limit_bytes=VMEM_LIMIT),
        cost_estimate=pl.CostEstimate(flops=flops, bytes_accessed=moved, transcendentals=0),
    )(*args)


def body(particle_spectra, class_spectra, shift_index, prior_rotation, particle_group, group_scale):
    count = lax.axis_size("cls")
    doms = lax.axis_size("dom")
    particles, candidates = shift_index.shape
    classes = class_spectra.shape[0]
    rows = particles * candidates
    width = COLS // doms
    padded = -(-(width + 3) // LANES) * LANES
    f32, bf16 = jnp.float32, jnp.bfloat16
    shape = jax.ShapeDtypeStruct

    (packed,) = call(
        pack_kernel,
        [shape((particles, COLS + META), bf16)],
        [
            pltpu.VMEM((particles, candidates), jnp.int32),
            pltpu.VMEM((1, particles), jnp.int32),
            pltpu.VMEM((1, particles), jnp.int32),
            pltpu.SemaphoreType.DMA((4,)),
        ],
        particles * COLS,
        4 * particles * COLS,
        particle_spectra, shift_index, prior_rotation[None, :], particle_group[None, :],
        hbm=(0, 1, 2, 3),
    )
    others = [exchange(packed, "cls", distance) for distance in range(1, count)]
    table = jnp.asarray(phase_table())
    scales = group_scale[None, :]
    stat_rows = -(-3 * count // 8) * 8
    work = 2 * rows * COLS * (ROTS * classes + 256)
    stats_shape = shape((stat_rows, LANES), f32)
    shifted_shape = shape((count * rows, COLS), bf16)
    exp_shape = shape((ROTS * classes, count * rows), f32)
    shifted, exps, stats_own, rotated, norm, table_on_chip, scales_on_chip = call(
        functools.partial(own_kernel, count),
        [
            shifted_shape,
            exp_shape,
            stats_shape,
            shape((ROTS * classes, COLS), bf16),
            shape((classes, LANES), f32),
            shape(table.shape, bf16),
            shape(scales.shape, f32),
        ],
        [pltpu.VMEM((classes, COLS), bf16), pltpu.SemaphoreType.DMA((3,))],
        work,
        4 * rows * COLS,
        packed, class_spectra, table, scales,
        hbm=(1, 2, 3),
    )
    shifted, exps, stats = call(
        functools.partial(rest_kernel, count),
        [shifted_shape, exp_shape, stats_shape],
        [],
        work * (count - 1),
        4 * (count - 1) * rows * COLS,
        *others, table_on_chip, scales_on_chip, rotated, norm, stats_own, shifted, exps,
        aliases={count + 4: 0, count + 5: 1},
        chip=(count + 4, count + 5),
    )
    all_stats = [stats] + [exchange(stats, "cls", distance) for distance in range(1, count)]
    own, *sends = call(
        functools.partial(sums_kernel, count, doms, width),
        [shape((classes, padded), f32)] + [shape((classes, padded), bf16)] * (doms - 1),
        [
            pltpu.VMEM((ROTS * classes, count * rows), bf16),
            pltpu.VMEM((classes, COLS), f32),
            pltpu.VMEM((doms, classes, padded), f32),
        ],
        2 * count * rows * COLS * ROTS * classes,
        4 * count * rows * COLS,
        *all_stats, exps, shifted,
        chip=(count, count + 1),
    )
    received = [exchange(sends[distance - 1], "dom", distance) for distance in range(1, doms)]
    class_sums, class_weights = call(
        functools.partial(final_kernel, width),
        [shape((classes, width), f32), shape((1, classes), f32)],
        [],
        doms * classes * padded,
        4 * doms * classes * padded,
        own, *received,
        pinned=False,
    )
    return class_sums, class_weights.reshape(classes)


def solution(mesh):
    placed = (
        P(("groups", "dom", "cls"), None),
        P(("groups", "cls"), None),
        P(("groups", "dom", "cls"), None),
        P(("groups", "dom", "cls")),
        P(("groups", "dom", "cls")),
        P("groups"),
    )
    return jax.shard_map(
        body,
        mesh=mesh,
        in_specs=placed,
        out_specs=(P(("groups", "cls"), "dom"), P(("groups", "cls"))),
        check_vma=False,
    )
```

```python
import functools
import math

import jax
import jax.numpy as jnp
import ml_dtypes
import numpy as np
from jax import lax
from jax.experimental import pallas as pl
from jax.experimental.pallas import tpu as pltpu
from jax.sharding import PartitionSpec as P

CYCLES = 18
ANG = 64
IMG = 64
ANG_STEP = 1
ROTS = 8
SHIFT_R = 5
SHIFTW = 11
HALF = CYCLES * ANG
COLS = 2 * HALF
LANES = 128
META = LANES
ROT_PRIOR = 0.5
VMEM_LIMIT = 20 * 1024 * 1024


def phase_table():
    angles = np.arange(ANG) * (2.0 * math.pi / ANG)
    radius = np.arange(CYCLES) + 1.0
    fx = (radius[:, None] * np.cos(angles)[None, :]).reshape(-1)
    fy = (radius[:, None] * np.sin(angles)[None, :]).reshape(-1)
    offsets = np.arange(SHIFTW * SHIFTW)
    dx = offsets % SHIFTW - SHIFT_R
    dy = offsets // SHIFTW - SHIFT_R
    phase = (2.0 * math.pi / IMG) * (dx[:, None] * fx[None, :] + dy[:, None] * fy[None, :])
    values = np.zeros((LANES, COLS), np.float32)
    values[: SHIFTW * SHIFTW] = np.concatenate([np.cos(phase), np.sin(phase)], axis=1)
    high = values.astype(ml_dtypes.bfloat16)
    low = (values - high.astype(np.float32)).astype(ml_dtypes.bfloat16)
    return np.concatenate([high, low], axis=0)


def exchange(array, axis, distance):
    return lax.ppermute(array, axis, [(i, i ^ distance) for i in range(lax.axis_size(axis))])


def lane_index(shape):
    return lax.broadcasted_iota(jnp.int32, shape, len(shape) - 1)


def rotate_classes(class_ref, rotated_ref, norm_ref):
    classes = class_ref.shape[0]
    total = jnp.zeros((classes, LANES), jnp.float32)
    lane = lane_index((classes, LANES)) % ANG
    for tile in range(COLS // LANES):
        columns = slice(tile * LANES, (tile + 1) * LANES)
        value = class_ref[:, columns].astype(jnp.float32)
        total = total + value * value
        other = pltpu.roll(value, ANG, 1)
        for rotation in range(ROTS):
            offset = ANG_STEP * rotation % ANG
            turned = value
            if offset:
                turned = pltpu.roll(jnp.where(lane < ANG - offset, value, other), offset, 1)
            rotated_ref[rotation * classes : (rotation + 1) * classes, columns] = turned.astype(
                jnp.bfloat16
            )
    norm_ref[...] = jnp.broadcast_to(jnp.sum(total, axis=1, keepdims=True), (classes, LANES))


def to_lanes(column, width):
    n = column.shape[0]
    row = lax.broadcasted_iota(jnp.int32, (n, width), 0)
    return jnp.sum(
        jnp.where(lane_index((n, width)) % n == row, column, 0.0), axis=0, keepdims=True
    )


def fold_lanes(row, period, combine):
    result = row[:, :LANES]
    for part in range(1, row.shape[1] // LANES):
        result = combine(result, row[:, part * LANES : (part + 1) * LANES])
    step = LANES // 2
    while step >= period:
        result = combine(result, pltpu.roll(result, step, 1))
        step //= 2
    return result


def to_column(row):
    n = row.shape[1]
    diagonal = lax.broadcasted_iota(jnp.int32, (n, n), 0) == lane_index((n, n))
    return jnp.sum(jnp.where(diagonal, row, 0.0), axis=1, keepdims=True)


def pack_kernel(
    particle_hbm, index_hbm, prior_hbm, group_hbm, class_hbm, scale_hbm,
    packed_ref, class_ref, scale_ref, index_ref, prior_ref, group_ref, sems,
):
    particles, candidates = index_ref.shape
    copies = [
        pltpu.make_async_copy(source, target, sems.at[i])
        for i, (source, target) in enumerate(
            [
                (index_hbm, index_ref),
                (prior_hbm, prior_ref),
                (group_hbm, group_ref),
                (particle_hbm, packed_ref.at[:, pl.ds(0, COLS)]),
                (class_hbm, class_ref),
                (scale_hbm, scale_ref),
            ]
        )
    ]
    for copy in copies:
        copy.start()
    for copy in copies[:3]:
        copy.wait()
    lane = lane_index((particles, META))
    index = jnp.concatenate(
        [index_ref[...].astype(jnp.float32), jnp.zeros((particles, META - candidates), jnp.float32)],
        axis=1,
    )
    prior = to_column(prior_ref[...].astype(jnp.float32))
    group = to_column(group_ref[...].astype(jnp.float32))
    meta = jnp.where(lane == candidates, prior, jnp.where(lane == candidates + 1, group, index))
    packed_ref[:, COLS:] = meta.astype(jnp.bfloat16)
    for copy in copies[3:]:
        copy.wait()


def score_block(block_ref, table_ref, scale_ref, rotated_ref, norm_ref, shifted_ref, out):
    particles = block_ref.shape[0]
    classes = norm_ref.shape[0]
    candidates = shifted_ref.shape[0] // particles
    rows = particles * candidates
    repeat = rows // LANES
    meta = block_ref[:, COLS : COLS + META].astype(jnp.float32)
    index = meta[:, :candidates].astype(jnp.int32)
    lane = lane_index((particles, LANES))
    hot = jnp.concatenate(
        [
            jnp.where(index[:, t : t + 1] == lane, 1.0, 0.0).astype(jnp.bfloat16)
            for t in range(candidates)
        ],
        axis=0,
    )
    hot = jnp.concatenate([hot, hot], axis=1)
    groups = scale_ref.shape[1]
    group = meta[:, candidates + 1 : candidates + 2].astype(jnp.int32)
    scale_column = jnp.sum(
        jnp.where(group == lane_index((particles, groups)), scale_ref[...], 0.0),
        axis=1,
        keepdims=True,
    )
    scale = to_lanes(scale_column, rows)
    prior = to_lanes(meta[:, candidates : candidates + 1], rows)
    width = 3 * LANES
    for start in range(0, HALF, width):
        real_columns = slice(start, start + width)
        imag_columns = slice(HALF + start, HALF + start + width)
        cosine = jnp.dot(hot, table_ref[:, real_columns], preferred_element_type=jnp.float32)
        sine = jnp.dot(hot, table_ref[:, imag_columns], preferred_element_type=jnp.float32)
        real = block_ref[:, real_columns].astype(jnp.float32)
        imag = block_ref[:, imag_columns].astype(jnp.float32)
        for t in range(candidates):
            part = slice(t * particles, (t + 1) * particles)
            c, s = cosine[part], sine[part]
            shifted_ref[part, real_columns] = (real * c - imag * s).astype(jnp.bfloat16)
            shifted_ref[part, imag_columns] = (real * s + imag * c).astype(jnp.bfloat16)
    product = lax.dot_general(
        rotated_ref[...],
        shifted_ref[...],
        (((1,), (1,)), ((), ())),
        preferred_element_type=jnp.float32,
    )
    norm = jnp.concatenate([norm_ref[...]] * repeat, axis=1)
    half_square = 0.5 * scale * scale
    scores = []
    highest = None
    for rotation in range(ROTS):
        distance = jnp.abs(rotation - prior)
        score = (
            scale * product[rotation * classes : (rotation + 1) * classes]
            - half_square * norm
            - ROT_PRIOR * (distance * distance)
        )
        scores.append(score)
        peak = jnp.max(score, axis=0, keepdims=True)
        highest = peak if highest is None else jnp.maximum(highest, peak)
    highest = fold_lanes(highest, particles, jnp.maximum)
    wide = jnp.concatenate([highest] * repeat, axis=1)
    total = None
    for rotation in range(ROTS):
        value = jnp.exp(scores[rotation] - wide)
        out(rotation, value)
        added = jnp.sum(value, axis=0, keepdims=True)
        total = added if total is None else total + added
    total = fold_lanes(total, particles, jnp.add)
    return highest, total, scale[:, :LANES]


def own_kernel(
    count, block_ref, class_ref, table_hbm, scale_ref,
    shifted_ref, exp_ref, stats_ref, rotated_ref, norm_ref, table_ref, sem,
):
    copy = pltpu.make_async_copy(table_hbm, table_ref, sem)
    copy.start()
    rotate_classes(class_ref, rotated_ref, norm_ref)
    copy.wait()
    classes = norm_ref.shape[0]
    rows = exp_ref.shape[1] // count

    def out(rotation, value):
        exp_ref[rotation * classes : (rotation + 1) * classes, 0:rows] = value

    highest, total, scale = score_block(
        block_ref, table_ref, scale_ref, rotated_ref, norm_ref, shifted_ref.at[0:rows, :], out
    )
    stats_ref[...] = jnp.zeros_like(stats_ref)
    stats_ref[0:1, :] = highest
    stats_ref[1:2, :] = total
    stats_ref[2 * count : 2 * count + 1, :] = scale


def rest_kernel(count, *refs):
    blocks = refs[: count - 1]
    table_ref, scale_ref, rotated_ref, norm_ref, own_ref = refs[count - 1 : count + 4]
    shifted_ref, exp_ref, stats_ref = refs[count + 6 :]
    classes = norm_ref.shape[0]
    rows = exp_ref.shape[1] // count
    stats_ref[...] = own_ref[...]
    for block in range(1, count):
        part = slice(block * rows, (block + 1) * rows)

        def out(rotation, value):
            exp_ref[rotation * classes : (rotation + 1) * classes, part] = value

        highest, total, scale = score_block(
            blocks[block - 1], table_ref, scale_ref, rotated_ref, norm_ref,
            shifted_ref.at[part, :], out,
        )
        stats_ref[2 * block : 2 * block + 1, :] = highest
        stats_ref[2 * block + 1 : 2 * block + 2, :] = total
        stats_ref[2 * count + block : 2 * count + block + 1, :] = scale


def weigh(count, stats, exp_ref, weight_ref):
    rows = exp_ref.shape[1] // count
    repeat = rows // LANES
    classes = weight_ref.shape[0] // ROTS
    mass = jnp.zeros((classes, rows), jnp.float32)
    for block in range(count):
        highs = [stats[c][2 * (c ^ block) : 2 * (c ^ block) + 1, :] for c in range(count)]
        lows = [stats[c][2 * (c ^ block) + 1 : 2 * (c ^ block) + 2, :] for c in range(count)]
        top = functools.reduce(jnp.maximum, highs)
        total = functools.reduce(jnp.add, [l * jnp.exp(h - top) for h, l in zip(highs, lows)])
        factor = jnp.exp(highs[0] - top) / total
        scale = stats[0][2 * count + block : 2 * count + block + 1, :]
        factor = jnp.concatenate([factor] * repeat, axis=1)
        scale = jnp.concatenate([scale] * repeat, axis=1)
        part = slice(block * rows, (block + 1) * rows)
        for rotation in range(ROTS):
            rotated = slice(rotation * classes, (rotation + 1) * classes)
            weight = exp_ref[rotated, part] * factor * scale
            mass = mass + weight * scale
            weight_ref[rotated, part] = weight.astype(jnp.bfloat16)
    return jnp.broadcast_to(jnp.sum(mass, axis=1, keepdims=True), (classes, LANES))


def sum_block(doms, width, distance, weight_ref, shifted_ref, mass, out_ref):
    classes, extent = out_ref.shape
    padded = -(-extent // LANES) * LANES
    place = lax.axis_index("dom") ^ distance
    first = place * width
    shifts = sorted({width * dom % LANES for dom in range(doms)})
    span = -(-(shifts[-1] + width) // LANES) * LANES
    base = first // LANES * LANES
    tiles = []
    for start in range(0, span, 2 * LANES):
        wide = min(2 * LANES, span - start)
        columns = pl.ds(pl.multiple_of(base + start, LANES), wide)
        product = jnp.dot(
            weight_ref[...], shifted_ref[:, columns], preferred_element_type=jnp.float32
        )
        for part in range(0, wide, LANES):
            lane = lane_index((classes, LANES)) % ANG
            inside = product[:classes, part : part + LANES]
            wrapped = None
            for rotation in range(1, ROTS):
                offset = ANG_STEP * rotation % ANG
                turned = pltpu.roll(
                    product[rotation * classes : (rotation + 1) * classes, part : part + LANES],
                    LANES - offset,
                    1,
                )
                within = lane < ANG - offset
                inside = inside + jnp.where(within, turned, 0.0)
                over = jnp.where(within, 0.0, turned)
                wrapped = over if wrapped is None else wrapped + over
            tiles.append(inside + pltpu.roll(wrapped, ANG, 1))
    total = jnp.concatenate(tiles, axis=1)
    aligned = total
    for shift in shifts:
        if shift:
            aligned = jnp.where(first - base == shift, pltpu.roll(total, span - shift, 1), aligned)
    if span < padded:
        aligned = jnp.concatenate(
            [aligned, jnp.zeros((classes, padded - span), jnp.float32)], axis=1
        )
    mass = jnp.concatenate([mass] * (padded // LANES), axis=1)
    high = mass.astype(jnp.bfloat16).astype(jnp.float32)
    middle = (mass - high).astype(jnp.bfloat16).astype(jnp.float32)
    low = (mass - high - middle).astype(jnp.bfloat16).astype(jnp.float32)
    lane = lane_index((classes, padded))
    tail = jnp.where(
        lane == width, high, jnp.where(lane == width + 1, middle, jnp.where(lane == width + 2, low, 0.0))
    )
    total = jnp.where(lane < width, aligned[:, :padded], tail)
    out_ref[...] = total[:, :extent].astype(out_ref.dtype)


def first_sums_kernel(count, doms, width, distance, *refs):
    stats = refs[:count]
    exp_ref, shifted_ref, out_ref, weight_ref, mass_ref = refs[count:]
    mass = weigh(count, stats, exp_ref, weight_ref)
    mass_ref[...] = mass
    sum_block(doms, width, distance, weight_ref, shifted_ref, mass, out_ref)


def next_sums_kernel(doms, width, distance, weight_ref, shifted_ref, mass_ref, done_ref, out_ref):
    sum_block(doms, width, distance, weight_ref, shifted_ref, mass_ref[...], out_ref)


def final_kernel(width, own_ref, *refs):
    received, sums_ref, weights_ref = refs[:-2], refs[-2], refs[-1]
    total, mass = None, None
    base = width // LANES * LANES
    for ref in (own_ref, *received):
        value = ref[:, :width].astype(jnp.float32)
        total = value if total is None else total + value
        tail = ref[:, base:].astype(jnp.float32)
        lane = base + lane_index(tail.shape)
        tail = jnp.where((lane >= width) & (lane < width + 3), tail, 0.0)
        tail = jnp.sum(tail, axis=1, keepdims=True)
        mass = tail if mass is None else mass + tail
    sums_ref[...] = total
    weights_ref[...] = to_lanes(mass, total.shape[0])


def call(kernel, shapes, scratch, flops, moved, *args, smem=(), hbm=(), chip=(), pinned=True, aliases=None):
    vmem = pl.BlockSpec(memory_space=pltpu.VMEM)
    scalar = pl.BlockSpec(memory_space=pltpu.SMEM)
    place = pl.BlockSpec(memory_space=pltpu.HBM)
    args = [
        pltpu.with_memory_space_constraint(a, pltpu.HBM) if i in hbm
        else pltpu.with_memory_space_constraint(a, pltpu.VMEM) if i in chip
        else a
        for i, a in enumerate(args)
    ]
    return pl.pallas_call(
        kernel,
        out_shape=[pltpu.VMEM(s.shape, s.dtype) if pinned else s for s in shapes],
        in_specs=[scalar if i in smem else place if i in hbm else vmem for i in range(len(args))],
        out_specs=[vmem] * len(shapes),
        scratch_shapes=scratch,
        input_output_aliases=aliases or {},
        compiler_params=pltpu.CompilerParams(vmem_limit_bytes=VMEM_LIMIT),
        cost_estimate=pl.CostEstimate(flops=flops, bytes_accessed=moved, transcendentals=0),
    )(*args)


def body(particle_spectra, class_spectra, shift_index, prior_rotation, particle_group, group_scale):
    count = lax.axis_size("cls")
    doms = lax.axis_size("dom")
    particles, candidates = shift_index.shape
    classes = class_spectra.shape[0]
    rows = particles * candidates
    width = COLS // doms
    padded = -(-(width + 3) // LANES) * LANES
    growth = (padded - width - 3) // (doms - 1)
    f32, bf16 = jnp.float32, jnp.bfloat16
    shape = jax.ShapeDtypeStruct

    packed, classes_on_chip, scales = call(
        pack_kernel,
        [
            shape((particles, COLS + META), bf16),
            shape(class_spectra.shape, bf16),
            shape((1, group_scale.shape[0]), f32),
        ],
        [
            pltpu.VMEM((particles, candidates), jnp.int32),
            pltpu.VMEM((1, particles), jnp.int32),
            pltpu.VMEM((1, particles), jnp.int32),
            pltpu.SemaphoreType.DMA((6,)),
        ],
        particles * COLS,
        4 * particles * COLS,
        particle_spectra, shift_index, prior_rotation[None, :], particle_group[None, :],
        class_spectra, group_scale[None, :],
        hbm=(0, 1, 2, 3, 4, 5),
    )
    others = [exchange(packed, "cls", distance) for distance in range(1, count)]
    table = jnp.asarray(phase_table())
    stat_rows = -(-3 * count // 8) * 8
    work = 2 * rows * COLS * (ROTS * classes + 256)
    stats_shape = shape((stat_rows, LANES), f32)
    shifted_shape = shape((count * rows, COLS), bf16)
    exp_shape = shape((ROTS * classes, count * rows), f32)
    shifted, exps, stats_own, rotated, norm, table_on_chip = call(
        functools.partial(own_kernel, count),
        [
            shifted_shape,
            exp_shape,
            stats_shape,
            shape((ROTS * classes, COLS), bf16),
            shape((classes, LANES), f32),
            shape(table.shape, bf16),
        ],
        [pltpu.SemaphoreType.DMA],
        work,
        4 * rows * COLS,
        packed, classes_on_chip, table, scales,
        hbm=(2,),
    )
    shifted, exps, stats = call(
        functools.partial(rest_kernel, count),
        [shifted_shape, exp_shape, stats_shape],
        [],
        work * (count - 1),
        4 * (count - 1) * rows * COLS,
        *others, table_on_chip, scales, rotated, norm, stats_own, shifted, exps,
        aliases={count + 4: 0, count + 5: 1},
        chip=(count + 4, count + 5),
    )
    all_stats = [stats] + [exchange(stats, "cls", distance) for distance in range(1, count)]
    order = list(range(doms - 1, -1, -1))
    blocks = {}
    work = 2 * count * rows * COLS * ROTS * classes // doms
    blocks[order[0]], weights, mass = call(
        functools.partial(first_sums_kernel, count, doms, width, order[0]),
        [
            shape((classes, width + 3 + order[0] * growth), bf16),
            shape((ROTS * classes, count * rows), bf16),
            shape((classes, LANES), f32),
        ],
        [],
        work,
        4 * count * rows * width,
        *all_stats, exps, shifted,
        chip=(count, count + 1),
    )
    received = []
    for before, distance in zip(order, order[1:]):
        received.append(exchange(blocks[before], "dom", before))
        (blocks[distance],) = call(
            functools.partial(next_sums_kernel, doms, width, distance),
            [shape((classes, width + 3 + distance * growth), bf16 if distance else f32)],
            [],
            1024,
            1024,
            weights, shifted, mass, blocks[before],
            chip=(1,),
        )
    own = blocks[0]
    class_sums, class_weights = call(
        functools.partial(final_kernel, width),
        [shape((classes, width), f32), shape((1, classes), f32)],
        [],
        doms * classes * padded,
        4 * doms * classes * padded,
        own, *received,
        pinned=False,
    )
    return class_sums, class_weights.reshape(classes)


def solution(mesh):
    placed = (
        P(("groups", "dom", "cls"), None),
        P(("groups", "cls"), None),
        P(("groups", "dom", "cls"), None),
        P(("groups", "dom", "cls")),
        P(("groups", "dom", "cls")),
        P("groups"),
    )
    return jax.shard_map(
        body,
        mesh=mesh,
        in_specs=placed,
        out_specs=(P(("groups", "cls"), "dom"), P(("groups", "cls"))),
        check_vma=False,
    )
```

```python
import functools
import math

import jax
import jax.numpy as jnp
import numpy as np
from jax import lax
from jax.experimental import pallas as pl
from jax.experimental.pallas import tpu as pltpu
from jax.sharding import PartitionSpec as P

CYCLES = 18
ANG = 64
IMG = 64
ANG_STEP = 1
ROTS = 8
SHIFT_R = 5
SHIFTW = 11
HALF = CYCLES * ANG
COLS = 2 * HALF
LANES = 128
SUB = 8
META = LANES
ROT_PRIOR = 0.5
VMEM_LIMIT = 20 * 1024 * 1024


def phase_rows():
    angles = np.arange(ANG) * (2.0 * math.pi / ANG)
    radius = np.arange(CYCLES) + 1.0
    fx = (radius[:, None] * np.cos(angles)[None, :]).reshape(-1)
    fy = (radius[:, None] * np.sin(angles)[None, :]).reshape(-1)
    offsets = np.arange(SHIFTW) - SHIFT_R
    unit = 2.0 * math.pi / IMG
    along_x = unit * offsets[:, None] * fx[None, :]
    along_y = unit * offsets[:, None] * fy[None, :]
    both = (along_x[SUB:, None, :] + along_y[None, SUB:, :]).reshape(-1, HALF)
    values = np.zeros((48, COLS), np.float32)
    for start, phase in ((0, along_x), (16, along_y), (32, both)):
        values[start : start + len(phase)] = np.concatenate([np.cos(phase), np.sin(phase)], axis=1)
    return values


def build_table(rows_ref, table_ref):
    width = 3 * LANES
    for start in range(0, HALF, width):
        real = slice(start, start + width)
        imag = slice(HALF + start, HALF + start + width)

        def product(block, row):
            c, s = rows_ref[block : block + SUB, real], rows_ref[block : block + SUB, imag]
            d, t = rows_ref[row : row + 1, real], rows_ref[row : row + 1, imag]
            return c * d - s * t, s * d + c * t

        blocks = [product(0, 16 + y) for y in range(SHIFTW)]
        blocks += [product(16, x) for x in range(SUB, SHIFTW)]
        blocks += [
            (rows_ref[row : row + SUB, real], rows_ref[row : row + SUB, imag])
            for row in (32, 32 + SUB)
        ]
        for pair in range(0, len(blocks), 2):
            for part, columns in ((0, real), (1, imag)):
                value = jnp.concatenate([blocks[pair][part], blocks[pair + 1][part]], axis=0)
                high = value.astype(jnp.bfloat16)
                low = (value - high.astype(jnp.float32)).astype(jnp.bfloat16)
                row = pair * SUB
                table_ref[row : row + 2 * SUB, columns] = high
                table_ref[LANES + row : LANES + row + 2 * SUB, columns] = low


def table_row(index):
    y = jnp.floor((index + 0.5) * (1.0 / SHIFTW))
    x = index - SHIFTW * y
    near = SUB * y + x
    side = SUB * (SHIFTW + x - SUB) + y
    corner = SUB * (2 * SHIFTW - SUB) + (SHIFTW - SUB) * (x - SUB) + (y - SUB)
    return jnp.where(x < SUB, near, jnp.where(y < SUB, side, corner))


def exchange(array, axis, distance):
    return lax.ppermute(array, axis, [(i, i ^ distance) for i in range(lax.axis_size(axis))])


def lane_index(shape):
    return lax.broadcasted_iota(jnp.int32, shape, len(shape) - 1)


def rotate_classes(class_ref, rotated_ref, norm_ref):
    classes = class_ref.shape[0]
    total = jnp.zeros((classes, LANES), jnp.float32)
    lane = lane_index((classes, LANES)) % ANG
    for tile in range(COLS // LANES):
        columns = slice(tile * LANES, (tile + 1) * LANES)
        value = class_ref[:, columns]
        wide = value.astype(jnp.float32)
        total = total + wide * wide
        other = pltpu.roll(value, ANG, 1)
        for rotation in range(ROTS):
            offset = ANG_STEP * rotation % ANG
            turned = value
            if offset:
                turned = pltpu.roll(jnp.where(lane < ANG - offset, value, other), offset, 1)
            rotated_ref[rotation * classes : (rotation + 1) * classes, columns] = turned
    norm_ref[...] = jnp.broadcast_to(jnp.sum(total, axis=1, keepdims=True), (classes, LANES))


def to_lanes(column, width):
    n = column.shape[0]
    row = lax.broadcasted_iota(jnp.int32, (n, width), 0)
    return jnp.sum(
        jnp.where(lane_index((n, width)) % n == row, column, 0.0), axis=0, keepdims=True
    )


def fold_lanes(row, period, combine):
    result = row[:, :LANES]
    for part in range(1, row.shape[1] // LANES):
        result = combine(result, row[:, part * LANES : (part + 1) * LANES])
    step = LANES // 2
    while step >= period:
        result = combine(result, pltpu.roll(result, step, 1))
        step //= 2
    return result


def to_column(row):
    n = row.shape[1]
    diagonal = lax.broadcasted_iota(jnp.int32, (n, n), 0) == lane_index((n, n))
    return jnp.sum(jnp.where(diagonal, row, 0.0), axis=1, keepdims=True)


def pack_kernel(
    particle_hbm, index_hbm, prior_hbm, group_hbm, class_hbm, scale_hbm, rows_hbm,
    packed_ref, class_ref, scale_ref, rows_ref, index_ref, prior_ref, group_ref, sems,
):
    particles, candidates = index_ref.shape
    copies = [
        pltpu.make_async_copy(source, target, sems.at[i])
        for i, (source, target) in enumerate(
            [
                (index_hbm, index_ref),
                (prior_hbm, prior_ref),
                (group_hbm, group_ref),
                (particle_hbm, packed_ref.at[:, pl.ds(0, COLS)]),
                (class_hbm, class_ref),
                (scale_hbm, scale_ref),
                (rows_hbm, rows_ref),
            ]
        )
    ]
    for copy in copies:
        copy.start()
    for copy in copies[:3]:
        copy.wait()
    lane = lane_index((particles, META))
    index = jnp.concatenate(
        [table_row(index_ref[...].astype(jnp.float32)), jnp.zeros((particles, META - candidates), jnp.float32)],
        axis=1,
    )
    prior = to_column(prior_ref[...].astype(jnp.float32))
    group = to_column(group_ref[...].astype(jnp.float32))
    meta = jnp.where(lane == candidates, prior, jnp.where(lane == candidates + 1, group, index))
    packed_ref[:, COLS:] = meta.astype(jnp.bfloat16)
    for copy in copies[3:]:
        copy.wait()


def score_block(block_ref, table_ref, scale_ref, rotated_ref, norm_ref, shifted_ref, out):
    particles = block_ref.shape[0]
    classes = norm_ref.shape[0]
    candidates = shifted_ref.shape[0] // particles
    rows = particles * candidates
    repeat = rows // LANES
    meta = block_ref[:, COLS : COLS + META].astype(jnp.float32)
    index = meta[:, :candidates].astype(jnp.int32)
    lane = lane_index((particles, LANES))
    hot = jnp.concatenate(
        [
            jnp.where(index[:, t : t + 1] == lane, 1.0, 0.0).astype(jnp.bfloat16)
            for t in range(candidates)
        ],
        axis=0,
    )
    hot = jnp.concatenate([hot, hot], axis=1)
    groups = scale_ref.shape[1]
    group = meta[:, candidates + 1 : candidates + 2].astype(jnp.int32)
    scale_column = jnp.sum(
        jnp.where(group == lane_index((particles, groups)), scale_ref[...], 0.0),
        axis=1,
        keepdims=True,
    )
    scale = to_lanes(scale_column, rows)
    prior = to_lanes(meta[:, candidates : candidates + 1], rows)
    width = 3 * LANES
    for start in range(0, HALF, width):
        real_columns = slice(start, start + width)
        imag_columns = slice(HALF + start, HALF + start + width)
        cosine = jnp.dot(hot, table_ref[:, real_columns], preferred_element_type=jnp.float32)
        sine = jnp.dot(hot, table_ref[:, imag_columns], preferred_element_type=jnp.float32)
        real = block_ref[:, real_columns].astype(jnp.float32)
        imag = block_ref[:, imag_columns].astype(jnp.float32)
        for t in range(candidates):
            part = slice(t * particles, (t + 1) * particles)
            c, s = cosine[part], sine[part]
            shifted_ref[part, real_columns] = (real * c - imag * s).astype(jnp.bfloat16)
            shifted_ref[part, imag_columns] = (real * s + imag * c).astype(jnp.bfloat16)
    product = lax.dot_general(
        rotated_ref[...],
        shifted_ref[...],
        (((1,), (1,)), ((), ())),
        preferred_element_type=jnp.float32,
    )
    norm = jnp.concatenate([norm_ref[...]] * repeat, axis=1)
    half_square = 0.5 * scale * scale
    scores = []
    highest = None
    for rotation in range(ROTS):
        distance = jnp.abs(rotation - prior)
        score = (
            scale * product[rotation * classes : (rotation + 1) * classes]
            - half_square * norm
            - ROT_PRIOR * (distance * distance)
        )
        scores.append(score)
        peak = jnp.max(score, axis=0, keepdims=True)
        highest = peak if highest is None else jnp.maximum(highest, peak)
    highest = fold_lanes(highest, particles, jnp.maximum)
    wide = jnp.concatenate([highest] * repeat, axis=1)
    total = None
    for rotation in range(ROTS):
        value = jnp.exp(scores[rotation] - wide)
        out(rotation, value)
        added = jnp.sum(value, axis=0, keepdims=True)
        total = added if total is None else total + added
    total = fold_lanes(total, particles, jnp.add)
    return highest, total, scale[:, :LANES]


def own_kernel(
    count, block_ref, class_ref, rows_ref, scale_ref,
    shifted_ref, exp_ref, stats_ref, rotated_ref, norm_ref, table_ref,
):
    build_table(rows_ref, table_ref)
    rotate_classes(class_ref, rotated_ref, norm_ref)
    classes = norm_ref.shape[0]
    rows = exp_ref.shape[1] // count

    def out(rotation, value):
        exp_ref[rotation * classes : (rotation + 1) * classes, 0:rows] = value

    highest, total, scale = score_block(
        block_ref, table_ref, scale_ref, rotated_ref, norm_ref, shifted_ref.at[0:rows, :], out
    )
    stats_ref[...] = jnp.zeros_like(stats_ref)
    stats_ref[0:1, :] = highest
    stats_ref[1:2, :] = total
    stats_ref[2 * count : 2 * count + 1, :] = scale


def rest_kernel(count, *refs):
    blocks = refs[: count - 1]
    table_ref, scale_ref, rotated_ref, norm_ref, own_ref = refs[count - 1 : count + 4]
    shifted_ref, exp_ref, stats_ref = refs[count + 6 :]
    classes = norm_ref.shape[0]
    rows = exp_ref.shape[1] // count
    stats_ref[...] = own_ref[...]
    for block in range(1, count):
        part = slice(block * rows, (block + 1) * rows)

        def out(rotation, value):
            exp_ref[rotation * classes : (rotation + 1) * classes, part] = value

        highest, total, scale = score_block(
            blocks[block - 1], table_ref, scale_ref, rotated_ref, norm_ref,
            shifted_ref.at[part, :], out,
        )
        stats_ref[2 * block : 2 * block + 1, :] = highest
        stats_ref[2 * block + 1 : 2 * block + 2, :] = total
        stats_ref[2 * count + block : 2 * count + block + 1, :] = scale


def weigh(count, stats, exp_ref, weight_ref):
    rows = exp_ref.shape[1] // count
    repeat = rows // LANES
    classes = weight_ref.shape[0] // ROTS
    mass = jnp.zeros((classes, rows), jnp.float32)
    for block in range(count):
        highs = [stats[c][2 * (c ^ block) : 2 * (c ^ block) + 1, :] for c in range(count)]
        lows = [stats[c][2 * (c ^ block) + 1 : 2 * (c ^ block) + 2, :] for c in range(count)]
        top = functools.reduce(jnp.maximum, highs)
        total = functools.reduce(jnp.add, [l * jnp.exp(h - top) for h, l in zip(highs, lows)])
        factor = jnp.exp(highs[0] - top) / total
        scale = stats[0][2 * count + block : 2 * count + block + 1, :]
        factor = jnp.concatenate([factor] * repeat, axis=1)
        scale = jnp.concatenate([scale] * repeat, axis=1)
        part = slice(block * rows, (block + 1) * rows)
        for rotation in range(ROTS):
            rotated = slice(rotation * classes, (rotation + 1) * classes)
            weight = exp_ref[rotated, part] * factor * scale
            mass = mass + weight * scale
            weight_ref[rotated, part] = weight.astype(jnp.bfloat16)
    return jnp.broadcast_to(jnp.sum(mass, axis=1, keepdims=True), (classes, LANES))


def sum_block(doms, width, distance, weight_ref, shifted_ref, mass, received, out_ref):
    classes, extent = out_ref.shape
    padded = -(-extent // LANES) * LANES
    place = lax.axis_index("dom") ^ distance
    first = place * width
    shifts = sorted({width * dom % LANES for dom in range(doms)})
    span = -(-(shifts[-1] + width) // LANES) * LANES
    base = first // LANES * LANES
    tiles = []
    for start in range(0, span, 2 * LANES):
        wide = min(2 * LANES, span - start)
        columns = pl.ds(pl.multiple_of(base + start, LANES), wide)
        product = jnp.dot(
            weight_ref[...], shifted_ref[:, columns], preferred_element_type=jnp.float32
        )
        for part in range(0, wide, LANES):
            lane = lane_index((classes, LANES)) % ANG
            inside = product[:classes, part : part + LANES]
            wrapped = None
            for rotation in range(1, ROTS):
                offset = ANG_STEP * rotation % ANG
                turned = pltpu.roll(
                    product[rotation * classes : (rotation + 1) * classes, part : part + LANES],
                    LANES - offset,
                    1,
                )
                within = lane < ANG - offset
                inside = inside + jnp.where(within, turned, 0.0)
                over = jnp.where(within, 0.0, turned)
                wrapped = over if wrapped is None else wrapped + over
            tiles.append(inside + pltpu.roll(wrapped, ANG, 1))
    total = jnp.concatenate(tiles, axis=1)
    aligned = total
    for shift in shifts:
        if shift:
            aligned = jnp.where(first - base == shift, pltpu.roll(total, span - shift, 1), aligned)
    if span < padded:
        aligned = jnp.concatenate(
            [aligned, jnp.zeros((classes, padded - span), jnp.float32)], axis=1
        )
    aligned = aligned[:, :padded]
    for ref in received:
        aligned = aligned + pad_columns(ref[...].astype(jnp.float32), padded)
        mass = mass + received_mass(width, ref)
    mass = jnp.concatenate([mass] * (padded // LANES), axis=1)
    high = mass.astype(jnp.bfloat16).astype(jnp.float32)
    middle = (mass - high).astype(jnp.bfloat16).astype(jnp.float32)
    low = (mass - high - middle).astype(jnp.bfloat16).astype(jnp.float32)
    lane = lane_index((classes, padded))
    tail = jnp.where(
        lane == width, high, jnp.where(lane == width + 1, middle, jnp.where(lane == width + 2, low, 0.0))
    )
    total = jnp.where(lane < width, aligned, tail)
    out_ref[...] = total[:, :extent].astype(out_ref.dtype)


def pad_columns(value, padded):
    if value.shape[1] < padded:
        added = jnp.zeros((value.shape[0], padded - value.shape[1]), value.dtype)
        return jnp.concatenate([value, added], axis=1)
    return value[:, :padded]


def received_mass(width, ref):
    base = width // LANES * LANES
    tail = ref[:, base:].astype(jnp.float32)
    lane = base + lane_index(tail.shape)
    tail = jnp.where((lane >= width) & (lane < width + 3), tail, 0.0)
    return jnp.sum(tail, axis=1, keepdims=True)


def first_sums_kernel(count, doms, width, distance, *refs):
    stats = refs[:count]
    exp_ref, shifted_ref, out_ref, weight_ref, mass_ref = refs[count:]
    mass = weigh(count, stats, exp_ref, weight_ref)
    mass_ref[...] = mass
    sum_block(doms, width, distance, weight_ref, shifted_ref, mass, (), out_ref)


def next_sums_kernel(doms, width, distance, weight_ref, shifted_ref, mass_ref, done_ref, *refs):
    received, out_ref = refs[:-1], refs[-1]
    sum_block(doms, width, distance, weight_ref, shifted_ref, mass_ref[...], received, out_ref)


def final_kernel(width, own_ref, *refs):
    received, sums_ref, weights_ref = refs[:-2], refs[-2], refs[-1]
    total, mass = None, None
    for ref in (own_ref, *received):
        value = ref[:, :width].astype(jnp.float32)
        total = value if total is None else total + value
        tail = received_mass(width, ref)
        mass = tail if mass is None else mass + tail
    sums_ref[...] = total
    weights_ref[...] = to_lanes(mass, total.shape[0])


def call(kernel, shapes, scratch, flops, moved, *args, smem=(), hbm=(), chip=(), pinned=True, aliases=None):
    vmem = pl.BlockSpec(memory_space=pltpu.VMEM)
    scalar = pl.BlockSpec(memory_space=pltpu.SMEM)
    place = pl.BlockSpec(memory_space=pltpu.HBM)
    args = [
        pltpu.with_memory_space_constraint(a, pltpu.HBM) if i in hbm
        else pltpu.with_memory_space_constraint(a, pltpu.VMEM) if i in chip
        else a
        for i, a in enumerate(args)
    ]
    return pl.pallas_call(
        kernel,
        out_shape=[pltpu.VMEM(s.shape, s.dtype) if pinned else s for s in shapes],
        in_specs=[scalar if i in smem else place if i in hbm else vmem for i in range(len(args))],
        out_specs=[vmem] * len(shapes),
        scratch_shapes=scratch,
        input_output_aliases=aliases or {},
        compiler_params=pltpu.CompilerParams(vmem_limit_bytes=VMEM_LIMIT),
        cost_estimate=pl.CostEstimate(flops=flops, bytes_accessed=moved, transcendentals=0),
    )(*args)


def body(particle_spectra, class_spectra, shift_index, prior_rotation, particle_group, group_scale):
    count = lax.axis_size("cls")
    doms = lax.axis_size("dom")
    particles, candidates = shift_index.shape
    classes = class_spectra.shape[0]
    rows = particles * candidates
    width = COLS // doms
    padded = -(-(width + 3) // LANES) * LANES
    growth = (padded - width - 3) // (doms - 1)
    f32, bf16 = jnp.float32, jnp.bfloat16
    shape = jax.ShapeDtypeStruct

    phases = jnp.asarray(phase_rows())
    packed, classes_on_chip, scales, phases_on_chip = call(
        pack_kernel,
        [
            shape((particles, COLS + META), bf16),
            shape(class_spectra.shape, bf16),
            shape((1, group_scale.shape[0]), f32),
            shape(phases.shape, f32),
        ],
        [
            pltpu.VMEM((particles, candidates), jnp.int32),
            pltpu.VMEM((1, particles), jnp.int32),
            pltpu.VMEM((1, particles), jnp.int32),
            pltpu.SemaphoreType.DMA((7,)),
        ],
        particles * COLS,
        4 * particles * COLS,
        particle_spectra, shift_index, prior_rotation[None, :], particle_group[None, :],
        class_spectra, group_scale[None, :], phases,
        hbm=(0, 1, 2, 3, 4, 5, 6),
    )
    others = [exchange(packed, "cls", distance) for distance in range(1, count)]
    stat_rows = -(-3 * count // 8) * 8
    work = 2 * rows * COLS * (ROTS * classes + 256)
    stats_shape = shape((stat_rows, LANES), f32)
    shifted_shape = shape((count * rows, COLS), bf16)
    exp_shape = shape((ROTS * classes, count * rows), f32)
    shifted, exps, stats_own, rotated, norm, table_on_chip = call(
        functools.partial(own_kernel, count),
        [
            shifted_shape,
            exp_shape,
            stats_shape,
            shape((ROTS * classes, COLS), bf16),
            shape((classes, LANES), f32),
            shape((2 * LANES, COLS), bf16),
        ],
        [],
        work,
        4 * rows * COLS,
        packed, classes_on_chip, phases_on_chip, scales,
    )
    shifted, exps, stats = call(
        functools.partial(rest_kernel, count),
        [shifted_shape, exp_shape, stats_shape],
        [],
        work * (count - 1),
        4 * (count - 1) * rows * COLS,
        *others, table_on_chip, scales, rotated, norm, stats_own, shifted, exps,
        aliases={count + 4: 0, count + 5: 1},
        chip=(count + 4, count + 5),
    )
    all_stats = [stats] + [exchange(stats, "cls", distance) for distance in range(1, count)]
    low_bit = lambda b: b & -b if b else doms
    order = sorted(range(doms), key=lambda b: (low_bit(b), -b))
    extents = {b: width + 3 + (doms - 1 - place) * growth for place, b in enumerate(order)}
    first = order[0]
    before, weights, mass = call(
        functools.partial(first_sums_kernel, count, doms, width, first),
        [
            shape((classes, extents[first]), bf16),
            shape((ROTS * classes, count * rows), bf16),
            shape((classes, LANES), f32),
        ],
        [],
        2 * count * rows * COLS * ROTS * classes // doms,
        4 * count * rows * width,
        *all_stats, exps, shifted,
        chip=(count, count + 1),
    )
    incoming = {b: [] for b in order}
    incoming[first ^ low_bit(first)].append(exchange(before, "dom", low_bit(first)))
    for block in order[1:]:
        arrived = incoming[block] if block else []
        (before,) = call(
            functools.partial(next_sums_kernel, doms, width, block),
            [shape((classes, extents[block]), bf16 if block else f32)],
            [],
            1024,
            1024,
            weights, shifted, mass, before, *arrived,
            chip=(1,),
        )
        if block:
            incoming[block ^ low_bit(block)].append(exchange(before, "dom", low_bit(block)))
    own, received = before, incoming[0]
    class_sums, class_weights = call(
        functools.partial(final_kernel, width),
        [shape((classes, width), f32), shape((1, classes), f32)],
        [],
        doms * classes * padded,
        4 * doms * classes * padded,
        own, *received,
        pinned=False,
    )
    return class_sums, class_weights.reshape(classes)


def solution(mesh):
    placed = (
        P(("groups", "dom", "cls"), None),
        P(("groups", "cls"), None),
        P(("groups", "dom", "cls"), None),
        P(("groups", "dom", "cls")),
        P(("groups", "dom", "cls")),
        P("groups"),
    )
    return jax.shard_map(
        body,
        mesh=mesh,
        in_specs=placed,
        out_specs=(P(("groups", "cls"), "dom"), P(("groups", "cls"))),
        check_vma=False,
    )
```

```python
import functools
import math

import jax
import jax.numpy as jnp
import numpy as np
from jax import lax
from jax.experimental import pallas as pl
from jax.experimental.pallas import tpu as pltpu
from jax.sharding import PartitionSpec as P

CYCLES = 18
ANG = 64
IMG = 64
ANG_STEP = 1
ROTS = 8
SHIFT_R = 5
SHIFTW = 11
HALF = CYCLES * ANG
COLS = 2 * HALF
LANES = 128
SUB = 8
META = LANES
ROT_PRIOR = 0.5
VMEM_LIMIT = 20 * 1024 * 1024


def phase_rows():
    angles = np.arange(ANG) * (2.0 * math.pi / ANG)
    radius = np.arange(CYCLES) + 1.0
    fx = (radius[:, None] * np.cos(angles)[None, :]).reshape(-1)
    fy = (radius[:, None] * np.sin(angles)[None, :]).reshape(-1)
    offsets = np.arange(SHIFTW) - SHIFT_R
    unit = 2.0 * math.pi / IMG
    along_x = unit * offsets[:, None] * fx[None, :]
    along_y = unit * offsets[:, None] * fy[None, :]
    both = (along_x[SUB:, None, :] + along_y[None, SUB:, :]).reshape(-1, HALF)
    values = np.zeros((48, COLS), np.float32)
    for start, phase in ((0, along_x), (16, along_y), (32, both)):
        values[start : start + len(phase)] = np.concatenate([np.cos(phase), np.sin(phase)], axis=1)
    return values


def build_table(rows_ref, table_ref):
    width = 3 * LANES
    for start in range(0, HALF, width):
        real = slice(start, start + width)
        imag = slice(HALF + start, HALF + start + width)

        def product(block, row):
            c, s = rows_ref[block : block + SUB, real], rows_ref[block : block + SUB, imag]
            d, t = rows_ref[row : row + 1, real], rows_ref[row : row + 1, imag]
            return c * d - s * t, s * d + c * t

        blocks = [product(0, 16 + y) for y in range(SHIFTW)]
        blocks += [product(16, x) for x in range(SUB, SHIFTW)]
        blocks += [
            (rows_ref[row : row + SUB, real], rows_ref[row : row + SUB, imag])
            for row in (32, 32 + SUB)
        ]
        for pair in range(0, len(blocks), 2):
            for part, columns in ((0, real), (1, imag)):
                value = jnp.concatenate([blocks[pair][part], blocks[pair + 1][part]], axis=0)
                high = value.astype(jnp.bfloat16)
                low = (value - high.astype(jnp.float32)).astype(jnp.bfloat16)
                row = pair * SUB
                table_ref[row : row + 2 * SUB, columns] = high
                table_ref[LANES + row : LANES + row + 2 * SUB, columns] = low


def table_row(index):
    y = jnp.floor((index + 0.5) * (1.0 / SHIFTW))
    x = index - SHIFTW * y
    near = SUB * y + x
    side = SUB * (SHIFTW + x - SUB) + y
    corner = SUB * (2 * SHIFTW - SUB) + (SHIFTW - SUB) * (x - SUB) + (y - SUB)
    return jnp.where(x < SUB, near, jnp.where(y < SUB, side, corner))


def exchange(array, axis, distance):
    return lax.ppermute(array, axis, [(i, i ^ distance) for i in range(lax.axis_size(axis))])


def lane_index(shape):
    return lax.broadcasted_iota(jnp.int32, shape, len(shape) - 1)


def rotate_classes(class_ref, rotated_ref, norm_ref):
    classes = class_ref.shape[0]
    total = jnp.zeros((classes, LANES), jnp.float32)
    lane = lane_index((classes, LANES)) % ANG
    for tile in range(COLS // LANES):
        columns = slice(tile * LANES, (tile + 1) * LANES)
        value = class_ref[:, columns]
        wide = value.astype(jnp.float32)
        total = total + wide * wide
        other = pltpu.roll(value, ANG, 1)
        for rotation in range(ROTS):
            offset = ANG_STEP * rotation % ANG
            turned = value
            if offset:
                turned = pltpu.roll(jnp.where(lane < ANG - offset, value, other), offset, 1)
            rotated_ref[rotation * classes : (rotation + 1) * classes, columns] = turned
    norm_ref[...] = jnp.broadcast_to(jnp.sum(total, axis=1, keepdims=True), (classes, LANES))


def to_lanes(column, width):
    n = column.shape[0]
    row = lax.broadcasted_iota(jnp.int32, (n, width), 0)
    return jnp.sum(
        jnp.where(lane_index((n, width)) % n == row, column, 0.0), axis=0, keepdims=True
    )


def fold_lanes(row, period, combine):
    result = row[:, :LANES]
    for part in range(1, row.shape[1] // LANES):
        result = combine(result, row[:, part * LANES : (part + 1) * LANES])
    step = LANES // 2
    while step >= period:
        result = combine(result, pltpu.roll(result, step, 1))
        step //= 2
    return result


def to_column(row):
    n = row.shape[1]
    diagonal = lax.broadcasted_iota(jnp.int32, (n, n), 0) == lane_index((n, n))
    return jnp.sum(jnp.where(diagonal, row, 0.0), axis=1, keepdims=True)


def pack_kernel(
    particle_hbm, index_hbm, prior_hbm, group_hbm, class_hbm, scale_hbm, rows_hbm,
    packed_ref, class_ref, scale_ref, rows_ref, index_ref, prior_ref, group_ref, sems,
):
    particles, candidates = index_ref.shape
    copies = [
        pltpu.make_async_copy(source, target, sems.at[i])
        for i, (source, target) in enumerate(
            [
                (index_hbm, index_ref),
                (prior_hbm, prior_ref),
                (group_hbm, group_ref),
                (particle_hbm, packed_ref.at[:, pl.ds(0, COLS)]),
                (class_hbm, class_ref),
                (scale_hbm, scale_ref),
                (rows_hbm, rows_ref),
            ]
        )
    ]
    for copy in copies:
        copy.start()
    for copy in copies[:3]:
        copy.wait()
    lane = lane_index((particles, META))
    index = jnp.concatenate(
        [table_row(index_ref[...].astype(jnp.float32)), jnp.zeros((particles, META - candidates), jnp.float32)],
        axis=1,
    )
    prior = to_column(prior_ref[...].astype(jnp.float32))
    group = to_column(group_ref[...].astype(jnp.float32))
    meta = jnp.where(lane == candidates, prior, jnp.where(lane == candidates + 1, group, index))
    packed_ref[:, COLS:] = meta.astype(jnp.bfloat16)
    for copy in copies[3:]:
        copy.wait()


def score_block(block_ref, table_ref, scale_ref, rotated_ref, norm_ref, shifted_ref, out):
    particles = block_ref.shape[0]
    classes = norm_ref.shape[0]
    candidates = shifted_ref.shape[0] // particles
    rows = particles * candidates
    repeat = rows // LANES
    meta = block_ref[:, COLS : COLS + META].astype(jnp.float32)
    index = meta[:, :candidates].astype(jnp.int32)
    lane = lane_index((particles, LANES))
    hot = jnp.concatenate(
        [
            jnp.where(index[:, t : t + 1] == lane, 1.0, 0.0).astype(jnp.bfloat16)
            for t in range(candidates)
        ],
        axis=0,
    )
    hot = jnp.concatenate([hot, hot], axis=1)
    groups = scale_ref.shape[1]
    group = meta[:, candidates + 1 : candidates + 2].astype(jnp.int32)
    scale_column = jnp.sum(
        jnp.where(group == lane_index((particles, groups)), scale_ref[...], 0.0),
        axis=1,
        keepdims=True,
    )
    scale = to_lanes(scale_column, rows)
    prior = to_lanes(meta[:, candidates : candidates + 1], rows)
    width = 3 * LANES
    for start in range(0, HALF, width):
        real_columns = slice(start, start + width)
        imag_columns = slice(HALF + start, HALF + start + width)
        cosine = jnp.dot(hot, table_ref[:, real_columns], preferred_element_type=jnp.float32)
        sine = jnp.dot(hot, table_ref[:, imag_columns], preferred_element_type=jnp.float32)
        real = block_ref[:, real_columns].astype(jnp.float32)
        imag = block_ref[:, imag_columns].astype(jnp.float32)
        for t in range(candidates):
            part = slice(t * particles, (t + 1) * particles)
            c, s = cosine[part], sine[part]
            shifted_ref[part, real_columns] = (real * c - imag * s).astype(jnp.bfloat16)
            shifted_ref[part, imag_columns] = (real * s + imag * c).astype(jnp.bfloat16)
    product = lax.dot_general(
        rotated_ref[...],
        shifted_ref[...],
        (((1,), (1,)), ((), ())),
        preferred_element_type=jnp.float32,
    )
    norm = jnp.concatenate([norm_ref[...]] * repeat, axis=1)
    half_square = 0.5 * scale * scale
    scores = []
    highest = None
    for rotation in range(ROTS):
        distance = jnp.abs(rotation - prior)
        score = (
            scale * product[rotation * classes : (rotation + 1) * classes]
            - half_square * norm
            - ROT_PRIOR * (distance * distance)
        )
        scores.append(score)
        peak = jnp.max(score, axis=0, keepdims=True)
        highest = peak if highest is None else jnp.maximum(highest, peak)
    highest = fold_lanes(highest, particles, jnp.maximum)
    wide = jnp.concatenate([highest] * repeat, axis=1)
    total = None
    for rotation in range(ROTS):
        value = jnp.exp(scores[rotation] - wide)
        out(rotation, value)
        added = jnp.sum(value, axis=0, keepdims=True)
        total = added if total is None else total + added
    total = fold_lanes(total, particles, jnp.add)
    return highest, total, scale[:, :LANES]


def own_kernel(
    count, block_ref, class_ref, rows_ref, scale_ref,
    shifted_ref, exp_ref, stats_ref, rotated_ref, norm_ref, table_ref,
):
    build_table(rows_ref, table_ref)
    rotate_classes(class_ref, rotated_ref, norm_ref)
    classes = norm_ref.shape[0]
    rows = exp_ref.shape[1] // count

    def out(rotation, value):
        exp_ref[rotation * classes : (rotation + 1) * classes, 0:rows] = value

    highest, total, scale = score_block(
        block_ref, table_ref, scale_ref, rotated_ref, norm_ref, shifted_ref.at[0:rows, :], out
    )
    stats_ref[...] = jnp.zeros_like(stats_ref)
    stats_ref[0:1, :] = highest
    stats_ref[1:2, :] = total
    stats_ref[2 * count : 2 * count + 1, :] = scale


def rest_kernel(count, chunks, *refs):
    blocks, refs = refs[: len(chunks)], refs[len(chunks) :]
    table_ref, scale_ref, rotated_ref, norm_ref, own_ref = refs[:5]
    shifted_ref, exp_ref, stats_ref = refs[7:]
    classes = norm_ref.shape[0]
    rows = exp_ref.shape[1] // count
    stats_ref[...] = own_ref[...]
    for block, block_ref in zip(chunks, blocks):
        part = slice(block * rows, (block + 1) * rows)

        def out(rotation, value):
            exp_ref[rotation * classes : (rotation + 1) * classes, part] = value

        highest, total, scale = score_block(
            block_ref, table_ref, scale_ref, rotated_ref, norm_ref,
            shifted_ref.at[part, :], out,
        )
        stats_ref[2 * block : 2 * block + 1, :] = highest
        stats_ref[2 * block + 1 : 2 * block + 2, :] = total
        stats_ref[2 * count + block : 2 * count + block + 1, :] = scale


def weigh(count, stats, exp_ref, weight_ref):
    rows = exp_ref.shape[1] // count
    repeat = rows // LANES
    classes = weight_ref.shape[0] // ROTS
    mass = jnp.zeros((classes, rows), jnp.float32)
    for block in range(count):
        highs = [stats[c][2 * (c ^ block) : 2 * (c ^ block) + 1, :] for c in range(count)]
        lows = [stats[c][2 * (c ^ block) + 1 : 2 * (c ^ block) + 2, :] for c in range(count)]
        top = functools.reduce(jnp.maximum, highs)
        total = functools.reduce(jnp.add, [l * jnp.exp(h - top) for h, l in zip(highs, lows)])
        factor = jnp.exp(highs[0] - top) / total
        scale = stats[0][2 * count + block : 2 * count + block + 1, :]
        factor = jnp.concatenate([factor] * repeat, axis=1)
        scale = jnp.concatenate([scale] * repeat, axis=1)
        part = slice(block * rows, (block + 1) * rows)
        for rotation in range(ROTS):
            rotated = slice(rotation * classes, (rotation + 1) * classes)
            weight = exp_ref[rotated, part] * factor * scale
            mass = mass + weight * scale
            weight_ref[rotated, part] = weight.astype(jnp.bfloat16)
    return jnp.broadcast_to(jnp.sum(mass, axis=1, keepdims=True), (classes, LANES))


def block_sums(doms, width, distance, weight_ref, shifted_ref):
    classes = weight_ref.shape[0] // ROTS
    padded = -(-(width + 3) // LANES) * LANES
    place = lax.axis_index("dom") ^ distance
    first = place * width
    shifts = sorted({width * dom % LANES for dom in range(doms)})
    span = -(-(shifts[-1] + width) // LANES) * LANES
    base = first // LANES * LANES
    tiles = []
    for start in range(0, span, 2 * LANES):
        wide = min(2 * LANES, span - start)
        columns = pl.ds(pl.multiple_of(base + start, LANES), wide)
        product = jnp.dot(
            weight_ref[...], shifted_ref[:, columns], preferred_element_type=jnp.float32
        )
        for part in range(0, wide, LANES):
            lane = lane_index((classes, LANES)) % ANG
            inside = product[:classes, part : part + LANES]
            wrapped = None
            for rotation in range(1, ROTS):
                offset = ANG_STEP * rotation % ANG
                turned = pltpu.roll(
                    product[rotation * classes : (rotation + 1) * classes, part : part + LANES],
                    LANES - offset,
                    1,
                )
                within = lane < ANG - offset
                inside = inside + jnp.where(within, turned, 0.0)
                over = jnp.where(within, 0.0, turned)
                wrapped = over if wrapped is None else wrapped + over
            tiles.append(inside + pltpu.roll(wrapped, ANG, 1))
    total = jnp.concatenate(tiles, axis=1)
    aligned = total
    for shift in shifts:
        if shift:
            aligned = jnp.where(first - base == shift, pltpu.roll(total, span - shift, 1), aligned)
    if span < padded:
        aligned = jnp.concatenate(
            [aligned, jnp.zeros((classes, padded - span), jnp.float32)], axis=1
        )
    return aligned[:, :padded]


def store_block(width, value, mass, out_ref):
    high = mass.astype(jnp.bfloat16).astype(jnp.float32)
    middle = (mass - high).astype(jnp.bfloat16).astype(jnp.float32)
    low = (mass - high - middle).astype(jnp.bfloat16).astype(jnp.float32)
    lane = lane_index(value.shape)
    tail = jnp.where(
        lane == width, high, jnp.where(lane == width + 1, middle, jnp.where(lane == width + 2, low, 0.0))
    )
    value = jnp.where(lane < width, value, tail)
    out_ref[...] = value[:, : out_ref.shape[1]].astype(out_ref.dtype)


def pad_columns(value, padded):
    if value.shape[1] < padded:
        added = jnp.zeros((value.shape[0], padded - value.shape[1]), value.dtype)
        return jnp.concatenate([value, added], axis=1)
    return value[:, :padded]


def received_mass(width, ref):
    base = width // LANES * LANES
    tail = ref[:, base:].astype(jnp.float32)
    lane = base + lane_index(tail.shape)
    tail = jnp.where((lane >= width) & (lane < width + 3), tail, 0.0)
    return jnp.sum(tail, axis=1, keepdims=True)


def first_sums_kernel(count, doms, width, blocks, *refs):
    stats = refs[:count]
    exp_ref, shifted_ref = refs[count : count + 2]
    weight_ref, mass_ref = refs[count + 2 : count + 4]
    mass = weigh(count, stats, exp_ref, weight_ref)
    mass_ref[...] = mass
    for block, out_ref in zip(blocks, refs[count + 4 :]):
        store_block(width, block_sums(doms, width, block, weight_ref, shifted_ref), mass[:, :1], out_ref)


def rest_sums_kernel(doms, width, blocks, weight_ref, shifted_ref, mass_ref, *refs):
    for block, out_ref in zip(blocks, refs[-len(blocks) :]):
        value = block_sums(doms, width, block, weight_ref, shifted_ref)
        store_block(width, value, mass_ref[:, :1], out_ref)


def add_kernel(width, *refs):
    out_ref = refs[-1]
    padded = -(-out_ref.shape[1] // LANES) * LANES
    total, mass = None, None
    for ref in refs[:-1]:
        value = pad_columns(ref[...].astype(jnp.float32), padded)
        total = value if total is None else total + value
        tail = received_mass(width, ref)
        mass = tail if mass is None else mass + tail
    store_block(width, total, mass, out_ref)


def final_kernel(width, own_ref, *refs):
    received, sums_ref, weights_ref = refs[:-2], refs[-2], refs[-1]
    total, mass = None, None
    for ref in (own_ref, *received):
        value = ref[:, :width].astype(jnp.float32)
        total = value if total is None else total + value
        tail = received_mass(width, ref)
        mass = tail if mass is None else mass + tail
    sums_ref[...] = total
    weights_ref[...] = to_lanes(mass, total.shape[0])


def call(kernel, shapes, scratch, flops, moved, *args, smem=(), hbm=(), chip=(), pinned=True, aliases=None):
    vmem = pl.BlockSpec(memory_space=pltpu.VMEM)
    scalar = pl.BlockSpec(memory_space=pltpu.SMEM)
    place = pl.BlockSpec(memory_space=pltpu.HBM)
    args = [
        pltpu.with_memory_space_constraint(a, pltpu.HBM) if i in hbm
        else pltpu.with_memory_space_constraint(a, pltpu.VMEM) if i in chip
        else a
        for i, a in enumerate(args)
    ]
    return pl.pallas_call(
        kernel,
        out_shape=[pltpu.VMEM(s.shape, s.dtype) if pinned else s for s in shapes],
        in_specs=[scalar if i in smem else place if i in hbm else vmem for i in range(len(args))],
        out_specs=[vmem] * len(shapes),
        scratch_shapes=scratch,
        input_output_aliases=aliases or {},
        compiler_params=pltpu.CompilerParams(vmem_limit_bytes=VMEM_LIMIT),
        cost_estimate=pl.CostEstimate(flops=flops, bytes_accessed=moved, transcendentals=0),
    )(*args)


def body(particle_spectra, class_spectra, shift_index, prior_rotation, particle_group, group_scale):
    count = lax.axis_size("cls")
    doms = lax.axis_size("dom")
    particles, candidates = shift_index.shape
    classes = class_spectra.shape[0]
    rows = particles * candidates
    width = COLS // doms
    padded = -(-(width + 3) // LANES) * LANES
    growth = (padded - width - 3) // (doms - 1)
    f32, bf16 = jnp.float32, jnp.bfloat16
    shape = jax.ShapeDtypeStruct

    phases = jnp.asarray(phase_rows())
    packed, classes_on_chip, scales, phases_on_chip = call(
        pack_kernel,
        [
            shape((particles, COLS + META), bf16),
            shape(class_spectra.shape, bf16),
            shape((1, group_scale.shape[0]), f32),
            shape(phases.shape, f32),
        ],
        [
            pltpu.VMEM((particles, candidates), jnp.int32),
            pltpu.VMEM((1, particles), jnp.int32),
            pltpu.VMEM((1, particles), jnp.int32),
            pltpu.SemaphoreType.DMA((7,)),
        ],
        particles * COLS,
        4 * particles * COLS,
        particle_spectra, shift_index, prior_rotation[None, :], particle_group[None, :],
        class_spectra, group_scale[None, :], phases,
        hbm=(0, 1, 2, 3, 4, 5, 6),
    )
    others = [exchange(packed, "cls", distance) for distance in range(1, count)]
    stat_rows = -(-3 * count // 8) * 8
    work = 2 * rows * COLS * (ROTS * classes + 256)
    stats_shape = shape((stat_rows, LANES), f32)
    shifted_shape = shape((count * rows, COLS), bf16)
    exp_shape = shape((ROTS * classes, count * rows), f32)
    shifted, exps, stats_own, rotated, norm, table_on_chip = call(
        functools.partial(own_kernel, count),
        [
            shifted_shape,
            exp_shape,
            stats_shape,
            shape((ROTS * classes, COLS), bf16),
            shape((classes, LANES), f32),
            shape((2 * LANES, COLS), bf16),
        ],
        [],
        work,
        4 * rows * COLS,
        packed, classes_on_chip, phases_on_chip, scales,
    )
    stats = stats_own
    for chunks in ([1], list(range(2, count))):
        shifted, exps, stats = call(
            functools.partial(rest_kernel, count, chunks),
            [shifted_shape, exp_shape, stats_shape],
            [],
            work * len(chunks),
            4 * len(chunks) * rows * COLS,
            *[others[b - 1] for b in chunks],
            table_on_chip, scales, rotated, norm, stats, shifted, exps,
            aliases={len(chunks) + 5: 0, len(chunks) + 6: 1},
            chip=(len(chunks) + 5, len(chunks) + 6),
        )
    all_stats = [stats] + [exchange(stats, "cls", distance) for distance in range(1, count)]
    low_bit = lambda b: b & -b
    early = list(range(doms - 1, 1, -2))
    order = early + sorted(range(2, doms, 2), key=lambda b: (low_bit(b), -b)) + [1]
    extents = {b: width + 3 + (doms - 1 - place) * growth for place, b in enumerate(order)}
    late = [1] + list(range(0, doms, 2))
    weights, mass, *made = call(
        functools.partial(first_sums_kernel, count, doms, width, early),
        [shape((ROTS * classes, count * rows), bf16), shape((classes, LANES), f32)]
        + [shape((classes, extents[b]), bf16) for b in early],
        [],
        2 * count * rows * COLS * ROTS * classes // doms,
        4 * count * rows * width,
        *all_stats, exps, shifted,
        chip=(count, count + 1),
    )
    incoming = {b: [] for b in range(doms)}
    for b, block in zip(early, made):
        incoming[b ^ 1].append(exchange(block, "dom", 1))
    rest = call(
        functools.partial(rest_sums_kernel, doms, width, late),
        [
            shape((classes, extents.get(b, width + 3)), bf16 if b == 1 else f32) for b in late
        ],
        [],
        1024,
        1024,
        weights, shifted, mass, *made,
        chip=(1,),
    )
    blocks = dict(zip(late, rest))
    for b in order[len(early) : -1]:
        (block,) = call(
            functools.partial(add_kernel, width),
            [shape((classes, extents[b]), bf16)],
            [],
            1024,
            1024,
            blocks[b], *incoming[b],
        )
        incoming[b ^ low_bit(b)].append(exchange(block, "dom", low_bit(b)))
    incoming[0].append(exchange(blocks[1], "dom", 1))
    own, received = blocks[0], incoming[0]
    class_sums, class_weights = call(
        functools.partial(final_kernel, width),
        [shape((classes, width), f32), shape((1, classes), f32)],
        [],
        doms * classes * padded,
        4 * doms * classes * padded,
        own, *received,
        pinned=False,
    )
    return class_sums, class_weights.reshape(classes)


def solution(mesh):
    placed = (
        P(("groups", "dom", "cls"), None),
        P(("groups", "cls"), None),
        P(("groups", "dom", "cls"), None),
        P(("groups", "dom", "cls")),
        P(("groups", "dom", "cls")),
        P("groups"),
    )
    return jax.shard_map(
        body,
        mesh=mesh,
        in_specs=placed,
        out_specs=(P(("groups", "cls"), "dom"), P(("groups", "cls"))),
        check_vma=False,
    )
```

```python
import functools
import math

import jax
import jax.numpy as jnp
import numpy as np
from jax import lax
from jax.experimental import pallas as pl
from jax.experimental.pallas import tpu as pltpu
from jax.sharding import PartitionSpec as P

CYCLES = 18
ANG = 64
IMG = 64
ANG_STEP = 1
ROTS = 8
SHIFT_R = 5
SHIFTW = 11
HALF = CYCLES * ANG
COLS = 2 * HALF
LANES = 128
SUB = 8
META = LANES
ROT_PRIOR = 0.5
VMEM_LIMIT = 20 * 1024 * 1024


def phase_rows():
    angles = np.arange(ANG) * (2.0 * math.pi / ANG)
    radius = np.arange(CYCLES) + 1.0
    fx = (radius[:, None] * np.cos(angles)[None, :]).reshape(-1)
    fy = (radius[:, None] * np.sin(angles)[None, :]).reshape(-1)
    offsets = np.arange(SHIFTW) - SHIFT_R
    unit = 2.0 * math.pi / IMG
    along_x = unit * offsets[:, None] * fx[None, :]
    along_y = unit * offsets[:, None] * fy[None, :]
    both = (along_x[SUB:, None, :] + along_y[None, SUB:, :]).reshape(-1, HALF)
    values = np.zeros((48, COLS), np.float32)
    for start, phase in ((0, along_x), (16, along_y), (32, both)):
        values[start : start + len(phase)] = np.concatenate([np.cos(phase), np.sin(phase)], axis=1)
    return values


def build_table(rows_ref, table_ref):
    width = 3 * LANES
    for start in range(0, HALF, width):
        real = slice(start, start + width)
        imag = slice(HALF + start, HALF + start + width)

        def product(block, row):
            c, s = rows_ref[block : block + SUB, real], rows_ref[block : block + SUB, imag]
            d, t = rows_ref[row : row + 1, real], rows_ref[row : row + 1, imag]
            return c * d - s * t, s * d + c * t

        blocks = [product(0, 16 + y) for y in range(SHIFTW)]
        blocks += [product(16, x) for x in range(SUB, SHIFTW)]
        blocks += [
            (rows_ref[row : row + SUB, real], rows_ref[row : row + SUB, imag])
            for row in (32, 32 + SUB)
        ]
        for pair in range(0, len(blocks), 2):
            for part, columns in ((0, real), (1, imag)):
                value = jnp.concatenate([blocks[pair][part], blocks[pair + 1][part]], axis=0)
                high = value.astype(jnp.bfloat16)
                low = (value - high.astype(jnp.float32)).astype(jnp.bfloat16)
                row = pair * SUB
                table_ref[row : row + 2 * SUB, columns] = high
                table_ref[LANES + row : LANES + row + 2 * SUB, columns] = low


def table_row(index):
    y = jnp.floor((index + 0.5) * (1.0 / SHIFTW))
    x = index - SHIFTW * y
    near = SUB * y + x
    side = SUB * (SHIFTW + x - SUB) + y
    corner = SUB * (2 * SHIFTW - SUB) + (SHIFTW - SUB) * (x - SUB) + (y - SUB)
    return jnp.where(x < SUB, near, jnp.where(y < SUB, side, corner))


def exchange(array, axis, distance):
    return lax.ppermute(array, axis, [(i, i ^ distance) for i in range(lax.axis_size(axis))])


def lane_index(shape):
    return lax.broadcasted_iota(jnp.int32, shape, len(shape) - 1)


def rotate_classes(class_ref, rotated_ref, norm_ref):
    classes = class_ref.shape[0]
    total = jnp.zeros((classes, LANES), jnp.float32)
    lane = lane_index((classes, LANES)) % ANG
    for tile in range(COLS // LANES):
        columns = slice(tile * LANES, (tile + 1) * LANES)
        value = class_ref[:, columns]
        wide = value.astype(jnp.float32)
        total = total + wide * wide
        other = pltpu.roll(value, ANG, 1)
        for rotation in range(ROTS):
            offset = ANG_STEP * rotation % ANG
            turned = value
            if offset:
                turned = pltpu.roll(jnp.where(lane < ANG - offset, value, other), offset, 1)
            rotated_ref[rotation * classes : (rotation + 1) * classes, columns] = turned
    norm_ref[...] = jnp.broadcast_to(jnp.sum(total, axis=1, keepdims=True), (classes, LANES))


def to_lanes(column, width):
    n = column.shape[0]
    row = lax.broadcasted_iota(jnp.int32, (n, width), 0)
    return jnp.sum(
        jnp.where(lane_index((n, width)) % n == row, column, 0.0), axis=0, keepdims=True
    )


def fold_lanes(row, period, combine):
    result = row[:, :LANES]
    for part in range(1, row.shape[1] // LANES):
        result = combine(result, row[:, part * LANES : (part + 1) * LANES])
    step = LANES // 2
    while step >= period:
        result = combine(result, pltpu.roll(result, step, 1))
        step //= 2
    return result


def to_column(row):
    n = row.shape[1]
    diagonal = lax.broadcasted_iota(jnp.int32, (n, n), 0) == lane_index((n, n))
    return jnp.sum(jnp.where(diagonal, row, 0.0), axis=1, keepdims=True)


def pack_kernel(
    particle_hbm, index_hbm, prior_hbm, group_hbm, class_hbm, scale_hbm, rows_hbm,
    packed_ref, class_ref, scale_ref, rows_ref, index_ref, prior_ref, group_ref, sems,
):
    particles, candidates = index_ref.shape
    copies = [
        pltpu.make_async_copy(source, target, sems.at[i])
        for i, (source, target) in enumerate(
            [
                (index_hbm, index_ref),
                (prior_hbm, prior_ref),
                (group_hbm, group_ref),
                (particle_hbm, packed_ref.at[:, pl.ds(0, COLS)]),
                (class_hbm, class_ref),
                (scale_hbm, scale_ref),
                (rows_hbm, rows_ref),
            ]
        )
    ]
    for copy in copies:
        copy.start()
    for copy in copies[:3]:
        copy.wait()
    lane = lane_index((particles, META))
    index = jnp.concatenate(
        [table_row(index_ref[...].astype(jnp.float32)), jnp.zeros((particles, META - candidates), jnp.float32)],
        axis=1,
    )
    prior = to_column(prior_ref[...].astype(jnp.float32))
    group = to_column(group_ref[...].astype(jnp.float32))
    meta = jnp.where(lane == candidates, prior, jnp.where(lane == candidates + 1, group, index))
    packed_ref[:, COLS:] = meta.astype(jnp.bfloat16)
    for copy in copies[3:]:
        copy.wait()


def score_block(block_ref, table_ref, scale_ref, rotated_ref, norm_ref, shifted_ref, out):
    particles = block_ref.shape[0]
    classes = norm_ref.shape[0]
    candidates = shifted_ref.shape[0] // particles
    rows = particles * candidates
    repeat = rows // LANES
    meta = block_ref[:, COLS : COLS + META].astype(jnp.float32)
    index = meta[:, :candidates].astype(jnp.int32)
    lane = lane_index((particles, LANES))
    hot = jnp.concatenate(
        [
            jnp.where(index[:, t : t + 1] == lane, 1.0, 0.0).astype(jnp.bfloat16)
            for t in range(candidates)
        ],
        axis=0,
    )
    hot = jnp.concatenate([hot, hot], axis=1)
    groups = scale_ref.shape[1]
    group = meta[:, candidates + 1 : candidates + 2].astype(jnp.int32)
    scale_column = jnp.sum(
        jnp.where(group == lane_index((particles, groups)), scale_ref[...], 0.0),
        axis=1,
        keepdims=True,
    )
    scale = to_lanes(scale_column, rows)
    prior = to_lanes(meta[:, candidates : candidates + 1], rows)
    width = 3 * LANES
    for start in range(0, HALF, width):
        real_columns = slice(start, start + width)
        imag_columns = slice(HALF + start, HALF + start + width)
        cosine = jnp.dot(hot, table_ref[:, real_columns], preferred_element_type=jnp.float32)
        sine = jnp.dot(hot, table_ref[:, imag_columns], preferred_element_type=jnp.float32)
        real = block_ref[:, real_columns].astype(jnp.float32)
        imag = block_ref[:, imag_columns].astype(jnp.float32)
        for t in range(candidates):
            part = slice(t * particles, (t + 1) * particles)
            c, s = cosine[part], sine[part]
            shifted_ref[part, real_columns] = (real * c - imag * s).astype(jnp.bfloat16)
            shifted_ref[part, imag_columns] = (real * s + imag * c).astype(jnp.bfloat16)
    product = lax.dot_general(
        rotated_ref[...],
        shifted_ref[...],
        (((1,), (1,)), ((), ())),
        preferred_element_type=jnp.float32,
    )
    norm = jnp.concatenate([norm_ref[...]] * repeat, axis=1)
    half_square = 0.5 * scale * scale
    scores = []
    highest = None
    for rotation in range(ROTS):
        distance = jnp.abs(rotation - prior)
        score = (
            scale * product[rotation * classes : (rotation + 1) * classes]
            - half_square * norm
            - ROT_PRIOR * (distance * distance)
        )
        scores.append(score)
        peak = jnp.max(score, axis=0, keepdims=True)
        highest = peak if highest is None else jnp.maximum(highest, peak)
    highest = fold_lanes(highest, particles, jnp.maximum)
    wide = jnp.concatenate([highest] * repeat, axis=1)
    total = None
    for rotation in range(ROTS):
        value = jnp.exp(scores[rotation] - wide)
        out(rotation, value)
        added = jnp.sum(value, axis=0, keepdims=True)
        total = added if total is None else total + added
    total = fold_lanes(total, particles, jnp.add)
    return highest, total, scale[:, :LANES]


def score_blocks(count, chunks, blocks, table_ref, scale_ref, rotated_ref, norm_ref, shifted_ref, exp_ref, stats_ref):
    classes = norm_ref.shape[0]
    rows = exp_ref.shape[1] // count
    for block, block_ref in zip(chunks, blocks):
        part = slice(block * rows, (block + 1) * rows)

        def out(rotation, value):
            exp_ref[rotation * classes : (rotation + 1) * classes, part] = value

        highest, total, scale = score_block(
            block_ref, table_ref, scale_ref, rotated_ref, norm_ref, shifted_ref.at[part, :], out
        )
        stats_ref[2 * block : 2 * block + 1, :] = highest
        stats_ref[2 * block + 1 : 2 * block + 2, :] = total
        stats_ref[2 * count + block : 2 * count + block + 1, :] = scale


def first_kernel(count, chunks, *refs):
    blocks, refs = refs[: len(chunks)], refs[len(chunks) :]
    class_ref, rows_ref, scale_ref = refs[:3]
    shifted_ref, exp_ref, stats_ref, rotated_ref, norm_ref, table_ref = refs[3:]
    build_table(rows_ref, table_ref)
    rotate_classes(class_ref, rotated_ref, norm_ref)
    stats_ref[...] = jnp.zeros_like(stats_ref)
    score_blocks(
        count, chunks, blocks, table_ref, scale_ref, rotated_ref, norm_ref,
        shifted_ref, exp_ref, stats_ref,
    )


def rest_kernel(count, chunks, *refs):
    blocks, refs = refs[: len(chunks)], refs[len(chunks) :]
    table_ref, scale_ref, rotated_ref, norm_ref, before_ref = refs[:5]
    shifted_ref, exp_ref, stats_ref = refs[7:]
    stats_ref[...] = before_ref[...]
    score_blocks(
        count, chunks, blocks, table_ref, scale_ref, rotated_ref, norm_ref,
        shifted_ref, exp_ref, stats_ref,
    )


def merged(mine, other, block, distance):
    twin = block ^ distance
    high, other_high = mine[2 * block : 2 * block + 1, :], other[2 * twin : 2 * twin + 1, :]
    top = jnp.maximum(high, other_high)
    total = mine[2 * block + 1 : 2 * block + 2, :] * jnp.exp(high - top)
    return top, total + other[2 * twin + 1 : 2 * twin + 2, :] * jnp.exp(other_high - top)


def merge_kernel(count, distance, mine, other, out_ref):
    out_ref[...] = jnp.zeros_like(out_ref)
    for block in range(count):
        top, total = merged(mine, other, block, distance)
        out_ref[2 * block : 2 * block + 1, :] = top
        out_ref[2 * block + 1 : 2 * block + 2, :] = total


def weigh(count, stats_ref, mine, other, exp_ref, weight_ref):
    rows = exp_ref.shape[1] // count
    repeat = rows // LANES
    classes = weight_ref.shape[0] // ROTS
    mass = jnp.zeros((classes, rows), jnp.float32)
    for block in range(count):
        top, total = merged(mine, other, block, count // 2)
        factor = jnp.exp(stats_ref[2 * block : 2 * block + 1, :] - top) / total
        scale = stats_ref[2 * count + block : 2 * count + block + 1, :]
        factor = jnp.concatenate([factor] * repeat, axis=1)
        scale = jnp.concatenate([scale] * repeat, axis=1)
        part = slice(block * rows, (block + 1) * rows)
        for rotation in range(ROTS):
            rotated = slice(rotation * classes, (rotation + 1) * classes)
            weight = exp_ref[rotated, part] * factor * scale
            mass = mass + weight * scale
            weight_ref[rotated, part] = weight.astype(jnp.bfloat16)
    return jnp.broadcast_to(jnp.sum(mass, axis=1, keepdims=True), (classes, LANES))


def block_sums(doms, width, distance, weight_ref, shifted_ref):
    classes = weight_ref.shape[0] // ROTS
    padded = -(-(width + 3) // LANES) * LANES
    place = lax.axis_index("dom") ^ distance
    first = place * width
    shifts = sorted({width * dom % LANES for dom in range(doms)})
    span = -(-(shifts[-1] + width) // LANES) * LANES
    base = first // LANES * LANES
    tiles = []
    for start in range(0, span, 2 * LANES):
        wide = min(2 * LANES, span - start)
        columns = pl.ds(pl.multiple_of(base + start, LANES), wide)
        product = jnp.dot(
            weight_ref[...], shifted_ref[:, columns], preferred_element_type=jnp.float32
        )
        for part in range(0, wide, LANES):
            lane = lane_index((classes, LANES)) % ANG
            inside = product[:classes, part : part + LANES]
            wrapped = None
            for rotation in range(1, ROTS):
                offset = ANG_STEP * rotation % ANG
                turned = pltpu.roll(
                    product[rotation * classes : (rotation + 1) * classes, part : part + LANES],
                    LANES - offset,
                    1,
                )
                within = lane < ANG - offset
                inside = inside + jnp.where(within, turned, 0.0)
                over = jnp.where(within, 0.0, turned)
                wrapped = over if wrapped is None else wrapped + over
            tiles.append(inside + pltpu.roll(wrapped, ANG, 1))
    total = jnp.concatenate(tiles, axis=1)
    aligned = total
    for shift in shifts:
        if shift:
            aligned = jnp.where(first - base == shift, pltpu.roll(total, span - shift, 1), aligned)
    if span < padded:
        aligned = jnp.concatenate(
            [aligned, jnp.zeros((classes, padded - span), jnp.float32)], axis=1
        )
    return aligned[:, :padded]


def store_block(width, value, mass, out_ref):
    high = mass.astype(jnp.bfloat16).astype(jnp.float32)
    middle = (mass - high).astype(jnp.bfloat16).astype(jnp.float32)
    low = (mass - high - middle).astype(jnp.bfloat16).astype(jnp.float32)
    lane = lane_index(value.shape)
    tail = jnp.where(
        lane == width, high, jnp.where(lane == width + 1, middle, jnp.where(lane == width + 2, low, 0.0))
    )
    value = jnp.where(lane < width, value, tail)
    out_ref[...] = value[:, : out_ref.shape[1]].astype(out_ref.dtype)


def pad_columns(value, padded):
    if value.shape[1] < padded:
        added = jnp.zeros((value.shape[0], padded - value.shape[1]), value.dtype)
        return jnp.concatenate([value, added], axis=1)
    return value[:, :padded]


def received_mass(width, ref):
    base = width // LANES * LANES
    tail = ref[:, base:].astype(jnp.float32)
    lane = base + lane_index(tail.shape)
    tail = jnp.where((lane >= width) & (lane < width + 3), tail, 0.0)
    return jnp.sum(tail, axis=1, keepdims=True)


def first_sums_kernel(count, doms, width, blocks, *refs):
    stats_ref, mine, other, exp_ref, shifted_ref, weight_ref, mass_ref = refs[:7]
    mass = weigh(count, stats_ref, mine, other, exp_ref, weight_ref)
    mass_ref[...] = mass
    for block, out_ref in zip(blocks, refs[7:]):
        store_block(width, block_sums(doms, width, block, weight_ref, shifted_ref), mass[:, :1], out_ref)


def rest_sums_kernel(doms, width, blocks, weight_ref, shifted_ref, mass_ref, *refs):
    for block, out_ref in zip(blocks, refs[-len(blocks) :]):
        value = block_sums(doms, width, block, weight_ref, shifted_ref)
        store_block(width, value, mass_ref[:, :1], out_ref)


def add_kernel(width, *refs):
    out_ref = refs[-1]
    padded = -(-out_ref.shape[1] // LANES) * LANES
    total, mass = None, None
    for ref in refs[:-1]:
        value = pad_columns(ref[...].astype(jnp.float32), padded)
        total = value if total is None else total + value
        tail = received_mass(width, ref)
        mass = tail if mass is None else mass + tail
    store_block(width, total, mass, out_ref)


def final_kernel(width, own_ref, *refs):
    received, sums_ref, weights_ref = refs[:-2], refs[-2], refs[-1]
    total, mass = None, None
    for ref in (own_ref, *received):
        value = ref[:, :width].astype(jnp.float32)
        total = value if total is None else total + value
        tail = received_mass(width, ref)
        mass = tail if mass is None else mass + tail
    sums_ref[...] = total
    weights_ref[...] = to_lanes(mass, total.shape[0])


def call(kernel, shapes, scratch, flops, moved, *args, smem=(), hbm=(), chip=(), pinned=True, aliases=None):
    vmem = pl.BlockSpec(memory_space=pltpu.VMEM)
    scalar = pl.BlockSpec(memory_space=pltpu.SMEM)
    place = pl.BlockSpec(memory_space=pltpu.HBM)
    args = [
        pltpu.with_memory_space_constraint(a, pltpu.HBM) if i in hbm
        else pltpu.with_memory_space_constraint(a, pltpu.VMEM) if i in chip
        else a
        for i, a in enumerate(args)
    ]
    return pl.pallas_call(
        kernel,
        out_shape=[pltpu.VMEM(s.shape, s.dtype) if pinned else s for s in shapes],
        in_specs=[scalar if i in smem else place if i in hbm else vmem for i in range(len(args))],
        out_specs=[vmem] * len(shapes),
        scratch_shapes=scratch,
        input_output_aliases=aliases or {},
        compiler_params=pltpu.CompilerParams(vmem_limit_bytes=VMEM_LIMIT),
        cost_estimate=pl.CostEstimate(flops=flops, bytes_accessed=moved, transcendentals=0),
    )(*args)


def body(particle_spectra, class_spectra, shift_index, prior_rotation, particle_group, group_scale):
    count = lax.axis_size("cls")
    doms = lax.axis_size("dom")
    particles, candidates = shift_index.shape
    classes = class_spectra.shape[0]
    rows = particles * candidates
    width = COLS // doms
    padded = -(-(width + 3) // LANES) * LANES
    growth = (padded - width - 3) // (doms - 1)
    f32, bf16 = jnp.float32, jnp.bfloat16
    shape = jax.ShapeDtypeStruct

    phases = jnp.asarray(phase_rows())
    packed, classes_on_chip, scales, phases_on_chip = call(
        pack_kernel,
        [
            shape((particles, COLS + META), bf16),
            shape(class_spectra.shape, bf16),
            shape((1, group_scale.shape[0]), f32),
            shape(phases.shape, f32),
        ],
        [
            pltpu.VMEM((particles, candidates), jnp.int32),
            pltpu.VMEM((1, particles), jnp.int32),
            pltpu.VMEM((1, particles), jnp.int32),
            pltpu.SemaphoreType.DMA((7,)),
        ],
        particles * COLS,
        4 * particles * COLS,
        particle_spectra, shift_index, prior_rotation[None, :], particle_group[None, :],
        class_spectra, group_scale[None, :], phases,
        hbm=(0, 1, 2, 3, 4, 5, 6),
    )
    chunks = [packed] + [exchange(packed, "cls", distance) for distance in range(1, count)]
    stat_rows = -(-3 * count // 8) * 8
    work = 2 * rows * COLS * (ROTS * classes + 256)
    stats_shape = shape((stat_rows, LANES), f32)
    shifted_shape = shape((count * rows, COLS), bf16)
    exp_shape = shape((ROTS * classes, count * rows), f32)
    near, far = [0, 1], list(range(2, count))
    shifted, exps, stats, rotated, norm, table = call(
        functools.partial(first_kernel, count, near),
        [
            shifted_shape,
            exp_shape,
            stats_shape,
            shape((ROTS * classes, COLS), bf16),
            shape((classes, LANES), f32),
            shape((2 * LANES, COLS), bf16),
        ],
        [],
        work * len(near),
        4 * len(near) * rows * COLS,
        *[chunks[b] for b in near], classes_on_chip, phases_on_chip, scales,
    )
    shifted, exps, stats = call(
        functools.partial(rest_kernel, count, far),
        [shifted_shape, exp_shape, stats_shape],
        [],
        work * len(far),
        4 * len(far) * rows * COLS,
        *[chunks[b] for b in far], table, scales, rotated, norm, stats, shifted, exps,
        aliases={len(far) + 5: 0, len(far) + 6: 1},
        chip=(len(far) + 5, len(far) + 6),
    )
    mine, distance = stats, 1
    other = exchange(mine, "cls", distance)
    while 2 * distance < count:
        (mine,) = call(
            functools.partial(merge_kernel, count, distance),
            [shape((-(-2 * count // 8) * 8, LANES), f32)],
            [],
            1024,
            1024,
            mine, other,
        )
        distance *= 2
        other = exchange(mine, "cls", distance)
    low_bit = lambda b: b & -b
    early = list(range(doms - 1, 1, -2))
    order = early + [1] + sorted(range(2, doms, 2), key=lambda b: (low_bit(b), -b))
    extents = {b: width + 3 + (doms - 1 - place) * growth for place, b in enumerate(order)}
    late = [1] + list(range(0, doms, 2))
    weights, mass, *made = call(
        functools.partial(first_sums_kernel, count, doms, width, early),
        [shape((ROTS * classes, count * rows), bf16), shape((classes, LANES), f32)]
        + [shape((classes, extents[b]), bf16) for b in early],
        [],
        2 * count * rows * COLS * ROTS * classes // doms,
        4 * count * rows * width,
        stats, mine, other, exps, shifted,
        chip=(3, 4),
    )
    incoming = {b: [] for b in range(doms)}
    for b, block in zip(early, made):
        incoming[b ^ 1].append(exchange(block, "dom", 1))
    rest = call(
        functools.partial(rest_sums_kernel, doms, width, late),
        [
            shape((classes, extents.get(b, width + 3)), bf16 if b == 1 else f32) for b in late
        ],
        [],
        1024,
        1024,
        weights, shifted, mass, *made,
        chip=(1,),
    )
    blocks = dict(zip(late, rest))
    incoming[0].append(exchange(blocks[1], "dom", 1))
    for b in order[len(early) + 1 :]:
        (block,) = call(
            functools.partial(add_kernel, width),
            [shape((classes, extents[b]), bf16)],
            [],
            1024,
            1024,
            blocks[b], *incoming[b],
        )
        incoming[b ^ low_bit(b)].append(exchange(block, "dom", low_bit(b)))
    own, received = blocks[0], incoming[0]
    class_sums, class_weights = call(
        functools.partial(final_kernel, width),
        [shape((classes, width), f32), shape((1, classes), f32)],
        [],
        doms * classes * padded,
        4 * doms * classes * padded,
        own, *received,
        pinned=False,
    )
    return class_sums, class_weights.reshape(classes)


def solution(mesh):
    placed = (
        P(("groups", "dom", "cls"), None),
        P(("groups", "cls"), None),
        P(("groups", "dom", "cls"), None),
        P(("groups", "dom", "cls")),
        P(("groups", "dom", "cls")),
        P("groups"),
    )
    return jax.shard_map(
        body,
        mesh=mesh,
        in_specs=placed,
        out_specs=(P(("groups", "cls"), "dom"), P(("groups", "cls"))),
        check_vma=False,
    )
```

```python
import functools
import math

import jax
import jax.numpy as jnp
import numpy as np
from jax import lax
from jax.experimental import pallas as pl
from jax.experimental.pallas import tpu as pltpu
from jax.sharding import PartitionSpec as P

CYCLES = 18
ANG = 64
IMG = 64
ANG_STEP = 1
ROTS = 8
SHIFT_R = 5
SHIFTW = 11
HALF = CYCLES * ANG
COLS = 2 * HALF
LANES = 128
SUB = 8
META = LANES
ROT_PRIOR = 0.5
VMEM_LIMIT = 20 * 1024 * 1024


def column_layout(doms):
    width = COLS // doms
    main = width - ANG
    half = doms // 2
    if width % ANG or main <= 0 or main % LANES or half * ANG % LANES:
        step = 3 * LANES
        segments = [(start, HALF + start, step) for start in range(0, HALF, step)]
        return list(range(COLS // ANG)), segments, 0
    per = width // ANG
    groups = [per * dom + group for dom in range(doms) for group in range(per - 1)]
    groups += [per * dom + per - 1 for dom in range(doms)]
    segments = [(dom * main, (half + dom) * main, main) for dom in range(half)]
    segments.append((doms * main, doms * main + half * ANG, half * ANG))
    return groups, segments, main


def tile_of(groups, tile, read):
    low, high = groups[2 * tile], groups[2 * tile + 1]
    if low % 2 == 0 and high == low + 1:
        return read(low // 2)
    first, second = read(low // 2), read(high // 2)
    first = pltpu.roll(first, ANG, 1) if low % 2 else first
    second = second if high % 2 else pltpu.roll(second, ANG, 1)
    return jnp.where(lane_index(first.shape) < ANG, first, second)


def phase_rows(groups):
    angles = np.arange(ANG) * (2.0 * math.pi / ANG)
    radius = np.arange(CYCLES) + 1.0
    fx = (radius[:, None] * np.cos(angles)[None, :]).reshape(-1)
    fy = (radius[:, None] * np.sin(angles)[None, :]).reshape(-1)
    offsets = np.arange(SHIFTW) - SHIFT_R
    unit = 2.0 * math.pi / IMG
    along_x = unit * offsets[:, None] * fx[None, :]
    along_y = unit * offsets[:, None] * fy[None, :]
    both = (along_x[SUB:, None, :] + along_y[None, SUB:, :]).reshape(-1, HALF)
    values = np.zeros((48, COLS), np.float32)
    for start, phase in ((0, along_x), (16, along_y), (32, both)):
        values[start : start + len(phase)] = np.concatenate([np.cos(phase), np.sin(phase)], axis=1)
    columns = np.concatenate([np.arange(ANG) + ANG * group for group in groups])
    return values[:, columns]


def build_table(segments, rows_ref, table_ref):
    for real_start, imag_start, width in segments:
        real = slice(real_start, real_start + width)
        imag = slice(imag_start, imag_start + width)

        def product(block, row):
            c, s = rows_ref[block : block + SUB, real], rows_ref[block : block + SUB, imag]
            d, t = rows_ref[row : row + 1, real], rows_ref[row : row + 1, imag]
            return c * d - s * t, s * d + c * t

        blocks = [product(0, 16 + y) for y in range(SHIFTW)]
        blocks += [product(16, x) for x in range(SUB, SHIFTW)]
        blocks += [
            (rows_ref[row : row + SUB, real], rows_ref[row : row + SUB, imag])
            for row in (32, 32 + SUB)
        ]
        for pair in range(0, len(blocks), 2):
            for part, columns in ((0, real), (1, imag)):
                value = jnp.concatenate([blocks[pair][part], blocks[pair + 1][part]], axis=0)
                high = value.astype(jnp.bfloat16)
                low = (value - high.astype(jnp.float32)).astype(jnp.bfloat16)
                row = pair * SUB
                table_ref[row : row + 2 * SUB, columns] = high
                table_ref[LANES + row : LANES + row + 2 * SUB, columns] = low


def table_row(index):
    y = jnp.floor((index + 0.5) * (1.0 / SHIFTW))
    x = index - SHIFTW * y
    near = SUB * y + x
    side = SUB * (SHIFTW + x - SUB) + y
    corner = SUB * (2 * SHIFTW - SUB) + (SHIFTW - SUB) * (x - SUB) + (y - SUB)
    return jnp.where(x < SUB, near, jnp.where(y < SUB, side, corner))


def exchange(array, axis, distance):
    return lax.ppermute(array, axis, [(i, i ^ distance) for i in range(lax.axis_size(axis))])


def lane_index(shape):
    return lax.broadcasted_iota(jnp.int32, shape, len(shape) - 1)


def rotate_classes(groups, class_ref, rotated_ref, norm_ref):
    classes = class_ref.shape[0]
    total = jnp.zeros((classes, LANES), jnp.float32)
    lane = lane_index((classes, LANES)) % ANG
    for tile in range(COLS // LANES):
        columns = slice(tile * LANES, (tile + 1) * LANES)
        value = tile_of(
            groups, tile, lambda k: class_ref[:, k * LANES : (k + 1) * LANES]
        )
        wide = value.astype(jnp.float32)
        total = total + wide * wide
        other = pltpu.roll(value, ANG, 1)
        for rotation in range(ROTS):
            offset = ANG_STEP * rotation % ANG
            turned = value
            if offset:
                turned = pltpu.roll(jnp.where(lane < ANG - offset, value, other), offset, 1)
            rotated_ref[rotation * classes : (rotation + 1) * classes, columns] = turned
    norm_ref[...] = jnp.broadcast_to(jnp.sum(total, axis=1, keepdims=True), (classes, LANES))


def to_lanes(column, width):
    n = column.shape[0]
    row = lax.broadcasted_iota(jnp.int32, (n, width), 0)
    return jnp.sum(
        jnp.where(lane_index((n, width)) % n == row, column, 0.0), axis=0, keepdims=True
    )


def fold_lanes(row, period, combine):
    result = row[:, :LANES]
    for part in range(1, row.shape[1] // LANES):
        result = combine(result, row[:, part * LANES : (part + 1) * LANES])
    step = LANES // 2
    while step >= period:
        result = combine(result, pltpu.roll(result, step, 1))
        step //= 2
    return result


def to_column(row):
    n = row.shape[1]
    diagonal = lax.broadcasted_iota(jnp.int32, (n, n), 0) == lane_index((n, n))
    return jnp.sum(jnp.where(diagonal, row, 0.0), axis=1, keepdims=True)


def pack_kernel(
    groups, particle_hbm, index_hbm, prior_hbm, group_hbm, class_hbm, scale_hbm, rows_hbm,
    packed_ref, class_ref, scale_ref, rows_ref, particle_ref, index_ref, prior_ref, group_ref, sems,
):
    particles, candidates = index_ref.shape
    copies = [
        pltpu.make_async_copy(source, target, sems.at[i])
        for i, (source, target) in enumerate(
            [
                (index_hbm, index_ref),
                (prior_hbm, prior_ref),
                (group_hbm, group_ref),
                (particle_hbm, particle_ref),
                (class_hbm, class_ref),
                (scale_hbm, scale_ref),
                (rows_hbm, rows_ref),
            ]
        )
    ]
    for copy in copies:
        copy.start()
    for copy in copies[:3]:
        copy.wait()
    lane = lane_index((particles, META))
    index = jnp.concatenate(
        [table_row(index_ref[...].astype(jnp.float32)), jnp.zeros((particles, META - candidates), jnp.float32)],
        axis=1,
    )
    prior = to_column(prior_ref[...].astype(jnp.float32))
    group = to_column(group_ref[...].astype(jnp.float32))
    meta = jnp.where(lane == candidates, prior, jnp.where(lane == candidates + 1, group, index))
    packed_ref[:, COLS:] = meta.astype(jnp.bfloat16)
    copies[3].wait()
    for tile in range(COLS // LANES):
        packed_ref[:, tile * LANES : (tile + 1) * LANES] = tile_of(
            groups, tile, lambda k: particle_ref[:, k * LANES : (k + 1) * LANES]
        )
    for copy in copies[4:]:
        copy.wait()


def score_block(segments, block_ref, table_ref, scale_ref, rotated_ref, norm_ref, shifted_ref, out):
    particles = block_ref.shape[0]
    classes = norm_ref.shape[0]
    candidates = shifted_ref.shape[0] // particles
    rows = particles * candidates
    repeat = rows // LANES
    meta = block_ref[:, COLS : COLS + META].astype(jnp.float32)
    index = meta[:, :candidates].astype(jnp.int32)
    lane = lane_index((particles, LANES))
    hot = jnp.concatenate(
        [
            jnp.where(index[:, t : t + 1] == lane, 1.0, 0.0).astype(jnp.bfloat16)
            for t in range(candidates)
        ],
        axis=0,
    )
    hot = jnp.concatenate([hot, hot], axis=1)
    groups = scale_ref.shape[1]
    group = meta[:, candidates + 1 : candidates + 2].astype(jnp.int32)
    scale_column = jnp.sum(
        jnp.where(group == lane_index((particles, groups)), scale_ref[...], 0.0),
        axis=1,
        keepdims=True,
    )
    scale = to_lanes(scale_column, rows)
    prior = to_lanes(meta[:, candidates : candidates + 1], rows)
    for real_start, imag_start, width in segments:
        real_columns = slice(real_start, real_start + width)
        imag_columns = slice(imag_start, imag_start + width)
        cosine = jnp.dot(hot, table_ref[:, real_columns], preferred_element_type=jnp.float32)
        sine = jnp.dot(hot, table_ref[:, imag_columns], preferred_element_type=jnp.float32)
        real = block_ref[:, real_columns].astype(jnp.float32)
        imag = block_ref[:, imag_columns].astype(jnp.float32)
        for t in range(candidates):
            part = slice(t * particles, (t + 1) * particles)
            c, s = cosine[part], sine[part]
            shifted_ref[part, real_columns] = (real * c - imag * s).astype(jnp.bfloat16)
            shifted_ref[part, imag_columns] = (real * s + imag * c).astype(jnp.bfloat16)
    product = lax.dot_general(
        rotated_ref[...],
        shifted_ref[...],
        (((1,), (1,)), ((), ())),
        preferred_element_type=jnp.float32,
    )
    norm = jnp.concatenate([norm_ref[...]] * repeat, axis=1)
    half_square = 0.5 * scale * scale
    scores = []
    highest = None
    for rotation in range(ROTS):
        distance = jnp.abs(rotation - prior)
        score = (
            scale * product[rotation * classes : (rotation + 1) * classes]
            - half_square * norm
            - ROT_PRIOR * (distance * distance)
        )
        scores.append(score)
        peak = jnp.max(score, axis=0, keepdims=True)
        highest = peak if highest is None else jnp.maximum(highest, peak)
    highest = fold_lanes(highest, particles, jnp.maximum)
    wide = jnp.concatenate([highest] * repeat, axis=1)
    total = None
    for rotation in range(ROTS):
        value = jnp.exp(scores[rotation] - wide)
        out(rotation, value)
        added = jnp.sum(value, axis=0, keepdims=True)
        total = added if total is None else total + added
    total = fold_lanes(total, particles, jnp.add)
    return highest, total, scale[:, :LANES]


def score_blocks(count, segments, chunks, blocks, table_ref, scale_ref, rotated_ref, norm_ref, shifted_ref, exp_ref, stats_ref):
    classes = norm_ref.shape[0]
    rows = exp_ref.shape[1] // count
    for block, block_ref in zip(chunks, blocks):
        part = slice(block * rows, (block + 1) * rows)

        def out(rotation, value):
            exp_ref[rotation * classes : (rotation + 1) * classes, part] = value

        highest, total, scale = score_block(
            segments, block_ref, table_ref, scale_ref, rotated_ref, norm_ref,
            shifted_ref.at[part, :], out,
        )
        stats_ref[2 * block : 2 * block + 1, :] = highest
        stats_ref[2 * block + 1 : 2 * block + 2, :] = total
        stats_ref[2 * count + block : 2 * count + block + 1, :] = scale


def first_kernel(count, groups, segments, chunks, *refs):
    blocks, refs = refs[: len(chunks)], refs[len(chunks) :]
    class_ref, rows_ref, scale_ref = refs[:3]
    shifted_ref, exp_ref, stats_ref, rotated_ref, norm_ref, table_ref = refs[3:]
    build_table(segments, rows_ref, table_ref)
    rotate_classes(groups, class_ref, rotated_ref, norm_ref)
    stats_ref[...] = jnp.zeros_like(stats_ref)
    score_blocks(
        count, segments, chunks, blocks, table_ref, scale_ref, rotated_ref, norm_ref,
        shifted_ref, exp_ref, stats_ref,
    )


def rest_kernel(count, segments, chunks, *refs):
    blocks, refs = refs[: len(chunks)], refs[len(chunks) :]
    table_ref, scale_ref, rotated_ref, norm_ref, before_ref = refs[:5]
    shifted_ref, exp_ref, stats_ref = refs[7:]
    stats_ref[...] = before_ref[...]
    score_blocks(
        count, segments, chunks, blocks, table_ref, scale_ref, rotated_ref, norm_ref,
        shifted_ref, exp_ref, stats_ref,
    )


def merged(mine, other, block, distance):
    twin = block ^ distance
    high, other_high = mine[2 * block : 2 * block + 1, :], other[2 * twin : 2 * twin + 1, :]
    top = jnp.maximum(high, other_high)
    total = mine[2 * block + 1 : 2 * block + 2, :] * jnp.exp(high - top)
    return top, total + other[2 * twin + 1 : 2 * twin + 2, :] * jnp.exp(other_high - top)


def merge_kernel(count, distance, mine, other, out_ref):
    out_ref[...] = jnp.zeros_like(out_ref)
    for block in range(count):
        top, total = merged(mine, other, block, distance)
        out_ref[2 * block : 2 * block + 1, :] = top
        out_ref[2 * block + 1 : 2 * block + 2, :] = total


def weigh(count, stats_ref, mine, other, exp_ref, weight_ref):
    rows = exp_ref.shape[1] // count
    repeat = rows // LANES
    classes = weight_ref.shape[0] // ROTS
    mass = jnp.zeros((classes, rows), jnp.float32)
    for block in range(count):
        top, total = merged(mine, other, block, count // 2)
        factor = jnp.exp(stats_ref[2 * block : 2 * block + 1, :] - top) / total
        scale = stats_ref[2 * count + block : 2 * count + block + 1, :]
        factor = jnp.concatenate([factor] * repeat, axis=1)
        scale = jnp.concatenate([scale] * repeat, axis=1)
        part = slice(block * rows, (block + 1) * rows)
        for rotation in range(ROTS):
            rotated = slice(rotation * classes, (rotation + 1) * classes)
            weight = exp_ref[rotated, part] * factor * scale
            mass = mass + weight * scale
            weight_ref[rotated, part] = weight.astype(jnp.bfloat16)
    return jnp.broadcast_to(jnp.sum(mass, axis=1, keepdims=True), (classes, LANES))


def window_sums(weight_ref, shifted_ref, start, wide):
    classes = weight_ref.shape[0] // ROTS
    product = jnp.dot(
        weight_ref[...], shifted_ref[:, pl.ds(start, wide)], preferred_element_type=jnp.float32
    )
    lane = lane_index((classes, LANES)) % ANG
    tiles = []
    for part in range(0, wide, LANES):
        inside = product[:classes, part : part + LANES]
        wrapped = None
        for rotation in range(1, ROTS):
            offset = ANG_STEP * rotation % ANG
            turned = pltpu.roll(
                product[rotation * classes : (rotation + 1) * classes, part : part + LANES],
                LANES - offset,
                1,
            )
            within = lane < ANG - offset
            inside = inside + jnp.where(within, turned, 0.0)
            over = jnp.where(within, 0.0, turned)
            wrapped = over if wrapped is None else wrapped + over
        tiles.append(inside + pltpu.roll(wrapped, ANG, 1))
    return tiles


def block_sums(doms, width, main, distance, weight_ref, shifted_ref, tails_ref):
    classes = weight_ref.shape[0] // ROTS
    padded = -(-(width + 3) // LANES) * LANES
    place = lax.axis_index("dom") ^ distance
    first = place * (main or width)
    shifts = [0] if main else sorted({width * dom % LANES for dom in range(doms)})
    span = main or -(-(shifts[-1] + width) // LANES) * LANES
    base = first // LANES * LANES
    tiles = []
    for start in range(0, span, 2 * LANES):
        tiles += window_sums(
            weight_ref,
            shifted_ref,
            pl.multiple_of(base + start, LANES),
            min(2 * LANES, span - start),
        )
    if main:
        tail = None
        for dom in range(doms):
            part = dom * ANG // LANES * LANES
            piece = tails_ref[:, part : part + LANES]
            piece = pltpu.roll(piece, ANG, 1) if dom % 2 else piece
            tail = piece if tail is None else jnp.where(place == dom, piece, tail)
        tiles.append(tail)
    total = jnp.concatenate(tiles, axis=1)
    aligned = total
    for shift in shifts:
        if shift:
            aligned = jnp.where(first - base == shift, pltpu.roll(total, span - shift, 1), aligned)
    return pad_columns(aligned, padded)


def store_block(width, value, mass, out_ref):
    high = mass.astype(jnp.bfloat16).astype(jnp.float32)
    middle = (mass - high).astype(jnp.bfloat16).astype(jnp.float32)
    low = (mass - high - middle).astype(jnp.bfloat16).astype(jnp.float32)
    lane = lane_index(value.shape)
    tail = jnp.where(
        lane == width, high, jnp.where(lane == width + 1, middle, jnp.where(lane == width + 2, low, 0.0))
    )
    value = jnp.where(lane < width, value, tail)
    out_ref[...] = value[:, : out_ref.shape[1]].astype(out_ref.dtype)


def pad_columns(value, padded):
    if value.shape[1] < padded:
        added = jnp.zeros((value.shape[0], padded - value.shape[1]), value.dtype)
        return jnp.concatenate([value, added], axis=1)
    return value[:, :padded]


def received_mass(width, ref):
    base = width // LANES * LANES
    tail = ref[:, base:].astype(jnp.float32)
    lane = base + lane_index(tail.shape)
    tail = jnp.where((lane >= width) & (lane < width + 3), tail, 0.0)
    return jnp.sum(tail, axis=1, keepdims=True)


def first_sums_kernel(count, doms, width, main, blocks, *refs):
    stats_ref, mine, other, exp_ref, shifted_ref, weight_ref, mass_ref, tails_ref = refs[:8]
    mass = weigh(count, stats_ref, mine, other, exp_ref, weight_ref)
    mass_ref[...] = mass
    tails_ref[...] = jnp.zeros_like(tails_ref)
    for start in range(0, doms * ANG if main else 0, 2 * LANES):
        tiles = window_sums(weight_ref, shifted_ref, doms * main + start, 2 * LANES)
        tails_ref[:, start : start + 2 * LANES] = jnp.concatenate(tiles, axis=1)
    for block, out_ref in zip(blocks, refs[8:]):
        value = block_sums(doms, width, main, block, weight_ref, shifted_ref, tails_ref)
        store_block(width, value, mass[:, :1], out_ref)


def rest_sums_kernel(doms, width, main, blocks, weight_ref, shifted_ref, mass_ref, tails_ref, *refs):
    for block, out_ref in zip(blocks, refs[-len(blocks) :]):
        value = block_sums(doms, width, main, block, weight_ref, shifted_ref, tails_ref)
        store_block(width, value, mass_ref[:, :1], out_ref)


def add_kernel(width, *refs):
    out_ref = refs[-1]
    padded = -(-out_ref.shape[1] // LANES) * LANES
    total, mass = None, None
    for ref in refs[:-1]:
        value = pad_columns(ref[...].astype(jnp.float32), padded)
        total = value if total is None else total + value
        tail = received_mass(width, ref)
        mass = tail if mass is None else mass + tail
    store_block(width, total, mass, out_ref)


def final_kernel(width, own_ref, *refs):
    received, sums_ref, weights_ref = refs[:-2], refs[-2], refs[-1]
    total, mass = None, None
    for ref in (own_ref, *received):
        value = ref[:, :width].astype(jnp.float32)
        total = value if total is None else total + value
        tail = received_mass(width, ref)
        mass = tail if mass is None else mass + tail
    sums_ref[...] = total
    weights_ref[...] = to_lanes(mass, total.shape[0])


def call(kernel, shapes, scratch, flops, moved, *args, smem=(), hbm=(), chip=(), pinned=True, aliases=None):
    vmem = pl.BlockSpec(memory_space=pltpu.VMEM)
    scalar = pl.BlockSpec(memory_space=pltpu.SMEM)
    place = pl.BlockSpec(memory_space=pltpu.HBM)
    args = [
        pltpu.with_memory_space_constraint(a, pltpu.HBM) if i in hbm
        else pltpu.with_memory_space_constraint(a, pltpu.VMEM) if i in chip
        else a
        for i, a in enumerate(args)
    ]
    return pl.pallas_call(
        kernel,
        out_shape=[pltpu.VMEM(s.shape, s.dtype) if pinned else s for s in shapes],
        in_specs=[scalar if i in smem else place if i in hbm else vmem for i in range(len(args))],
        out_specs=[vmem] * len(shapes),
        scratch_shapes=scratch,
        input_output_aliases=aliases or {},
        compiler_params=pltpu.CompilerParams(vmem_limit_bytes=VMEM_LIMIT),
        cost_estimate=pl.CostEstimate(flops=flops, bytes_accessed=moved, transcendentals=0),
    )(*args)


def body(particle_spectra, class_spectra, shift_index, prior_rotation, particle_group, group_scale):
    count = lax.axis_size("cls")
    doms = lax.axis_size("dom")
    particles, candidates = shift_index.shape
    classes = class_spectra.shape[0]
    rows = particles * candidates
    width = COLS // doms
    padded = -(-(width + 3) // LANES) * LANES
    growth = (padded - width - 3) // (doms - 1)
    f32, bf16 = jnp.float32, jnp.bfloat16
    shape = jax.ShapeDtypeStruct

    groups, segments, main = column_layout(doms)
    phases = jnp.asarray(phase_rows(groups))
    packed, classes_on_chip, scales, phases_on_chip = call(
        functools.partial(pack_kernel, groups),
        [
            shape((particles, COLS + META), bf16),
            shape(class_spectra.shape, bf16),
            shape((1, group_scale.shape[0]), f32),
            shape(phases.shape, f32),
        ],
        [
            pltpu.VMEM((particles, COLS), bf16),
            pltpu.VMEM((particles, candidates), jnp.int32),
            pltpu.VMEM((1, particles), jnp.int32),
            pltpu.VMEM((1, particles), jnp.int32),
            pltpu.SemaphoreType.DMA((7,)),
        ],
        particles * COLS,
        4 * particles * COLS,
        particle_spectra, shift_index, prior_rotation[None, :], particle_group[None, :],
        class_spectra, group_scale[None, :], phases,
        hbm=(0, 1, 2, 3, 4, 5, 6),
    )
    chunks = [packed] + [exchange(packed, "cls", distance) for distance in range(1, count)]
    stat_rows = -(-3 * count // 8) * 8
    work = 2 * rows * COLS * (ROTS * classes + 256)
    stats_shape = shape((stat_rows, LANES), f32)
    shifted_shape = shape((count * rows, COLS), bf16)
    exp_shape = shape((ROTS * classes, count * rows), f32)
    near, far = [0, 1], list(range(2, count))
    shifted, exps, stats, rotated, norm, table = call(
        functools.partial(first_kernel, count, groups, segments, near),
        [
            shifted_shape,
            exp_shape,
            stats_shape,
            shape((ROTS * classes, COLS), bf16),
            shape((classes, LANES), f32),
            shape((2 * LANES, COLS), bf16),
        ],
        [],
        work * len(near),
        4 * len(near) * rows * COLS,
        *[chunks[b] for b in near], classes_on_chip, phases_on_chip, scales,
    )
    shifted, exps, stats = call(
        functools.partial(rest_kernel, count, segments, far),
        [shifted_shape, exp_shape, stats_shape],
        [],
        work * len(far),
        4 * len(far) * rows * COLS,
        *[chunks[b] for b in far], table, scales, rotated, norm, stats, shifted, exps,
        aliases={len(far) + 5: 0, len(far) + 6: 1},
        chip=(len(far) + 5, len(far) + 6),
    )
    mine, distance = stats, 1
    other = exchange(mine, "cls", distance)
    while 2 * distance < count:
        (mine,) = call(
            functools.partial(merge_kernel, count, distance),
            [shape((-(-2 * count // 8) * 8, LANES), f32)],
            [],
            1024,
            1024,
            mine, other,
        )
        distance *= 2
        other = exchange(mine, "cls", distance)
    low_bit = lambda b: b & -b
    early = list(range(doms - 1, 0, -2))
    order = early + sorted(range(2, doms, 2), key=lambda b: (low_bit(b), -b))
    extents = {b: width + 3 + (doms - 1 - place) * growth for place, b in enumerate(order)}
    late = list(range(0, doms, 2))
    weights, mass, tails, *made = call(
        functools.partial(first_sums_kernel, count, doms, width, main, early),
        [
            shape((ROTS * classes, count * rows), bf16),
            shape((classes, LANES), f32),
            shape((classes, doms * ANG if main else LANES), f32),
        ]
        + [shape((classes, extents[b]), bf16) for b in early],
        [],
        2 * count * rows * COLS * ROTS * classes // doms,
        4 * count * rows * width,
        stats, mine, other, exps, shifted,
        chip=(3, 4),
    )
    incoming = {b: [] for b in range(doms)}
    for b, block in zip(early, made):
        incoming[b ^ 1].append(exchange(block, "dom", 1))
    rest = call(
        functools.partial(rest_sums_kernel, doms, width, main, late),
        [shape((classes, width + 3), f32) for b in late],
        [],
        1024,
        1024,
        weights, shifted, mass, tails, *made,
        chip=(1,),
    )
    blocks = dict(zip(late, rest))
    for b in order[len(early) :]:
        (block,) = call(
            functools.partial(add_kernel, width),
            [shape((classes, extents[b]), bf16)],
            [],
            1024,
            1024,
            blocks[b], *incoming[b],
        )
        incoming[b ^ low_bit(b)].append(exchange(block, "dom", low_bit(b)))
    own, received = blocks[0], incoming[0]
    class_sums, class_weights = call(
        functools.partial(final_kernel, width),
        [shape((classes, width), f32), shape((1, classes), f32)],
        [],
        doms * classes * padded,
        4 * doms * classes * padded,
        own, *received,
        pinned=False,
    )
    return class_sums, class_weights.reshape(classes)


def solution(mesh):
    placed = (
        P(("groups", "dom", "cls"), None),
        P(("groups", "cls"), None),
        P(("groups", "dom", "cls"), None),
        P(("groups", "dom", "cls")),
        P(("groups", "dom", "cls")),
        P("groups"),
    )
    return jax.shard_map(
        body,
        mesh=mesh,
        in_specs=placed,
        out_specs=(P(("groups", "cls"), "dom"), P(("groups", "cls"))),
        check_vma=False,
    )
```

```python
import functools
import math

import jax
import jax.numpy as jnp
import numpy as np
from jax import lax
from jax.experimental import pallas as pl
from jax.experimental.pallas import tpu as pltpu
from jax.sharding import PartitionSpec as P

CYCLES = 18
ANG = 64
IMG = 64
ANG_STEP = 1
ROTS = 8
SHIFT_R = 5
SHIFTW = 11
HALF = CYCLES * ANG
COLS = 2 * HALF
LANES = 128
SUB = 8
META = LANES
ROT_PRIOR = 0.5
VMEM_LIMIT = 20 * 1024 * 1024


def column_layout(doms):
    width = COLS // doms
    main = width - ANG
    half = doms // 2
    if width % ANG or main <= 0 or main % LANES or half * ANG % LANES:
        step = 3 * LANES
        segments = [(start, HALF + start, step) for start in range(0, HALF, step)]
        return list(range(COLS // ANG)), segments, 0
    per = width // ANG
    groups = [per * dom + group for dom in range(doms) for group in range(per - 1)]
    groups += [per * dom + per - 1 for dom in range(doms)]
    segments = [(dom * main, (half + dom) * main, main) for dom in range(half)]
    segments.append((doms * main, doms * main + half * ANG, half * ANG))
    return groups, segments, main


def tile_of(groups, tile, read):
    low, high = groups[2 * tile], groups[2 * tile + 1]
    if low % 2 == 0 and high == low + 1:
        return read(low // 2)
    first, second = read(low // 2), read(high // 2)
    first = pltpu.roll(first, ANG, 1) if low % 2 else first
    second = second if high % 2 else pltpu.roll(second, ANG, 1)
    return jnp.where(lane_index(first.shape) < ANG, first, second)


def phase_rows(groups):
    angles = np.arange(ANG) * (2.0 * math.pi / ANG)
    radius = np.arange(CYCLES) + 1.0
    fx = (radius[:, None] * np.cos(angles)[None, :]).reshape(-1)
    fy = (radius[:, None] * np.sin(angles)[None, :]).reshape(-1)
    offsets = np.arange(SHIFTW) - SHIFT_R
    unit = 2.0 * math.pi / IMG
    along_x = unit * offsets[:, None] * fx[None, :]
    along_y = unit * offsets[:, None] * fy[None, :]
    both = (along_x[SUB:, None, :] + along_y[None, SUB:, :]).reshape(-1, HALF)
    values = np.zeros((48, COLS), np.float32)
    for start, phase in ((0, along_x), (16, along_y), (32, both)):
        values[start : start + len(phase)] = np.concatenate([np.cos(phase), np.sin(phase)], axis=1)
    columns = np.concatenate([np.arange(ANG) + ANG * group for group in groups])
    return values[:, columns]


def build_table(segments, rows_ref, table_ref):
    for real_start, imag_start, width in segments:
        real = slice(real_start, real_start + width)
        imag = slice(imag_start, imag_start + width)

        def product(block, row):
            c, s = rows_ref[block : block + SUB, real], rows_ref[block : block + SUB, imag]
            d, t = rows_ref[row : row + 1, real], rows_ref[row : row + 1, imag]
            return c * d - s * t, s * d + c * t

        blocks = [product(0, 16 + y) for y in range(SHIFTW)]
        blocks += [product(16, x) for x in range(SUB, SHIFTW)]
        blocks += [
            (rows_ref[row : row + SUB, real], rows_ref[row : row + SUB, imag])
            for row in (32, 32 + SUB)
        ]
        for pair in range(0, len(blocks), 2):
            for part, columns in ((0, real), (1, imag)):
                value = jnp.concatenate([blocks[pair][part], blocks[pair + 1][part]], axis=0)
                high = value.astype(jnp.bfloat16)
                low = (value - high.astype(jnp.float32)).astype(jnp.bfloat16)
                row = pair * SUB
                table_ref[row : row + 2 * SUB, columns] = high
                table_ref[LANES + row : LANES + row + 2 * SUB, columns] = low


def table_row(index):
    y = jnp.floor((index + 0.5) * (1.0 / SHIFTW))
    x = index - SHIFTW * y
    near = SUB * y + x
    side = SUB * (SHIFTW + x - SUB) + y
    corner = SUB * (2 * SHIFTW - SUB) + (SHIFTW - SUB) * (x - SUB) + (y - SUB)
    return jnp.where(x < SUB, near, jnp.where(y < SUB, side, corner))


def exchange(array, axis, distance):
    return lax.ppermute(array, axis, [(i, i ^ distance) for i in range(lax.axis_size(axis))])


def lane_index(shape):
    return lax.broadcasted_iota(jnp.int32, shape, len(shape) - 1)


def rotate_classes(groups, class_ref, rotated_ref, norm_ref):
    classes = class_ref.shape[0]
    total = jnp.zeros((classes, LANES), jnp.float32)
    lane = lane_index((classes, LANES)) % ANG
    for tile in range(COLS // LANES):
        columns = slice(tile * LANES, (tile + 1) * LANES)
        value = tile_of(
            groups, tile, lambda k: class_ref[:, k * LANES : (k + 1) * LANES]
        )
        wide = value.astype(jnp.float32)
        total = total + wide * wide
        other = pltpu.roll(value, ANG, 1)
        for rotation in range(ROTS):
            offset = ANG_STEP * rotation % ANG
            turned = value
            if offset:
                turned = pltpu.roll(jnp.where(lane < ANG - offset, value, other), offset, 1)
            rotated_ref[rotation * classes : (rotation + 1) * classes, columns] = turned
    norm_ref[...] = jnp.broadcast_to(jnp.sum(total, axis=1, keepdims=True), (classes, LANES))


def to_lanes(column, width):
    n = column.shape[0]
    row = lax.broadcasted_iota(jnp.int32, (n, width), 0)
    return jnp.sum(
        jnp.where(lane_index((n, width)) % n == row, column, 0.0), axis=0, keepdims=True
    )


def fold_lanes(row, period, combine):
    result = row[:, :LANES]
    for part in range(1, row.shape[1] // LANES):
        result = combine(result, row[:, part * LANES : (part + 1) * LANES])
    step = LANES // 2
    while step >= period:
        result = combine(result, pltpu.roll(result, step, 1))
        step //= 2
    return result


def to_column(row):
    n = row.shape[1]
    diagonal = lax.broadcasted_iota(jnp.int32, (n, n), 0) == lane_index((n, n))
    return jnp.sum(jnp.where(diagonal, row, 0.0), axis=1, keepdims=True)


def pack_kernel(
    groups, particle_hbm, index_hbm, prior_hbm, group_hbm, class_hbm, scale_hbm, rows_hbm,
    packed_ref, class_ref, scale_ref, rows_ref, particle_ref, index_ref, prior_ref, group_ref, sems,
):
    particles, candidates = index_ref.shape
    copies = [
        pltpu.make_async_copy(source, target, sems.at[i])
        for i, (source, target) in enumerate(
            [
                (index_hbm, index_ref),
                (prior_hbm, prior_ref),
                (group_hbm, group_ref),
                (particle_hbm, particle_ref),
                (class_hbm, class_ref),
                (scale_hbm, scale_ref),
                (rows_hbm, rows_ref),
            ]
        )
    ]
    for copy in copies:
        copy.start()
    for copy in copies[:3]:
        copy.wait()
    lane = lane_index((particles, META))
    index = jnp.concatenate(
        [table_row(index_ref[...].astype(jnp.float32)), jnp.zeros((particles, META - candidates), jnp.float32)],
        axis=1,
    )
    prior = to_column(prior_ref[...].astype(jnp.float32))
    group = to_column(group_ref[...].astype(jnp.float32))
    meta = jnp.where(lane == candidates, prior, jnp.where(lane == candidates + 1, group, index))
    packed_ref[:, COLS:] = meta.astype(jnp.bfloat16)
    copies[3].wait()
    for tile in range(COLS // LANES):
        packed_ref[:, tile * LANES : (tile + 1) * LANES] = tile_of(
            groups, tile, lambda k: particle_ref[:, k * LANES : (k + 1) * LANES]
        )
    for copy in copies[4:]:
        copy.wait()


def score_block(segments, block_ref, table_ref, scale_ref, rotated_ref, norm_ref, shifted_ref, out):
    particles = block_ref.shape[0]
    classes = norm_ref.shape[0]
    candidates = shifted_ref.shape[0] // particles
    rows = particles * candidates
    repeat = rows // LANES
    meta = block_ref[:, COLS : COLS + META].astype(jnp.float32)
    index = meta[:, :candidates].astype(jnp.int32)
    lane = lane_index((particles, LANES))
    hot = jnp.concatenate(
        [
            jnp.where(index[:, t : t + 1] == lane, 1.0, 0.0).astype(jnp.bfloat16)
            for t in range(candidates)
        ],
        axis=0,
    )
    hot = jnp.concatenate([hot, hot], axis=1)
    groups = scale_ref.shape[1]
    group = meta[:, candidates + 1 : candidates + 2].astype(jnp.int32)
    scale_column = jnp.sum(
        jnp.where(group == lane_index((particles, groups)), scale_ref[...], 0.0),
        axis=1,
        keepdims=True,
    )
    scale = to_lanes(scale_column, rows)
    prior = to_lanes(meta[:, candidates : candidates + 1], rows)
    for real_start, imag_start, width in segments:
        real_columns = slice(real_start, real_start + width)
        imag_columns = slice(imag_start, imag_start + width)
        cosine = jnp.dot(hot, table_ref[:, real_columns], preferred_element_type=jnp.float32)
        sine = jnp.dot(hot, table_ref[:, imag_columns], preferred_element_type=jnp.float32)
        real = block_ref[:, real_columns].astype(jnp.float32)
        imag = block_ref[:, imag_columns].astype(jnp.float32)
        for t in range(candidates):
            part = slice(t * particles, (t + 1) * particles)
            c, s = cosine[part], sine[part]
            shifted_ref[part, real_columns] = (real * c - imag * s).astype(jnp.bfloat16)
            shifted_ref[part, imag_columns] = (real * s + imag * c).astype(jnp.bfloat16)
    product = lax.dot_general(
        rotated_ref[...],
        shifted_ref[...],
        (((1,), (1,)), ((), ())),
        preferred_element_type=jnp.float32,
    )
    norm = jnp.concatenate([norm_ref[...]] * repeat, axis=1)
    half_square = 0.5 * scale * scale
    scores = []
    highest = None
    for rotation in range(ROTS):
        distance = jnp.abs(rotation - prior)
        score = (
            scale * product[rotation * classes : (rotation + 1) * classes]
            - half_square * norm
            - ROT_PRIOR * (distance * distance)
        )
        scores.append(score)
        peak = jnp.max(score, axis=0, keepdims=True)
        highest = peak if highest is None else jnp.maximum(highest, peak)
    highest = fold_lanes(highest, particles, jnp.maximum)
    wide = jnp.concatenate([highest] * repeat, axis=1)
    total = None
    for rotation in range(ROTS):
        value = jnp.exp(scores[rotation] - wide)
        out(rotation, value)
        added = jnp.sum(value, axis=0, keepdims=True)
        total = added if total is None else total + added
    total = fold_lanes(total, particles, jnp.add)
    return highest, total, scale[:, :LANES]


def score_blocks(count, segments, chunks, blocks, table_ref, scale_ref, rotated_ref, norm_ref, shifted_ref, exp_ref, stats_ref):
    classes = norm_ref.shape[0]
    rows = exp_ref.shape[1] // count
    for block, block_ref in zip(chunks, blocks):
        part = slice(block * rows, (block + 1) * rows)

        def out(rotation, value):
            exp_ref[rotation * classes : (rotation + 1) * classes, part] = value

        highest, total, scale = score_block(
            segments, block_ref, table_ref, scale_ref, rotated_ref, norm_ref,
            shifted_ref.at[part, :], out,
        )
        stats_ref[2 * block : 2 * block + 1, :] = highest
        stats_ref[2 * block + 1 : 2 * block + 2, :] = total
        stats_ref[2 * count + block : 2 * count + block + 1, :] = scale


def first_kernel(count, groups, segments, chunks, *refs):
    blocks, refs = refs[: len(chunks)], refs[len(chunks) :]
    class_ref, rows_ref, scale_ref = refs[:3]
    shifted_ref, exp_ref, stats_ref, rotated_ref, norm_ref, table_ref = refs[3:]
    build_table(segments, rows_ref, table_ref)
    rotate_classes(groups, class_ref, rotated_ref, norm_ref)
    stats_ref[...] = jnp.zeros_like(stats_ref)
    score_blocks(
        count, segments, chunks, blocks, table_ref, scale_ref, rotated_ref, norm_ref,
        shifted_ref, exp_ref, stats_ref,
    )


def rest_kernel(count, segments, chunks, *refs):
    blocks, refs = refs[: len(chunks)], refs[len(chunks) :]
    table_ref, scale_ref, rotated_ref, norm_ref, before_ref = refs[:5]
    shifted_ref, exp_ref, stats_ref = refs[7:]
    stats_ref[...] = before_ref[...]
    score_blocks(
        count, segments, chunks, blocks, table_ref, scale_ref, rotated_ref, norm_ref,
        shifted_ref, exp_ref, stats_ref,
    )


def merged(mine, other, block, distance):
    twin = block ^ distance
    high, other_high = mine[2 * block : 2 * block + 1, :], other[2 * twin : 2 * twin + 1, :]
    top = jnp.maximum(high, other_high)
    total = mine[2 * block + 1 : 2 * block + 2, :] * jnp.exp(high - top)
    return top, total + other[2 * twin + 1 : 2 * twin + 2, :] * jnp.exp(other_high - top)


def merge_kernel(count, distance, mine, other, out_ref):
    out_ref[...] = jnp.zeros_like(out_ref)
    for block in range(count):
        top, total = merged(mine, other, block, distance)
        out_ref[2 * block : 2 * block + 1, :] = top
        out_ref[2 * block + 1 : 2 * block + 2, :] = total


def weigh(count, stats_ref, mine, other, exp_ref, weight_ref):
    rows = exp_ref.shape[1] // count
    repeat = rows // LANES
    classes = weight_ref.shape[0] // ROTS
    mass = jnp.zeros((classes, rows), jnp.float32)
    for block in range(count):
        top, total = merged(mine, other, block, count // 2)
        factor = jnp.exp(stats_ref[2 * block : 2 * block + 1, :] - top) / total
        scale = stats_ref[2 * count + block : 2 * count + block + 1, :]
        factor = jnp.concatenate([factor] * repeat, axis=1)
        scale = jnp.concatenate([scale] * repeat, axis=1)
        part = slice(block * rows, (block + 1) * rows)
        for rotation in range(ROTS):
            rotated = slice(rotation * classes, (rotation + 1) * classes)
            weight = exp_ref[rotated, part] * factor * scale
            mass = mass + weight * scale
            weight_ref[rotated, part] = weight.astype(jnp.bfloat16)
    return jnp.broadcast_to(jnp.sum(mass, axis=1, keepdims=True), (classes, LANES))


def window_sums(weight_ref, shifted_ref, start, wide):
    classes = weight_ref.shape[0] // ROTS
    product = jnp.dot(
        weight_ref[...], shifted_ref[:, pl.ds(start, wide)], preferred_element_type=jnp.float32
    )
    lane = lane_index((classes, LANES)) % ANG
    tiles = []
    for part in range(0, wide, LANES):
        inside = product[:classes, part : part + LANES]
        wrapped = None
        for rotation in range(1, ROTS):
            offset = ANG_STEP * rotation % ANG
            turned = pltpu.roll(
                product[rotation * classes : (rotation + 1) * classes, part : part + LANES],
                LANES - offset,
                1,
            )
            within = lane < ANG - offset
            inside = inside + jnp.where(within, turned, 0.0)
            over = jnp.where(within, 0.0, turned)
            wrapped = over if wrapped is None else wrapped + over
        tiles.append(inside + pltpu.roll(wrapped, ANG, 1))
    return tiles


def block_sums(doms, width, main, distance, weight_ref, shifted_ref, tails_ref):
    classes = weight_ref.shape[0] // ROTS
    padded = -(-(width + 3) // LANES) * LANES
    place = lax.axis_index("dom") ^ distance
    first = place * (main or width)
    shifts = [0] if main else sorted({width * dom % LANES for dom in range(doms)})
    span = main or -(-(shifts[-1] + width) // LANES) * LANES
    base = first // LANES * LANES
    tiles = []
    for start in range(0, span, 2 * LANES):
        tiles += window_sums(
            weight_ref,
            shifted_ref,
            pl.multiple_of(base + start, LANES),
            min(2 * LANES, span - start),
        )
    if main:
        tail = None
        for dom in range(doms):
            part = dom * ANG // LANES * LANES
            piece = tails_ref[:, part : part + LANES]
            piece = pltpu.roll(piece, ANG, 1) if dom % 2 else piece
            tail = piece if tail is None else jnp.where(place == dom, piece, tail)
        tiles.append(tail)
    total = jnp.concatenate(tiles, axis=1)
    aligned = total
    for shift in shifts:
        if shift:
            aligned = jnp.where(first - base == shift, pltpu.roll(total, span - shift, 1), aligned)
    return pad_columns(aligned, padded)


def store_block(width, value, mass, out_ref):
    high = mass.astype(jnp.bfloat16).astype(jnp.float32)
    middle = (mass - high).astype(jnp.bfloat16).astype(jnp.float32)
    low = (mass - high - middle).astype(jnp.bfloat16).astype(jnp.float32)
    lane = lane_index(value.shape)
    tail = jnp.where(
        lane == width, high, jnp.where(lane == width + 1, middle, jnp.where(lane == width + 2, low, 0.0))
    )
    value = jnp.where(lane < width, value, tail)
    out_ref[...] = value[:, : out_ref.shape[1]].astype(out_ref.dtype)


def pad_columns(value, padded):
    if value.shape[1] < padded:
        added = jnp.zeros((value.shape[0], padded - value.shape[1]), value.dtype)
        return jnp.concatenate([value, added], axis=1)
    return value[:, :padded]


def received_mass(width, ref):
    base = width // LANES * LANES
    tail = ref[:, base:].astype(jnp.float32)
    lane = base + lane_index(tail.shape)
    tail = jnp.where((lane >= width) & (lane < width + 3), tail, 0.0)
    return jnp.sum(tail, axis=1, keepdims=True)


def first_sums_kernel(count, doms, width, main, blocks, *refs):
    stats_ref, mine, other, exp_ref, shifted_ref, weight_ref, mass_ref, tails_ref = refs[:8]
    mass = weigh(count, stats_ref, mine, other, exp_ref, weight_ref)
    mass_ref[...] = mass
    tails_ref[...] = jnp.zeros_like(tails_ref)
    for start in range(0, doms * ANG if main else 0, 2 * LANES):
        tiles = window_sums(weight_ref, shifted_ref, doms * main + start, 2 * LANES)
        tails_ref[:, start : start + 2 * LANES] = jnp.concatenate(tiles, axis=1)
    for block, out_ref in zip(blocks, refs[8:]):
        value = block_sums(doms, width, main, block, weight_ref, shifted_ref, tails_ref)
        store_block(width, value, mass[:, :1], out_ref)


def rest_sums_kernel(doms, width, main, blocks, weight_ref, shifted_ref, mass_ref, tails_ref, *refs):
    for block, out_ref in zip(blocks, refs[-len(blocks) :]):
        value = block_sums(doms, width, main, block, weight_ref, shifted_ref, tails_ref)
        store_block(width, value, mass_ref[:, :1], out_ref)


def final_kernel(width, own_ref, *refs):
    received, sums_ref, weights_ref = refs[:-2], refs[-2], refs[-1]
    total, mass = None, None
    for ref in (own_ref, *received):
        value = ref[:, :width].astype(jnp.float32)
        total = value if total is None else total + value
        tail = received_mass(width, ref)
        mass = tail if mass is None else mass + tail
    sums_ref[...] = total
    weights_ref[...] = to_lanes(mass, total.shape[0])


def call(kernel, shapes, scratch, flops, moved, *args, smem=(), hbm=(), chip=(), pinned=True, aliases=None):
    vmem = pl.BlockSpec(memory_space=pltpu.VMEM)
    scalar = pl.BlockSpec(memory_space=pltpu.SMEM)
    place = pl.BlockSpec(memory_space=pltpu.HBM)
    args = [
        pltpu.with_memory_space_constraint(a, pltpu.HBM) if i in hbm
        else pltpu.with_memory_space_constraint(a, pltpu.VMEM) if i in chip
        else a
        for i, a in enumerate(args)
    ]
    return pl.pallas_call(
        kernel,
        out_shape=[pltpu.VMEM(s.shape, s.dtype) if pinned else s for s in shapes],
        in_specs=[scalar if i in smem else place if i in hbm else vmem for i in range(len(args))],
        out_specs=[vmem] * len(shapes),
        scratch_shapes=scratch,
        input_output_aliases=aliases or {},
        compiler_params=pltpu.CompilerParams(vmem_limit_bytes=VMEM_LIMIT),
        cost_estimate=pl.CostEstimate(flops=flops, bytes_accessed=moved, transcendentals=0),
    )(*args)


def body(particle_spectra, class_spectra, shift_index, prior_rotation, particle_group, group_scale):
    count = lax.axis_size("cls")
    doms = lax.axis_size("dom")
    particles, candidates = shift_index.shape
    classes = class_spectra.shape[0]
    rows = particles * candidates
    width = COLS // doms
    padded = -(-(width + 3) // LANES) * LANES
    growth = (padded - width - 3) // (doms - 1)
    f32, bf16 = jnp.float32, jnp.bfloat16
    shape = jax.ShapeDtypeStruct

    groups, segments, main = column_layout(doms)
    phases = jnp.asarray(phase_rows(groups))
    packed, classes_on_chip, scales, phases_on_chip = call(
        functools.partial(pack_kernel, groups),
        [
            shape((particles, COLS + META), bf16),
            shape(class_spectra.shape, bf16),
            shape((1, group_scale.shape[0]), f32),
            shape(phases.shape, f32),
        ],
        [
            pltpu.VMEM((particles, COLS), bf16),
            pltpu.VMEM((particles, candidates), jnp.int32),
            pltpu.VMEM((1, particles), jnp.int32),
            pltpu.VMEM((1, particles), jnp.int32),
            pltpu.SemaphoreType.DMA((7,)),
        ],
        particles * COLS,
        4 * particles * COLS,
        particle_spectra, shift_index, prior_rotation[None, :], particle_group[None, :],
        class_spectra, group_scale[None, :], phases,
        hbm=(0, 1, 2, 3, 4, 5, 6),
    )
    chunks = [packed] + [exchange(packed, "cls", distance) for distance in range(1, count)]
    stat_rows = -(-3 * count // 8) * 8
    work = 2 * rows * COLS * (ROTS * classes + 256)
    stats_shape = shape((stat_rows, LANES), f32)
    shifted_shape = shape((count * rows, COLS), bf16)
    exp_shape = shape((ROTS * classes, count * rows), f32)
    near, far = [0, 1], list(range(2, count))
    shifted, exps, stats, rotated, norm, table = call(
        functools.partial(first_kernel, count, groups, segments, near),
        [
            shifted_shape,
            exp_shape,
            stats_shape,
            shape((ROTS * classes, COLS), bf16),
            shape((classes, LANES), f32),
            shape((2 * LANES, COLS), bf16),
        ],
        [],
        work * len(near),
        4 * len(near) * rows * COLS,
        *[chunks[b] for b in near], classes_on_chip, phases_on_chip, scales,
    )
    shifted, exps, stats = call(
        functools.partial(rest_kernel, count, segments, far),
        [shifted_shape, exp_shape, stats_shape],
        [],
        work * len(far),
        4 * len(far) * rows * COLS,
        *[chunks[b] for b in far], table, scales, rotated, norm, stats, shifted, exps,
        aliases={len(far) + 5: 0, len(far) + 6: 1},
        chip=(len(far) + 5, len(far) + 6),
    )
    mine, distance = stats, 1
    other = exchange(mine, "cls", distance)
    while 2 * distance < count:
        (mine,) = call(
            functools.partial(merge_kernel, count, distance),
            [shape((-(-2 * count // 8) * 8, LANES), f32)],
            [],
            1024,
            1024,
            mine, other,
        )
        distance *= 2
        other = exchange(mine, "cls", distance)
    early, late = [doms - 1], list(range(doms - 2, -1, -1))
    extents = {b: width + 3 + b * growth for b in range(doms)}
    weights, mass, tails, *made = call(
        functools.partial(first_sums_kernel, count, doms, width, main, early),
        [
            shape((ROTS * classes, count * rows), bf16),
            shape((classes, LANES), f32),
            shape((classes, doms * ANG if main else LANES), f32),
        ]
        + [shape((classes, extents[b]), bf16) for b in early],
        [],
        2 * count * rows * COLS * ROTS * classes // doms,
        4 * count * rows * width,
        stats, mine, other, exps, shifted,
        chip=(3, 4),
    )
    rest = call(
        functools.partial(rest_sums_kernel, doms, width, main, late),
        [shape((classes, extents[b]), bf16 if b else f32) for b in late],
        [],
        1024,
        1024,
        weights, shifted, mass, tails, *made,
        chip=(1,),
    )
    blocks = dict(zip(early + late, [*made, *rest]))
    own = blocks[0]
    received = [exchange(blocks[b], "dom", b) for b in range(doms - 1, 0, -1)]
    class_sums, class_weights = call(
        functools.partial(final_kernel, width),
        [shape((classes, width), f32), shape((1, classes), f32)],
        [],
        doms * classes * padded,
        4 * doms * classes * padded,
        own, *received,
        pinned=False,
    )
    return class_sums, class_weights.reshape(classes)


def solution(mesh):
    placed = (
        P(("groups", "dom", "cls"), None),
        P(("groups", "cls"), None),
        P(("groups", "dom", "cls"), None),
        P(("groups", "dom", "cls")),
        P(("groups", "dom", "cls")),
        P("groups"),
    )
    return jax.shard_map(
        body,
        mesh=mesh,
        in_specs=placed,
        out_specs=(P(("groups", "cls"), "dom"), P(("groups", "cls"))),
        check_vma=False,
    )
```

```python
import functools
import math

import jax
import jax.numpy as jnp
import numpy as np
from jax import lax
from jax.experimental import pallas as pl
from jax.experimental.pallas import tpu as pltpu
from jax.sharding import PartitionSpec as P

CYCLES = 18
ANG = 64
IMG = 64
ANG_STEP = 1
ROTS = 8
SHIFT_R = 5
SHIFTW = 11
HALF = CYCLES * ANG
COLS = 2 * HALF
LANES = 128
SUB = 8
META = LANES
ROT_PRIOR = 0.5
VMEM_LIMIT = 20 * 1024 * 1024


def column_layout(doms):
    width = COLS // doms
    main = width - ANG
    half = doms // 2
    if width % ANG or main <= 0 or main % LANES or half * ANG % LANES:
        step = 3 * LANES
        segments = [(start, HALF + start, step) for start in range(0, HALF, step)]
        return list(range(COLS // ANG)), segments, 0
    per = width // ANG
    groups = [per * dom + group for dom in range(doms) for group in range(per - 1)]
    groups += [per * dom + per - 1 for dom in range(doms)]
    segments = [(dom * main, (half + dom) * main, main) for dom in range(half)]
    segments.append((doms * main, doms * main + half * ANG, half * ANG))
    return groups, segments, main


def tile_of(groups, tile, read):
    low, high = groups[2 * tile], groups[2 * tile + 1]
    if low % 2 == 0 and high == low + 1:
        return read(low // 2)
    first, second = read(low // 2), read(high // 2)
    first = pltpu.roll(first, ANG, 1) if low % 2 else first
    second = second if high % 2 else pltpu.roll(second, ANG, 1)
    return jnp.where(lane_index(first.shape) < ANG, first, second)


def phase_rows(groups):
    angles = np.arange(ANG) * (2.0 * math.pi / ANG)
    radius = np.arange(CYCLES) + 1.0
    fx = (radius[:, None] * np.cos(angles)[None, :]).reshape(-1)
    fy = (radius[:, None] * np.sin(angles)[None, :]).reshape(-1)
    offsets = np.arange(SHIFTW) - SHIFT_R
    unit = 2.0 * math.pi / IMG
    along_x = unit * offsets[:, None] * fx[None, :]
    along_y = unit * offsets[:, None] * fy[None, :]
    both = (along_x[SUB:, None, :] + along_y[None, SUB:, :]).reshape(-1, HALF)
    values = np.zeros((48, COLS), np.float32)
    for start, phase in ((0, along_x), (16, along_y), (32, both)):
        values[start : start + len(phase)] = np.concatenate([np.cos(phase), np.sin(phase)], axis=1)
    columns = np.concatenate([np.arange(ANG) + ANG * group for group in groups])
    return values[:, columns]


def build_table(segments, rows_ref, table_ref):
    for real_start, imag_start, width in segments:
        real = slice(real_start, real_start + width)
        imag = slice(imag_start, imag_start + width)

        def product(block, row):
            c, s = rows_ref[block : block + SUB, real], rows_ref[block : block + SUB, imag]
            d, t = rows_ref[row : row + 1, real], rows_ref[row : row + 1, imag]
            return c * d - s * t, s * d + c * t

        blocks = [product(0, 16 + y) for y in range(SHIFTW)]
        blocks += [product(16, x) for x in range(SUB, SHIFTW)]
        blocks += [
            (rows_ref[row : row + SUB, real], rows_ref[row : row + SUB, imag])
            for row in (32, 32 + SUB)
        ]
        for pair in range(0, len(blocks), 2):
            for part, columns in ((0, real), (1, imag)):
                value = jnp.concatenate([blocks[pair][part], blocks[pair + 1][part]], axis=0)
                high = value.astype(jnp.bfloat16)
                low = (value - high.astype(jnp.float32)).astype(jnp.bfloat16)
                row = pair * SUB
                table_ref[row : row + 2 * SUB, columns] = high
                table_ref[LANES + row : LANES + row + 2 * SUB, columns] = low


def table_row(index):
    y = jnp.floor((index + 0.5) * (1.0 / SHIFTW))
    x = index - SHIFTW * y
    near = SUB * y + x
    side = SUB * (SHIFTW + x - SUB) + y
    corner = SUB * (2 * SHIFTW - SUB) + (SHIFTW - SUB) * (x - SUB) + (y - SUB)
    return jnp.where(x < SUB, near, jnp.where(y < SUB, side, corner))


def exchange(array, axis, distance):
    return lax.ppermute(array, axis, [(i, i ^ distance) for i in range(lax.axis_size(axis))])


def lane_index(shape):
    return lax.broadcasted_iota(jnp.int32, shape, len(shape) - 1)


def rotate_classes(groups, class_ref, rotated_ref, norm_ref):
    classes = class_ref.shape[0]
    total = jnp.zeros((classes, LANES), jnp.float32)
    lane = lane_index((classes, LANES)) % ANG
    for tile in range(COLS // LANES):
        columns = slice(tile * LANES, (tile + 1) * LANES)
        value = tile_of(
            groups, tile, lambda k: class_ref[:, k * LANES : (k + 1) * LANES]
        )
        wide = value.astype(jnp.float32)
        total = total + wide * wide
        other = pltpu.roll(value, ANG, 1)
        for rotation in range(ROTS):
            offset = ANG_STEP * rotation % ANG
            turned = value
            if offset:
                turned = pltpu.roll(jnp.where(lane < ANG - offset, value, other), offset, 1)
            rotated_ref[rotation * classes : (rotation + 1) * classes, columns] = turned
    norm_ref[...] = jnp.broadcast_to(jnp.sum(total, axis=1, keepdims=True), (classes, LANES))


def to_lanes(column, width):
    n = column.shape[0]
    row = lax.broadcasted_iota(jnp.int32, (n, width), 0)
    return jnp.sum(
        jnp.where(lane_index((n, width)) % n == row, column, 0.0), axis=0, keepdims=True
    )


def fold_lanes(row, period, combine):
    result = row[:, :LANES]
    for part in range(1, row.shape[1] // LANES):
        result = combine(result, row[:, part * LANES : (part + 1) * LANES])
    step = LANES // 2
    while step >= period:
        result = combine(result, pltpu.roll(result, step, 1))
        step //= 2
    return result


def to_column(row):
    n = row.shape[1]
    diagonal = lax.broadcasted_iota(jnp.int32, (n, n), 0) == lane_index((n, n))
    return jnp.sum(jnp.where(diagonal, row, 0.0), axis=1, keepdims=True)


def pack_kernel(
    groups, particle_hbm, index_hbm, prior_hbm, group_hbm, class_hbm, scale_hbm, rows_hbm,
    packed_ref, class_ref, scale_ref, rows_ref, particle_ref, index_ref, prior_ref, group_ref, sems,
):
    particles, candidates = index_ref.shape
    copies = [
        pltpu.make_async_copy(source, target, sems.at[i])
        for i, (source, target) in enumerate(
            [
                (index_hbm, index_ref),
                (prior_hbm, prior_ref),
                (group_hbm, group_ref),
                (particle_hbm, particle_ref),
                (class_hbm, class_ref),
                (scale_hbm, scale_ref),
                (rows_hbm, rows_ref),
            ]
        )
    ]
    for copy in copies:
        copy.start()
    for copy in copies[:3]:
        copy.wait()
    lane = lane_index((particles, META))
    index = jnp.concatenate(
        [table_row(index_ref[...].astype(jnp.float32)), jnp.zeros((particles, META - candidates), jnp.float32)],
        axis=1,
    )
    prior = to_column(prior_ref[...].astype(jnp.float32))
    group = to_column(group_ref[...].astype(jnp.float32))
    meta = jnp.where(lane == candidates, prior, jnp.where(lane == candidates + 1, group, index))
    packed_ref[:, COLS:] = meta.astype(jnp.bfloat16)
    copies[3].wait()
    for tile in range(COLS // LANES):
        packed_ref[:, tile * LANES : (tile + 1) * LANES] = tile_of(
            groups, tile, lambda k: particle_ref[:, k * LANES : (k + 1) * LANES]
        )
    for copy in copies[4:]:
        copy.wait()


def score_block(segments, block_ref, table_ref, scale_ref, rotated_ref, norm_ref, shifted_ref, out):
    particles = block_ref.shape[0]
    classes = norm_ref.shape[0]
    candidates = shifted_ref.shape[0] // particles
    rows = particles * candidates
    repeat = rows // LANES
    meta = block_ref[:, COLS : COLS + META].astype(jnp.float32)
    index = meta[:, :candidates].astype(jnp.int32)
    lane = lane_index((particles, LANES))
    hot = jnp.concatenate(
        [
            jnp.where(index[:, t : t + 1] == lane, 1.0, 0.0).astype(jnp.bfloat16)
            for t in range(candidates)
        ],
        axis=0,
    )
    hot = jnp.concatenate([hot, hot], axis=1)
    groups = scale_ref.shape[1]
    group = meta[:, candidates + 1 : candidates + 2].astype(jnp.int32)
    scale_column = jnp.sum(
        jnp.where(group == lane_index((particles, groups)), scale_ref[...], 0.0),
        axis=1,
        keepdims=True,
    )
    scale = to_lanes(scale_column, rows)
    prior = to_lanes(meta[:, candidates : candidates + 1], rows)
    for real_start, imag_start, width in segments:
        real_columns = slice(real_start, real_start + width)
        imag_columns = slice(imag_start, imag_start + width)
        cosine = jnp.dot(hot, table_ref[:, real_columns], preferred_element_type=jnp.float32)
        sine = jnp.dot(hot, table_ref[:, imag_columns], preferred_element_type=jnp.float32)
        real = block_ref[:, real_columns].astype(jnp.float32)
        imag = block_ref[:, imag_columns].astype(jnp.float32)
        for t in range(candidates):
            part = slice(t * particles, (t + 1) * particles)
            c, s = cosine[part], sine[part]
            shifted_ref[part, real_columns] = (real * c - imag * s).astype(jnp.bfloat16)
            shifted_ref[part, imag_columns] = (real * s + imag * c).astype(jnp.bfloat16)
    product = lax.dot_general(
        rotated_ref[...],
        shifted_ref[...],
        (((1,), (1,)), ((), ())),
        preferred_element_type=jnp.float32,
    )
    norm = jnp.concatenate([norm_ref[...]] * repeat, axis=1)
    half_square = 0.5 * scale * scale
    scores = []
    highest = None
    for rotation in range(ROTS):
        distance = jnp.abs(rotation - prior)
        score = (
            scale * product[rotation * classes : (rotation + 1) * classes]
            - half_square * norm
            - ROT_PRIOR * (distance * distance)
        )
        scores.append(score)
        peak = jnp.max(score, axis=0, keepdims=True)
        highest = peak if highest is None else jnp.maximum(highest, peak)
    highest = fold_lanes(highest, particles, jnp.maximum)
    wide = jnp.concatenate([highest] * repeat, axis=1)
    total = None
    for rotation in range(ROTS):
        value = jnp.exp(scores[rotation] - wide)
        out(rotation, value)
        added = jnp.sum(value, axis=0, keepdims=True)
        total = added if total is None else total + added
    total = fold_lanes(total, particles, jnp.add)
    return highest, total, scale[:, :LANES]


def score_blocks(count, segments, chunks, blocks, table_ref, scale_ref, rotated_ref, norm_ref, shifted_ref, exp_ref, stats_ref):
    classes = norm_ref.shape[0]
    rows = exp_ref.shape[1] // count
    for block, block_ref in zip(chunks, blocks):
        part = slice(block * rows, (block + 1) * rows)

        def out(rotation, value):
            exp_ref[rotation * classes : (rotation + 1) * classes, part] = value

        highest, total, scale = score_block(
            segments, block_ref, table_ref, scale_ref, rotated_ref, norm_ref,
            shifted_ref.at[part, :], out,
        )
        stats_ref[2 * block : 2 * block + 1, :] = highest
        stats_ref[2 * block + 1 : 2 * block + 2, :] = total
        stats_ref[2 * count + block : 2 * count + block + 1, :] = scale


def first_kernel(count, groups, segments, chunks, *refs):
    blocks, refs = refs[: len(chunks)], refs[len(chunks) :]
    class_ref, rows_ref, scale_ref = refs[:3]
    shifted_ref, exp_ref, stats_ref, rotated_ref, norm_ref, table_ref = refs[3:]
    build_table(segments, rows_ref, table_ref)
    rotate_classes(groups, class_ref, rotated_ref, norm_ref)
    stats_ref[...] = jnp.zeros_like(stats_ref)
    score_blocks(
        count, segments, chunks, blocks, table_ref, scale_ref, rotated_ref, norm_ref,
        shifted_ref, exp_ref, stats_ref,
    )


def rest_kernel(count, segments, chunks, *refs):
    blocks, refs = refs[: len(chunks)], refs[len(chunks) :]
    table_ref, scale_ref, rotated_ref, norm_ref, before_ref = refs[:5]
    shifted_ref, exp_ref, stats_ref = refs[7:]
    stats_ref[...] = before_ref[...]
    score_blocks(
        count, segments, chunks, blocks, table_ref, scale_ref, rotated_ref, norm_ref,
        shifted_ref, exp_ref, stats_ref,
    )


def merged(mine, other, block, distance):
    twin = block ^ distance
    high, other_high = mine[2 * block : 2 * block + 1, :], other[2 * twin : 2 * twin + 1, :]
    top = jnp.maximum(high, other_high)
    total = mine[2 * block + 1 : 2 * block + 2, :] * jnp.exp(high - top)
    return top, total + other[2 * twin + 1 : 2 * twin + 2, :] * jnp.exp(other_high - top)


def merge_kernel(count, distance, mine, other, out_ref):
    out_ref[...] = jnp.zeros_like(out_ref)
    for block in range(count):
        top, total = merged(mine, other, block, distance)
        out_ref[2 * block : 2 * block + 1, :] = top
        out_ref[2 * block + 1 : 2 * block + 2, :] = total


def weigh(count, stats_ref, mine, other, exp_ref, weight_ref):
    rows = exp_ref.shape[1] // count
    repeat = rows // LANES
    classes = weight_ref.shape[0] // ROTS
    mass = jnp.zeros((classes, rows), jnp.float32)
    for block in range(count):
        top, total = merged(mine, other, block, count // 2)
        factor = jnp.exp(stats_ref[2 * block : 2 * block + 1, :] - top) / total
        scale = stats_ref[2 * count + block : 2 * count + block + 1, :]
        factor = jnp.concatenate([factor] * repeat, axis=1)
        scale = jnp.concatenate([scale] * repeat, axis=1)
        part = slice(block * rows, (block + 1) * rows)
        for rotation in range(ROTS):
            rotated = slice(rotation * classes, (rotation + 1) * classes)
            weight = exp_ref[rotated, part] * factor * scale
            mass = mass + weight * scale
            weight_ref[rotated, part] = weight.astype(jnp.bfloat16)
    return jnp.broadcast_to(jnp.sum(mass, axis=1, keepdims=True), (classes, LANES))


def window_sums(weight_ref, shifted_ref, start, wide):
    classes = weight_ref.shape[0] // ROTS
    product = jnp.dot(
        weight_ref[...], shifted_ref[:, pl.ds(start, wide)], preferred_element_type=jnp.float32
    )
    lane = lane_index((classes, LANES)) % ANG
    tiles = []
    for part in range(0, wide, LANES):
        inside = product[:classes, part : part + LANES]
        wrapped = None
        for rotation in range(1, ROTS):
            offset = ANG_STEP * rotation % ANG
            turned = pltpu.roll(
                product[rotation * classes : (rotation + 1) * classes, part : part + LANES],
                LANES - offset,
                1,
            )
            within = lane < ANG - offset
            inside = inside + jnp.where(within, turned, 0.0)
            over = jnp.where(within, 0.0, turned)
            wrapped = over if wrapped is None else wrapped + over
        tiles.append(inside + pltpu.roll(wrapped, ANG, 1))
    return tiles


def block_sums(doms, width, main, distance, weight_ref, shifted_ref, tails_ref):
    classes = weight_ref.shape[0] // ROTS
    padded = -(-(width + 3) // LANES) * LANES
    place = lax.axis_index("dom") ^ distance
    first = place * (main or width)
    shifts = [0] if main else sorted({width * dom % LANES for dom in range(doms)})
    span = main or -(-(shifts[-1] + width) // LANES) * LANES
    base = first // LANES * LANES
    tiles = []
    for start in range(0, span, 2 * LANES):
        tiles += window_sums(
            weight_ref,
            shifted_ref,
            pl.multiple_of(base + start, LANES),
            min(2 * LANES, span - start),
        )
    if main:
        tail = None
        for dom in range(doms):
            part = dom * ANG // LANES * LANES
            piece = tails_ref[:, part : part + LANES]
            piece = pltpu.roll(piece, ANG, 1) if dom % 2 else piece
            tail = piece if tail is None else jnp.where(place == dom, piece, tail)
        tiles.append(tail)
    total = jnp.concatenate(tiles, axis=1)
    aligned = total
    for shift in shifts:
        if shift:
            aligned = jnp.where(first - base == shift, pltpu.roll(total, span - shift, 1), aligned)
    return pad_columns(aligned, padded)


def store_block(width, value, mass, out_ref):
    high = mass.astype(jnp.bfloat16).astype(jnp.float32)
    middle = (mass - high).astype(jnp.bfloat16).astype(jnp.float32)
    low = (mass - high - middle).astype(jnp.bfloat16).astype(jnp.float32)
    lane = lane_index(value.shape)
    tail = jnp.where(
        lane == width, high, jnp.where(lane == width + 1, middle, jnp.where(lane == width + 2, low, 0.0))
    )
    value = jnp.where(lane < width, value, tail)
    out_ref[...] = value[:, : out_ref.shape[1]].astype(out_ref.dtype)


def pad_columns(value, padded):
    if value.shape[1] < padded:
        added = jnp.zeros((value.shape[0], padded - value.shape[1]), value.dtype)
        return jnp.concatenate([value, added], axis=1)
    return value[:, :padded]


def received_mass(width, ref):
    base = width // LANES * LANES
    tail = ref[:, base:].astype(jnp.float32)
    lane = base + lane_index(tail.shape)
    tail = jnp.where((lane >= width) & (lane < width + 3), tail, 0.0)
    return jnp.sum(tail, axis=1, keepdims=True)


def first_sums_kernel(count, doms, width, main, blocks, *refs):
    stats_ref, mine, other, exp_ref, shifted_ref, weight_ref, mass_ref, tails_ref = refs[:8]
    mass = weigh(count, stats_ref, mine, other, exp_ref, weight_ref)
    mass_ref[...] = mass
    tails_ref[...] = jnp.zeros_like(tails_ref)
    for start in range(0, doms * ANG if main else 0, 2 * LANES):
        tiles = window_sums(weight_ref, shifted_ref, doms * main + start, 2 * LANES)
        tails_ref[:, start : start + 2 * LANES] = jnp.concatenate(tiles, axis=1)
    for block, out_ref in zip(blocks, refs[8:]):
        value = block_sums(doms, width, main, block, weight_ref, shifted_ref, tails_ref)
        store_block(width, value, mass[:, :1], out_ref)


def rest_sums_kernel(doms, width, main, blocks, weight_ref, shifted_ref, mass_ref, tails_ref, *refs):
    for block, out_ref in zip(blocks, refs[-len(blocks) :]):
        value = block_sums(doms, width, main, block, weight_ref, shifted_ref, tails_ref)
        store_block(width, value, mass_ref[:, :1], out_ref)


def final_kernel(width, own_ref, *refs):
    received, sums_ref, weights_ref = refs[:-2], refs[-2], refs[-1]
    total, mass = None, None
    for ref in (own_ref, *received):
        value = ref[:, :width].astype(jnp.float32)
        total = value if total is None else total + value
        tail = received_mass(width, ref)
        mass = tail if mass is None else mass + tail
    sums_ref[...] = total
    weights_ref[...] = to_lanes(mass, total.shape[0])


def call(kernel, shapes, scratch, flops, moved, *args, smem=(), hbm=(), chip=(), pinned=True, aliases=None):
    vmem = pl.BlockSpec(memory_space=pltpu.VMEM)
    scalar = pl.BlockSpec(memory_space=pltpu.SMEM)
    place = pl.BlockSpec(memory_space=pltpu.HBM)
    args = [
        pltpu.with_memory_space_constraint(a, pltpu.HBM) if i in hbm
        else pltpu.with_memory_space_constraint(a, pltpu.VMEM) if i in chip
        else a
        for i, a in enumerate(args)
    ]
    return pl.pallas_call(
        kernel,
        out_shape=[pltpu.VMEM(s.shape, s.dtype) if pinned else s for s in shapes],
        in_specs=[scalar if i in smem else place if i in hbm else vmem for i in range(len(args))],
        out_specs=[vmem] * len(shapes),
        scratch_shapes=scratch,
        input_output_aliases=aliases or {},
        compiler_params=pltpu.CompilerParams(vmem_limit_bytes=VMEM_LIMIT),
        cost_estimate=pl.CostEstimate(flops=flops, bytes_accessed=moved, transcendentals=0),
    )(*args)


def body(particle_spectra, class_spectra, shift_index, prior_rotation, particle_group, group_scale):
    count = lax.axis_size("cls")
    doms = lax.axis_size("dom")
    particles, candidates = shift_index.shape
    classes = class_spectra.shape[0]
    rows = particles * candidates
    width = COLS // doms
    padded = -(-(width + 3) // LANES) * LANES
    growth = (padded - width - 3) // (doms - 1)
    f32, bf16 = jnp.float32, jnp.bfloat16
    shape = jax.ShapeDtypeStruct

    groups, segments, main = column_layout(doms)
    phases = jnp.asarray(phase_rows(groups))
    packed, classes_on_chip, scales, phases_on_chip = call(
        functools.partial(pack_kernel, groups),
        [
            shape((particles, COLS + META), bf16),
            shape(class_spectra.shape, bf16),
            shape((1, group_scale.shape[0]), f32),
            shape(phases.shape, f32),
        ],
        [
            pltpu.VMEM((particles, COLS), bf16),
            pltpu.VMEM((particles, candidates), jnp.int32),
            pltpu.VMEM((1, particles), jnp.int32),
            pltpu.VMEM((1, particles), jnp.int32),
            pltpu.SemaphoreType.DMA((7,)),
        ],
        particles * COLS,
        4 * particles * COLS,
        particle_spectra, shift_index, prior_rotation[None, :], particle_group[None, :],
        class_spectra, group_scale[None, :], phases,
        hbm=(0, 1, 2, 3, 4, 5, 6),
    )
    chunks = [packed] + [exchange(packed, "cls", distance) for distance in range(1, count)]
    stat_rows = -(-3 * count // 8) * 8
    work = 2 * rows * COLS * (ROTS * classes + 256)
    stats_shape = shape((stat_rows, LANES), f32)
    shifted_shape = shape((count * rows, COLS), bf16)
    exp_shape = shape((ROTS * classes, count * rows), f32)
    near, far = [0, 1], list(range(2, count))
    shifted, exps, stats, rotated, norm, table = call(
        functools.partial(first_kernel, count, groups, segments, near),
        [
            shifted_shape,
            exp_shape,
            stats_shape,
            shape((ROTS * classes, COLS), bf16),
            shape((classes, LANES), f32),
            shape((2 * LANES, COLS), bf16),
        ],
        [],
        work * len(near),
        4 * len(near) * rows * COLS,
        *[chunks[b] for b in near], classes_on_chip, phases_on_chip, scales,
    )
    shifted, exps, stats = call(
        functools.partial(rest_kernel, count, segments, far),
        [shifted_shape, exp_shape, stats_shape],
        [],
        work * len(far),
        4 * len(far) * rows * COLS,
        *[chunks[b] for b in far], table, scales, rotated, norm, stats, shifted, exps,
        aliases={len(far) + 5: 0, len(far) + 6: 1},
        chip=(len(far) + 5, len(far) + 6),
    )
    mine, distance = stats, 1
    other = exchange(mine, "cls", distance)
    while 2 * distance < count:
        (mine,) = call(
            functools.partial(merge_kernel, count, distance),
            [shape((-(-2 * count // 8) * 8, LANES), f32)],
            [],
            1024,
            1024,
            mine, other,
        )
        distance *= 2
        other = exchange(mine, "cls", distance)
    early, late = list(range(doms - 1, 0, -1)), [0]
    extents = {b: width + 3 + b * growth for b in range(doms)}
    weights, mass, tails, *made = call(
        functools.partial(first_sums_kernel, count, doms, width, main, early),
        [
            shape((ROTS * classes, count * rows), bf16),
            shape((classes, LANES), f32),
            shape((classes, doms * ANG if main else LANES), f32),
        ]
        + [shape((classes, extents[b]), bf16) for b in early],
        [],
        2 * count * rows * COLS * ROTS * classes // doms,
        4 * count * rows * width,
        stats, mine, other, exps, shifted,
        chip=(3, 4),
    )
    rest = call(
        functools.partial(rest_sums_kernel, doms, width, main, late),
        [shape((classes, extents[b]), bf16 if b else f32) for b in late],
        [],
        1024,
        1024,
        weights, shifted, mass, tails, *made,
        chip=(1,),
    )
    blocks = dict(zip(early + late, [*made, *rest]))
    own = blocks[0]
    received = [exchange(blocks[b], "dom", b) for b in range(doms - 1, 0, -1)]
    class_sums, class_weights = call(
        functools.partial(final_kernel, width),
        [shape((classes, width), f32), shape((1, classes), f32)],
        [],
        doms * classes * padded,
        4 * doms * classes * padded,
        own, *received,
        pinned=False,
    )
    return class_sums, class_weights.reshape(classes)


def solution(mesh):
    placed = (
        P(("groups", "dom", "cls"), None),
        P(("groups", "cls"), None),
        P(("groups", "dom", "cls"), None),
        P(("groups", "dom", "cls")),
        P(("groups", "dom", "cls")),
        P("groups"),
    )
    return jax.shard_map(
        body,
        mesh=mesh,
        in_specs=placed,
        out_specs=(P(("groups", "cls"), "dom"), P(("groups", "cls"))),
        check_vma=False,
    )
```

```python
import functools
import math

import jax
import jax.numpy as jnp
import numpy as np
from jax import lax
from jax.experimental import pallas as pl
from jax.experimental.pallas import tpu as pltpu
from jax.sharding import PartitionSpec as P

CYCLES = 18
ANG = 64
IMG = 64
ANG_STEP = 1
ROTS = 8
SHIFT_R = 5
SHIFTW = 11
HALF = CYCLES * ANG
COLS = 2 * HALF
LANES = 128
SUB = 8
META = LANES
ROT_PRIOR = 0.5
VMEM_LIMIT = 20 * 1024 * 1024


def column_layout(doms):
    width = COLS // doms
    main = width - ANG
    half = doms // 2
    if width % ANG or main <= 0 or main % LANES or half * ANG % LANES:
        step = 3 * LANES
        segments = [(start, HALF + start, step) for start in range(0, HALF, step)]
        return list(range(COLS // ANG)), segments, 0
    per = width // ANG
    groups = [per * dom + group for dom in range(doms) for group in range(per - 1)]
    groups += [per * dom + per - 1 for dom in range(doms)]
    segments = [(dom * main, (half + dom) * main, main) for dom in range(half)]
    segments.append((doms * main, doms * main + half * ANG, half * ANG))
    return groups, segments, main


def tile_of(groups, tile, read):
    low, high = groups[2 * tile], groups[2 * tile + 1]
    if low % 2 == 0 and high == low + 1:
        return read(low // 2)
    first, second = read(low // 2), read(high // 2)
    first = pltpu.roll(first, ANG, 1) if low % 2 else first
    second = second if high % 2 else pltpu.roll(second, ANG, 1)
    return jnp.where(lane_index(first.shape) < ANG, first, second)


def phase_rows(groups):
    angles = np.arange(ANG) * (2.0 * math.pi / ANG)
    radius = np.arange(CYCLES) + 1.0
    fx = (radius[:, None] * np.cos(angles)[None, :]).reshape(-1)
    fy = (radius[:, None] * np.sin(angles)[None, :]).reshape(-1)
    offsets = np.arange(SHIFTW) - SHIFT_R
    unit = 2.0 * math.pi / IMG
    along_x = unit * offsets[:, None] * fx[None, :]
    along_y = unit * offsets[:, None] * fy[None, :]
    both = (along_x[SUB:, None, :] + along_y[None, SUB:, :]).reshape(-1, HALF)
    values = np.zeros((48, COLS), np.float32)
    for start, phase in ((0, along_x), (16, along_y), (32, both)):
        values[start : start + len(phase)] = np.concatenate([np.cos(phase), np.sin(phase)], axis=1)
    columns = np.concatenate([np.arange(ANG) + ANG * group for group in groups])
    return values[:, columns]


def build_table(segments, rows_ref, table_ref):
    for real_start, imag_start, width in segments:
        real = slice(real_start, real_start + width)
        imag = slice(imag_start, imag_start + width)

        def product(block, row):
            c, s = rows_ref[block : block + SUB, real], rows_ref[block : block + SUB, imag]
            d, t = rows_ref[row : row + 1, real], rows_ref[row : row + 1, imag]
            return c * d - s * t, s * d + c * t

        blocks = [product(0, 16 + y) for y in range(SHIFTW)]
        blocks += [product(16, x) for x in range(SUB, SHIFTW)]
        blocks += [
            (rows_ref[row : row + SUB, real], rows_ref[row : row + SUB, imag])
            for row in (32, 32 + SUB)
        ]
        for pair in range(0, len(blocks), 2):
            for part, columns in ((0, real), (1, imag)):
                value = jnp.concatenate([blocks[pair][part], blocks[pair + 1][part]], axis=0)
                high = value.astype(jnp.bfloat16)
                low = (value - high.astype(jnp.float32)).astype(jnp.bfloat16)
                row = pair * SUB
                table_ref[row : row + 2 * SUB, columns] = high
                table_ref[LANES + row : LANES + row + 2 * SUB, columns] = low


def table_row(index):
    y = jnp.floor((index + 0.5) * (1.0 / SHIFTW))
    x = index - SHIFTW * y
    near = SUB * y + x
    side = SUB * (SHIFTW + x - SUB) + y
    corner = SUB * (2 * SHIFTW - SUB) + (SHIFTW - SUB) * (x - SUB) + (y - SUB)
    return jnp.where(x < SUB, near, jnp.where(y < SUB, side, corner))


def exchange(array, axis, distance):
    return lax.ppermute(array, axis, [(i, i ^ distance) for i in range(lax.axis_size(axis))])


def lane_index(shape):
    return lax.broadcasted_iota(jnp.int32, shape, len(shape) - 1)


def rotate_classes(groups, class_ref, rotated_ref, norm_ref):
    classes = class_ref.shape[0]
    total = jnp.zeros((classes, LANES), jnp.float32)
    lane = lane_index((classes, LANES)) % ANG
    for tile in range(COLS // LANES):
        columns = slice(tile * LANES, (tile + 1) * LANES)
        value = tile_of(
            groups, tile, lambda k: class_ref[:, k * LANES : (k + 1) * LANES]
        )
        wide = value.astype(jnp.float32)
        total = total + wide * wide
        other = pltpu.roll(value, ANG, 1)
        for rotation in range(ROTS):
            offset = ANG_STEP * rotation % ANG
            turned = value
            if offset:
                turned = pltpu.roll(jnp.where(lane < ANG - offset, value, other), offset, 1)
            rotated_ref[rotation * classes : (rotation + 1) * classes, columns] = turned
    norm_ref[...] = jnp.broadcast_to(jnp.sum(total, axis=1, keepdims=True), (classes, LANES))


def to_lanes(column, width):
    n = column.shape[0]
    row = lax.broadcasted_iota(jnp.int32, (n, width), 0)
    return jnp.sum(
        jnp.where(lane_index((n, width)) % n == row, column, 0.0), axis=0, keepdims=True
    )


def fold_lanes(row, period, combine):
    result = row[:, :LANES]
    for part in range(1, row.shape[1] // LANES):
        result = combine(result, row[:, part * LANES : (part + 1) * LANES])
    step = LANES // 2
    while step >= period:
        result = combine(result, pltpu.roll(result, step, 1))
        step //= 2
    return result


def to_column(row):
    n = row.shape[1]
    diagonal = lax.broadcasted_iota(jnp.int32, (n, n), 0) == lane_index((n, n))
    return jnp.sum(jnp.where(diagonal, row, 0.0), axis=1, keepdims=True)


def pack_kernel(
    groups, particle_hbm, index_hbm, prior_hbm, group_hbm, class_hbm, scale_hbm, rows_hbm,
    packed_ref, class_ref, scale_ref, rows_ref, particle_ref, index_ref, prior_ref, group_ref, sems,
):
    particles, candidates = index_ref.shape
    copies = [
        pltpu.make_async_copy(source, target, sems.at[i])
        for i, (source, target) in enumerate(
            [
                (index_hbm, index_ref),
                (prior_hbm, prior_ref),
                (group_hbm, group_ref),
                (particle_hbm, particle_ref),
                (class_hbm, class_ref),
                (scale_hbm, scale_ref),
                (rows_hbm, rows_ref),
            ]
        )
    ]
    for copy in copies:
        copy.start()
    for copy in copies[:3]:
        copy.wait()
    lane = lane_index((particles, META))
    index = jnp.concatenate(
        [table_row(index_ref[...].astype(jnp.float32)), jnp.zeros((particles, META - candidates), jnp.float32)],
        axis=1,
    )
    prior = to_column(prior_ref[...].astype(jnp.float32))
    group = to_column(group_ref[...].astype(jnp.float32))
    meta = jnp.where(lane == candidates, prior, jnp.where(lane == candidates + 1, group, index))
    packed_ref[:, COLS:] = meta.astype(jnp.bfloat16)
    copies[3].wait()
    for tile in range(COLS // LANES):
        packed_ref[:, tile * LANES : (tile + 1) * LANES] = tile_of(
            groups, tile, lambda k: particle_ref[:, k * LANES : (k + 1) * LANES]
        )
    for copy in copies[4:]:
        copy.wait()


def score_block(segments, block_ref, table_ref, scale_ref, rotated_ref, norm_ref, shifted_ref, out):
    particles = block_ref.shape[0]
    classes = norm_ref.shape[0]
    candidates = shifted_ref.shape[0] // particles
    rows = particles * candidates
    repeat = rows // LANES
    meta = block_ref[:, COLS : COLS + META].astype(jnp.float32)
    index = meta[:, :candidates].astype(jnp.int32)
    lane = lane_index((particles, LANES))
    hot = jnp.concatenate(
        [
            jnp.where(index[:, t : t + 1] == lane, 1.0, 0.0).astype(jnp.bfloat16)
            for t in range(candidates)
        ],
        axis=0,
    )
    hot = jnp.concatenate([hot, hot], axis=1)
    groups = scale_ref.shape[1]
    group = meta[:, candidates + 1 : candidates + 2].astype(jnp.int32)
    scale_column = jnp.sum(
        jnp.where(group == lane_index((particles, groups)), scale_ref[...], 0.0),
        axis=1,
        keepdims=True,
    )
    scale = to_lanes(scale_column, rows)
    prior = to_lanes(meta[:, candidates : candidates + 1], rows)
    for real_start, imag_start, width in segments:
        real_columns = slice(real_start, real_start + width)
        imag_columns = slice(imag_start, imag_start + width)
        cosine = jnp.dot(hot, table_ref[:, real_columns], preferred_element_type=jnp.float32)
        sine = jnp.dot(hot, table_ref[:, imag_columns], preferred_element_type=jnp.float32)
        real = block_ref[:, real_columns].astype(jnp.float32)
        imag = block_ref[:, imag_columns].astype(jnp.float32)
        for t in range(candidates):
            part = slice(t * particles, (t + 1) * particles)
            c, s = cosine[part], sine[part]
            shifted_ref[part, real_columns] = (real * c - imag * s).astype(jnp.bfloat16)
            shifted_ref[part, imag_columns] = (real * s + imag * c).astype(jnp.bfloat16)
    product = lax.dot_general(
        rotated_ref[...],
        shifted_ref[...],
        (((1,), (1,)), ((), ())),
        preferred_element_type=jnp.float32,
    )
    norm = jnp.concatenate([norm_ref[...]] * repeat, axis=1)
    half_square = 0.5 * scale * scale
    scores = []
    highest = None
    for rotation in range(ROTS):
        distance = jnp.abs(rotation - prior)
        score = (
            scale * product[rotation * classes : (rotation + 1) * classes]
            - half_square * norm
            - ROT_PRIOR * (distance * distance)
        )
        scores.append(score)
        peak = jnp.max(score, axis=0, keepdims=True)
        highest = peak if highest is None else jnp.maximum(highest, peak)
    highest = fold_lanes(highest, particles, jnp.maximum)
    wide = jnp.concatenate([highest] * repeat, axis=1)
    total = None
    for rotation in range(ROTS):
        value = jnp.exp(scores[rotation] - wide)
        out(rotation, value)
        added = jnp.sum(value, axis=0, keepdims=True)
        total = added if total is None else total + added
    total = fold_lanes(total, particles, jnp.add)
    return highest, total, scale[:, :LANES]


def score_blocks(count, segments, chunks, blocks, table_ref, scale_ref, rotated_ref, norm_ref, shifted_ref, exp_ref, stats_ref):
    classes = norm_ref.shape[0]
    rows = exp_ref.shape[1] // count
    for block, block_ref in zip(chunks, blocks):
        part = slice(block * rows, (block + 1) * rows)

        def out(rotation, value):
            exp_ref[rotation * classes : (rotation + 1) * classes, part] = value

        highest, total, scale = score_block(
            segments, block_ref, table_ref, scale_ref, rotated_ref, norm_ref,
            shifted_ref.at[part, :], out,
        )
        stats_ref[2 * block : 2 * block + 1, :] = highest
        stats_ref[2 * block + 1 : 2 * block + 2, :] = total
        stats_ref[2 * count + block : 2 * count + block + 1, :] = scale


def first_kernel(count, groups, segments, chunks, *refs):
    blocks, refs = refs[: len(chunks)], refs[len(chunks) :]
    class_ref, rows_ref, scale_ref = refs[:3]
    shifted_ref, exp_ref, stats_ref, rotated_ref, norm_ref, table_ref = refs[3:]
    build_table(segments, rows_ref, table_ref)
    rotate_classes(groups, class_ref, rotated_ref, norm_ref)
    stats_ref[...] = jnp.zeros_like(stats_ref)
    score_blocks(
        count, segments, chunks, blocks, table_ref, scale_ref, rotated_ref, norm_ref,
        shifted_ref, exp_ref, stats_ref,
    )


def rest_kernel(count, segments, chunks, *refs):
    blocks, refs = refs[: len(chunks)], refs[len(chunks) :]
    table_ref, scale_ref, rotated_ref, norm_ref, before_ref = refs[:5]
    shifted_ref, exp_ref, stats_ref = refs[7:]
    stats_ref[...] = before_ref[...]
    score_blocks(
        count, segments, chunks, blocks, table_ref, scale_ref, rotated_ref, norm_ref,
        shifted_ref, exp_ref, stats_ref,
    )


def merged(mine, other, block, distance):
    twin = block ^ distance
    high, other_high = mine[2 * block : 2 * block + 1, :], other[2 * twin : 2 * twin + 1, :]
    top = jnp.maximum(high, other_high)
    total = mine[2 * block + 1 : 2 * block + 2, :] * jnp.exp(high - top)
    return top, total + other[2 * twin + 1 : 2 * twin + 2, :] * jnp.exp(other_high - top)


def merge_kernel(count, distance, mine, other, out_ref):
    out_ref[...] = jnp.zeros_like(out_ref)
    for block in range(count):
        top, total = merged(mine, other, block, distance)
        out_ref[2 * block : 2 * block + 1, :] = top
        out_ref[2 * block + 1 : 2 * block + 2, :] = total


def weigh(count, stats_ref, mine, other, exp_ref, weight_ref):
    rows = exp_ref.shape[1] // count
    repeat = rows // LANES
    classes = weight_ref.shape[0] // ROTS
    mass = jnp.zeros((classes, rows), jnp.float32)
    for block in range(count):
        top, total = merged(mine, other, block, count // 2)
        factor = jnp.exp(stats_ref[2 * block : 2 * block + 1, :] - top) / total
        scale = stats_ref[2 * count + block : 2 * count + block + 1, :]
        factor = jnp.concatenate([factor] * repeat, axis=1)
        scale = jnp.concatenate([scale] * repeat, axis=1)
        part = slice(block * rows, (block + 1) * rows)
        for rotation in range(ROTS):
            rotated = slice(rotation * classes, (rotation + 1) * classes)
            weight = exp_ref[rotated, part] * factor * scale
            mass = mass + weight * scale
            weight_ref[rotated, part] = weight.astype(jnp.bfloat16)
    return jnp.broadcast_to(jnp.sum(mass, axis=1, keepdims=True), (classes, LANES))


def window_sums(weight_ref, shifted_ref, start, wide):
    classes = weight_ref.shape[0] // ROTS
    product = jnp.dot(
        weight_ref[...], shifted_ref[:, pl.ds(start, wide)], preferred_element_type=jnp.float32
    )
    lane = lane_index((classes, LANES)) % ANG
    tiles = []
    for part in range(0, wide, LANES):
        inside = product[:classes, part : part + LANES]
        wrapped = None
        for rotation in range(1, ROTS):
            offset = ANG_STEP * rotation % ANG
            turned = pltpu.roll(
                product[rotation * classes : (rotation + 1) * classes, part : part + LANES],
                LANES - offset,
                1,
            )
            within = lane < ANG - offset
            inside = inside + jnp.where(within, turned, 0.0)
            over = jnp.where(within, 0.0, turned)
            wrapped = over if wrapped is None else wrapped + over
        tiles.append(inside + pltpu.roll(wrapped, ANG, 1))
    return tiles


def block_sums(doms, width, main, distance, weight_ref, shifted_ref, tails_ref):
    classes = weight_ref.shape[0] // ROTS
    padded = -(-(width + 3) // LANES) * LANES
    place = lax.axis_index("dom") ^ distance
    first = place * (main or width)
    shifts = [0] if main else sorted({width * dom % LANES for dom in range(doms)})
    span = main or -(-(shifts[-1] + width) // LANES) * LANES
    base = first // LANES * LANES
    tiles = []
    for start in range(0, span, 2 * LANES):
        tiles += window_sums(
            weight_ref,
            shifted_ref,
            pl.multiple_of(base + start, LANES),
            min(2 * LANES, span - start),
        )
    if main:
        tail = None
        for dom in range(doms):
            part = dom * ANG // LANES * LANES
            piece = tails_ref[:, part : part + LANES]
            piece = pltpu.roll(piece, ANG, 1) if dom % 2 else piece
            tail = piece if tail is None else jnp.where(place == dom, piece, tail)
        tiles.append(tail)
    total = jnp.concatenate(tiles, axis=1)
    aligned = total
    for shift in shifts:
        if shift:
            aligned = jnp.where(first - base == shift, pltpu.roll(total, span - shift, 1), aligned)
    return pad_columns(aligned, padded)


def store_block(width, value, mass, out_ref):
    high = mass.astype(jnp.bfloat16).astype(jnp.float32)
    middle = (mass - high).astype(jnp.bfloat16).astype(jnp.float32)
    low = (mass - high - middle).astype(jnp.bfloat16).astype(jnp.float32)
    lane = lane_index(value.shape)
    tail = jnp.where(
        lane == width, high, jnp.where(lane == width + 1, middle, jnp.where(lane == width + 2, low, 0.0))
    )
    value = jnp.where(lane < width, value, tail)
    out_ref[...] = value[:, : out_ref.shape[1]].astype(out_ref.dtype)


def pad_columns(value, padded):
    if value.shape[1] < padded:
        added = jnp.zeros((value.shape[0], padded - value.shape[1]), value.dtype)
        return jnp.concatenate([value, added], axis=1)
    return value[:, :padded]


def received_mass(width, ref):
    base = width // LANES * LANES
    tail = ref[:, base:].astype(jnp.float32)
    lane = base + lane_index(tail.shape)
    tail = jnp.where((lane >= width) & (lane < width + 3), tail, 0.0)
    return jnp.sum(tail, axis=1, keepdims=True)


def first_sums_kernel(count, doms, width, main, blocks, *refs):
    stats_ref, mine, other, exp_ref, shifted_ref, weight_ref, mass_ref, tails_ref = refs[:8]
    mass = weigh(count, stats_ref, mine, other, exp_ref, weight_ref)
    mass_ref[...] = mass
    tails_ref[...] = jnp.zeros_like(tails_ref)
    for start in range(0, doms * ANG if main else 0, 2 * LANES):
        tiles = window_sums(weight_ref, shifted_ref, doms * main + start, 2 * LANES)
        tails_ref[:, start : start + 2 * LANES] = jnp.concatenate(tiles, axis=1)
    for block, out_ref in zip(blocks, refs[8:]):
        value = block_sums(doms, width, main, block, weight_ref, shifted_ref, tails_ref)
        store_block(width, value, mass[:, :1], out_ref)


def rest_sums_kernel(doms, width, main, blocks, weight_ref, shifted_ref, mass_ref, tails_ref, *refs):
    for block, out_ref in zip(blocks, refs[-len(blocks) :]):
        value = block_sums(doms, width, main, block, weight_ref, shifted_ref, tails_ref)
        store_block(width, value, mass_ref[:, :1], out_ref)


def add_kernel(width, *refs):
    out_ref = refs[-1]
    padded = -(-out_ref.shape[1] // LANES) * LANES
    total, mass = None, None
    for ref in refs[:-1]:
        value = pad_columns(ref[...].astype(jnp.float32), padded)
        total = value if total is None else total + value
        tail = received_mass(width, ref)
        mass = tail if mass is None else mass + tail
    store_block(width, total, mass, out_ref)


def final_kernel(width, own_ref, *refs):
    received, sums_ref, weights_ref = refs[:-2], refs[-2], refs[-1]
    total, mass = None, None
    for ref in (own_ref, *received):
        value = ref[:, :width].astype(jnp.float32)
        total = value if total is None else total + value
        tail = received_mass(width, ref)
        mass = tail if mass is None else mass + tail
    sums_ref[...] = total
    weights_ref[...] = to_lanes(mass, total.shape[0])


def call(kernel, shapes, scratch, flops, moved, *args, smem=(), hbm=(), chip=(), pinned=True, aliases=None):
    vmem = pl.BlockSpec(memory_space=pltpu.VMEM)
    scalar = pl.BlockSpec(memory_space=pltpu.SMEM)
    place = pl.BlockSpec(memory_space=pltpu.HBM)
    args = [
        pltpu.with_memory_space_constraint(a, pltpu.HBM) if i in hbm
        else pltpu.with_memory_space_constraint(a, pltpu.VMEM) if i in chip
        else a
        for i, a in enumerate(args)
    ]
    return pl.pallas_call(
        kernel,
        out_shape=[pltpu.VMEM(s.shape, s.dtype) if pinned else s for s in shapes],
        in_specs=[scalar if i in smem else place if i in hbm else vmem for i in range(len(args))],
        out_specs=[vmem] * len(shapes),
        scratch_shapes=scratch,
        input_output_aliases=aliases or {},
        compiler_params=pltpu.CompilerParams(vmem_limit_bytes=VMEM_LIMIT),
        cost_estimate=pl.CostEstimate(flops=flops, bytes_accessed=moved, transcendentals=0),
    )(*args)


def body(particle_spectra, class_spectra, shift_index, prior_rotation, particle_group, group_scale):
    count = lax.axis_size("cls")
    doms = lax.axis_size("dom")
    particles, candidates = shift_index.shape
    classes = class_spectra.shape[0]
    rows = particles * candidates
    width = COLS // doms
    padded = -(-(width + 3) // LANES) * LANES
    growth = (padded - width - 3) // (doms - 1)
    f32, bf16 = jnp.float32, jnp.bfloat16
    shape = jax.ShapeDtypeStruct

    groups, segments, main = column_layout(doms)
    phases = jnp.asarray(phase_rows(groups))
    packed, classes_on_chip, scales, phases_on_chip = call(
        functools.partial(pack_kernel, groups),
        [
            shape((particles, COLS + META), bf16),
            shape(class_spectra.shape, bf16),
            shape((1, group_scale.shape[0]), f32),
            shape(phases.shape, f32),
        ],
        [
            pltpu.VMEM((particles, COLS), bf16),
            pltpu.VMEM((particles, candidates), jnp.int32),
            pltpu.VMEM((1, particles), jnp.int32),
            pltpu.VMEM((1, particles), jnp.int32),
            pltpu.SemaphoreType.DMA((7,)),
        ],
        particles * COLS,
        4 * particles * COLS,
        particle_spectra, shift_index, prior_rotation[None, :], particle_group[None, :],
        class_spectra, group_scale[None, :], phases,
        hbm=(0, 1, 2, 3, 4, 5, 6),
    )
    chunks = [packed] + [exchange(packed, "cls", distance) for distance in range(1, count)]
    stat_rows = -(-3 * count // 8) * 8
    work = 2 * rows * COLS * (ROTS * classes + 256)
    stats_shape = shape((stat_rows, LANES), f32)
    shifted_shape = shape((count * rows, COLS), bf16)
    exp_shape = shape((ROTS * classes, count * rows), f32)
    near, far = [0, 1], list(range(2, count))
    shifted, exps, stats, rotated, norm, table = call(
        functools.partial(first_kernel, count, groups, segments, near),
        [
            shifted_shape,
            exp_shape,
            stats_shape,
            shape((ROTS * classes, COLS), bf16),
            shape((classes, LANES), f32),
            shape((2 * LANES, COLS), bf16),
        ],
        [],
        work * len(near),
        4 * len(near) * rows * COLS,
        *[chunks[b] for b in near], classes_on_chip, phases_on_chip, scales,
    )
    shifted, exps, stats = call(
        functools.partial(rest_kernel, count, segments, far),
        [shifted_shape, exp_shape, stats_shape],
        [],
        work * len(far),
        4 * len(far) * rows * COLS,
        *[chunks[b] for b in far], table, scales, rotated, norm, stats, shifted, exps,
        aliases={len(far) + 5: 0, len(far) + 6: 1},
        chip=(len(far) + 5, len(far) + 6),
    )
    mine, distance = stats, 1
    other = exchange(mine, "cls", distance)
    while 2 * distance < count:
        (mine,) = call(
            functools.partial(merge_kernel, count, distance),
            [shape((-(-2 * count // 8) * 8, LANES), f32)],
            [],
            1024,
            1024,
            mine, other,
        )
        distance *= 2
        other = exchange(mine, "cls", distance)
    low_bit = lambda b: b & -b
    early = list(range(doms - 1, 1, -2))
    order = early + [1] + sorted(range(2, doms, 2), key=lambda b: (low_bit(b), -b))
    extents = {b: width + 3 + (doms - 1 - place) * growth for place, b in enumerate(order)}
    late = [1] + list(range(0, doms, 2))
    weights, mass, tails, *made = call(
        functools.partial(first_sums_kernel, count, doms, width, main, early),
        [
            shape((ROTS * classes, count * rows), bf16),
            shape((classes, LANES), f32),
            shape((classes, doms * ANG if main else LANES), f32),
        ]
        + [shape((classes, extents[b]), bf16) for b in early],
        [],
        2 * count * rows * COLS * ROTS * classes // doms,
        4 * count * rows * width,
        stats, mine, other, exps, shifted,
        chip=(3, 4),
    )
    incoming = {b: [] for b in range(doms)}
    for b, block in zip(early, made):
        incoming[b ^ 1].append(exchange(block, "dom", 1))
    rest = call(
        functools.partial(rest_sums_kernel, doms, width, main, late),
        [
            shape((classes, extents.get(b, width + 3)), bf16 if b == 1 else f32) for b in late
        ],
        [],
        1024,
        1024,
        weights, shifted, mass, tails, *made,
        chip=(1,),
    )
    blocks = dict(zip(late, rest))
    incoming[0].append(exchange(blocks[1], "dom", 1))
    for b in order[len(early) + 1 :]:
        (block,) = call(
            functools.partial(add_kernel, width),
            [shape((classes, extents[b]), bf16)],
            [],
            1024,
            1024,
            blocks[b], *incoming[b],
        )
        incoming[b ^ low_bit(b)].append(exchange(block, "dom", low_bit(b)))
    own, received = blocks[0], incoming[0]
    class_sums, class_weights = call(
        functools.partial(final_kernel, width),
        [shape((classes, width), f32), shape((1, classes), f32)],
        [],
        doms * classes * padded,
        4 * doms * classes * padded,
        own, *received,
        pinned=False,
    )
    return class_sums, class_weights.reshape(classes)


def solution(mesh):
    placed = (
        P(("groups", "dom", "cls"), None),
        P(("groups", "cls"), None),
        P(("groups", "dom", "cls"), None),
        P(("groups", "dom", "cls")),
        P(("groups", "dom", "cls")),
        P("groups"),
    )
    return jax.shard_map(
        body,
        mesh=mesh,
        in_specs=placed,
        out_specs=(P(("groups", "cls"), "dom"), P(("groups", "cls"))),
        check_vma=False,
    )
```

```python
import functools
import math

import jax
import jax.numpy as jnp
import numpy as np
from jax import lax
from jax.experimental import pallas as pl
from jax.experimental.pallas import tpu as pltpu
from jax.sharding import PartitionSpec as P

CYCLES = 18
ANG = 64
IMG = 64
ANG_STEP = 1
ROTS = 8
SHIFT_R = 5
SHIFTW = 11
HALF = CYCLES * ANG
COLS = 2 * HALF
LANES = 128
SUB = 8
META = LANES
ROT_PRIOR = 0.5
VMEM_LIMIT = 20 * 1024 * 1024


def column_layout(doms):
    width = COLS // doms
    main = width - ANG
    half = doms // 2
    if width % ANG or main <= 0 or main % LANES or half * ANG % LANES:
        step = 3 * LANES
        segments = [(start, HALF + start, step) for start in range(0, HALF, step)]
        return list(range(COLS // ANG)), segments, 0
    per = width // ANG
    groups = [per * dom + group for dom in range(doms) for group in range(per - 1)]
    groups += [per * dom + per - 1 for dom in range(doms)]
    segments = [(dom * main, (half + dom) * main, main) for dom in range(half)]
    segments.append((doms * main, doms * main + half * ANG, half * ANG))
    return groups, segments, main


def tile_of(groups, tile, read):
    low, high = groups[2 * tile], groups[2 * tile + 1]
    if low % 2 == 0 and high == low + 1:
        return read(low // 2)
    first, second = read(low // 2), read(high // 2)
    first = pltpu.roll(first, ANG, 1) if low % 2 else first
    second = second if high % 2 else pltpu.roll(second, ANG, 1)
    return jnp.where(lane_index(first.shape) < ANG, first, second)


def phase_rows(groups):
    angles = np.arange(ANG) * (2.0 * math.pi / ANG)
    radius = np.arange(CYCLES) + 1.0
    fx = (radius[:, None] * np.cos(angles)[None, :]).reshape(-1)
    fy = (radius[:, None] * np.sin(angles)[None, :]).reshape(-1)
    offsets = np.arange(SHIFTW) - SHIFT_R
    unit = 2.0 * math.pi / IMG
    along_x = unit * offsets[:, None] * fx[None, :]
    along_y = unit * offsets[:, None] * fy[None, :]
    both = (along_x[SUB:, None, :] + along_y[None, SUB:, :]).reshape(-1, HALF)
    values = np.zeros((48, COLS), np.float32)
    for start, phase in ((0, along_x), (16, along_y), (32, both)):
        values[start : start + len(phase)] = np.concatenate([np.cos(phase), np.sin(phase)], axis=1)
    columns = np.concatenate([np.arange(ANG) + ANG * group for group in groups])
    return values[:, columns]


def build_table(segments, rows_ref, table_ref):
    for real_start, imag_start, width in segments:
        real = slice(real_start, real_start + width)
        imag = slice(imag_start, imag_start + width)

        def product(block, row):
            c, s = rows_ref[block : block + SUB, real], rows_ref[block : block + SUB, imag]
            d, t = rows_ref[row : row + 1, real], rows_ref[row : row + 1, imag]
            return c * d - s * t, s * d + c * t

        blocks = [product(0, 16 + y) for y in range(SHIFTW)]
        blocks += [product(16, x) for x in range(SUB, SHIFTW)]
        blocks += [
            (rows_ref[row : row + SUB, real], rows_ref[row : row + SUB, imag])
            for row in (32, 32 + SUB)
        ]
        for pair in range(0, len(blocks), 2):
            for part, columns in ((0, real), (1, imag)):
                value = jnp.concatenate([blocks[pair][part], blocks[pair + 1][part]], axis=0)
                high = value.astype(jnp.bfloat16)
                low = (value - high.astype(jnp.float32)).astype(jnp.bfloat16)
                row = pair * SUB
                table_ref[row : row + 2 * SUB, columns] = high
                table_ref[LANES + row : LANES + row + 2 * SUB, columns] = low


def table_row(index):
    y = jnp.floor((index + 0.5) * (1.0 / SHIFTW))
    x = index - SHIFTW * y
    near = SUB * y + x
    side = SUB * (SHIFTW + x - SUB) + y
    corner = SUB * (2 * SHIFTW - SUB) + (SHIFTW - SUB) * (x - SUB) + (y - SUB)
    return jnp.where(x < SUB, near, jnp.where(y < SUB, side, corner))


def exchange(array, axis, distance):
    return lax.ppermute(array, axis, [(i, i ^ distance) for i in range(lax.axis_size(axis))])


def lane_index(shape):
    return lax.broadcasted_iota(jnp.int32, shape, len(shape) - 1)


def rotate_classes(groups, class_ref, rotated_ref, norm_ref):
    classes = class_ref.shape[0]
    total = jnp.zeros((classes, LANES), jnp.float32)
    lane = lane_index((classes, LANES)) % ANG
    for tile in range(COLS // LANES):
        columns = slice(tile * LANES, (tile + 1) * LANES)
        value = tile_of(
            groups, tile, lambda k: class_ref[:, k * LANES : (k + 1) * LANES]
        )
        wide = value.astype(jnp.float32)
        total = total + wide * wide
        other = pltpu.roll(value, ANG, 1)
        for rotation in range(ROTS):
            offset = ANG_STEP * rotation % ANG
            turned = value
            if offset:
                turned = pltpu.roll(jnp.where(lane < ANG - offset, value, other), offset, 1)
            rotated_ref[rotation * classes : (rotation + 1) * classes, columns] = turned
    norm_ref[...] = jnp.broadcast_to(jnp.sum(total, axis=1, keepdims=True), (classes, LANES))


def to_lanes(column, width):
    n = column.shape[0]
    row = lax.broadcasted_iota(jnp.int32, (n, width), 0)
    return jnp.sum(
        jnp.where(lane_index((n, width)) % n == row, column, 0.0), axis=0, keepdims=True
    )


def fold_lanes(row, period, combine):
    result = row[:, :LANES]
    for part in range(1, row.shape[1] // LANES):
        result = combine(result, row[:, part * LANES : (part + 1) * LANES])
    step = LANES // 2
    while step >= period:
        result = combine(result, pltpu.roll(result, step, 1))
        step //= 2
    return result


def to_column(row):
    n = row.shape[1]
    diagonal = lax.broadcasted_iota(jnp.int32, (n, n), 0) == lane_index((n, n))
    return jnp.sum(jnp.where(diagonal, row, 0.0), axis=1, keepdims=True)


def pack_kernel(
    groups, particle_hbm, index_hbm, prior_hbm, group_hbm, class_hbm, scale_hbm, rows_hbm,
    packed_ref, class_ref, scale_ref, rows_ref, particle_ref, index_ref, prior_ref, group_ref, sems,
):
    particles, candidates = index_ref.shape
    copies = [
        pltpu.make_async_copy(source, target, sems.at[i])
        for i, (source, target) in enumerate(
            [
                (index_hbm, index_ref),
                (prior_hbm, prior_ref),
                (group_hbm, group_ref),
                (particle_hbm, particle_ref),
                (class_hbm, class_ref),
                (scale_hbm, scale_ref),
                (rows_hbm, rows_ref),
            ]
        )
    ]
    for copy in copies:
        copy.start()
    for copy in copies[:3]:
        copy.wait()
    lane = lane_index((particles, META))
    index = jnp.concatenate(
        [table_row(index_ref[...].astype(jnp.float32)), jnp.zeros((particles, META - candidates), jnp.float32)],
        axis=1,
    )
    prior = to_column(prior_ref[...].astype(jnp.float32))
    group = to_column(group_ref[...].astype(jnp.float32))
    meta = jnp.where(lane == candidates, prior, jnp.where(lane == candidates + 1, group, index))
    packed_ref[:, COLS:] = meta.astype(jnp.bfloat16)
    copies[3].wait()
    for tile in range(COLS // LANES):
        packed_ref[:, tile * LANES : (tile + 1) * LANES] = tile_of(
            groups, tile, lambda k: particle_ref[:, k * LANES : (k + 1) * LANES]
        )
    for copy in copies[4:]:
        copy.wait()


def score_block(segments, block_ref, table_ref, scale_ref, rotated_ref, norm_ref, shifted_ref, out):
    particles = block_ref.shape[0]
    classes = norm_ref.shape[0]
    candidates = shifted_ref.shape[0] // particles
    rows = particles * candidates
    repeat = rows // LANES
    meta = block_ref[:, COLS : COLS + META].astype(jnp.float32)
    index = meta[:, :candidates].astype(jnp.int32)
    lane = lane_index((particles, LANES))
    hot = jnp.concatenate(
        [
            jnp.where(index[:, t : t + 1] == lane, 1.0, 0.0).astype(jnp.bfloat16)
            for t in range(candidates)
        ],
        axis=0,
    )
    hot = jnp.concatenate([hot, hot], axis=1)
    groups = scale_ref.shape[1]
    group = meta[:, candidates + 1 : candidates + 2].astype(jnp.int32)
    scale_column = jnp.sum(
        jnp.where(group == lane_index((particles, groups)), scale_ref[...], 0.0),
        axis=1,
        keepdims=True,
    )
    scale = to_lanes(scale_column, rows)
    prior = to_lanes(meta[:, candidates : candidates + 1], rows)
    for real_start, imag_start, width in segments:
        real_columns = slice(real_start, real_start + width)
        imag_columns = slice(imag_start, imag_start + width)
        cosine = jnp.dot(hot, table_ref[:, real_columns], preferred_element_type=jnp.float32)
        sine = jnp.dot(hot, table_ref[:, imag_columns], preferred_element_type=jnp.float32)
        real = block_ref[:, real_columns].astype(jnp.float32)
        imag = block_ref[:, imag_columns].astype(jnp.float32)
        for t in range(candidates):
            part = slice(t * particles, (t + 1) * particles)
            c, s = cosine[part], sine[part]
            shifted_ref[part, real_columns] = (real * c - imag * s).astype(jnp.bfloat16)
            shifted_ref[part, imag_columns] = (real * s + imag * c).astype(jnp.bfloat16)
    product = lax.dot_general(
        rotated_ref[...],
        shifted_ref[...],
        (((1,), (1,)), ((), ())),
        preferred_element_type=jnp.float32,
    )
    norm = jnp.concatenate([norm_ref[...]] * repeat, axis=1)
    half_square = 0.5 * scale * scale
    scores = []
    highest = None
    for rotation in range(ROTS):
        distance = jnp.abs(rotation - prior)
        score = (
            scale * product[rotation * classes : (rotation + 1) * classes]
            - half_square * norm
            - ROT_PRIOR * (distance * distance)
        )
        scores.append(score)
        peak = jnp.max(score, axis=0, keepdims=True)
        highest = peak if highest is None else jnp.maximum(highest, peak)
    highest = fold_lanes(highest, particles, jnp.maximum)
    wide = jnp.concatenate([highest] * repeat, axis=1)
    total = None
    for rotation in range(ROTS):
        value = jnp.exp(scores[rotation] - wide)
        out(rotation, value)
        added = jnp.sum(value, axis=0, keepdims=True)
        total = added if total is None else total + added
    total = fold_lanes(total, particles, jnp.add)
    return highest, total, scale[:, :LANES]


def score_blocks(count, segments, chunks, blocks, table_ref, scale_ref, rotated_ref, norm_ref, shifted_ref, exp_ref, stats_ref):
    classes = norm_ref.shape[0]
    rows = exp_ref.shape[1] // count
    for block, block_ref in zip(chunks, blocks):
        part = slice(block * rows, (block + 1) * rows)

        def out(rotation, value):
            exp_ref[rotation * classes : (rotation + 1) * classes, part] = value

        highest, total, scale = score_block(
            segments, block_ref, table_ref, scale_ref, rotated_ref, norm_ref,
            shifted_ref.at[part, :], out,
        )
        stats_ref[2 * block : 2 * block + 1, :] = highest
        stats_ref[2 * block + 1 : 2 * block + 2, :] = total
        stats_ref[2 * count + block : 2 * count + block + 1, :] = scale


def first_kernel(count, groups, segments, chunks, *refs):
    blocks, refs = refs[: len(chunks)], refs[len(chunks) :]
    class_ref, rows_ref, scale_ref = refs[:3]
    shifted_ref, exp_ref, stats_ref, rotated_ref, norm_ref, table_ref = refs[3:]
    build_table(segments, rows_ref, table_ref)
    rotate_classes(groups, class_ref, rotated_ref, norm_ref)
    stats_ref[...] = jnp.zeros_like(stats_ref)
    score_blocks(
        count, segments, chunks, blocks, table_ref, scale_ref, rotated_ref, norm_ref,
        shifted_ref, exp_ref, stats_ref,
    )


def rest_kernel(count, segments, chunks, *refs):
    blocks, refs = refs[: len(chunks)], refs[len(chunks) :]
    table_ref, scale_ref, rotated_ref, norm_ref, before_ref = refs[:5]
    shifted_ref, exp_ref, stats_ref = refs[7:]
    stats_ref[...] = before_ref[...]
    score_blocks(
        count, segments, chunks, blocks, table_ref, scale_ref, rotated_ref, norm_ref,
        shifted_ref, exp_ref, stats_ref,
    )


def merged(mine, other, block, distance):
    twin = block ^ distance
    high, other_high = mine[2 * block : 2 * block + 1, :], other[2 * twin : 2 * twin + 1, :]
    top = jnp.maximum(high, other_high)
    total = mine[2 * block + 1 : 2 * block + 2, :] * jnp.exp(high - top)
    return top, total + other[2 * twin + 1 : 2 * twin + 2, :] * jnp.exp(other_high - top)


def merge_kernel(count, distance, mine, other, out_ref):
    out_ref[...] = jnp.zeros_like(out_ref)
    for block in range(count):
        top, total = merged(mine, other, block, distance)
        out_ref[2 * block : 2 * block + 1, :] = top
        out_ref[2 * block + 1 : 2 * block + 2, :] = total


def weigh(count, stats_ref, mine, other, exp_ref, weight_ref):
    rows = exp_ref.shape[1] // count
    repeat = rows // LANES
    classes = weight_ref.shape[0] // ROTS
    mass = jnp.zeros((classes, rows), jnp.float32)
    for block in range(count):
        top, total = merged(mine, other, block, count // 2)
        factor = jnp.exp(stats_ref[2 * block : 2 * block + 1, :] - top) / total
        scale = stats_ref[2 * count + block : 2 * count + block + 1, :]
        factor = jnp.concatenate([factor] * repeat, axis=1)
        scale = jnp.concatenate([scale] * repeat, axis=1)
        part = slice(block * rows, (block + 1) * rows)
        for rotation in range(ROTS):
            rotated = slice(rotation * classes, (rotation + 1) * classes)
            weight = exp_ref[rotated, part] * factor * scale
            mass = mass + weight * scale
            weight_ref[rotated, part] = weight.astype(jnp.bfloat16)
    return jnp.broadcast_to(jnp.sum(mass, axis=1, keepdims=True), (classes, LANES))


def window_sums(weight_ref, shifted_ref, start, wide):
    classes = weight_ref.shape[0] // ROTS
    product = jnp.dot(
        weight_ref[...], shifted_ref[:, pl.ds(start, wide)], preferred_element_type=jnp.float32
    )
    lane = lane_index((classes, LANES)) % ANG
    tiles = []
    for part in range(0, wide, LANES):
        inside = product[:classes, part : part + LANES]
        wrapped = None
        for rotation in range(1, ROTS):
            offset = ANG_STEP * rotation % ANG
            turned = pltpu.roll(
                product[rotation * classes : (rotation + 1) * classes, part : part + LANES],
                LANES - offset,
                1,
            )
            within = lane < ANG - offset
            inside = inside + jnp.where(within, turned, 0.0)
            over = jnp.where(within, 0.0, turned)
            wrapped = over if wrapped is None else wrapped + over
        tiles.append(inside + pltpu.roll(wrapped, ANG, 1))
    return tiles


def block_sums(doms, width, main, distance, weight_ref, shifted_ref, tails_ref):
    classes = weight_ref.shape[0] // ROTS
    padded = -(-(width + 3) // LANES) * LANES
    place = lax.axis_index("dom") ^ distance
    first = place * (main or width)
    shifts = [0] if main else sorted({width * dom % LANES for dom in range(doms)})
    span = main or -(-(shifts[-1] + width) // LANES) * LANES
    base = first // LANES * LANES
    tiles = []
    for start in range(0, span, 2 * LANES):
        tiles += window_sums(
            weight_ref,
            shifted_ref,
            pl.multiple_of(base + start, LANES),
            min(2 * LANES, span - start),
        )
    if main:
        tail = None
        for dom in range(doms):
            part = dom * ANG // LANES * LANES
            piece = tails_ref[:, part : part + LANES]
            piece = pltpu.roll(piece, ANG, 1) if dom % 2 else piece
            tail = piece if tail is None else jnp.where(place == dom, piece, tail)
        tiles.append(tail)
    total = jnp.concatenate(tiles, axis=1)
    aligned = total
    for shift in shifts:
        if shift:
            aligned = jnp.where(first - base == shift, pltpu.roll(total, span - shift, 1), aligned)
    return pad_columns(aligned, padded)


def store_block(width, value, mass, out_ref):
    high = mass.astype(jnp.bfloat16).astype(jnp.float32)
    middle = (mass - high).astype(jnp.bfloat16).astype(jnp.float32)
    low = (mass - high - middle).astype(jnp.bfloat16).astype(jnp.float32)
    lane = lane_index(value.shape)
    tail = jnp.where(
        lane == width, high, jnp.where(lane == width + 1, middle, jnp.where(lane == width + 2, low, 0.0))
    )
    value = jnp.where(lane < width, value, tail)
    out_ref[...] = value[:, : out_ref.shape[1]].astype(out_ref.dtype)


def pad_columns(value, padded):
    if value.shape[1] < padded:
        added = jnp.zeros((value.shape[0], padded - value.shape[1]), value.dtype)
        return jnp.concatenate([value, added], axis=1)
    return value[:, :padded]


def received_mass(width, ref):
    base = width // LANES * LANES
    tail = ref[:, base:].astype(jnp.float32)
    lane = base + lane_index(tail.shape)
    tail = jnp.where((lane >= width) & (lane < width + 3), tail, 0.0)
    return jnp.sum(tail, axis=1, keepdims=True)


def first_sums_kernel(count, doms, width, main, blocks, *refs):
    stats_ref, mine, other, exp_ref, shifted_ref, weight_ref, mass_ref, tails_ref = refs[:8]
    mass = weigh(count, stats_ref, mine, other, exp_ref, weight_ref)
    mass_ref[...] = mass
    tails_ref[...] = jnp.zeros_like(tails_ref)
    for start in range(0, doms * ANG if main else 0, 2 * LANES):
        tiles = window_sums(weight_ref, shifted_ref, doms * main + start, 2 * LANES)
        tails_ref[:, start : start + 2 * LANES] = jnp.concatenate(tiles, axis=1)
    for block, out_ref in zip(blocks, refs[8:]):
        value = block_sums(doms, width, main, block, weight_ref, shifted_ref, tails_ref)
        store_block(width, value, mass[:, :1], out_ref)


def rest_sums_kernel(doms, width, main, blocks, weight_ref, shifted_ref, mass_ref, tails_ref, *refs):
    for block, out_ref in zip(blocks, refs[-len(blocks) :]):
        value = block_sums(doms, width, main, block, weight_ref, shifted_ref, tails_ref)
        store_block(width, value, mass_ref[:, :1], out_ref)


def add_kernel(width, *refs):
    out_ref = refs[-1]
    padded = -(-out_ref.shape[1] // LANES) * LANES
    total, mass = None, None
    for ref in refs[:-1]:
        value = pad_columns(ref[...].astype(jnp.float32), padded)
        total = value if total is None else total + value
        tail = received_mass(width, ref)
        mass = tail if mass is None else mass + tail
    store_block(width, total, mass, out_ref)


def final_kernel(width, own_ref, *refs):
    received, sums_ref, weights_ref = refs[:-2], refs[-2], refs[-1]
    total, mass = None, None
    for ref in (own_ref, *received):
        value = ref[:, :width].astype(jnp.float32)
        total = value if total is None else total + value
        tail = received_mass(width, ref)
        mass = tail if mass is None else mass + tail
    sums_ref[...] = total
    weights_ref[...] = to_lanes(mass, total.shape[0])


def call(kernel, shapes, scratch, flops, moved, *args, smem=(), hbm=(), chip=(), pinned=True, aliases=None):
    vmem = pl.BlockSpec(memory_space=pltpu.VMEM)
    scalar = pl.BlockSpec(memory_space=pltpu.SMEM)
    place = pl.BlockSpec(memory_space=pltpu.HBM)
    args = [
        pltpu.with_memory_space_constraint(a, pltpu.HBM) if i in hbm
        else pltpu.with_memory_space_constraint(a, pltpu.VMEM) if i in chip
        else a
        for i, a in enumerate(args)
    ]
    return pl.pallas_call(
        kernel,
        out_shape=[pltpu.VMEM(s.shape, s.dtype) if pinned else s for s in shapes],
        in_specs=[scalar if i in smem else place if i in hbm else vmem for i in range(len(args))],
        out_specs=[vmem] * len(shapes),
        scratch_shapes=scratch,
        input_output_aliases=aliases or {},
        compiler_params=pltpu.CompilerParams(vmem_limit_bytes=VMEM_LIMIT),
        cost_estimate=pl.CostEstimate(flops=flops, bytes_accessed=moved, transcendentals=0),
    )(*args)


def body(particle_spectra, class_spectra, shift_index, prior_rotation, particle_group, group_scale):
    count = lax.axis_size("cls")
    doms = lax.axis_size("dom")
    particles, candidates = shift_index.shape
    classes = class_spectra.shape[0]
    rows = particles * candidates
    width = COLS // doms
    padded = -(-(width + 3) // LANES) * LANES
    growth = (padded - width - 3) // (doms - 1)
    f32, bf16 = jnp.float32, jnp.bfloat16
    shape = jax.ShapeDtypeStruct

    groups, segments, main = column_layout(doms)
    phases = jnp.asarray(phase_rows(groups))
    packed, classes_on_chip, scales, phases_on_chip = call(
        functools.partial(pack_kernel, groups),
        [
            shape((particles, COLS + META), bf16),
            shape(class_spectra.shape, bf16),
            shape((1, group_scale.shape[0]), f32),
            shape(phases.shape, f32),
        ],
        [
            pltpu.VMEM((particles, COLS), bf16),
            pltpu.VMEM((particles, candidates), jnp.int32),
            pltpu.VMEM((1, particles), jnp.int32),
            pltpu.VMEM((1, particles), jnp.int32),
            pltpu.SemaphoreType.DMA((7,)),
        ],
        particles * COLS,
        4 * particles * COLS,
        particle_spectra, shift_index, prior_rotation[None, :], particle_group[None, :],
        class_spectra, group_scale[None, :], phases,
        hbm=(0, 1, 2, 3, 4, 5, 6),
    )
    chunks = {0: packed, 1: exchange(packed, "cls", 1)}
    for b in range(2, count, 2):
        chunks[b] = exchange(packed, "cls", b)
    stat_rows = -(-3 * count // 8) * 8
    work = 2 * rows * COLS * (ROTS * classes + 256)
    stats_shape = shape((stat_rows, LANES), f32)
    shifted_shape = shape((count * rows, COLS), bf16)
    exp_shape = shape((ROTS * classes, count * rows), f32)
    near = [0, 1]
    shifted, exps, stats, rotated, norm, table = call(
        functools.partial(first_kernel, count, groups, segments, near),
        [
            shifted_shape,
            exp_shape,
            stats_shape,
            shape((ROTS * classes, COLS), bf16),
            shape((classes, LANES), f32),
            shape((2 * LANES, COLS), bf16),
        ],
        [],
        work * len(near),
        4 * len(near) * rows * COLS,
        *[chunks[b] for b in near], classes_on_chip, phases_on_chip, scales,
    )
    for b in range(2, count, 2):
        arrived, stats = lax.optimization_barrier((chunks[b], stats))
        chunks[b + 1] = exchange(arrived, "cls", 1)
    for far in (list(range(2, count, 2)), list(range(3, count, 2))):
        shifted, exps, stats = call(
            functools.partial(rest_kernel, count, segments, far),
            [shifted_shape, exp_shape, stats_shape],
            [],
            work * len(far),
            4 * len(far) * rows * COLS,
            *[chunks[b] for b in far], table, scales, rotated, norm, stats, shifted, exps,
            aliases={len(far) + 5: 0, len(far) + 6: 1},
            chip=(len(far) + 5, len(far) + 6),
        )
    mine, distance = stats, 1
    other = exchange(mine, "cls", distance)
    while 2 * distance < count:
        (mine,) = call(
            functools.partial(merge_kernel, count, distance),
            [shape((-(-2 * count // 8) * 8, LANES), f32)],
            [],
            1024,
            1024,
            mine, other,
        )
        distance *= 2
        other = exchange(mine, "cls", distance)
    low_bit = lambda b: b & -b
    early = list(range(doms - 1, 1, -2))
    order = early + [1] + sorted(range(2, doms, 2), key=lambda b: (low_bit(b), -b))
    extents = {b: width + 3 + (doms - 1 - place) * growth for place, b in enumerate(order)}
    late = [1] + list(range(0, doms, 2))
    weights, mass, tails, *made = call(
        functools.partial(first_sums_kernel, count, doms, width, main, early),
        [
            shape((ROTS * classes, count * rows), bf16),
            shape((classes, LANES), f32),
            shape((classes, doms * ANG if main else LANES), f32),
        ]
        + [shape((classes, extents[b]), bf16) for b in early],
        [],
        2 * count * rows * COLS * ROTS * classes // doms,
        4 * count * rows * width,
        stats, mine, other, exps, shifted,
        chip=(3, 4),
    )
    incoming = {b: [] for b in range(doms)}
    for b, block in zip(early, made):
        incoming[b ^ 1].append(exchange(block, "dom", 1))
    rest = call(
        functools.partial(rest_sums_kernel, doms, width, main, late),
        [
            shape((classes, extents.get(b, width + 3)), bf16 if b == 1 else f32) for b in late
        ],
        [],
        1024,
        1024,
        weights, shifted, mass, tails, *made,
        chip=(1,),
    )
    blocks = dict(zip(late, rest))
    incoming[0].append(exchange(blocks[1], "dom", 1))
    for b in order[len(early) + 1 :]:
        (block,) = call(
            functools.partial(add_kernel, width),
            [shape((classes, extents[b]), bf16)],
            [],
            1024,
            1024,
            blocks[b], *incoming[b],
        )
        incoming[b ^ low_bit(b)].append(exchange(block, "dom", low_bit(b)))
    own, received = blocks[0], incoming[0]
    class_sums, class_weights = call(
        functools.partial(final_kernel, width),
        [shape((classes, width), f32), shape((1, classes), f32)],
        [],
        doms * classes * padded,
        4 * doms * classes * padded,
        own, *received,
        pinned=False,
    )
    return class_sums, class_weights.reshape(classes)


def solution(mesh):
    placed = (
        P(("groups", "dom", "cls"), None),
        P(("groups", "cls"), None),
        P(("groups", "dom", "cls"), None),
        P(("groups", "dom", "cls")),
        P(("groups", "dom", "cls")),
        P("groups"),
    )
    return jax.shard_map(
        body,
        mesh=mesh,
        in_specs=placed,
        out_specs=(P(("groups", "cls"), "dom"), P(("groups", "cls"))),
        check_vma=False,
    )
```

```python
import functools
import math

import jax
import jax.numpy as jnp
import numpy as np
from jax import lax
from jax.experimental import pallas as pl
from jax.experimental.pallas import tpu as pltpu
from jax.sharding import PartitionSpec as P

CYCLES = 18
ANG = 64
IMG = 64
ANG_STEP = 1
ROTS = 8
SHIFT_R = 5
SHIFTW = 11
HALF = CYCLES * ANG
COLS = 2 * HALF
LANES = 128
SUB = 8
META = LANES
ROT_PRIOR = 0.5
VMEM_LIMIT = 20 * 1024 * 1024


def column_layout(doms):
    width = COLS // doms
    main = width - ANG
    half = doms // 2
    if width % ANG or main <= 0 or main % LANES or half * ANG % LANES:
        step = 3 * LANES
        segments = [(start, HALF + start, step) for start in range(0, HALF, step)]
        return list(range(COLS // ANG)), segments, 0
    per = width // ANG
    groups = [per * dom + group for dom in range(doms) for group in range(per - 1)]
    groups += [per * dom + per - 1 for dom in range(doms)]
    segments = [(dom * main, (half + dom) * main, main) for dom in range(half)]
    segments.append((doms * main, doms * main + half * ANG, half * ANG))
    return groups, segments, main


def tile_of(groups, tile, read):
    low, high = groups[2 * tile], groups[2 * tile + 1]
    if low % 2 == 0 and high == low + 1:
        return read(low // 2)
    first, second = read(low // 2), read(high // 2)
    first = pltpu.roll(first, ANG, 1) if low % 2 else first
    second = second if high % 2 else pltpu.roll(second, ANG, 1)
    return jnp.where(lane_index(first.shape) < ANG, first, second)


def phase_rows(groups):
    angles = np.arange(ANG) * (2.0 * math.pi / ANG)
    radius = np.arange(CYCLES) + 1.0
    fx = (radius[:, None] * np.cos(angles)[None, :]).reshape(-1)
    fy = (radius[:, None] * np.sin(angles)[None, :]).reshape(-1)
    offsets = np.arange(SHIFTW) - SHIFT_R
    unit = 2.0 * math.pi / IMG
    along_x = unit * offsets[:, None] * fx[None, :]
    along_y = unit * offsets[:, None] * fy[None, :]
    both = (along_x[SUB:, None, :] + along_y[None, SUB:, :]).reshape(-1, HALF)
    values = np.zeros((48, COLS), np.float32)
    for start, phase in ((0, along_x), (16, along_y), (32, both)):
        values[start : start + len(phase)] = np.concatenate([np.cos(phase), np.sin(phase)], axis=1)
    columns = np.concatenate([np.arange(ANG) + ANG * group for group in groups])
    return values[:, columns]


def build_table(segments, rows_ref, table_ref):
    for real_start, imag_start, width in segments:
        real = slice(real_start, real_start + width)
        imag = slice(imag_start, imag_start + width)

        def product(block, row):
            c, s = rows_ref[block : block + SUB, real], rows_ref[block : block + SUB, imag]
            d, t = rows_ref[row : row + 1, real], rows_ref[row : row + 1, imag]
            return c * d - s * t, s * d + c * t

        blocks = [product(0, 16 + y) for y in range(SHIFTW)]
        blocks += [product(16, x) for x in range(SUB, SHIFTW)]
        blocks += [
            (rows_ref[row : row + SUB, real], rows_ref[row : row + SUB, imag])
            for row in (32, 32 + SUB)
        ]
        for pair in range(0, len(blocks), 2):
            for part, columns in ((0, real), (1, imag)):
                value = jnp.concatenate([blocks[pair][part], blocks[pair + 1][part]], axis=0)
                high = value.astype(jnp.bfloat16)
                low = (value - high.astype(jnp.float32)).astype(jnp.bfloat16)
                row = pair * SUB
                table_ref[row : row + 2 * SUB, columns] = high
                table_ref[LANES + row : LANES + row + 2 * SUB, columns] = low


def table_row(index):
    y = jnp.floor((index + 0.5) * (1.0 / SHIFTW))
    x = index - SHIFTW * y
    near = SUB * y + x
    side = SUB * (SHIFTW + x - SUB) + y
    corner = SUB * (2 * SHIFTW - SUB) + (SHIFTW - SUB) * (x - SUB) + (y - SUB)
    return jnp.where(x < SUB, near, jnp.where(y < SUB, side, corner))


def exchange(array, axis, distance):
    return lax.ppermute(array, axis, [(i, i ^ distance) for i in range(lax.axis_size(axis))])


def lane_index(shape):
    return lax.broadcasted_iota(jnp.int32, shape, len(shape) - 1)


def rotate_classes(groups, class_ref, rotated_ref, norm_ref):
    classes = class_ref.shape[0]
    total = jnp.zeros((classes, LANES), jnp.float32)
    lane = lane_index((classes, LANES)) % ANG
    for tile in range(COLS // LANES):
        columns = slice(tile * LANES, (tile + 1) * LANES)
        value = tile_of(
            groups, tile, lambda k: class_ref[:, k * LANES : (k + 1) * LANES]
        )
        wide = value.astype(jnp.float32)
        total = total + wide * wide
        other = pltpu.roll(value, ANG, 1)
        for rotation in range(ROTS):
            offset = ANG_STEP * rotation % ANG
            turned = value
            if offset:
                turned = pltpu.roll(jnp.where(lane < ANG - offset, value, other), offset, 1)
            rotated_ref[rotation * classes : (rotation + 1) * classes, columns] = turned
    norm_ref[...] = jnp.broadcast_to(jnp.sum(total, axis=1, keepdims=True), (classes, LANES))


def to_lanes(column, width):
    n = column.shape[0]
    row = lax.broadcasted_iota(jnp.int32, (n, width), 0)
    return jnp.sum(
        jnp.where(lane_index((n, width)) % n == row, column, 0.0), axis=0, keepdims=True
    )


def fold_lanes(row, period, combine):
    result = row[:, :LANES]
    for part in range(1, row.shape[1] // LANES):
        result = combine(result, row[:, part * LANES : (part + 1) * LANES])
    step = LANES // 2
    while step >= period:
        result = combine(result, pltpu.roll(result, step, 1))
        step //= 2
    return result


def to_column(row):
    n = row.shape[1]
    diagonal = lax.broadcasted_iota(jnp.int32, (n, n), 0) == lane_index((n, n))
    return jnp.sum(jnp.where(diagonal, row, 0.0), axis=1, keepdims=True)


def pack_kernel(
    groups, particle_hbm, index_hbm, prior_hbm, group_hbm, class_hbm, scale_hbm, rows_hbm,
    packed_ref, class_ref, scale_ref, rows_ref, particle_ref, index_ref, prior_ref, group_ref, sems,
):
    particles, candidates = index_ref.shape
    copies = [
        pltpu.make_async_copy(source, target, sems.at[i])
        for i, (source, target) in enumerate(
            [
                (index_hbm, index_ref),
                (prior_hbm, prior_ref),
                (group_hbm, group_ref),
                (particle_hbm, particle_ref),
                (class_hbm, class_ref),
                (scale_hbm, scale_ref),
                (rows_hbm, rows_ref),
            ]
        )
    ]
    for copy in copies:
        copy.start()
    for copy in copies[:3]:
        copy.wait()
    lane = lane_index((particles, META))
    index = jnp.concatenate(
        [table_row(index_ref[...].astype(jnp.float32)), jnp.zeros((particles, META - candidates), jnp.float32)],
        axis=1,
    )
    prior = to_column(prior_ref[...].astype(jnp.float32))
    group = to_column(group_ref[...].astype(jnp.float32))
    meta = jnp.where(lane == candidates, prior, jnp.where(lane == candidates + 1, group, index))
    packed_ref[:, COLS:] = meta.astype(jnp.bfloat16)
    copies[3].wait()
    for tile in range(COLS // LANES):
        packed_ref[:, tile * LANES : (tile + 1) * LANES] = tile_of(
            groups, tile, lambda k: particle_ref[:, k * LANES : (k + 1) * LANES]
        )
    for copy in copies[4:]:
        copy.wait()


def score_block(segments, block_ref, table_ref, scale_ref, rotated_ref, norm_ref, shifted_ref, out):
    particles = block_ref.shape[0]
    classes = norm_ref.shape[0]
    candidates = shifted_ref.shape[0] // particles
    rows = particles * candidates
    repeat = rows // LANES
    meta = block_ref[:, COLS : COLS + META].astype(jnp.float32)
    index = meta[:, :candidates].astype(jnp.int32)
    lane = lane_index((particles, LANES))
    hot = jnp.concatenate(
        [
            jnp.where(index[:, t : t + 1] == lane, 1.0, 0.0).astype(jnp.bfloat16)
            for t in range(candidates)
        ],
        axis=0,
    )
    hot = jnp.concatenate([hot, hot], axis=1)
    groups = scale_ref.shape[1]
    group = meta[:, candidates + 1 : candidates + 2].astype(jnp.int32)
    scale_column = jnp.sum(
        jnp.where(group == lane_index((particles, groups)), scale_ref[...], 0.0),
        axis=1,
        keepdims=True,
    )
    scale = to_lanes(scale_column, rows)
    prior = to_lanes(meta[:, candidates : candidates + 1], rows)
    for real_start, imag_start, width in segments:
        real_columns = slice(real_start, real_start + width)
        imag_columns = slice(imag_start, imag_start + width)
        cosine = jnp.dot(hot, table_ref[:, real_columns], preferred_element_type=jnp.float32)
        sine = jnp.dot(hot, table_ref[:, imag_columns], preferred_element_type=jnp.float32)
        real = block_ref[:, real_columns].astype(jnp.float32)
        imag = block_ref[:, imag_columns].astype(jnp.float32)
        for t in range(candidates):
            part = slice(t * particles, (t + 1) * particles)
            c, s = cosine[part], sine[part]
            shifted_ref[part, real_columns] = (real * c - imag * s).astype(jnp.bfloat16)
            shifted_ref[part, imag_columns] = (real * s + imag * c).astype(jnp.bfloat16)
    product = lax.dot_general(
        rotated_ref[...],
        shifted_ref[...],
        (((1,), (1,)), ((), ())),
        preferred_element_type=jnp.float32,
    )
    norm = jnp.concatenate([norm_ref[...]] * repeat, axis=1)
    half_square = 0.5 * scale * scale
    scores = []
    highest = None
    for rotation in range(ROTS):
        distance = jnp.abs(rotation - prior)
        score = (
            scale * product[rotation * classes : (rotation + 1) * classes]
            - half_square * norm
            - ROT_PRIOR * (distance * distance)
        )
        scores.append(score)
        peak = jnp.max(score, axis=0, keepdims=True)
        highest = peak if highest is None else jnp.maximum(highest, peak)
    highest = fold_lanes(highest, particles, jnp.maximum)
    wide = jnp.concatenate([highest] * repeat, axis=1)
    total = None
    for rotation in range(ROTS):
        value = jnp.exp(scores[rotation] - wide)
        out(rotation, value)
        added = jnp.sum(value, axis=0, keepdims=True)
        total = added if total is None else total + added
    total = fold_lanes(total, particles, jnp.add)
    return highest, total, scale[:, :LANES]


def score_blocks(count, segments, chunks, blocks, table_ref, scale_ref, rotated_ref, norm_ref, shifted_ref, exp_ref, stats_ref):
    classes = norm_ref.shape[0]
    rows = exp_ref.shape[1] // count
    for block, block_ref in zip(chunks, blocks):
        part = slice(block * rows, (block + 1) * rows)

        def out(rotation, value):
            exp_ref[rotation * classes : (rotation + 1) * classes, part] = value

        highest, total, scale = score_block(
            segments, block_ref, table_ref, scale_ref, rotated_ref, norm_ref,
            shifted_ref.at[part, :], out,
        )
        stats_ref[2 * block : 2 * block + 1, :] = highest
        stats_ref[2 * block + 1 : 2 * block + 2, :] = total
        stats_ref[2 * count + block : 2 * count + block + 1, :] = scale


def first_kernel(count, groups, segments, chunks, *refs):
    blocks, refs = refs[: len(chunks)], refs[len(chunks) :]
    class_ref, rows_ref, scale_ref = refs[:3]
    shifted_ref, exp_ref, stats_ref, rotated_ref, norm_ref, table_ref = refs[3:]
    build_table(segments, rows_ref, table_ref)
    rotate_classes(groups, class_ref, rotated_ref, norm_ref)
    stats_ref[...] = jnp.zeros_like(stats_ref)
    score_blocks(
        count, segments, chunks, blocks, table_ref, scale_ref, rotated_ref, norm_ref,
        shifted_ref, exp_ref, stats_ref,
    )


def rest_kernel(count, segments, chunks, *refs):
    blocks, refs = refs[: len(chunks)], refs[len(chunks) :]
    table_ref, scale_ref, rotated_ref, norm_ref, before_ref = refs[:5]
    shifted_ref, exp_ref, stats_ref = refs[7:]
    stats_ref[...] = before_ref[...]
    score_blocks(
        count, segments, chunks, blocks, table_ref, scale_ref, rotated_ref, norm_ref,
        shifted_ref, exp_ref, stats_ref,
    )


def merged(mine, other, block, distance):
    twin = block ^ distance
    high, other_high = mine[2 * block : 2 * block + 1, :], other[2 * twin : 2 * twin + 1, :]
    top = jnp.maximum(high, other_high)
    total = mine[2 * block + 1 : 2 * block + 2, :] * jnp.exp(high - top)
    return top, total + other[2 * twin + 1 : 2 * twin + 2, :] * jnp.exp(other_high - top)


def merge_kernel(count, distance, mine, other, out_ref):
    out_ref[...] = jnp.zeros_like(out_ref)
    for block in range(count):
        top, total = merged(mine, other, block, distance)
        out_ref[2 * block : 2 * block + 1, :] = top
        out_ref[2 * block + 1 : 2 * block + 2, :] = total


def weigh(count, stats_ref, mine, other, exp_ref, weight_ref):
    rows = exp_ref.shape[1] // count
    repeat = rows // LANES
    classes = weight_ref.shape[0] // ROTS
    mass = jnp.zeros((classes, rows), jnp.float32)
    for block in range(count):
        top, total = merged(mine, other, block, count - 1)
        factor = jnp.exp(stats_ref[2 * block : 2 * block + 1, :] - top) / total
        scale = stats_ref[2 * count + block : 2 * count + block + 1, :]
        factor = jnp.concatenate([factor] * repeat, axis=1)
        scale = jnp.concatenate([scale] * repeat, axis=1)
        part = slice(block * rows, (block + 1) * rows)
        for rotation in range(ROTS):
            rotated = slice(rotation * classes, (rotation + 1) * classes)
            weight = exp_ref[rotated, part] * factor * scale
            mass = mass + weight * scale
            weight_ref[rotated, part] = weight.astype(jnp.bfloat16)
    return jnp.broadcast_to(jnp.sum(mass, axis=1, keepdims=True), (classes, LANES))


def window_sums(weight_ref, shifted_ref, start, wide):
    classes = weight_ref.shape[0] // ROTS
    product = jnp.dot(
        weight_ref[...], shifted_ref[:, pl.ds(start, wide)], preferred_element_type=jnp.float32
    )
    lane = lane_index((classes, LANES)) % ANG
    tiles = []
    for part in range(0, wide, LANES):
        inside = product[:classes, part : part + LANES]
        wrapped = None
        for rotation in range(1, ROTS):
            offset = ANG_STEP * rotation % ANG
            turned = pltpu.roll(
                product[rotation * classes : (rotation + 1) * classes, part : part + LANES],
                LANES - offset,
                1,
            )
            within = lane < ANG - offset
            inside = inside + jnp.where(within, turned, 0.0)
            over = jnp.where(within, 0.0, turned)
            wrapped = over if wrapped is None else wrapped + over
        tiles.append(inside + pltpu.roll(wrapped, ANG, 1))
    return tiles


def block_sums(doms, width, main, distance, weight_ref, shifted_ref, tails_ref):
    classes = weight_ref.shape[0] // ROTS
    padded = -(-(width + 3) // LANES) * LANES
    place = lax.axis_index("dom") ^ distance
    first = place * (main or width)
    shifts = [0] if main else sorted({width * dom % LANES for dom in range(doms)})
    span = main or -(-(shifts[-1] + width) // LANES) * LANES
    base = first // LANES * LANES
    tiles = []
    for start in range(0, span, 2 * LANES):
        tiles += window_sums(
            weight_ref,
            shifted_ref,
            pl.multiple_of(base + start, LANES),
            min(2 * LANES, span - start),
        )
    if main:
        tail = None
        for dom in range(doms):
            part = dom * ANG // LANES * LANES
            piece = tails_ref[:, part : part + LANES]
            piece = pltpu.roll(piece, ANG, 1) if dom % 2 else piece
            tail = piece if tail is None else jnp.where(place == dom, piece, tail)
        tiles.append(tail)
    total = jnp.concatenate(tiles, axis=1)
    aligned = total
    for shift in shifts:
        if shift:
            aligned = jnp.where(first - base == shift, pltpu.roll(total, span - shift, 1), aligned)
    return pad_columns(aligned, padded)


def store_block(width, value, mass, out_ref):
    high = mass.astype(jnp.bfloat16).astype(jnp.float32)
    middle = (mass - high).astype(jnp.bfloat16).astype(jnp.float32)
    low = (mass - high - middle).astype(jnp.bfloat16).astype(jnp.float32)
    lane = lane_index(value.shape)
    tail = jnp.where(
        lane == width, high, jnp.where(lane == width + 1, middle, jnp.where(lane == width + 2, low, 0.0))
    )
    value = jnp.where(lane < width, value, tail)
    out_ref[...] = value[:, : out_ref.shape[1]].astype(out_ref.dtype)


def pad_columns(value, padded):
    if value.shape[1] < padded:
        added = jnp.zeros((value.shape[0], padded - value.shape[1]), value.dtype)
        return jnp.concatenate([value, added], axis=1)
    return value[:, :padded]


def received_mass(width, ref):
    base = width // LANES * LANES
    tail = ref[:, base:].astype(jnp.float32)
    lane = base + lane_index(tail.shape)
    tail = jnp.where((lane >= width) & (lane < width + 3), tail, 0.0)
    return jnp.sum(tail, axis=1, keepdims=True)


def first_sums_kernel(count, doms, width, main, blocks, *refs):
    stats_ref, mine, other, exp_ref, shifted_ref, weight_ref, mass_ref, tails_ref = refs[:8]
    mass = weigh(count, stats_ref, mine, other, exp_ref, weight_ref)
    mass_ref[...] = mass
    tails_ref[...] = jnp.zeros_like(tails_ref)
    for start in range(0, doms * ANG if main else 0, 2 * LANES):
        tiles = window_sums(weight_ref, shifted_ref, doms * main + start, 2 * LANES)
        tails_ref[:, start : start + 2 * LANES] = jnp.concatenate(tiles, axis=1)
    for block, out_ref in zip(blocks, refs[8:]):
        value = block_sums(doms, width, main, block, weight_ref, shifted_ref, tails_ref)
        store_block(width, value, mass[:, :1], out_ref)


def rest_sums_kernel(doms, width, main, blocks, weight_ref, shifted_ref, mass_ref, tails_ref, *refs):
    for block, out_ref in zip(blocks, refs[-len(blocks) :]):
        value = block_sums(doms, width, main, block, weight_ref, shifted_ref, tails_ref)
        store_block(width, value, mass_ref[:, :1], out_ref)


def add_kernel(width, *refs):
    out_ref = refs[-1]
    padded = -(-out_ref.shape[1] // LANES) * LANES
    total, mass = None, None
    for ref in refs[:-1]:
        value = pad_columns(ref[...].astype(jnp.float32), padded)
        total = value if total is None else total + value
        tail = received_mass(width, ref)
        mass = tail if mass is None else mass + tail
    store_block(width, total, mass, out_ref)


def final_kernel(width, own_ref, *refs):
    received, sums_ref, weights_ref = refs[:-2], refs[-2], refs[-1]
    total, mass = None, None
    for ref in (own_ref, *received):
        value = ref[:, :width].astype(jnp.float32)
        total = value if total is None else total + value
        tail = received_mass(width, ref)
        mass = tail if mass is None else mass + tail
    sums_ref[...] = total
    weights_ref[...] = to_lanes(mass, total.shape[0])


def call(kernel, shapes, scratch, flops, moved, *args, smem=(), hbm=(), chip=(), pinned=True, aliases=None):
    vmem = pl.BlockSpec(memory_space=pltpu.VMEM)
    scalar = pl.BlockSpec(memory_space=pltpu.SMEM)
    place = pl.BlockSpec(memory_space=pltpu.HBM)
    args = [
        pltpu.with_memory_space_constraint(a, pltpu.HBM) if i in hbm
        else pltpu.with_memory_space_constraint(a, pltpu.VMEM) if i in chip
        else a
        for i, a in enumerate(args)
    ]
    return pl.pallas_call(
        kernel,
        out_shape=[pltpu.VMEM(s.shape, s.dtype) if pinned else s for s in shapes],
        in_specs=[scalar if i in smem else place if i in hbm else vmem for i in range(len(args))],
        out_specs=[vmem] * len(shapes),
        scratch_shapes=scratch,
        input_output_aliases=aliases or {},
        compiler_params=pltpu.CompilerParams(vmem_limit_bytes=VMEM_LIMIT),
        cost_estimate=pl.CostEstimate(flops=flops, bytes_accessed=moved, transcendentals=0),
    )(*args)


def body(particle_spectra, class_spectra, shift_index, prior_rotation, particle_group, group_scale):
    count = lax.axis_size("cls")
    doms = lax.axis_size("dom")
    particles, candidates = shift_index.shape
    classes = class_spectra.shape[0]
    rows = particles * candidates
    width = COLS // doms
    padded = -(-(width + 3) // LANES) * LANES
    growth = (padded - width - 3) // (doms - 1)
    f32, bf16 = jnp.float32, jnp.bfloat16
    shape = jax.ShapeDtypeStruct

    groups, segments, main = column_layout(doms)
    phases = jnp.asarray(phase_rows(groups))
    packed, classes_on_chip, scales, phases_on_chip = call(
        functools.partial(pack_kernel, groups),
        [
            shape((particles, COLS + META), bf16),
            shape(class_spectra.shape, bf16),
            shape((1, group_scale.shape[0]), f32),
            shape(phases.shape, f32),
        ],
        [
            pltpu.VMEM((particles, COLS), bf16),
            pltpu.VMEM((particles, candidates), jnp.int32),
            pltpu.VMEM((1, particles), jnp.int32),
            pltpu.VMEM((1, particles), jnp.int32),
            pltpu.SemaphoreType.DMA((7,)),
        ],
        particles * COLS,
        4 * particles * COLS,
        particle_spectra, shift_index, prior_rotation[None, :], particle_group[None, :],
        class_spectra, group_scale[None, :], phases,
        hbm=(0, 1, 2, 3, 4, 5, 6),
    )
    chunks = {0: packed, 1: exchange(packed, "cls", 1)}
    for b in range(2, count, 2):
        chunks[b + 1] = exchange(packed, "cls", b + 1)
    stat_rows = -(-3 * count // 8) * 8
    work = 2 * rows * COLS * (ROTS * classes + 256)
    stats_shape = shape((stat_rows, LANES), f32)
    shifted_shape = shape((count * rows, COLS), bf16)
    exp_shape = shape((ROTS * classes, count * rows), f32)
    near = [0, 1]
    shifted, exps, stats, rotated, norm, table = call(
        functools.partial(first_kernel, count, groups, segments, near),
        [
            shifted_shape,
            exp_shape,
            stats_shape,
            shape((ROTS * classes, COLS), bf16),
            shape((classes, LANES), f32),
            shape((2 * LANES, COLS), bf16),
        ],
        [],
        work * len(near),
        4 * len(near) * rows * COLS,
        *[chunks[b] for b in near], classes_on_chip, phases_on_chip, scales,
    )
    for b in range(2, count, 2):
        arrived, stats = lax.optimization_barrier((chunks[b + 1], stats))
        chunks[b] = exchange(arrived, "cls", 1)
    for far in (list(range(3, count, 2)), list(range(2, count, 2))):
        shifted, exps, stats = call(
            functools.partial(rest_kernel, count, segments, far),
            [shifted_shape, exp_shape, stats_shape],
            [],
            work * len(far),
            4 * len(far) * rows * COLS,
            *[chunks[b] for b in far], table, scales, rotated, norm, stats, shifted, exps,
            aliases={len(far) + 5: 0, len(far) + 6: 1},
            chip=(len(far) + 5, len(far) + 6),
        )
    mine, distance = stats, 1
    other = exchange(mine, "cls", distance)
    while distance + 1 < count:
        (mine,) = call(
            functools.partial(merge_kernel, count, distance),
            [shape((-(-2 * count // 8) * 8, LANES), f32)],
            [],
            1024,
            1024,
            mine, other,
        )
        distance = 2 * distance + 1
        other = exchange(mine, "cls", distance)
    low_bit = lambda b: b & -b
    early = list(range(doms - 1, 1, -2))
    order = early + [1] + sorted(range(2, doms, 2), key=lambda b: (low_bit(b), -b))
    extents = {b: width + 3 + (doms - 1 - place) * growth for place, b in enumerate(order)}
    late = [1] + list(range(0, doms, 2))
    weights, mass, tails, *made = call(
        functools.partial(first_sums_kernel, count, doms, width, main, early),
        [
            shape((ROTS * classes, count * rows), bf16),
            shape((classes, LANES), f32),
            shape((classes, doms * ANG if main else LANES), f32),
        ]
        + [shape((classes, extents[b]), bf16) for b in early],
        [],
        2 * count * rows * COLS * ROTS * classes // doms,
        4 * count * rows * width,
        stats, mine, other, exps, shifted,
        chip=(3, 4),
    )
    incoming = {b: [] for b in range(doms)}
    for b, block in zip(early, made):
        incoming[b ^ 1].append(exchange(block, "dom", 1))
    rest = call(
        functools.partial(rest_sums_kernel, doms, width, main, late),
        [
            shape((classes, extents.get(b, width + 3)), bf16 if b == 1 else f32) for b in late
        ],
        [],
        1024,
        1024,
        weights, shifted, mass, tails, *made,
        chip=(1,),
    )
    blocks = dict(zip(late, rest))
    incoming[0].append(exchange(blocks[1], "dom", 1))
    for b in order[len(early) + 1 :]:
        (block,) = call(
            functools.partial(add_kernel, width),
            [shape((classes, extents[b]), bf16)],
            [],
            1024,
            1024,
            blocks[b], *incoming[b],
        )
        incoming[b ^ low_bit(b)].append(exchange(block, "dom", low_bit(b)))
    own, received = blocks[0], incoming[0]
    class_sums, class_weights = call(
        functools.partial(final_kernel, width),
        [shape((classes, width), f32), shape((1, classes), f32)],
        [],
        doms * classes * padded,
        4 * doms * classes * padded,
        own, *received,
        pinned=False,
    )
    return class_sums, class_weights.reshape(classes)


def solution(mesh):
    placed = (
        P(("groups", "dom", "cls"), None),
        P(("groups", "cls"), None),
        P(("groups", "dom", "cls"), None),
        P(("groups", "dom", "cls")),
        P(("groups", "dom", "cls")),
        P("groups"),
    )
    return jax.shard_map(
        body,
        mesh=mesh,
        in_specs=placed,
        out_specs=(P(("groups", "cls"), "dom"), P(("groups", "cls"))),
        check_vma=False,
    )
```

```python
import functools
import math

import jax
import jax.numpy as jnp
import numpy as np
from jax import lax
from jax.experimental import pallas as pl
from jax.experimental.pallas import tpu as pltpu
from jax.sharding import PartitionSpec as P

CYCLES = 18
ANG = 64
IMG = 64
ANG_STEP = 1
ROTS = 8
SHIFT_R = 5
SHIFTW = 11
HALF = CYCLES * ANG
COLS = 2 * HALF
LANES = 128
SUB = 8
META = LANES
ROT_PRIOR = 0.5
VMEM_LIMIT = 20 * 1024 * 1024


def column_layout(doms):
    width = COLS // doms
    main = width - ANG
    half = doms // 2
    if width % ANG or main <= 0 or main % LANES or half * ANG % LANES:
        step = 3 * LANES
        segments = [(start, HALF + start, step) for start in range(0, HALF, step)]
        return list(range(COLS // ANG)), segments, 0
    per = width // ANG
    groups = [per * dom + group for dom in range(doms) for group in range(per - 1)]
    groups += [per * dom + per - 1 for dom in range(doms)]
    segments = [(dom * main, (half + dom) * main, main) for dom in range(half)]
    segments.append((doms * main, doms * main + half * ANG, half * ANG))
    return groups, segments, main


def tile_of(groups, tile, read):
    low, high = groups[2 * tile], groups[2 * tile + 1]
    if low % 2 == 0 and high == low + 1:
        return read(low // 2)
    first, second = read(low // 2), read(high // 2)
    first = pltpu.roll(first, ANG, 1) if low % 2 else first
    second = second if high % 2 else pltpu.roll(second, ANG, 1)
    return jnp.where(lane_index(first.shape) < ANG, first, second)


def phase_rows(groups):
    angles = np.arange(ANG) * (2.0 * math.pi / ANG)
    radius = np.arange(CYCLES) + 1.0
    fx = (radius[:, None] * np.cos(angles)[None, :]).reshape(-1)
    fy = (radius[:, None] * np.sin(angles)[None, :]).reshape(-1)
    offsets = np.arange(SHIFTW) - SHIFT_R
    unit = 2.0 * math.pi / IMG
    along_x = unit * offsets[:, None] * fx[None, :]
    along_y = unit * offsets[:, None] * fy[None, :]
    both = (along_x[SUB:, None, :] + along_y[None, SUB:, :]).reshape(-1, HALF)
    values = np.zeros((48, COLS), np.float32)
    for start, phase in ((0, along_x), (16, along_y), (32, both)):
        values[start : start + len(phase)] = np.concatenate([np.cos(phase), np.sin(phase)], axis=1)
    columns = np.concatenate([np.arange(ANG) + ANG * group for group in groups])
    return values[:, columns]


def build_table(segments, rows_ref, table_ref):
    for real_start, imag_start, width in segments:
        real = slice(real_start, real_start + width)
        imag = slice(imag_start, imag_start + width)

        def product(block, row):
            c, s = rows_ref[block : block + SUB, real], rows_ref[block : block + SUB, imag]
            d, t = rows_ref[row : row + 1, real], rows_ref[row : row + 1, imag]
            return c * d - s * t, s * d + c * t

        blocks = [product(0, 16 + y) for y in range(SHIFTW)]
        blocks += [product(16, x) for x in range(SUB, SHIFTW)]
        blocks += [
            (rows_ref[row : row + SUB, real], rows_ref[row : row + SUB, imag])
            for row in (32, 32 + SUB)
        ]
        for pair in range(0, len(blocks), 2):
            for part, columns in ((0, real), (1, imag)):
                value = jnp.concatenate([blocks[pair][part], blocks[pair + 1][part]], axis=0)
                high = value.astype(jnp.bfloat16)
                low = (value - high.astype(jnp.float32)).astype(jnp.bfloat16)
                row = pair * SUB
                table_ref[row : row + 2 * SUB, columns] = high
                table_ref[LANES + row : LANES + row + 2 * SUB, columns] = low


def table_row(index):
    y = jnp.floor((index + 0.5) * (1.0 / SHIFTW))
    x = index - SHIFTW * y
    near = SUB * y + x
    side = SUB * (SHIFTW + x - SUB) + y
    corner = SUB * (2 * SHIFTW - SUB) + (SHIFTW - SUB) * (x - SUB) + (y - SUB)
    return jnp.where(x < SUB, near, jnp.where(y < SUB, side, corner))


def exchange(array, axis, distance):
    return lax.ppermute(array, axis, [(i, i ^ distance) for i in range(lax.axis_size(axis))])


def lane_index(shape):
    return lax.broadcasted_iota(jnp.int32, shape, len(shape) - 1)


def rotate_classes(groups, class_ref, rotated_ref, norm_ref):
    classes = class_ref.shape[0]
    total = jnp.zeros((classes, LANES), jnp.float32)
    lane = lane_index((classes, LANES)) % ANG
    for tile in range(COLS // LANES):
        columns = slice(tile * LANES, (tile + 1) * LANES)
        value = tile_of(
            groups, tile, lambda k: class_ref[:, k * LANES : (k + 1) * LANES]
        )
        wide = value.astype(jnp.float32)
        total = total + wide * wide
        other = pltpu.roll(value, ANG, 1)
        for rotation in range(ROTS):
            offset = ANG_STEP * rotation % ANG
            turned = value
            if offset:
                turned = pltpu.roll(jnp.where(lane < ANG - offset, value, other), offset, 1)
            rotated_ref[rotation * classes : (rotation + 1) * classes, columns] = turned
    norm_ref[...] = jnp.broadcast_to(jnp.sum(total, axis=1, keepdims=True), (classes, LANES))


def to_lanes(column, width):
    n = column.shape[0]
    row = lax.broadcasted_iota(jnp.int32, (n, width), 0)
    return jnp.sum(
        jnp.where(lane_index((n, width)) % n == row, column, 0.0), axis=0, keepdims=True
    )


def fold_lanes(row, period, combine):
    result = row[:, :LANES]
    for part in range(1, row.shape[1] // LANES):
        result = combine(result, row[:, part * LANES : (part + 1) * LANES])
    step = LANES // 2
    while step >= period:
        result = combine(result, pltpu.roll(result, step, 1))
        step //= 2
    return result


def to_column(row):
    n = row.shape[1]
    diagonal = lax.broadcasted_iota(jnp.int32, (n, n), 0) == lane_index((n, n))
    return jnp.sum(jnp.where(diagonal, row, 0.0), axis=1, keepdims=True)


def pack_kernel(
    groups, particle_hbm, index_hbm, prior_hbm, group_hbm, class_hbm, scale_hbm, rows_hbm,
    packed_ref, class_ref, scale_ref, rows_ref, particle_ref, index_ref, prior_ref, group_ref, sems,
):
    particles, candidates = index_ref.shape
    copies = [
        pltpu.make_async_copy(source, target, sems.at[i])
        for i, (source, target) in enumerate(
            [
                (index_hbm, index_ref),
                (prior_hbm, prior_ref),
                (group_hbm, group_ref),
                (particle_hbm, particle_ref),
                (class_hbm, class_ref),
                (scale_hbm, scale_ref),
                (rows_hbm, rows_ref),
            ]
        )
    ]
    for copy in copies:
        copy.start()
    for copy in copies[:3]:
        copy.wait()
    lane = lane_index((particles, META))
    index = jnp.concatenate(
        [table_row(index_ref[...].astype(jnp.float32)), jnp.zeros((particles, META - candidates), jnp.float32)],
        axis=1,
    )
    prior = to_column(prior_ref[...].astype(jnp.float32))
    group = to_column(group_ref[...].astype(jnp.float32))
    meta = jnp.where(lane == candidates, prior, jnp.where(lane == candidates + 1, group, index))
    packed_ref[:, COLS:] = meta.astype(jnp.bfloat16)
    copies[3].wait()
    for tile in range(COLS // LANES):
        packed_ref[:, tile * LANES : (tile + 1) * LANES] = tile_of(
            groups, tile, lambda k: particle_ref[:, k * LANES : (k + 1) * LANES]
        )
    for copy in copies[4:]:
        copy.wait()


def match_block(segments, block_ref, table_ref, scale_ref, rotated_ref, shifted_ref):
    particles = block_ref.shape[0]
    candidates = shifted_ref.shape[0] // particles
    meta = block_ref[:, COLS : COLS + META].astype(jnp.float32)
    index = meta[:, :candidates].astype(jnp.int32)
    lane = lane_index((particles, LANES))
    hot = jnp.concatenate(
        [
            jnp.where(index[:, t : t + 1] == lane, 1.0, 0.0).astype(jnp.bfloat16)
            for t in range(candidates)
        ],
        axis=0,
    )
    hot = jnp.concatenate([hot, hot], axis=1)
    groups = scale_ref.shape[1]
    group = meta[:, candidates + 1 : candidates + 2].astype(jnp.int32)
    scale_column = jnp.sum(
        jnp.where(group == lane_index((particles, groups)), scale_ref[...], 0.0),
        axis=1,
        keepdims=True,
    )
    scale = to_lanes(scale_column, LANES)
    prior = to_lanes(meta[:, candidates : candidates + 1], LANES)
    for real_start, imag_start, width in segments:
        real_columns = slice(real_start, real_start + width)
        imag_columns = slice(imag_start, imag_start + width)
        cosine = jnp.dot(hot, table_ref[:, real_columns], preferred_element_type=jnp.float32)
        sine = jnp.dot(hot, table_ref[:, imag_columns], preferred_element_type=jnp.float32)
        real = block_ref[:, real_columns].astype(jnp.float32)
        imag = block_ref[:, imag_columns].astype(jnp.float32)
        for t in range(candidates):
            part = slice(t * particles, (t + 1) * particles)
            c, s = cosine[part], sine[part]
            shifted_ref[part, real_columns] = (real * c - imag * s).astype(jnp.bfloat16)
            shifted_ref[part, imag_columns] = (real * s + imag * c).astype(jnp.bfloat16)
    product = lax.dot_general(
        rotated_ref[...],
        shifted_ref[...],
        (((1,), (1,)), ((), ())),
        preferred_element_type=jnp.float32,
    )
    return product, scale, prior


def soften_block(product, scale, prior, norm_ref, particles, rows, out):
    repeat = rows // LANES
    norm = jnp.concatenate([norm_ref[...]] * repeat, axis=1)
    scale = jnp.concatenate([scale] * repeat, axis=1)
    prior = jnp.concatenate([prior] * repeat, axis=1)
    half_square = 0.5 * scale * scale
    scores = []
    highest = None
    for rotation in range(ROTS):
        distance = jnp.abs(rotation - prior)
        score = (
            scale * product(rotation)
            - half_square * norm
            - ROT_PRIOR * (distance * distance)
        )
        scores.append(score)
        peak = jnp.max(score, axis=0, keepdims=True)
        highest = peak if highest is None else jnp.maximum(highest, peak)
    highest = fold_lanes(highest, particles, jnp.maximum)
    wide = jnp.concatenate([highest] * repeat, axis=1)
    total = None
    for rotation in range(ROTS):
        value = jnp.exp(scores[rotation] - wide)
        out(rotation, value)
        added = jnp.sum(value, axis=0, keepdims=True)
        total = added if total is None else total + added
    total = fold_lanes(total, particles, jnp.add)
    return highest, total


def score_blocks(
    count, segments, pending, chunks, last, blocks, table_ref, scale_ref, rotated_ref, norm_ref,
    shifted_ref, exp_ref, stats_ref,
):
    classes = norm_ref.shape[0]
    rows = exp_ref.shape[1] // count
    particles = blocks[0].shape[0]

    def soften(block, product):
        part = slice(block * rows, (block + 1) * rows)

        def out(rotation, value):
            exp_ref[rotation * classes : (rotation + 1) * classes, part] = value

        scale = stats_ref[2 * count + block : 2 * count + block + 1, :]
        prior = stats_ref[3 * count + block : 3 * count + block + 1, :]
        highest, total = soften_block(product, scale, prior, norm_ref, particles, rows, out)
        stats_ref[2 * block : 2 * block + 1, :] = highest
        stats_ref[2 * block + 1 : 2 * block + 2, :] = total

    for block in pending:
        part = slice(block * rows, (block + 1) * rows)
        soften(block, lambda rotation: exp_ref[rotation * classes : (rotation + 1) * classes, part])
    for block, block_ref in zip(chunks, blocks):
        part = slice(block * rows, (block + 1) * rows)
        product, scale, prior = match_block(
            segments, block_ref, table_ref, scale_ref, rotated_ref, shifted_ref.at[part, :]
        )
        stats_ref[2 * count + block : 2 * count + block + 1, :] = scale
        stats_ref[3 * count + block : 3 * count + block + 1, :] = prior
        if block != chunks[-1] or last:
            soften(block, lambda rotation: product[rotation * classes : (rotation + 1) * classes])
        else:
            exp_ref[0 : ROTS * classes, part] = product


def first_kernel(count, groups, segments, chunks, *refs):
    blocks, refs = refs[: len(chunks)], refs[len(chunks) :]
    class_ref, rows_ref, scale_ref = refs[:3]
    shifted_ref, exp_ref, stats_ref, rotated_ref, norm_ref, table_ref = refs[3:]
    build_table(segments, rows_ref, table_ref)
    rotate_classes(groups, class_ref, rotated_ref, norm_ref)
    stats_ref[...] = jnp.zeros_like(stats_ref)
    score_blocks(
        count, segments, [], chunks, False, blocks, table_ref, scale_ref, rotated_ref, norm_ref,
        shifted_ref, exp_ref, stats_ref,
    )


def rest_kernel(count, segments, pending, chunks, last, *refs):
    blocks, refs = refs[: len(chunks)], refs[len(chunks) :]
    table_ref, scale_ref, rotated_ref, norm_ref, before_ref = refs[:5]
    shifted_ref, exp_ref, stats_ref = refs[7:]
    stats_ref[...] = before_ref[...]
    score_blocks(
        count, segments, pending, chunks, last, blocks, table_ref, scale_ref, rotated_ref, norm_ref,
        shifted_ref, exp_ref, stats_ref,
    )


def merged(mine, other, block, distance):
    twin = block ^ distance
    high, other_high = mine[2 * block : 2 * block + 1, :], other[2 * twin : 2 * twin + 1, :]
    top = jnp.maximum(high, other_high)
    total = mine[2 * block + 1 : 2 * block + 2, :] * jnp.exp(high - top)
    return top, total + other[2 * twin + 1 : 2 * twin + 2, :] * jnp.exp(other_high - top)


def merge_kernel(count, distance, mine, other, out_ref):
    out_ref[...] = jnp.zeros_like(out_ref)
    for block in range(count):
        top, total = merged(mine, other, block, distance)
        out_ref[2 * block : 2 * block + 1, :] = top
        out_ref[2 * block + 1 : 2 * block + 2, :] = total


def weigh(count, stats_ref, mine, other, exp_ref, weight_ref):
    rows = exp_ref.shape[1] // count
    repeat = rows // LANES
    classes = weight_ref.shape[0] // ROTS
    mass = jnp.zeros((classes, rows), jnp.float32)
    for block in range(count):
        top, total = merged(mine, other, block, count // 2)
        factor = jnp.exp(stats_ref[2 * block : 2 * block + 1, :] - top) / total
        scale = stats_ref[2 * count + block : 2 * count + block + 1, :]
        factor = jnp.concatenate([factor] * repeat, axis=1)
        scale = jnp.concatenate([scale] * repeat, axis=1)
        part = slice(block * rows, (block + 1) * rows)
        for rotation in range(ROTS):
            rotated = slice(rotation * classes, (rotation + 1) * classes)
            weight = exp_ref[rotated, part] * factor * scale
            mass = mass + weight * scale
            weight_ref[rotated, part] = weight.astype(jnp.bfloat16)
    return jnp.broadcast_to(jnp.sum(mass, axis=1, keepdims=True), (classes, LANES))


def window_sums(weight_ref, shifted_ref, start, wide):
    classes = weight_ref.shape[0] // ROTS
    product = jnp.dot(
        weight_ref[...], shifted_ref[:, pl.ds(start, wide)], preferred_element_type=jnp.float32
    )
    lane = lane_index((classes, LANES)) % ANG
    tiles = []
    for part in range(0, wide, LANES):
        inside = product[:classes, part : part + LANES]
        wrapped = None
        for rotation in range(1, ROTS):
            offset = ANG_STEP * rotation % ANG
            turned = pltpu.roll(
                product[rotation * classes : (rotation + 1) * classes, part : part + LANES],
                LANES - offset,
                1,
            )
            within = lane < ANG - offset
            inside = inside + jnp.where(within, turned, 0.0)
            over = jnp.where(within, 0.0, turned)
            wrapped = over if wrapped is None else wrapped + over
        tiles.append(inside + pltpu.roll(wrapped, ANG, 1))
    return tiles


def block_sums(doms, width, main, distance, weight_ref, shifted_ref, tails_ref):
    classes = weight_ref.shape[0] // ROTS
    padded = -(-(width + 3) // LANES) * LANES
    place = lax.axis_index("dom") ^ distance
    first = place * (main or width)
    shifts = [0] if main else sorted({width * dom % LANES for dom in range(doms)})
    span = main or -(-(shifts[-1] + width) // LANES) * LANES
    base = first // LANES * LANES
    tiles = []
    for start in range(0, span, 2 * LANES):
        tiles += window_sums(
            weight_ref,
            shifted_ref,
            pl.multiple_of(base + start, LANES),
            min(2 * LANES, span - start),
        )
    if main:
        tail = None
        for dom in range(doms):
            part = dom * ANG // LANES * LANES
            piece = tails_ref[:, part : part + LANES]
            piece = pltpu.roll(piece, ANG, 1) if dom % 2 else piece
            tail = piece if tail is None else jnp.where(place == dom, piece, tail)
        tiles.append(tail)
    total = jnp.concatenate(tiles, axis=1)
    aligned = total
    for shift in shifts:
        if shift:
            aligned = jnp.where(first - base == shift, pltpu.roll(total, span - shift, 1), aligned)
    return pad_columns(aligned, padded)


def store_block(width, value, mass, out_ref):
    high = mass.astype(jnp.bfloat16).astype(jnp.float32)
    middle = (mass - high).astype(jnp.bfloat16).astype(jnp.float32)
    low = (mass - high - middle).astype(jnp.bfloat16).astype(jnp.float32)
    lane = lane_index(value.shape)
    tail = jnp.where(
        lane == width, high, jnp.where(lane == width + 1, middle, jnp.where(lane == width + 2, low, 0.0))
    )
    value = jnp.where(lane < width, value, tail)
    out_ref[...] = value[:, : out_ref.shape[1]].astype(out_ref.dtype)


def pad_columns(value, padded):
    if value.shape[1] < padded:
        added = jnp.zeros((value.shape[0], padded - value.shape[1]), value.dtype)
        return jnp.concatenate([value, added], axis=1)
    return value[:, :padded]


def received_mass(width, ref):
    base = width // LANES * LANES
    tail = ref[:, base:].astype(jnp.float32)
    lane = base + lane_index(tail.shape)
    tail = jnp.where((lane >= width) & (lane < width + 3), tail, 0.0)
    return jnp.sum(tail, axis=1, keepdims=True)


def first_sums_kernel(count, doms, width, main, blocks, *refs):
    stats_ref, mine, other, exp_ref, shifted_ref, weight_ref, mass_ref, tails_ref = refs[:8]
    mass = weigh(count, stats_ref, mine, other, exp_ref, weight_ref)
    mass_ref[...] = mass
    tails_ref[...] = jnp.zeros_like(tails_ref)
    for start in range(0, doms * ANG if main else 0, 2 * LANES):
        tiles = window_sums(weight_ref, shifted_ref, doms * main + start, 2 * LANES)
        tails_ref[:, start : start + 2 * LANES] = jnp.concatenate(tiles, axis=1)
    for block, out_ref in zip(blocks, refs[8:]):
        value = block_sums(doms, width, main, block, weight_ref, shifted_ref, tails_ref)
        store_block(width, value, mass[:, :1], out_ref)


def rest_sums_kernel(doms, width, main, blocks, weight_ref, shifted_ref, mass_ref, tails_ref, *refs):
    for block, out_ref in zip(blocks, refs[-len(blocks) :]):
        value = block_sums(doms, width, main, block, weight_ref, shifted_ref, tails_ref)
        store_block(width, value, mass_ref[:, :1], out_ref)


def add_kernel(width, *refs):
    out_ref = refs[-1]
    padded = -(-out_ref.shape[1] // LANES) * LANES
    total, mass = None, None
    for ref in refs[:-1]:
        value = pad_columns(ref[...].astype(jnp.float32), padded)
        total = value if total is None else total + value
        tail = received_mass(width, ref)
        mass = tail if mass is None else mass + tail
    store_block(width, total, mass, out_ref)


def final_kernel(width, own_ref, *refs):
    received, sums_ref, weights_ref = refs[:-2], refs[-2], refs[-1]
    total, mass = None, None
    for ref in (own_ref, *received):
        value = ref[:, :width].astype(jnp.float32)
        total = value if total is None else total + value
        tail = received_mass(width, ref)
        mass = tail if mass is None else mass + tail
    sums_ref[...] = total
    weights_ref[...] = to_lanes(mass, total.shape[0])


def call(kernel, shapes, scratch, flops, moved, *args, smem=(), hbm=(), chip=(), pinned=True, aliases=None):
    vmem = pl.BlockSpec(memory_space=pltpu.VMEM)
    scalar = pl.BlockSpec(memory_space=pltpu.SMEM)
    place = pl.BlockSpec(memory_space=pltpu.HBM)
    args = [
        pltpu.with_memory_space_constraint(a, pltpu.HBM) if i in hbm
        else pltpu.with_memory_space_constraint(a, pltpu.VMEM) if i in chip
        else a
        for i, a in enumerate(args)
    ]
    return pl.pallas_call(
        kernel,
        out_shape=[pltpu.VMEM(s.shape, s.dtype) if pinned else s for s in shapes],
        in_specs=[scalar if i in smem else place if i in hbm else vmem for i in range(len(args))],
        out_specs=[vmem] * len(shapes),
        scratch_shapes=scratch,
        input_output_aliases=aliases or {},
        compiler_params=pltpu.CompilerParams(vmem_limit_bytes=VMEM_LIMIT),
        cost_estimate=pl.CostEstimate(flops=flops, bytes_accessed=moved, transcendentals=0),
    )(*args)


def body(particle_spectra, class_spectra, shift_index, prior_rotation, particle_group, group_scale):
    count = lax.axis_size("cls")
    doms = lax.axis_size("dom")
    particles, candidates = shift_index.shape
    classes = class_spectra.shape[0]
    rows = particles * candidates
    width = COLS // doms
    padded = -(-(width + 3) // LANES) * LANES
    growth = (padded - width - 3) // (doms - 1)
    f32, bf16 = jnp.float32, jnp.bfloat16
    shape = jax.ShapeDtypeStruct

    groups, segments, main = column_layout(doms)
    phases = jnp.asarray(phase_rows(groups))
    packed, classes_on_chip, scales, phases_on_chip = call(
        functools.partial(pack_kernel, groups),
        [
            shape((particles, COLS + META), bf16),
            shape(class_spectra.shape, bf16),
            shape((1, group_scale.shape[0]), f32),
            shape(phases.shape, f32),
        ],
        [
            pltpu.VMEM((particles, COLS), bf16),
            pltpu.VMEM((particles, candidates), jnp.int32),
            pltpu.VMEM((1, particles), jnp.int32),
            pltpu.VMEM((1, particles), jnp.int32),
            pltpu.SemaphoreType.DMA((7,)),
        ],
        particles * COLS,
        4 * particles * COLS,
        particle_spectra, shift_index, prior_rotation[None, :], particle_group[None, :],
        class_spectra, group_scale[None, :], phases,
        hbm=(0, 1, 2, 3, 4, 5, 6),
    )
    chunks = {0: packed, 1: exchange(packed, "cls", 1)}
    for b in range(2, count, 2):
        chunks[b] = exchange(packed, "cls", b)
    stat_rows = -(-4 * count // 8) * 8
    work = 2 * rows * COLS * (ROTS * classes + 256)
    stats_shape = shape((stat_rows, LANES), f32)
    shifted_shape = shape((count * rows, COLS), bf16)
    exp_shape = shape((ROTS * classes, count * rows), f32)
    near = [0, 1]
    shifted, exps, stats, rotated, norm, table = call(
        functools.partial(first_kernel, count, groups, segments, near),
        [
            shifted_shape,
            exp_shape,
            stats_shape,
            shape((ROTS * classes, COLS), bf16),
            shape((classes, LANES), f32),
            shape((2 * LANES, COLS), bf16),
        ],
        [],
        work * len(near),
        4 * len(near) * rows * COLS,
        *[chunks[b] for b in near], classes_on_chip, phases_on_chip, scales,
    )
    for b in range(2, count, 2):
        arrived, stats = lax.optimization_barrier((chunks[b], stats))
        chunks[b + 1] = exchange(arrived, "cls", 1)
    evens, odds = list(range(2, count, 2)), list(range(3, count, 2))
    for pending, far in ((near[-1:], evens), (evens[-1:], odds)):
        shifted, exps, stats = call(
            functools.partial(rest_kernel, count, segments, pending, far, far is odds),
            [shifted_shape, exp_shape, stats_shape],
            [],
            work * len(far),
            4 * len(far) * rows * COLS,
            *[chunks[b] for b in far], table, scales, rotated, norm, stats, shifted, exps,
            aliases={len(far) + 5: 0, len(far) + 6: 1},
            chip=(len(far) + 5, len(far) + 6),
        )
    mine, distance = stats, 1
    other = exchange(mine, "cls", distance)
    while 2 * distance < count:
        (mine,) = call(
            functools.partial(merge_kernel, count, distance),
            [shape((-(-2 * count // 8) * 8, LANES), f32)],
            [],
            1024,
            1024,
            mine, other,
        )
        distance *= 2
        other = exchange(mine, "cls", distance)
    low_bit = lambda b: b & -b
    early = list(range(doms - 1, 1, -2))
    order = early + [1] + sorted(range(2, doms, 2), key=lambda b: (low_bit(b), -b))
    extents = {b: width + 3 + (doms - 1 - place) * growth for place, b in enumerate(order)}
    late = [1] + list(range(0, doms, 2))
    weights, mass, tails, *made = call(
        functools.partial(first_sums_kernel, count, doms, width, main, early),
        [
            shape((ROTS * classes, count * rows), bf16),
            shape((classes, LANES), f32),
            shape((classes, doms * ANG if main else LANES), f32),
        ]
        + [shape((classes, extents[b]), bf16) for b in early],
        [],
        2 * count * rows * COLS * ROTS * classes // doms,
        4 * count * rows * width,
        stats, mine, other, exps, shifted,
        chip=(3, 4),
    )
    incoming = {b: [] for b in range(doms)}
    for b, block in zip(early, made):
        incoming[b ^ 1].append(exchange(block, "dom", 1))
    rest = call(
        functools.partial(rest_sums_kernel, doms, width, main, late),
        [
            shape((classes, extents.get(b, width + 3)), bf16 if b == 1 else f32) for b in late
        ],
        [],
        1024,
        1024,
        weights, shifted, mass, tails, *made,
        chip=(1,),
    )
    blocks = dict(zip(late, rest))
    incoming[0].append(exchange(blocks[1], "dom", 1))
    for b in order[len(early) + 1 :]:
        (block,) = call(
            functools.partial(add_kernel, width),
            [shape((classes, extents[b]), bf16)],
            [],
            1024,
            1024,
            blocks[b], *incoming[b],
        )
        incoming[b ^ low_bit(b)].append(exchange(block, "dom", low_bit(b)))
    own, received = blocks[0], incoming[0]
    class_sums, class_weights = call(
        functools.partial(final_kernel, width),
        [shape((classes, width), f32), shape((1, classes), f32)],
        [],
        doms * classes * padded,
        4 * doms * classes * padded,
        own, *received,
        pinned=False,
    )
    return class_sums, class_weights.reshape(classes)


def solution(mesh):
    placed = (
        P(("groups", "dom", "cls"), None),
        P(("groups", "cls"), None),
        P(("groups", "dom", "cls"), None),
        P(("groups", "dom", "cls")),
        P(("groups", "dom", "cls")),
        P("groups"),
    )
    return jax.shard_map(
        body,
        mesh=mesh,
        in_specs=placed,
        out_specs=(P(("groups", "cls"), "dom"), P(("groups", "cls"))),
        check_vma=False,
    )
```

```python
import functools
import math

import jax
import jax.numpy as jnp
import numpy as np
from jax import lax
from jax.experimental import pallas as pl
from jax.experimental.pallas import tpu as pltpu
from jax.sharding import PartitionSpec as P

CYCLES = 18
ANG = 64
IMG = 64
ANG_STEP = 1
ROTS = 8
SHIFT_R = 5
SHIFTW = 11
HALF = CYCLES * ANG
COLS = 2 * HALF
LANES = 128
SUB = 8
META = LANES
ROT_PRIOR = 0.5
VMEM_LIMIT = 20 * 1024 * 1024


def column_layout(doms):
    width = COLS // doms
    main = width - ANG
    half = doms // 2
    if width % ANG or main <= 0 or main % LANES or half * ANG % LANES:
        step = 3 * LANES
        segments = [(start, HALF + start, step) for start in range(0, HALF, step)]
        return list(range(COLS // ANG)), segments, 0
    per = width // ANG
    groups = [per * dom + group for dom in range(doms) for group in range(per - 1)]
    groups += [per * dom + per - 1 for dom in range(doms)]
    segments = [(dom * main, (half + dom) * main, main) for dom in range(half)]
    segments.append((doms * main, doms * main + half * ANG, half * ANG))
    return groups, segments, main


def tile_of(groups, tile, read):
    low, high = groups[2 * tile], groups[2 * tile + 1]
    if low % 2 == 0 and high == low + 1:
        return read(low // 2)
    first, second = read(low // 2), read(high // 2)
    first = pltpu.roll(first, ANG, 1) if low % 2 else first
    second = second if high % 2 else pltpu.roll(second, ANG, 1)
    return jnp.where(lane_index(first.shape) < ANG, first, second)


def phase_rows(groups):
    angles = np.arange(ANG) * (2.0 * math.pi / ANG)
    radius = np.arange(CYCLES) + 1.0
    fx = (radius[:, None] * np.cos(angles)[None, :]).reshape(-1)
    fy = (radius[:, None] * np.sin(angles)[None, :]).reshape(-1)
    offsets = np.arange(SHIFTW) - SHIFT_R
    unit = 2.0 * math.pi / IMG
    along_x = unit * offsets[:, None] * fx[None, :]
    along_y = unit * offsets[:, None] * fy[None, :]
    both = (along_x[SUB:, None, :] + along_y[None, SUB:, :]).reshape(-1, HALF)
    values = np.zeros((48, COLS), np.float32)
    for start, phase in ((0, along_x), (16, along_y), (32, both)):
        values[start : start + len(phase)] = np.concatenate([np.cos(phase), np.sin(phase)], axis=1)
    columns = np.concatenate([np.arange(ANG) + ANG * group for group in groups])
    return values[:, columns]


def build_table(segments, rows_ref, table_ref):
    for real_start, imag_start, width in segments:
        real = slice(real_start, real_start + width)
        imag = slice(imag_start, imag_start + width)

        def product(block, row):
            c, s = rows_ref[block : block + SUB, real], rows_ref[block : block + SUB, imag]
            d, t = rows_ref[row : row + 1, real], rows_ref[row : row + 1, imag]
            return c * d - s * t, s * d + c * t

        blocks = [product(0, 16 + y) for y in range(SHIFTW)]
        blocks += [product(16, x) for x in range(SUB, SHIFTW)]
        blocks += [
            (rows_ref[row : row + SUB, real], rows_ref[row : row + SUB, imag])
            for row in (32, 32 + SUB)
        ]
        for pair in range(0, len(blocks), 2):
            for part, columns in ((0, real), (1, imag)):
                value = jnp.concatenate([blocks[pair][part], blocks[pair + 1][part]], axis=0)
                high = value.astype(jnp.bfloat16)
                low = (value - high.astype(jnp.float32)).astype(jnp.bfloat16)
                row = pair * SUB
                table_ref[row : row + 2 * SUB, columns] = high
                table_ref[LANES + row : LANES + row + 2 * SUB, columns] = low


def table_row(index):
    y = jnp.floor((index + 0.5) * (1.0 / SHIFTW))
    x = index - SHIFTW * y
    near = SUB * y + x
    side = SUB * (SHIFTW + x - SUB) + y
    corner = SUB * (2 * SHIFTW - SUB) + (SHIFTW - SUB) * (x - SUB) + (y - SUB)
    return jnp.where(x < SUB, near, jnp.where(y < SUB, side, corner))


def exchange(array, axis, distance):
    return lax.ppermute(array, axis, [(i, i ^ distance) for i in range(lax.axis_size(axis))])


def lane_index(shape):
    return lax.broadcasted_iota(jnp.int32, shape, len(shape) - 1)


def rotate_classes(groups, class_ref, rotated_ref, norm_ref):
    classes = class_ref.shape[0]
    total = jnp.zeros((classes, LANES), jnp.float32)
    lane = lane_index((classes, LANES)) % ANG
    for tile in range(COLS // LANES):
        columns = slice(tile * LANES, (tile + 1) * LANES)
        value = tile_of(
            groups, tile, lambda k: class_ref[:, k * LANES : (k + 1) * LANES]
        )
        wide = value.astype(jnp.float32)
        total = total + wide * wide
        other = pltpu.roll(value, ANG, 1)
        for rotation in range(ROTS):
            offset = ANG_STEP * rotation % ANG
            turned = value
            if offset:
                turned = pltpu.roll(jnp.where(lane < ANG - offset, value, other), offset, 1)
            rotated_ref[rotation * classes : (rotation + 1) * classes, columns] = turned
    norm_ref[...] = jnp.broadcast_to(jnp.sum(total, axis=1, keepdims=True), (classes, LANES))


def to_lanes(column, width):
    n = column.shape[0]
    row = lax.broadcasted_iota(jnp.int32, (n, width), 0)
    return jnp.sum(
        jnp.where(lane_index((n, width)) % n == row, column, 0.0), axis=0, keepdims=True
    )


def fold_lanes(row, period, combine):
    result = row[:, :LANES]
    for part in range(1, row.shape[1] // LANES):
        result = combine(result, row[:, part * LANES : (part + 1) * LANES])
    step = LANES // 2
    while step >= period:
        result = combine(result, pltpu.roll(result, step, 1))
        step //= 2
    return result


def to_column(row):
    n = row.shape[1]
    diagonal = lax.broadcasted_iota(jnp.int32, (n, n), 0) == lane_index((n, n))
    return jnp.sum(jnp.where(diagonal, row, 0.0), axis=1, keepdims=True)


def pack_kernel(
    groups, particle_hbm, index_hbm, prior_hbm, group_hbm, class_hbm, scale_hbm, rows_hbm,
    packed_ref, class_ref, scale_ref, rows_ref, particle_ref, index_ref, prior_ref, group_ref, sems,
):
    particles, candidates = index_ref.shape
    copies = [
        pltpu.make_async_copy(source, target, sems.at[i])
        for i, (source, target) in enumerate(
            [
                (index_hbm, index_ref),
                (prior_hbm, prior_ref),
                (group_hbm, group_ref),
                (particle_hbm, particle_ref),
                (class_hbm, class_ref),
                (scale_hbm, scale_ref),
                (rows_hbm, rows_ref),
            ]
        )
    ]
    for copy in copies:
        copy.start()
    for copy in copies[:3]:
        copy.wait()
    lane = lane_index((particles, META))
    index = jnp.concatenate(
        [table_row(index_ref[...].astype(jnp.float32)), jnp.zeros((particles, META - candidates), jnp.float32)],
        axis=1,
    )
    prior = to_column(prior_ref[...].astype(jnp.float32))
    group = to_column(group_ref[...].astype(jnp.float32))
    meta = jnp.where(lane == candidates, prior, jnp.where(lane == candidates + 1, group, index))
    packed_ref[:, COLS:] = meta.astype(jnp.bfloat16)
    copies[3].wait()
    for tile in range(COLS // LANES):
        packed_ref[:, tile * LANES : (tile + 1) * LANES] = tile_of(
            groups, tile, lambda k: particle_ref[:, k * LANES : (k + 1) * LANES]
        )
    for copy in copies[4:]:
        copy.wait()


def match_block(segments, block_ref, table_ref, scale_ref, rotated_ref, shifted_ref):
    particles = block_ref.shape[0]
    candidates = shifted_ref.shape[0] // particles
    meta = block_ref[:, COLS : COLS + META].astype(jnp.float32)
    index = meta[:, :candidates].astype(jnp.int32)
    lane = lane_index((particles, LANES))
    hot = jnp.concatenate(
        [
            jnp.where(index[:, t : t + 1] == lane, 1.0, 0.0).astype(jnp.bfloat16)
            for t in range(candidates)
        ],
        axis=0,
    )
    hot = jnp.concatenate([hot, hot], axis=1)
    groups = scale_ref.shape[1]
    group = meta[:, candidates + 1 : candidates + 2].astype(jnp.int32)
    scale_column = jnp.sum(
        jnp.where(group == lane_index((particles, groups)), scale_ref[...], 0.0),
        axis=1,
        keepdims=True,
    )
    scale = to_lanes(scale_column, LANES)
    prior = to_lanes(meta[:, candidates : candidates + 1], LANES)
    for real_start, imag_start, width in segments:
        real_columns = slice(real_start, real_start + width)
        imag_columns = slice(imag_start, imag_start + width)
        cosine = jnp.dot(hot, table_ref[:, real_columns], preferred_element_type=jnp.float32)
        sine = jnp.dot(hot, table_ref[:, imag_columns], preferred_element_type=jnp.float32)
        real = block_ref[:, real_columns].astype(jnp.float32)
        imag = block_ref[:, imag_columns].astype(jnp.float32)
        for t in range(candidates):
            part = slice(t * particles, (t + 1) * particles)
            c, s = cosine[part], sine[part]
            shifted_ref[part, real_columns] = (real * c - imag * s).astype(jnp.bfloat16)
            shifted_ref[part, imag_columns] = (real * s + imag * c).astype(jnp.bfloat16)
    product = lax.dot_general(
        rotated_ref[...],
        shifted_ref[...],
        (((1,), (1,)), ((), ())),
        preferred_element_type=jnp.float32,
    )
    return product, scale, prior


def soften_block(product, scale, prior, norm_ref, particles, rows, out):
    repeat = rows // LANES
    norm = jnp.concatenate([norm_ref[...]] * repeat, axis=1)
    scale = jnp.concatenate([scale] * repeat, axis=1)
    prior = jnp.concatenate([prior] * repeat, axis=1)
    half_square = 0.5 * scale * scale
    scores = []
    highest = None
    for rotation in range(ROTS):
        distance = jnp.abs(rotation - prior)
        score = (
            scale * product(rotation)
            - half_square * norm
            - ROT_PRIOR * (distance * distance)
        )
        scores.append(score)
        peak = jnp.max(score, axis=0, keepdims=True)
        highest = peak if highest is None else jnp.maximum(highest, peak)
    highest = fold_lanes(highest, particles, jnp.maximum)
    wide = jnp.concatenate([highest] * repeat, axis=1)
    total = None
    for rotation in range(ROTS):
        value = jnp.exp(scores[rotation] - wide)
        out(rotation, value)
        added = jnp.sum(value, axis=0, keepdims=True)
        total = added if total is None else total + added
    total = fold_lanes(total, particles, jnp.add)
    return highest, total


def score_blocks(
    count, segments, pending, chunks, last, blocks, table_ref, scale_ref, rotated_ref, norm_ref,
    shifted_ref, exp_ref, stats_ref,
):
    classes = norm_ref.shape[0]
    rows = exp_ref.shape[1] // count
    particles = blocks[0].shape[0]

    def soften(block, product):
        part = slice(block * rows, (block + 1) * rows)

        def out(rotation, value):
            exp_ref[rotation * classes : (rotation + 1) * classes, part] = value

        scale = stats_ref[2 * count + block : 2 * count + block + 1, :]
        prior = stats_ref[3 * count + block : 3 * count + block + 1, :]
        highest, total = soften_block(product, scale, prior, norm_ref, particles, rows, out)
        stats_ref[2 * block : 2 * block + 1, :] = highest
        stats_ref[2 * block + 1 : 2 * block + 2, :] = total

    for block in pending:
        part = slice(block * rows, (block + 1) * rows)
        soften(block, lambda rotation: exp_ref[rotation * classes : (rotation + 1) * classes, part])
    for block, block_ref in zip(chunks, blocks):
        part = slice(block * rows, (block + 1) * rows)
        product, scale, prior = match_block(
            segments, block_ref, table_ref, scale_ref, rotated_ref, shifted_ref.at[part, :]
        )
        stats_ref[2 * count + block : 2 * count + block + 1, :] = scale
        stats_ref[3 * count + block : 3 * count + block + 1, :] = prior
        if block != chunks[-1] or last:
            soften(block, lambda rotation: product[rotation * classes : (rotation + 1) * classes])
        else:
            exp_ref[0 : ROTS * classes, part] = product


def first_kernel(count, groups, segments, chunks, *refs):
    blocks, refs = refs[: len(chunks)], refs[len(chunks) :]
    class_ref, rows_ref, scale_ref = refs[:3]
    shifted_ref, exp_ref, stats_ref, rotated_ref, norm_ref, table_ref = refs[3:]
    build_table(segments, rows_ref, table_ref)
    rotate_classes(groups, class_ref, rotated_ref, norm_ref)
    stats_ref[...] = jnp.zeros_like(stats_ref)
    score_blocks(
        count, segments, [], chunks, False, blocks, table_ref, scale_ref, rotated_ref, norm_ref,
        shifted_ref, exp_ref, stats_ref,
    )


def rest_kernel(count, segments, pending, chunks, last, *refs):
    blocks, refs = refs[: len(chunks)], refs[len(chunks) :]
    table_ref, scale_ref, rotated_ref, norm_ref, before_ref = refs[:5]
    shifted_ref, exp_ref, stats_ref = refs[7:]
    stats_ref[...] = before_ref[...]
    score_blocks(
        count, segments, pending, chunks, last, blocks, table_ref, scale_ref, rotated_ref, norm_ref,
        shifted_ref, exp_ref, stats_ref,
    )


def merged(mine, other, block, distance):
    twin = block ^ distance
    high, other_high = mine[2 * block : 2 * block + 1, :], other[2 * twin : 2 * twin + 1, :]
    top = jnp.maximum(high, other_high)
    total = mine[2 * block + 1 : 2 * block + 2, :] * jnp.exp(high - top)
    return top, total + other[2 * twin + 1 : 2 * twin + 2, :] * jnp.exp(other_high - top)


def merge_kernel(count, distance, mine, other, out_ref):
    out_ref[...] = jnp.zeros_like(out_ref)
    for block in range(count):
        top, total = merged(mine, other, block, distance)
        out_ref[2 * block : 2 * block + 1, :] = top
        out_ref[2 * block + 1 : 2 * block + 2, :] = total


def weigh(count, stats_ref, mine, other, exp_ref, weight_ref):
    rows = exp_ref.shape[1] // count
    repeat = rows // LANES
    classes = weight_ref.shape[0] // ROTS
    mass = jnp.zeros((classes, rows), jnp.float32)
    for block in range(count):
        top, total = merged(mine, other, block, count // 2)
        factor = jnp.exp(stats_ref[2 * block : 2 * block + 1, :] - top) / total
        scale = stats_ref[2 * count + block : 2 * count + block + 1, :]
        factor = jnp.concatenate([factor] * repeat, axis=1)
        scale = jnp.concatenate([scale] * repeat, axis=1)
        part = slice(block * rows, (block + 1) * rows)
        for rotation in range(ROTS):
            rotated = slice(rotation * classes, (rotation + 1) * classes)
            weight = exp_ref[rotated, part] * factor * scale
            mass = mass + weight * scale
            weight_ref[rotated, part] = weight.astype(jnp.bfloat16)
    return jnp.broadcast_to(jnp.sum(mass, axis=1, keepdims=True), (classes, LANES))


def window_sums(weight_ref, shifted_ref, start, wide):
    classes = weight_ref.shape[0] // ROTS
    product = jnp.dot(
        weight_ref[...], shifted_ref[:, pl.ds(start, wide)], preferred_element_type=jnp.float32
    )
    lane = lane_index((classes, LANES)) % ANG
    tiles = []
    for part in range(0, wide, LANES):
        inside = product[:classes, part : part + LANES]
        wrapped = None
        for rotation in range(1, ROTS):
            offset = ANG_STEP * rotation % ANG
            turned = pltpu.roll(
                product[rotation * classes : (rotation + 1) * classes, part : part + LANES],
                LANES - offset,
                1,
            )
            within = lane < ANG - offset
            inside = inside + jnp.where(within, turned, 0.0)
            over = jnp.where(within, 0.0, turned)
            wrapped = over if wrapped is None else wrapped + over
        tiles.append(inside + pltpu.roll(wrapped, ANG, 1))
    return tiles


def block_sums(doms, width, main, distance, weight_ref, shifted_ref, tails_ref):
    classes = weight_ref.shape[0] // ROTS
    padded = -(-(width + 3) // LANES) * LANES
    place = lax.axis_index("dom") ^ distance
    first = place * (main or width)
    shifts = [0] if main else sorted({width * dom % LANES for dom in range(doms)})
    span = main or -(-(shifts[-1] + width) // LANES) * LANES
    base = first // LANES * LANES
    tiles = []
    for start in range(0, span, 2 * LANES):
        tiles += window_sums(
            weight_ref,
            shifted_ref,
            pl.multiple_of(base + start, LANES),
            min(2 * LANES, span - start),
        )
    if main:
        tail = None
        for dom in range(doms):
            part = dom * ANG // LANES * LANES
            piece = tails_ref[:, part : part + LANES]
            piece = pltpu.roll(piece, ANG, 1) if dom % 2 else piece
            tail = piece if tail is None else jnp.where(place == dom, piece, tail)
        tiles.append(tail)
    total = jnp.concatenate(tiles, axis=1)
    aligned = total
    for shift in shifts:
        if shift:
            aligned = jnp.where(first - base == shift, pltpu.roll(total, span - shift, 1), aligned)
    return pad_columns(aligned, padded)


def store_block(width, value, mass, out_ref):
    high = mass.astype(jnp.bfloat16).astype(jnp.float32)
    middle = (mass - high).astype(jnp.bfloat16).astype(jnp.float32)
    low = (mass - high - middle).astype(jnp.bfloat16).astype(jnp.float32)
    lane = lane_index(value.shape)
    tail = jnp.where(
        lane == width, high, jnp.where(lane == width + 1, middle, jnp.where(lane == width + 2, low, 0.0))
    )
    value = jnp.where(lane < width, value, tail)
    out_ref[...] = value[:, : out_ref.shape[1]].astype(out_ref.dtype)


def pad_columns(value, padded):
    if value.shape[1] < padded:
        added = jnp.zeros((value.shape[0], padded - value.shape[1]), value.dtype)
        return jnp.concatenate([value, added], axis=1)
    return value[:, :padded]


def received_mass(width, ref):
    base = width // LANES * LANES
    tail = ref[:, base:].astype(jnp.float32)
    lane = base + lane_index(tail.shape)
    tail = jnp.where((lane >= width) & (lane < width + 3), tail, 0.0)
    return jnp.sum(tail, axis=1, keepdims=True)


def first_sums_kernel(count, doms, width, main, blocks, *refs):
    stats_ref, mine, other, exp_ref, shifted_ref, weight_ref, mass_ref, tails_ref = refs[:8]
    mass = weigh(count, stats_ref, mine, other, exp_ref, weight_ref)
    mass_ref[...] = mass
    tails_ref[...] = jnp.zeros_like(tails_ref)
    for start in range(0, doms * ANG if main else 0, 2 * LANES):
        tiles = window_sums(weight_ref, shifted_ref, doms * main + start, 2 * LANES)
        tails_ref[:, start : start + 2 * LANES] = jnp.concatenate(tiles, axis=1)
    for block, out_ref in zip(blocks, refs[8:]):
        value = block_sums(doms, width, main, block, weight_ref, shifted_ref, tails_ref)
        store_block(width, value, mass[:, :1], out_ref)


def rest_sums_kernel(doms, width, main, blocks, weight_ref, shifted_ref, mass_ref, tails_ref, *refs):
    for block, out_ref in zip(blocks, refs[-len(blocks) :]):
        value = block_sums(doms, width, main, block, weight_ref, shifted_ref, tails_ref)
        store_block(width, value, mass_ref[:, :1], out_ref)


def add_kernel(width, *refs):
    out_ref = refs[-1]
    padded = -(-out_ref.shape[1] // LANES) * LANES
    total, mass = None, None
    for ref in refs[:-1]:
        value = pad_columns(ref[...].astype(jnp.float32), padded)
        total = value if total is None else total + value
        tail = received_mass(width, ref)
        mass = tail if mass is None else mass + tail
    store_block(width, total, mass, out_ref)


def final_kernel(width, own_ref, *refs):
    received, sums_ref, weights_ref = refs[:-2], refs[-2], refs[-1]
    total, mass = None, None
    for ref in (own_ref, *received):
        value = ref[:, :width].astype(jnp.float32)
        total = value if total is None else total + value
        tail = received_mass(width, ref)
        mass = tail if mass is None else mass + tail
    sums_ref[...] = total
    weights_ref[...] = to_lanes(mass, total.shape[0])


def call(kernel, shapes, scratch, flops, moved, *args, smem=(), hbm=(), chip=(), pinned=True, aliases=None):
    vmem = pl.BlockSpec(memory_space=pltpu.VMEM)
    scalar = pl.BlockSpec(memory_space=pltpu.SMEM)
    place = pl.BlockSpec(memory_space=pltpu.HBM)
    args = [
        pltpu.with_memory_space_constraint(a, pltpu.HBM) if i in hbm
        else pltpu.with_memory_space_constraint(a, pltpu.VMEM) if i in chip
        else a
        for i, a in enumerate(args)
    ]
    return pl.pallas_call(
        kernel,
        out_shape=[pltpu.VMEM(s.shape, s.dtype) if pinned else s for s in shapes],
        in_specs=[scalar if i in smem else place if i in hbm else vmem for i in range(len(args))],
        out_specs=[vmem] * len(shapes),
        scratch_shapes=scratch,
        input_output_aliases=aliases or {},
        compiler_params=pltpu.CompilerParams(vmem_limit_bytes=VMEM_LIMIT),
        cost_estimate=pl.CostEstimate(flops=flops, bytes_accessed=moved, transcendentals=0),
    )(*args)


def body(particle_spectra, class_spectra, shift_index, prior_rotation, particle_group, group_scale):
    count = lax.axis_size("cls")
    doms = lax.axis_size("dom")
    particles, candidates = shift_index.shape
    classes = class_spectra.shape[0]
    rows = particles * candidates
    width = COLS // doms
    padded = -(-(width + 3) // LANES) * LANES
    growth = (padded - width - 3) // (doms - 1)
    f32, bf16 = jnp.float32, jnp.bfloat16
    shape = jax.ShapeDtypeStruct

    groups, segments, main = column_layout(doms)
    phases = jnp.asarray(phase_rows(groups))
    packed, classes_on_chip, scales, phases_on_chip = call(
        functools.partial(pack_kernel, groups),
        [
            shape((particles, COLS + META), bf16),
            shape(class_spectra.shape, bf16),
            shape((1, group_scale.shape[0]), f32),
            shape(phases.shape, f32),
        ],
        [
            pltpu.VMEM((particles, COLS), bf16),
            pltpu.VMEM((particles, candidates), jnp.int32),
            pltpu.VMEM((1, particles), jnp.int32),
            pltpu.VMEM((1, particles), jnp.int32),
            pltpu.SemaphoreType.DMA((7,)),
        ],
        particles * COLS,
        4 * particles * COLS,
        particle_spectra, shift_index, prior_rotation[None, :], particle_group[None, :],
        class_spectra, group_scale[None, :], phases,
        hbm=(0, 1, 2, 3, 4, 5, 6),
    )
    chunks = {0: packed, 1: exchange(packed, "cls", 1)}
    for b in range(2, count, 2):
        chunks[b] = exchange(packed, "cls", b)
    stat_rows = -(-4 * count // 8) * 8
    work = 2 * rows * COLS * (ROTS * classes + 256)
    stats_shape = shape((stat_rows, LANES), f32)
    shifted_shape = shape((count * rows, COLS), bf16)
    exp_shape = shape((ROTS * classes, count * rows), f32)
    near = [0, 1]
    shifted, exps, stats, rotated, norm, table = call(
        functools.partial(first_kernel, count, groups, segments, near),
        [
            shifted_shape,
            exp_shape,
            stats_shape,
            shape((ROTS * classes, COLS), bf16),
            shape((classes, LANES), f32),
            shape((2 * LANES, COLS), bf16),
        ],
        [],
        work * len(near),
        4 * len(near) * rows * COLS,
        *[chunks[b] for b in near], classes_on_chip, phases_on_chip, scales,
    )
    for b in range(2, count, 2):
        arrived, stats = lax.optimization_barrier((chunks[b], stats))
        chunks[b + 1] = exchange(arrived, "cls", 1)
    evens, odds = list(range(2, count, 2)), list(range(3, count, 2))
    for pending, far in ((near[-1:], evens), (evens[-1:], odds)):
        shifted, exps, stats = call(
            functools.partial(rest_kernel, count, segments, pending, far, far is odds),
            [shifted_shape, exp_shape, stats_shape],
            [],
            work * len(far),
            4 * len(far) * rows * COLS,
            *[chunks[b] for b in far], table, scales, rotated, norm, stats, shifted, exps,
            aliases={len(far) + 5: 0, len(far) + 6: 1},
            chip=(len(far) + 5, len(far) + 6),
        )
    mine, distance = stats, 1
    other = exchange(mine, "cls", distance)
    while 2 * distance < count:
        (mine,) = call(
            functools.partial(merge_kernel, count, distance),
            [shape((-(-2 * count // 8) * 8, LANES), f32)],
            [],
            1024,
            1024,
            mine, other,
        )
        distance *= 2
        other = exchange(mine, "cls", distance)
    low_bit = lambda b: b & -b
    early = list(range(doms - 1, 1, -2))
    order = early + [1] + sorted(range(2, doms, 2), key=lambda b: (low_bit(b), -b))
    extents = {b: width + 3 + (doms - 1 - place) * growth for place, b in enumerate(order)}
    late = [1] + list(range(2, doms, 2))
    weights, mass, tails, *made = call(
        functools.partial(first_sums_kernel, count, doms, width, main, early),
        [
            shape((ROTS * classes, count * rows), bf16),
            shape((classes, LANES), f32),
            shape((classes, doms * ANG if main else LANES), f32),
        ]
        + [shape((classes, extents[b]), bf16) for b in early],
        [],
        2 * count * rows * COLS * ROTS * classes // doms,
        4 * count * rows * width,
        stats, mine, other, exps, shifted,
        chip=(3, 4),
    )
    incoming = {b: [] for b in range(doms)}
    for b, block in zip(early, made):
        incoming[b ^ 1].append(exchange(block, "dom", 1))
    rest = call(
        functools.partial(rest_sums_kernel, doms, width, main, late),
        [
            shape((classes, extents.get(b, width + 3)), bf16 if b == 1 else f32) for b in late
        ],
        [],
        1024,
        1024,
        weights, shifted, mass, tails, *made,
        chip=(1,),
    )
    blocks = dict(zip(late, rest))
    incoming[0].append(exchange(blocks[1], "dom", 1))
    for b in order[len(early) + 1 :]:
        (block,) = call(
            functools.partial(add_kernel, width),
            [shape((classes, extents[b]), bf16)],
            [],
            1024,
            1024,
            blocks[b], *incoming[b],
        )
        incoming[b ^ low_bit(b)].append(exchange(block, "dom", low_bit(b)))
    (own,) = call(
        functools.partial(rest_sums_kernel, doms, width, main, [0]),
        [shape((classes, width + 3), f32)],
        [],
        1024,
        1024,
        weights, shifted, mass, tails, block,
        chip=(1,),
    )
    received = incoming[0]
    class_sums, class_weights = call(
        functools.partial(final_kernel, width),
        [shape((classes, width), f32), shape((1, classes), f32)],
        [],
        doms * classes * padded,
        4 * doms * classes * padded,
        own, *received,
        pinned=False,
    )
    return class_sums, class_weights.reshape(classes)


def solution(mesh):
    placed = (
        P(("groups", "dom", "cls"), None),
        P(("groups", "cls"), None),
        P(("groups", "dom", "cls"), None),
        P(("groups", "dom", "cls")),
        P(("groups", "dom", "cls")),
        P("groups"),
    )
    return jax.shard_map(
        body,
        mesh=mesh,
        in_specs=placed,
        out_specs=(P(("groups", "cls"), "dom"), P(("groups", "cls"))),
        check_vma=False,
    )
```

```python
import functools
import math

import jax
import jax.numpy as jnp
import numpy as np
from jax import lax
from jax.experimental import pallas as pl
from jax.experimental.pallas import tpu as pltpu
from jax.sharding import PartitionSpec as P

CYCLES = 18
ANG = 64
IMG = 64
ANG_STEP = 1
ROTS = 8
SHIFT_R = 5
SHIFTW = 11
HALF = CYCLES * ANG
COLS = 2 * HALF
LANES = 128
SUB = 8
META = LANES
ROT_PRIOR = 0.5
VMEM_LIMIT = 20 * 1024 * 1024


def column_layout(doms):
    width = COLS // doms
    main = width - ANG
    half = doms // 2
    if width % ANG or main <= 0 or main % LANES or half * ANG % LANES:
        step = 3 * LANES
        segments = [(start, HALF + start, step) for start in range(0, HALF, step)]
        return list(range(COLS // ANG)), segments, 0
    per = width // ANG
    groups = [per * dom + group for dom in range(doms) for group in range(per - 1)]
    groups += [per * dom + per - 1 for dom in range(doms)]
    segments = [(dom * main, (half + dom) * main, main) for dom in range(half)]
    segments.append((doms * main, doms * main + half * ANG, half * ANG))
    return groups, segments, main


def tile_of(groups, tile, read):
    low, high = groups[2 * tile], groups[2 * tile + 1]
    if low % 2 == 0 and high == low + 1:
        return read(low // 2)
    first, second = read(low // 2), read(high // 2)
    first = pltpu.roll(first, ANG, 1) if low % 2 else first
    second = second if high % 2 else pltpu.roll(second, ANG, 1)
    return jnp.where(lane_index(first.shape) < ANG, first, second)


def phase_rows(groups):
    angles = np.arange(ANG) * (2.0 * math.pi / ANG)
    radius = np.arange(CYCLES) + 1.0
    fx = (radius[:, None] * np.cos(angles)[None, :]).reshape(-1)
    fy = (radius[:, None] * np.sin(angles)[None, :]).reshape(-1)
    offsets = np.arange(SHIFTW) - SHIFT_R
    unit = 2.0 * math.pi / IMG
    along_x = unit * offsets[:, None] * fx[None, :]
    along_y = unit * offsets[:, None] * fy[None, :]
    both = (along_x[SUB:, None, :] + along_y[None, SUB:, :]).reshape(-1, HALF)
    values = np.zeros((48, COLS), np.float32)
    for start, phase in ((0, along_x), (16, along_y), (32, both)):
        values[start : start + len(phase)] = np.concatenate([np.cos(phase), np.sin(phase)], axis=1)
    columns = np.concatenate([np.arange(ANG) + ANG * group for group in groups])
    return values[:, columns]


def build_table(segments, rows_ref, table_ref):
    for real_start, imag_start, width in segments:
        real = slice(real_start, real_start + width)
        imag = slice(imag_start, imag_start + width)

        def product(block, row):
            c, s = rows_ref[block : block + SUB, real], rows_ref[block : block + SUB, imag]
            d, t = rows_ref[row : row + 1, real], rows_ref[row : row + 1, imag]
            return c * d - s * t, s * d + c * t

        blocks = [product(0, 16 + y) for y in range(SHIFTW)]
        blocks += [product(16, x) for x in range(SUB, SHIFTW)]
        blocks += [
            (rows_ref[row : row + SUB, real], rows_ref[row : row + SUB, imag])
            for row in (32, 32 + SUB)
        ]
        for pair in range(0, len(blocks), 2):
            for part, columns in ((0, real), (1, imag)):
                value = jnp.concatenate([blocks[pair][part], blocks[pair + 1][part]], axis=0)
                high = value.astype(jnp.bfloat16)
                low = (value - high.astype(jnp.float32)).astype(jnp.bfloat16)
                row = pair * SUB
                table_ref[row : row + 2 * SUB, columns] = high
                table_ref[LANES + row : LANES + row + 2 * SUB, columns] = low


def table_row(index):
    y = jnp.floor((index + 0.5) * (1.0 / SHIFTW))
    x = index - SHIFTW * y
    near = SUB * y + x
    side = SUB * (SHIFTW + x - SUB) + y
    corner = SUB * (2 * SHIFTW - SUB) + (SHIFTW - SUB) * (x - SUB) + (y - SUB)
    return jnp.where(x < SUB, near, jnp.where(y < SUB, side, corner))


def exchange(array, axis, distance):
    return lax.ppermute(array, axis, [(i, i ^ distance) for i in range(lax.axis_size(axis))])


def lane_index(shape):
    return lax.broadcasted_iota(jnp.int32, shape, len(shape) - 1)


def rotate_classes(groups, class_ref, rotated_ref, norm_ref):
    classes = class_ref.shape[0]
    total = jnp.zeros((classes, LANES), jnp.float32)
    lane = lane_index((classes, LANES)) % ANG
    for tile in range(COLS // LANES):
        columns = slice(tile * LANES, (tile + 1) * LANES)
        value = tile_of(
            groups, tile, lambda k: class_ref[:, k * LANES : (k + 1) * LANES]
        )
        wide = value.astype(jnp.float32)
        total = total + wide * wide
        other = pltpu.roll(value, ANG, 1)
        for rotation in range(ROTS):
            offset = ANG_STEP * rotation % ANG
            turned = value
            if offset:
                turned = pltpu.roll(jnp.where(lane < ANG - offset, value, other), offset, 1)
            rotated_ref[rotation * classes : (rotation + 1) * classes, columns] = turned
    norm_ref[...] = jnp.broadcast_to(jnp.sum(total, axis=1, keepdims=True), (classes, LANES))


def to_lanes(column, width):
    n = column.shape[0]
    row = lax.broadcasted_iota(jnp.int32, (n, width), 0)
    return jnp.sum(
        jnp.where(lane_index((n, width)) % n == row, column, 0.0), axis=0, keepdims=True
    )


def fold_lanes(row, period, combine):
    result = row[:, :LANES]
    for part in range(1, row.shape[1] // LANES):
        result = combine(result, row[:, part * LANES : (part + 1) * LANES])
    step = LANES // 2
    while step >= period:
        result = combine(result, pltpu.roll(result, step, 1))
        step //= 2
    return result


def to_column(row):
    n = row.shape[1]
    diagonal = lax.broadcasted_iota(jnp.int32, (n, n), 0) == lane_index((n, n))
    return jnp.sum(jnp.where(diagonal, row, 0.0), axis=1, keepdims=True)


def pack_kernel(
    groups, particle_hbm, index_hbm, prior_hbm, group_hbm, class_hbm, scale_hbm, rows_hbm,
    packed_ref, class_ref, scale_ref, rows_ref, particle_ref, index_ref, prior_ref, group_ref, sems,
):
    particles, candidates = index_ref.shape
    copies = [
        pltpu.make_async_copy(source, target, sems.at[i])
        for i, (source, target) in enumerate(
            [
                (index_hbm, index_ref),
                (prior_hbm, prior_ref),
                (group_hbm, group_ref),
                (particle_hbm, particle_ref),
                (class_hbm, class_ref),
                (scale_hbm, scale_ref),
                (rows_hbm, rows_ref),
            ]
        )
    ]
    for copy in copies:
        copy.start()
    for copy in copies[:3]:
        copy.wait()
    lane = lane_index((particles, META))
    index = jnp.concatenate(
        [table_row(index_ref[...].astype(jnp.float32)), jnp.zeros((particles, META - candidates), jnp.float32)],
        axis=1,
    )
    prior = to_column(prior_ref[...].astype(jnp.float32))
    group = to_column(group_ref[...].astype(jnp.float32))
    meta = jnp.where(lane == candidates, prior, jnp.where(lane == candidates + 1, group, index))
    packed_ref[:, COLS:] = meta.astype(jnp.bfloat16)
    copies[3].wait()
    for tile in range(COLS // LANES):
        packed_ref[:, tile * LANES : (tile + 1) * LANES] = tile_of(
            groups, tile, lambda k: particle_ref[:, k * LANES : (k + 1) * LANES]
        )
    for copy in copies[4:]:
        copy.wait()


def match_block(segments, block_ref, table_ref, scale_ref, rotated_ref, shifted_ref):
    particles = block_ref.shape[0]
    candidates = shifted_ref.shape[0] // particles
    meta = block_ref[:, COLS : COLS + META].astype(jnp.float32)
    index = meta[:, :candidates].astype(jnp.int32)
    lane = lane_index((particles, LANES))
    hot = jnp.concatenate(
        [
            jnp.where(index[:, t : t + 1] == lane, 1.0, 0.0).astype(jnp.bfloat16)
            for t in range(candidates)
        ],
        axis=0,
    )
    hot = jnp.concatenate([hot, hot], axis=1)
    groups = scale_ref.shape[1]
    group = meta[:, candidates + 1 : candidates + 2].astype(jnp.int32)
    scale_column = jnp.sum(
        jnp.where(group == lane_index((particles, groups)), scale_ref[...], 0.0),
        axis=1,
        keepdims=True,
    )
    scale = to_lanes(scale_column, LANES)
    prior = to_lanes(meta[:, candidates : candidates + 1], LANES)
    for real_start, imag_start, width in segments:
        real_columns = slice(real_start, real_start + width)
        imag_columns = slice(imag_start, imag_start + width)
        cosine = jnp.dot(hot, table_ref[:, real_columns], preferred_element_type=jnp.float32)
        sine = jnp.dot(hot, table_ref[:, imag_columns], preferred_element_type=jnp.float32)
        real = block_ref[:, real_columns].astype(jnp.float32)
        imag = block_ref[:, imag_columns].astype(jnp.float32)
        for t in range(candidates):
            part = slice(t * particles, (t + 1) * particles)
            c, s = cosine[part], sine[part]
            shifted_ref[part, real_columns] = (real * c - imag * s).astype(jnp.bfloat16)
            shifted_ref[part, imag_columns] = (real * s + imag * c).astype(jnp.bfloat16)
    product = lax.dot_general(
        rotated_ref[...],
        shifted_ref[...],
        (((1,), (1,)), ((), ())),
        preferred_element_type=jnp.float32,
    )
    return product, scale, prior


def soften_block(product, scale, prior, norm_ref, particles, rows, out):
    repeat = rows // LANES
    norm = jnp.concatenate([norm_ref[...]] * repeat, axis=1)
    scale = jnp.concatenate([scale] * repeat, axis=1)
    prior = jnp.concatenate([prior] * repeat, axis=1)
    half_square = 0.5 * scale * scale
    scores = []
    highest = None
    for rotation in range(ROTS):
        distance = jnp.abs(rotation - prior)
        score = (
            scale * product(rotation)
            - half_square * norm
            - ROT_PRIOR * (distance * distance)
        )
        scores.append(score)
        peak = jnp.max(score, axis=0, keepdims=True)
        highest = peak if highest is None else jnp.maximum(highest, peak)
    highest = fold_lanes(highest, particles, jnp.maximum)
    wide = jnp.concatenate([highest] * repeat, axis=1)
    total = None
    for rotation in range(ROTS):
        value = jnp.exp(scores[rotation] - wide)
        out(rotation, value)
        added = jnp.sum(value, axis=0, keepdims=True)
        total = added if total is None else total + added
    total = fold_lanes(total, particles, jnp.add)
    return highest, total


def score_blocks(
    count, segments, pending, chunks, last, blocks, table_ref, scale_ref, rotated_ref, norm_ref,
    shifted_ref, exp_ref, stats_ref,
):
    classes = norm_ref.shape[0]
    rows = exp_ref.shape[1] // count
    particles = blocks[0].shape[0]

    def soften(block, product):
        part = slice(block * rows, (block + 1) * rows)

        def out(rotation, value):
            exp_ref[rotation * classes : (rotation + 1) * classes, part] = value

        scale = stats_ref[2 * count + block : 2 * count + block + 1, :]
        prior = stats_ref[3 * count + block : 3 * count + block + 1, :]
        highest, total = soften_block(product, scale, prior, norm_ref, particles, rows, out)
        stats_ref[2 * block : 2 * block + 1, :] = highest
        stats_ref[2 * block + 1 : 2 * block + 2, :] = total

    for block in pending:
        part = slice(block * rows, (block + 1) * rows)
        soften(block, lambda rotation: exp_ref[rotation * classes : (rotation + 1) * classes, part])
    for block, block_ref in zip(chunks, blocks):
        part = slice(block * rows, (block + 1) * rows)
        product, scale, prior = match_block(
            segments, block_ref, table_ref, scale_ref, rotated_ref, shifted_ref.at[part, :]
        )
        stats_ref[2 * count + block : 2 * count + block + 1, :] = scale
        stats_ref[3 * count + block : 3 * count + block + 1, :] = prior
        if block != chunks[-1] or last:
            soften(block, lambda rotation: product[rotation * classes : (rotation + 1) * classes])
        else:
            exp_ref[0 : ROTS * classes, part] = product


def first_kernel(count, groups, segments, chunks, *refs):
    blocks, refs = refs[: len(chunks)], refs[len(chunks) :]
    class_ref, rows_ref, scale_ref = refs[:3]
    shifted_ref, exp_ref, stats_ref, rotated_ref, norm_ref, table_ref = refs[3:]
    build_table(segments, rows_ref, table_ref)
    rotate_classes(groups, class_ref, rotated_ref, norm_ref)
    stats_ref[...] = jnp.zeros_like(stats_ref)
    score_blocks(
        count, segments, [], chunks, False, blocks, table_ref, scale_ref, rotated_ref, norm_ref,
        shifted_ref, exp_ref, stats_ref,
    )


def rest_kernel(count, segments, pending, chunks, last, *refs):
    blocks, refs = refs[: len(chunks)], refs[len(chunks) :]
    table_ref, scale_ref, rotated_ref, norm_ref, before_ref = refs[:5]
    shifted_ref, exp_ref, stats_ref = refs[7:]
    stats_ref[...] = before_ref[...]
    score_blocks(
        count, segments, pending, chunks, last, blocks, table_ref, scale_ref, rotated_ref, norm_ref,
        shifted_ref, exp_ref, stats_ref,
    )


def merged(mine, other, block, distance):
    twin = block ^ distance
    high, other_high = mine[2 * block : 2 * block + 1, :], other[2 * twin : 2 * twin + 1, :]
    top = jnp.maximum(high, other_high)
    total = mine[2 * block + 1 : 2 * block + 2, :] * jnp.exp(high - top)
    return top, total + other[2 * twin + 1 : 2 * twin + 2, :] * jnp.exp(other_high - top)


def merge_kernel(count, distance, mine, other, out_ref):
    out_ref[...] = jnp.zeros_like(out_ref)
    for block in range(count):
        top, total = merged(mine, other, block, distance)
        out_ref[2 * block : 2 * block + 1, :] = top
        out_ref[2 * block + 1 : 2 * block + 2, :] = total


def weigh(count, stats_ref, mine, other, exp_ref, weight_ref):
    rows = exp_ref.shape[1] // count
    repeat = rows // LANES
    classes = weight_ref.shape[0] // ROTS
    mass = jnp.zeros((classes, rows), jnp.float32)
    for block in range(count):
        top, total = merged(mine, other, block, count // 2)
        factor = jnp.exp(stats_ref[2 * block : 2 * block + 1, :] - top) / total
        scale = stats_ref[2 * count + block : 2 * count + block + 1, :]
        factor = jnp.concatenate([factor] * repeat, axis=1)
        scale = jnp.concatenate([scale] * repeat, axis=1)
        part = slice(block * rows, (block + 1) * rows)
        for rotation in range(ROTS):
            rotated = slice(rotation * classes, (rotation + 1) * classes)
            weight = exp_ref[rotated, part] * factor * scale
            mass = mass + weight * scale
            weight_ref[rotated, part] = weight.astype(jnp.bfloat16)
    return jnp.broadcast_to(jnp.sum(mass, axis=1, keepdims=True), (classes, LANES))


def window_sums(weight_ref, shifted_ref, start, wide):
    classes = weight_ref.shape[0] // ROTS
    product = jnp.dot(
        weight_ref[...], shifted_ref[:, pl.ds(start, wide)], preferred_element_type=jnp.float32
    )
    lane = lane_index((classes, LANES)) % ANG
    tiles = []
    for part in range(0, wide, LANES):
        inside = product[:classes, part : part + LANES]
        wrapped = None
        for rotation in range(1, ROTS):
            offset = ANG_STEP * rotation % ANG
            turned = pltpu.roll(
                product[rotation * classes : (rotation + 1) * classes, part : part + LANES],
                LANES - offset,
                1,
            )
            within = lane < ANG - offset
            inside = inside + jnp.where(within, turned, 0.0)
            over = jnp.where(within, 0.0, turned)
            wrapped = over if wrapped is None else wrapped + over
        tiles.append(inside + pltpu.roll(wrapped, ANG, 1))
    return tiles


def block_sums(doms, width, main, distance, weight_ref, shifted_ref, tails_ref):
    classes = weight_ref.shape[0] // ROTS
    padded = -(-(width + 3) // LANES) * LANES
    place = lax.axis_index("dom") ^ distance
    first = place * (main or width)
    shifts = [0] if main else sorted({width * dom % LANES for dom in range(doms)})
    span = main or -(-(shifts[-1] + width) // LANES) * LANES
    base = first // LANES * LANES
    tiles = []
    for start in range(0, span, 2 * LANES):
        tiles += window_sums(
            weight_ref,
            shifted_ref,
            pl.multiple_of(base + start, LANES),
            min(2 * LANES, span - start),
        )
    if main:
        tail = None
        for dom in range(doms):
            part = dom * ANG // LANES * LANES
            piece = tails_ref[:, part : part + LANES]
            piece = pltpu.roll(piece, ANG, 1) if dom % 2 else piece
            tail = piece if tail is None else jnp.where(place == dom, piece, tail)
        tiles.append(tail)
    total = jnp.concatenate(tiles, axis=1)
    aligned = total
    for shift in shifts:
        if shift:
            aligned = jnp.where(first - base == shift, pltpu.roll(total, span - shift, 1), aligned)
    return pad_columns(aligned, padded)


def store_block(width, value, mass, out_ref):
    high = mass.astype(jnp.bfloat16).astype(jnp.float32)
    middle = (mass - high).astype(jnp.bfloat16).astype(jnp.float32)
    low = (mass - high - middle).astype(jnp.bfloat16).astype(jnp.float32)
    lane = lane_index(value.shape)
    tail = jnp.where(
        lane == width, high, jnp.where(lane == width + 1, middle, jnp.where(lane == width + 2, low, 0.0))
    )
    value = jnp.where(lane < width, value, tail)
    out_ref[...] = value[:, : out_ref.shape[1]].astype(out_ref.dtype)


def pad_columns(value, padded):
    if value.shape[1] < padded:
        added = jnp.zeros((value.shape[0], padded - value.shape[1]), value.dtype)
        return jnp.concatenate([value, added], axis=1)
    return value[:, :padded]


def received_mass(width, ref):
    base = width // LANES * LANES
    tail = ref[:, base:].astype(jnp.float32)
    lane = base + lane_index(tail.shape)
    tail = jnp.where((lane >= width) & (lane < width + 3), tail, 0.0)
    return jnp.sum(tail, axis=1, keepdims=True)


def first_sums_kernel(count, doms, width, main, blocks, *refs):
    stats_ref, mine, other, exp_ref, shifted_ref, weight_ref, mass_ref, tails_ref = refs[:8]
    mass = weigh(count, stats_ref, mine, other, exp_ref, weight_ref)
    mass_ref[...] = mass
    tails_ref[...] = jnp.zeros_like(tails_ref)
    for start in range(0, doms * ANG if main else 0, 2 * LANES):
        tiles = window_sums(weight_ref, shifted_ref, doms * main + start, 2 * LANES)
        tails_ref[:, start : start + 2 * LANES] = jnp.concatenate(tiles, axis=1)
    for block, out_ref in zip(blocks, refs[8:]):
        value = block_sums(doms, width, main, block, weight_ref, shifted_ref, tails_ref)
        store_block(width, value, mass[:, :1], out_ref)


def rest_sums_kernel(doms, width, main, blocks, weight_ref, shifted_ref, mass_ref, tails_ref, *refs):
    for block, out_ref in zip(blocks, refs[-len(blocks) :]):
        value = block_sums(doms, width, main, block, weight_ref, shifted_ref, tails_ref)
        store_block(width, value, mass_ref[:, :1], out_ref)


def add_kernel(width, *refs):
    out_ref = refs[-1]
    padded = -(-out_ref.shape[1] // LANES) * LANES
    total, mass = None, None
    for ref in refs[:-1]:
        value = pad_columns(ref[...].astype(jnp.float32), padded)
        total = value if total is None else total + value
        tail = received_mass(width, ref)
        mass = tail if mass is None else mass + tail
    store_block(width, total, mass, out_ref)


def final_kernel(width, own_ref, *refs):
    received, sums_ref, weights_ref = refs[:-2], refs[-2], refs[-1]
    total, mass = None, None
    for ref in (own_ref, *received):
        value = ref[:, :width].astype(jnp.float32)
        total = value if total is None else total + value
        tail = received_mass(width, ref)
        mass = tail if mass is None else mass + tail
    sums_ref[...] = total
    weights_ref[...] = to_lanes(mass, total.shape[0])


def call(kernel, shapes, scratch, flops, moved, *args, smem=(), hbm=(), chip=(), pinned=True, aliases=None):
    vmem = pl.BlockSpec(memory_space=pltpu.VMEM)
    scalar = pl.BlockSpec(memory_space=pltpu.SMEM)
    place = pl.BlockSpec(memory_space=pltpu.HBM)
    args = [
        pltpu.with_memory_space_constraint(a, pltpu.HBM) if i in hbm
        else pltpu.with_memory_space_constraint(a, pltpu.VMEM) if i in chip
        else a
        for i, a in enumerate(args)
    ]
    return pl.pallas_call(
        kernel,
        out_shape=[pltpu.VMEM(s.shape, s.dtype) if pinned else s for s in shapes],
        in_specs=[scalar if i in smem else place if i in hbm else vmem for i in range(len(args))],
        out_specs=[vmem] * len(shapes),
        scratch_shapes=scratch,
        input_output_aliases=aliases or {},
        compiler_params=pltpu.CompilerParams(vmem_limit_bytes=VMEM_LIMIT),
        cost_estimate=pl.CostEstimate(flops=flops, bytes_accessed=moved, transcendentals=0),
    )(*args)


def body(particle_spectra, class_spectra, shift_index, prior_rotation, particle_group, group_scale):
    count = lax.axis_size("cls")
    doms = lax.axis_size("dom")
    particles, candidates = shift_index.shape
    classes = class_spectra.shape[0]
    rows = particles * candidates
    width = COLS // doms
    padded = -(-(width + 3) // LANES) * LANES
    growth = (padded - width - 3) // (doms - 1)
    f32, bf16 = jnp.float32, jnp.bfloat16
    shape = jax.ShapeDtypeStruct

    groups, segments, main = column_layout(doms)
    phases = jnp.asarray(phase_rows(groups))
    packed, classes_on_chip, scales, phases_on_chip = call(
        functools.partial(pack_kernel, groups),
        [
            shape((particles, COLS + META), bf16),
            shape(class_spectra.shape, bf16),
            shape((1, group_scale.shape[0]), f32),
            shape(phases.shape, f32),
        ],
        [
            pltpu.VMEM((particles, COLS), bf16),
            pltpu.VMEM((particles, candidates), jnp.int32),
            pltpu.VMEM((1, particles), jnp.int32),
            pltpu.VMEM((1, particles), jnp.int32),
            pltpu.SemaphoreType.DMA((7,)),
        ],
        particles * COLS,
        4 * particles * COLS,
        particle_spectra, shift_index, prior_rotation[None, :], particle_group[None, :],
        class_spectra, group_scale[None, :], phases,
        hbm=(0, 1, 2, 3, 4, 5, 6),
    )
    chunks = {0: packed, 1: exchange(packed, "cls", 1)}
    for b in range(2, count, 2):
        chunks[b] = exchange(packed, "cls", b)
    stat_rows = -(-4 * count // 8) * 8
    work = 2 * rows * COLS * (ROTS * classes + 256)
    stats_shape = shape((stat_rows, LANES), f32)
    shifted_shape = shape((count * rows, COLS), bf16)
    exp_shape = shape((ROTS * classes, count * rows), f32)
    near = [0, 1]
    shifted, exps, stats, rotated, norm, table = call(
        functools.partial(first_kernel, count, groups, segments, near),
        [
            shifted_shape,
            exp_shape,
            stats_shape,
            shape((ROTS * classes, COLS), bf16),
            shape((classes, LANES), f32),
            shape((2 * LANES, COLS), bf16),
        ],
        [],
        work * len(near),
        4 * len(near) * rows * COLS,
        *[chunks[b] for b in near], classes_on_chip, phases_on_chip, scales,
    )
    for b in range(2, count, 2):
        arrived, stats = lax.optimization_barrier((chunks[b], stats))
        chunks[b + 1] = exchange(arrived, "cls", 1)
    evens, odds = list(range(2, count, 2)), list(range(3, count, 2))
    for pending, far in ((near[-1:], evens), (evens[-1:], odds)):
        shifted, exps, stats = call(
            functools.partial(rest_kernel, count, segments, pending, far, far is odds),
            [shifted_shape, exp_shape, stats_shape],
            [],
            work * len(far),
            4 * len(far) * rows * COLS,
            *[chunks[b] for b in far], table, scales, rotated, norm, stats, shifted, exps,
            aliases={len(far) + 5: 0, len(far) + 6: 1},
            chip=(len(far) + 5, len(far) + 6),
        )
    mine, distance = stats, 1
    other = exchange(mine, "cls", distance)
    while 2 * distance < count:
        (mine,) = call(
            functools.partial(merge_kernel, count, distance),
            [shape((-(-2 * count // 8) * 8, LANES), f32)],
            [],
            1024,
            1024,
            mine, other,
        )
        distance *= 2
        other = exchange(mine, "cls", distance)
    low_bit = lambda b: b & -b
    early = list(range(doms - 1, 1, -2))
    order = early + [1] + sorted(range(2, doms, 2), key=lambda b: (low_bit(b), -b))
    extents = {b: width + 3 + (doms - 1 - place) * growth for place, b in enumerate(order)}
    late = [1] + list(range(2, doms, 2))
    weights, mass, tails, *made = call(
        functools.partial(first_sums_kernel, count, doms, width, main, early),
        [
            shape((ROTS * classes, count * rows), bf16),
            shape((classes, LANES), f32),
            shape((classes, doms * ANG if main else LANES), f32),
        ]
        + [shape((classes, extents[b]), bf16) for b in early],
        [],
        2 * count * rows * COLS * ROTS * classes // doms,
        4 * count * rows * width,
        stats, mine, other, exps, shifted,
        chip=(3, 4),
    )
    incoming = {b: [] for b in range(doms)}
    for b, block in zip(early, made):
        incoming[b ^ 1].append(exchange(block, "dom", 1))
    rest = call(
        functools.partial(rest_sums_kernel, doms, width, main, late),
        [
            shape((classes, extents.get(b, width + 3)), bf16 if b == 1 else f32) for b in late
        ],
        [],
        1024,
        1024,
        weights, shifted, mass, tails, *made,
        chip=(1,),
    )
    blocks = dict(zip(late, rest))
    forwarded = [array for b in range(doms) for array in incoming[b]]
    direct, *_ = lax.optimization_barrier((blocks[1], *forwarded))
    incoming[0].append(exchange(direct, "dom", 1))
    for b in order[len(early) + 1 :]:
        (block,) = call(
            functools.partial(add_kernel, width),
            [shape((classes, extents[b]), bf16)],
            [],
            1024,
            1024,
            blocks[b], *incoming[b],
        )
        incoming[b ^ low_bit(b)].append(exchange(block, "dom", low_bit(b)))
    (own,) = call(
        functools.partial(rest_sums_kernel, doms, width, main, [0]),
        [shape((classes, width + 3), f32)],
        [],
        1024,
        1024,
        weights, shifted, mass, tails, block,
        chip=(1,),
    )
    received = incoming[0]
    class_sums, class_weights = call(
        functools.partial(final_kernel, width),
        [shape((classes, width), f32), shape((1, classes), f32)],
        [],
        doms * classes * padded,
        4 * doms * classes * padded,
        own, *received,
        pinned=False,
    )
    return class_sums, class_weights.reshape(classes)


def solution(mesh):
    placed = (
        P(("groups", "dom", "cls"), None),
        P(("groups", "cls"), None),
        P(("groups", "dom", "cls"), None),
        P(("groups", "dom", "cls")),
        P(("groups", "dom", "cls")),
        P("groups"),
    )
    return jax.shard_map(
        body,
        mesh=mesh,
        in_specs=placed,
        out_specs=(P(("groups", "cls"), "dom"), P(("groups", "cls"))),
        check_vma=False,
    )
```

```python
import functools
import math

import jax
import jax.numpy as jnp
import numpy as np
from jax import lax
from jax.experimental import pallas as pl
from jax.experimental.pallas import tpu as pltpu
from jax.sharding import PartitionSpec as P

CYCLES = 18
ANG = 64
IMG = 64
ANG_STEP = 1
ROTS = 8
SHIFT_R = 5
SHIFTW = 11
HALF = CYCLES * ANG
COLS = 2 * HALF
LANES = 128
SUB = 8
META = LANES
ROT_PRIOR = 0.5
VMEM_LIMIT = 20 * 1024 * 1024


def column_layout(doms):
    width = COLS // doms
    main = width - ANG
    half = doms // 2
    if width % ANG or main <= 0 or main % LANES or half * ANG % LANES:
        step = 3 * LANES
        segments = [(start, HALF + start, step) for start in range(0, HALF, step)]
        return list(range(COLS // ANG)), segments, 0
    per = width // ANG
    groups = [per * dom + group for dom in range(doms) for group in range(per - 1)]
    groups += [per * dom + per - 1 for dom in range(doms)]
    segments = [(dom * main, (half + dom) * main, main) for dom in range(half)]
    segments.append((doms * main, doms * main + half * ANG, half * ANG))
    return groups, segments, main


def tile_of(groups, tile, read):
    low, high = groups[2 * tile], groups[2 * tile + 1]
    if low % 2 == 0 and high == low + 1:
        return read(low // 2)
    first, second = read(low // 2), read(high // 2)
    first = pltpu.roll(first, ANG, 1) if low % 2 else first
    second = second if high % 2 else pltpu.roll(second, ANG, 1)
    return jnp.where(lane_index(first.shape) < ANG, first, second)


def phase_rows(groups):
    angles = np.arange(ANG) * (2.0 * math.pi / ANG)
    radius = np.arange(CYCLES) + 1.0
    fx = (radius[:, None] * np.cos(angles)[None, :]).reshape(-1)
    fy = (radius[:, None] * np.sin(angles)[None, :]).reshape(-1)
    offsets = np.arange(SHIFTW) - SHIFT_R
    unit = 2.0 * math.pi / IMG
    along_x = unit * offsets[:, None] * fx[None, :]
    along_y = unit * offsets[:, None] * fy[None, :]
    both = (along_x[SUB:, None, :] + along_y[None, SUB:, :]).reshape(-1, HALF)
    values = np.zeros((48, COLS), np.float32)
    for start, phase in ((0, along_x), (16, along_y), (32, both)):
        values[start : start + len(phase)] = np.concatenate([np.cos(phase), np.sin(phase)], axis=1)
    columns = np.concatenate([np.arange(ANG) + ANG * group for group in groups])
    return values[:, columns]


def build_table(segments, rows_ref, table_ref):
    for real_start, imag_start, width in segments:
        real = slice(real_start, real_start + width)
        imag = slice(imag_start, imag_start + width)

        def product(block, row):
            c, s = rows_ref[block : block + SUB, real], rows_ref[block : block + SUB, imag]
            d, t = rows_ref[row : row + 1, real], rows_ref[row : row + 1, imag]
            return c * d - s * t, s * d + c * t

        blocks = [product(0, 16 + y) for y in range(SHIFTW)]
        blocks += [product(16, x) for x in range(SUB, SHIFTW)]
        blocks += [
            (rows_ref[row : row + SUB, real], rows_ref[row : row + SUB, imag])
            for row in (32, 32 + SUB)
        ]
        for pair in range(0, len(blocks), 2):
            for part, columns in ((0, real), (1, imag)):
                value = jnp.concatenate([blocks[pair][part], blocks[pair + 1][part]], axis=0)
                high = value.astype(jnp.bfloat16)
                low = (value - high.astype(jnp.float32)).astype(jnp.bfloat16)
                row = pair * SUB
                table_ref[row : row + 2 * SUB, columns] = high
                table_ref[LANES + row : LANES + row + 2 * SUB, columns] = low


def table_row(index):
    y = jnp.floor((index + 0.5) * (1.0 / SHIFTW))
    x = index - SHIFTW * y
    near = SUB * y + x
    side = SUB * (SHIFTW + x - SUB) + y
    corner = SUB * (2 * SHIFTW - SUB) + (SHIFTW - SUB) * (x - SUB) + (y - SUB)
    return jnp.where(x < SUB, near, jnp.where(y < SUB, side, corner))


def exchange(array, axis, distance):
    return lax.ppermute(array, axis, [(i, i ^ distance) for i in range(lax.axis_size(axis))])


def lane_index(shape):
    return lax.broadcasted_iota(jnp.int32, shape, len(shape) - 1)


def rotate_classes(groups, class_ref, rotated_ref, norm_ref):
    classes = class_ref.shape[0]
    total = jnp.zeros((classes, LANES), jnp.float32)
    lane = lane_index((classes, LANES)) % ANG
    for tile in range(COLS // LANES):
        columns = slice(tile * LANES, (tile + 1) * LANES)
        value = tile_of(
            groups, tile, lambda k: class_ref[:, k * LANES : (k + 1) * LANES]
        )
        wide = value.astype(jnp.float32)
        total = total + wide * wide
        other = pltpu.roll(value, ANG, 1)
        for rotation in range(ROTS):
            offset = ANG_STEP * rotation % ANG
            turned = value
            if offset:
                turned = pltpu.roll(jnp.where(lane < ANG - offset, value, other), offset, 1)
            rotated_ref[rotation * classes : (rotation + 1) * classes, columns] = turned
    norm_ref[...] = jnp.broadcast_to(jnp.sum(total, axis=1, keepdims=True), (classes, LANES))


def to_lanes(column, width):
    n = column.shape[0]
    row = lax.broadcasted_iota(jnp.int32, (n, width), 0)
    return jnp.sum(
        jnp.where(lane_index((n, width)) % n == row, column, 0.0), axis=0, keepdims=True
    )


def fold_lanes(row, period, combine):
    result = row[:, :LANES]
    for part in range(1, row.shape[1] // LANES):
        result = combine(result, row[:, part * LANES : (part + 1) * LANES])
    step = LANES // 2
    while step >= period:
        result = combine(result, pltpu.roll(result, step, 1))
        step //= 2
    return result


def to_column(row):
    n = row.shape[1]
    diagonal = lax.broadcasted_iota(jnp.int32, (n, n), 0) == lane_index((n, n))
    return jnp.sum(jnp.where(diagonal, row, 0.0), axis=1, keepdims=True)


def pack_kernel(
    groups, particle_hbm, index_hbm, prior_hbm, group_hbm, class_hbm, scale_hbm, rows_hbm,
    packed_ref, class_ref, scale_ref, rows_ref, particle_ref, index_ref, prior_ref, group_ref, sems,
):
    particles, candidates = index_ref.shape
    copies = [
        pltpu.make_async_copy(source, target, sems.at[i])
        for i, (source, target) in enumerate(
            [
                (index_hbm, index_ref),
                (prior_hbm, prior_ref),
                (group_hbm, group_ref),
                (particle_hbm, particle_ref),
                (class_hbm, class_ref),
                (scale_hbm, scale_ref),
                (rows_hbm, rows_ref),
            ]
        )
    ]
    for copy in copies:
        copy.start()
    for copy in copies[:3]:
        copy.wait()
    lane = lane_index((particles, META))
    index = jnp.concatenate(
        [table_row(index_ref[...].astype(jnp.float32)), jnp.zeros((particles, META - candidates), jnp.float32)],
        axis=1,
    )
    prior = to_column(prior_ref[...].astype(jnp.float32))
    group = to_column(group_ref[...].astype(jnp.float32))
    meta = jnp.where(lane == candidates, prior, jnp.where(lane == candidates + 1, group, index))
    packed_ref[:, COLS:] = meta.astype(jnp.bfloat16)
    copies[3].wait()
    for tile in range(COLS // LANES):
        packed_ref[:, tile * LANES : (tile + 1) * LANES] = tile_of(
            groups, tile, lambda k: particle_ref[:, k * LANES : (k + 1) * LANES]
        )
    for copy in copies[4:]:
        copy.wait()


def match_block(segments, block_ref, table_ref, scale_ref, rotated_ref, shifted_ref):
    particles = block_ref.shape[0]
    candidates = shifted_ref.shape[0] // particles
    meta = block_ref[:, COLS : COLS + META].astype(jnp.float32)
    index = meta[:, :candidates].astype(jnp.int32)
    lane = lane_index((particles, LANES))
    hot = jnp.concatenate(
        [
            jnp.where(index[:, t : t + 1] == lane, 1.0, 0.0).astype(jnp.bfloat16)
            for t in range(candidates)
        ],
        axis=0,
    )
    hot = jnp.concatenate([hot, hot], axis=1)
    groups = scale_ref.shape[1]
    group = meta[:, candidates + 1 : candidates + 2].astype(jnp.int32)
    scale_column = jnp.sum(
        jnp.where(group == lane_index((particles, groups)), scale_ref[...], 0.0),
        axis=1,
        keepdims=True,
    )
    scale = to_lanes(scale_column, LANES)
    prior = to_lanes(meta[:, candidates : candidates + 1], LANES)
    for real_start, imag_start, width in segments:
        real_columns = slice(real_start, real_start + width)
        imag_columns = slice(imag_start, imag_start + width)
        cosine = jnp.dot(hot, table_ref[:, real_columns], preferred_element_type=jnp.float32)
        sine = jnp.dot(hot, table_ref[:, imag_columns], preferred_element_type=jnp.float32)
        real = block_ref[:, real_columns].astype(jnp.float32)
        imag = block_ref[:, imag_columns].astype(jnp.float32)
        for t in range(candidates):
            part = slice(t * particles, (t + 1) * particles)
            c, s = cosine[part], sine[part]
            shifted_ref[part, real_columns] = (real * c - imag * s).astype(jnp.bfloat16)
            shifted_ref[part, imag_columns] = (real * s + imag * c).astype(jnp.bfloat16)
    product = lax.dot_general(
        rotated_ref[...],
        shifted_ref[...],
        (((1,), (1,)), ((), ())),
        preferred_element_type=jnp.float32,
    )
    return product, scale, prior


def soften_block(product, scale, prior, norm_ref, particles, rows, out):
    repeat = rows // LANES
    norm = jnp.concatenate([norm_ref[...]] * repeat, axis=1)
    scale = jnp.concatenate([scale] * repeat, axis=1)
    prior = jnp.concatenate([prior] * repeat, axis=1)
    half_square = 0.5 * scale * scale
    scores = []
    highest = None
    for rotation in range(ROTS):
        distance = jnp.abs(rotation - prior)
        score = (
            scale * product(rotation)
            - half_square * norm
            - ROT_PRIOR * (distance * distance)
        )
        scores.append(score)
        peak = jnp.max(score, axis=0, keepdims=True)
        highest = peak if highest is None else jnp.maximum(highest, peak)
    highest = fold_lanes(highest, particles, jnp.maximum)
    wide = jnp.concatenate([highest] * repeat, axis=1)
    total = None
    for rotation in range(ROTS):
        value = jnp.exp(scores[rotation] - wide)
        out(rotation, value)
        added = jnp.sum(value, axis=0, keepdims=True)
        total = added if total is None else total + added
    total = fold_lanes(total, particles, jnp.add)
    return highest, total


def score_blocks(
    count, segments, pending, chunks, last, blocks, table_ref, scale_ref, rotated_ref, norm_ref,
    shifted_ref, exp_ref, stats_ref,
):
    classes = norm_ref.shape[0]
    rows = exp_ref.shape[1] // count
    particles = blocks[0].shape[0]

    def soften(block, product):
        part = slice(block * rows, (block + 1) * rows)

        def out(rotation, value):
            exp_ref[rotation * classes : (rotation + 1) * classes, part] = value

        scale = stats_ref[2 * count + block : 2 * count + block + 1, :]
        prior = stats_ref[3 * count + block : 3 * count + block + 1, :]
        highest, total = soften_block(product, scale, prior, norm_ref, particles, rows, out)
        stats_ref[2 * block : 2 * block + 1, :] = highest
        stats_ref[2 * block + 1 : 2 * block + 2, :] = total

    for block in pending:
        part = slice(block * rows, (block + 1) * rows)
        soften(block, lambda rotation: exp_ref[rotation * classes : (rotation + 1) * classes, part])
    for block, block_ref in zip(chunks, blocks):
        part = slice(block * rows, (block + 1) * rows)
        product, scale, prior = match_block(
            segments, block_ref, table_ref, scale_ref, rotated_ref, shifted_ref.at[part, :]
        )
        stats_ref[2 * count + block : 2 * count + block + 1, :] = scale
        stats_ref[3 * count + block : 3 * count + block + 1, :] = prior
        if block != chunks[-1] or last:
            soften(block, lambda rotation: product[rotation * classes : (rotation + 1) * classes])
        else:
            exp_ref[0 : ROTS * classes, part] = product


def first_kernel(count, groups, segments, chunks, *refs):
    blocks, refs = refs[: len(chunks)], refs[len(chunks) :]
    class_ref, rows_ref, scale_ref = refs[:3]
    shifted_ref, exp_ref, stats_ref, rotated_ref, norm_ref, table_ref = refs[3:]
    build_table(segments, rows_ref, table_ref)
    rotate_classes(groups, class_ref, rotated_ref, norm_ref)
    stats_ref[...] = jnp.zeros_like(stats_ref)
    score_blocks(
        count, segments, [], chunks, False, blocks, table_ref, scale_ref, rotated_ref, norm_ref,
        shifted_ref, exp_ref, stats_ref,
    )


def rest_kernel(count, segments, pending, chunks, last, *refs):
    blocks, refs = refs[: len(chunks)], refs[len(chunks) :]
    table_ref, scale_ref, rotated_ref, norm_ref, before_ref = refs[:5]
    shifted_ref, exp_ref, stats_ref = refs[7:]
    stats_ref[...] = before_ref[...]
    score_blocks(
        count, segments, pending, chunks, last, blocks, table_ref, scale_ref, rotated_ref, norm_ref,
        shifted_ref, exp_ref, stats_ref,
    )


def merged(mine, other, block, distance):
    twin = block ^ distance
    high, other_high = mine[2 * block : 2 * block + 1, :], other[2 * twin : 2 * twin + 1, :]
    top = jnp.maximum(high, other_high)
    total = mine[2 * block + 1 : 2 * block + 2, :] * jnp.exp(high - top)
    return top, total + other[2 * twin + 1 : 2 * twin + 2, :] * jnp.exp(other_high - top)


def merge_kernel(count, distance, mine, other, out_ref):
    out_ref[...] = jnp.zeros_like(out_ref)
    for block in range(count):
        top, total = merged(mine, other, block, distance)
        out_ref[2 * block : 2 * block + 1, :] = top
        out_ref[2 * block + 1 : 2 * block + 2, :] = total


def weigh(count, stats_ref, mine, other, exp_ref, weight_ref):
    rows = exp_ref.shape[1] // count
    repeat = rows // LANES
    classes = weight_ref.shape[0] // ROTS
    mass = jnp.zeros((classes, rows), jnp.float32)
    for block in range(count):
        top, total = merged(mine, other, block, count // 2)
        factor = jnp.exp(stats_ref[2 * block : 2 * block + 1, :] - top) / total
        scale = stats_ref[2 * count + block : 2 * count + block + 1, :]
        factor = jnp.concatenate([factor * scale] * repeat, axis=1)
        scale = jnp.concatenate([scale] * repeat, axis=1)
        part = slice(block * rows, (block + 1) * rows)
        turned = None
        for rotation in range(ROTS):
            rotated = slice(rotation * classes, (rotation + 1) * classes)
            weight = exp_ref[rotated, part] * factor
            turned = weight if turned is None else turned + weight
            weight_ref[rotated, part] = weight.astype(jnp.bfloat16)
        mass = mass + turned * scale
    return jnp.broadcast_to(jnp.sum(mass, axis=1, keepdims=True), (classes, LANES))


def window_sums(weight_ref, shifted_ref, start, wide):
    classes = weight_ref.shape[0] // ROTS
    product = jnp.dot(
        weight_ref[...], shifted_ref[:, pl.ds(start, wide)], preferred_element_type=jnp.float32
    )
    lane = lane_index((classes, LANES)) % ANG
    tiles = []
    for part in range(0, wide, LANES):
        inside = product[:classes, part : part + LANES]
        wrapped = None
        for rotation in range(1, ROTS):
            offset = ANG_STEP * rotation % ANG
            turned = pltpu.roll(
                product[rotation * classes : (rotation + 1) * classes, part : part + LANES],
                LANES - offset,
                1,
            )
            within = lane < ANG - offset
            inside = inside + jnp.where(within, turned, 0.0)
            over = jnp.where(within, 0.0, turned)
            wrapped = over if wrapped is None else wrapped + over
        tiles.append(inside + pltpu.roll(wrapped, ANG, 1))
    return tiles


def block_sums(doms, width, main, distance, weight_ref, shifted_ref, tails_ref):
    classes = weight_ref.shape[0] // ROTS
    padded = -(-(width + 3) // LANES) * LANES
    place = lax.axis_index("dom") ^ distance
    first = place * (main or width)
    shifts = [0] if main else sorted({width * dom % LANES for dom in range(doms)})
    span = main or -(-(shifts[-1] + width) // LANES) * LANES
    base = first // LANES * LANES
    tiles = []
    for start in range(0, span, 2 * LANES):
        tiles += window_sums(
            weight_ref,
            shifted_ref,
            pl.multiple_of(base + start, LANES),
            min(2 * LANES, span - start),
        )
    if main:
        tail = None
        for dom in range(doms):
            part = dom * ANG // LANES * LANES
            piece = tails_ref[:, part : part + LANES]
            piece = pltpu.roll(piece, ANG, 1) if dom % 2 else piece
            tail = piece if tail is None else jnp.where(place == dom, piece, tail)
        tiles.append(tail)
    total = jnp.concatenate(tiles, axis=1)
    aligned = total
    for shift in shifts:
        if shift:
            aligned = jnp.where(first - base == shift, pltpu.roll(total, span - shift, 1), aligned)
    return pad_columns(aligned, padded)


def store_block(width, value, mass, out_ref):
    high = mass.astype(jnp.bfloat16).astype(jnp.float32)
    middle = (mass - high).astype(jnp.bfloat16).astype(jnp.float32)
    low = (mass - high - middle).astype(jnp.bfloat16).astype(jnp.float32)
    lane = lane_index(value.shape)
    tail = jnp.where(
        lane == width, high, jnp.where(lane == width + 1, middle, jnp.where(lane == width + 2, low, 0.0))
    )
    value = jnp.where(lane < width, value, tail)
    out_ref[...] = value[:, : out_ref.shape[1]].astype(out_ref.dtype)


def pad_columns(value, padded):
    if value.shape[1] < padded:
        added = jnp.zeros((value.shape[0], padded - value.shape[1]), value.dtype)
        return jnp.concatenate([value, added], axis=1)
    return value[:, :padded]


def received_mass(width, ref):
    base = width // LANES * LANES
    tail = ref[:, base:].astype(jnp.float32)
    lane = base + lane_index(tail.shape)
    tail = jnp.where((lane >= width) & (lane < width + 3), tail, 0.0)
    return jnp.sum(tail, axis=1, keepdims=True)


def first_sums_kernel(count, doms, width, main, blocks, *refs):
    stats_ref, mine, other, exp_ref, shifted_ref, weight_ref, mass_ref, tails_ref = refs[:8]
    mass = weigh(count, stats_ref, mine, other, exp_ref, weight_ref)
    mass_ref[...] = mass
    tails_ref[...] = jnp.zeros_like(tails_ref)
    for start in range(0, doms * ANG if main else 0, 2 * LANES):
        tiles = window_sums(weight_ref, shifted_ref, doms * main + start, 2 * LANES)
        tails_ref[:, start : start + 2 * LANES] = jnp.concatenate(tiles, axis=1)
    for block, out_ref in zip(blocks, refs[8:]):
        value = block_sums(doms, width, main, block, weight_ref, shifted_ref, tails_ref)
        store_block(width, value, mass[:, :1], out_ref)


def rest_sums_kernel(doms, width, main, blocks, weight_ref, shifted_ref, mass_ref, tails_ref, *refs):
    for block, out_ref in zip(blocks, refs[-len(blocks) :]):
        value = block_sums(doms, width, main, block, weight_ref, shifted_ref, tails_ref)
        store_block(width, value, mass_ref[:, :1], out_ref)


def add_kernel(width, *refs):
    out_ref = refs[-1]
    padded = -(-out_ref.shape[1] // LANES) * LANES
    total, mass = None, None
    for ref in refs[:-1]:
        value = pad_columns(ref[...].astype(jnp.float32), padded)
        total = value if total is None else total + value
        tail = received_mass(width, ref)
        mass = tail if mass is None else mass + tail
    store_block(width, total, mass, out_ref)


def final_kernel(width, own_ref, *refs):
    received, sums_ref, weights_ref = refs[:-2], refs[-2], refs[-1]
    total, mass = None, None
    for ref in (own_ref, *received):
        value = ref[:, :width].astype(jnp.float32)
        total = value if total is None else total + value
        tail = received_mass(width, ref)
        mass = tail if mass is None else mass + tail
    sums_ref[...] = total
    weights_ref[...] = to_lanes(mass, total.shape[0])


def call(kernel, shapes, scratch, flops, moved, *args, smem=(), hbm=(), chip=(), pinned=True, aliases=None):
    vmem = pl.BlockSpec(memory_space=pltpu.VMEM)
    scalar = pl.BlockSpec(memory_space=pltpu.SMEM)
    place = pl.BlockSpec(memory_space=pltpu.HBM)
    args = [
        pltpu.with_memory_space_constraint(a, pltpu.HBM) if i in hbm
        else pltpu.with_memory_space_constraint(a, pltpu.VMEM) if i in chip
        else a
        for i, a in enumerate(args)
    ]
    return pl.pallas_call(
        kernel,
        out_shape=[pltpu.VMEM(s.shape, s.dtype) if pinned else s for s in shapes],
        in_specs=[scalar if i in smem else place if i in hbm else vmem for i in range(len(args))],
        out_specs=[vmem] * len(shapes),
        scratch_shapes=scratch,
        input_output_aliases=aliases or {},
        compiler_params=pltpu.CompilerParams(vmem_limit_bytes=VMEM_LIMIT),
        cost_estimate=pl.CostEstimate(flops=flops, bytes_accessed=moved, transcendentals=0),
    )(*args)


def body(particle_spectra, class_spectra, shift_index, prior_rotation, particle_group, group_scale):
    count = lax.axis_size("cls")
    doms = lax.axis_size("dom")
    particles, candidates = shift_index.shape
    classes = class_spectra.shape[0]
    rows = particles * candidates
    width = COLS // doms
    padded = -(-(width + 3) // LANES) * LANES
    growth = (padded - width - 3) // (doms - 1)
    f32, bf16 = jnp.float32, jnp.bfloat16
    shape = jax.ShapeDtypeStruct

    groups, segments, main = column_layout(doms)
    phases = jnp.asarray(phase_rows(groups))
    packed, classes_on_chip, scales, phases_on_chip = call(
        functools.partial(pack_kernel, groups),
        [
            shape((particles, COLS + META), bf16),
            shape(class_spectra.shape, bf16),
            shape((1, group_scale.shape[0]), f32),
            shape(phases.shape, f32),
        ],
        [
            pltpu.VMEM((particles, COLS), bf16),
            pltpu.VMEM((particles, candidates), jnp.int32),
            pltpu.VMEM((1, particles), jnp.int32),
            pltpu.VMEM((1, particles), jnp.int32),
            pltpu.SemaphoreType.DMA((7,)),
        ],
        particles * COLS,
        4 * particles * COLS,
        particle_spectra, shift_index, prior_rotation[None, :], particle_group[None, :],
        class_spectra, group_scale[None, :], phases,
        hbm=(0, 1, 2, 3, 4, 5, 6),
    )
    chunks = {0: packed, 1: exchange(packed, "cls", 1)}
    for b in range(2, count, 2):
        chunks[b] = exchange(packed, "cls", b)
    stat_rows = -(-4 * count // 8) * 8
    work = 2 * rows * COLS * (ROTS * classes + 256)
    stats_shape = shape((stat_rows, LANES), f32)
    shifted_shape = shape((count * rows, COLS), bf16)
    exp_shape = shape((ROTS * classes, count * rows), f32)
    near = [0, 1]
    shifted, exps, stats, rotated, norm, table = call(
        functools.partial(first_kernel, count, groups, segments, near),
        [
            shifted_shape,
            exp_shape,
            stats_shape,
            shape((ROTS * classes, COLS), bf16),
            shape((classes, LANES), f32),
            shape((2 * LANES, COLS), bf16),
        ],
        [],
        work * len(near),
        4 * len(near) * rows * COLS,
        *[chunks[b] for b in near], classes_on_chip, phases_on_chip, scales,
    )
    for b in range(2, count, 2):
        arrived, stats = lax.optimization_barrier((chunks[b], stats))
        chunks[b + 1] = exchange(arrived, "cls", 1)
    evens, odds = list(range(2, count, 2)), list(range(3, count, 2))
    for pending, far in ((near[-1:], evens), (evens[-1:], odds)):
        shifted, exps, stats = call(
            functools.partial(rest_kernel, count, segments, pending, far, far is odds),
            [shifted_shape, exp_shape, stats_shape],
            [],
            work * len(far),
            4 * len(far) * rows * COLS,
            *[chunks[b] for b in far], table, scales, rotated, norm, stats, shifted, exps,
            aliases={len(far) + 5: 0, len(far) + 6: 1},
            chip=(len(far) + 5, len(far) + 6),
        )
    mine, distance = stats, 1
    other = exchange(mine, "cls", distance)
    while 2 * distance < count:
        (mine,) = call(
            functools.partial(merge_kernel, count, distance),
            [shape((-(-2 * count // 8) * 8, LANES), f32)],
            [],
            1024,
            1024,
            mine, other,
        )
        distance *= 2
        other = exchange(mine, "cls", distance)
    low_bit = lambda b: b & -b
    early = list(range(doms - 1, 1, -2))
    order = early + [1] + sorted(range(2, doms, 2), key=lambda b: (low_bit(b), -b))
    extents = {b: width + 3 + (doms - 1 - place) * growth for place, b in enumerate(order)}
    late = [1] + list(range(2, doms, 2))
    weights, mass, tails, *made = call(
        functools.partial(first_sums_kernel, count, doms, width, main, early),
        [
            shape((ROTS * classes, count * rows), bf16),
            shape((classes, LANES), f32),
            shape((classes, doms * ANG if main else LANES), f32),
        ]
        + [shape((classes, extents[b]), bf16) for b in early],
        [],
        2 * count * rows * COLS * ROTS * classes // doms,
        4 * count * rows * width,
        stats, mine, other, exps, shifted,
        chip=(3, 4),
    )
    incoming = {b: [] for b in range(doms)}
    for b, block in zip(early, made):
        incoming[b ^ 1].append(exchange(block, "dom", 1))
    rest = call(
        functools.partial(rest_sums_kernel, doms, width, main, late),
        [
            shape((classes, extents.get(b, width + 3)), bf16 if b == 1 else f32) for b in late
        ],
        [],
        1024,
        1024,
        weights, shifted, mass, tails, *made,
        chip=(1,),
    )
    blocks = dict(zip(late, rest))
    incoming[0].append(exchange(blocks[1], "dom", 1))
    for b in order[len(early) + 1 :]:
        (block,) = call(
            functools.partial(add_kernel, width),
            [shape((classes, extents[b]), bf16)],
            [],
            1024,
            1024,
            blocks[b], *incoming[b],
        )
        incoming[b ^ low_bit(b)].append(exchange(block, "dom", low_bit(b)))
    (own,) = call(
        functools.partial(rest_sums_kernel, doms, width, main, [0]),
        [shape((classes, width + 3), f32)],
        [],
        1024,
        1024,
        weights, shifted, mass, tails, block,
        chip=(1,),
    )
    received = incoming[0]
    class_sums, class_weights = call(
        functools.partial(final_kernel, width),
        [shape((classes, width), f32), shape((1, classes), f32)],
        [],
        doms * classes * padded,
        4 * doms * classes * padded,
        own, *received,
        pinned=False,
    )
    return class_sums, class_weights.reshape(classes)


def solution(mesh):
    placed = (
        P(("groups", "dom", "cls"), None),
        P(("groups", "cls"), None),
        P(("groups", "dom", "cls"), None),
        P(("groups", "dom", "cls")),
        P(("groups", "dom", "cls")),
        P("groups"),
    )
    return jax.shard_map(
        body,
        mesh=mesh,
        in_specs=placed,
        out_specs=(P(("groups", "cls"), "dom"), P(("groups", "cls"))),
        check_vma=False,
    )
```

```python
import functools
import math

import jax
import jax.numpy as jnp
import numpy as np
from jax import lax
from jax.experimental import pallas as pl
from jax.experimental.pallas import tpu as pltpu
from jax.sharding import PartitionSpec as P

CYCLES = 18
ANG = 64
IMG = 64
ANG_STEP = 1
ROTS = 8
SHIFT_R = 5
SHIFTW = 11
HALF = CYCLES * ANG
COLS = 2 * HALF
LANES = 128
SUB = 8
META = LANES
ROT_PRIOR = 0.5
VMEM_LIMIT = 20 * 1024 * 1024


def column_layout(doms):
    width = COLS // doms
    main = width - ANG
    half = doms // 2
    if width % ANG or main <= 0 or main % LANES or half * ANG % LANES:
        step = 3 * LANES
        segments = [(start, HALF + start, step) for start in range(0, HALF, step)]
        return list(range(COLS // ANG)), segments, 0
    per = width // ANG
    groups = [per * dom + group for dom in range(doms) for group in range(per - 1)]
    groups += [per * dom + per - 1 for dom in range(doms)]
    segments = [(dom * main, (half + dom) * main, main) for dom in range(half)]
    segments.append((doms * main, doms * main + half * ANG, half * ANG))
    return groups, segments, main


def tile_of(groups, tile, read):
    low, high = groups[2 * tile], groups[2 * tile + 1]
    if low % 2 == 0 and high == low + 1:
        return read(low // 2)
    first, second = read(low // 2), read(high // 2)
    first = pltpu.roll(first, ANG, 1) if low % 2 else first
    second = second if high % 2 else pltpu.roll(second, ANG, 1)
    return jnp.where(lane_index(first.shape) < ANG, first, second)


def phase_rows(groups):
    angles = np.arange(ANG) * (2.0 * math.pi / ANG)
    radius = np.arange(CYCLES) + 1.0
    fx = (radius[:, None] * np.cos(angles)[None, :]).reshape(-1)
    fy = (radius[:, None] * np.sin(angles)[None, :]).reshape(-1)
    offsets = np.arange(SHIFTW) - SHIFT_R
    unit = 2.0 * math.pi / IMG
    along_x = unit * offsets[:, None] * fx[None, :]
    along_y = unit * offsets[:, None] * fy[None, :]
    both = (along_x[SUB:, None, :] + along_y[None, SUB:, :]).reshape(-1, HALF)
    values = np.zeros((48, COLS), np.float32)
    for start, phase in ((0, along_x), (16, along_y), (32, both)):
        values[start : start + len(phase)] = np.concatenate([np.cos(phase), np.sin(phase)], axis=1)
    columns = np.concatenate([np.arange(ANG) + ANG * group for group in groups])
    return values[:, columns]


def build_table(segments, rows_ref, table_ref):
    for real_start, imag_start, width in segments:
        real = slice(real_start, real_start + width)
        imag = slice(imag_start, imag_start + width)

        def product(block, row):
            c, s = rows_ref[block : block + SUB, real], rows_ref[block : block + SUB, imag]
            d, t = rows_ref[row : row + 1, real], rows_ref[row : row + 1, imag]
            return c * d - s * t, s * d + c * t

        blocks = [product(0, 16 + y) for y in range(SHIFTW)]
        blocks += [product(16, x) for x in range(SUB, SHIFTW)]
        blocks += [
            (rows_ref[row : row + SUB, real], rows_ref[row : row + SUB, imag])
            for row in (32, 32 + SUB)
        ]
        for pair in range(0, len(blocks), 2):
            for part, columns in ((0, real), (1, imag)):
                value = jnp.concatenate([blocks[pair][part], blocks[pair + 1][part]], axis=0)
                high = value.astype(jnp.bfloat16)
                low = (value - high.astype(jnp.float32)).astype(jnp.bfloat16)
                row = pair * SUB
                table_ref[row : row + 2 * SUB, columns] = high
                table_ref[LANES + row : LANES + row + 2 * SUB, columns] = low


def table_row(index):
    y = jnp.floor((index + 0.5) * (1.0 / SHIFTW))
    x = index - SHIFTW * y
    near = SUB * y + x
    side = SUB * (SHIFTW + x - SUB) + y
    corner = SUB * (2 * SHIFTW - SUB) + (SHIFTW - SUB) * (x - SUB) + (y - SUB)
    return jnp.where(x < SUB, near, jnp.where(y < SUB, side, corner))


def exchange(array, axis, distance):
    return lax.ppermute(array, axis, [(i, i ^ distance) for i in range(lax.axis_size(axis))])


def lane_index(shape):
    return lax.broadcasted_iota(jnp.int32, shape, len(shape) - 1)


def rotate_classes(groups, class_ref, rotated_ref, norm_ref):
    classes = class_ref.shape[0]
    total = jnp.zeros((classes, LANES), jnp.float32)
    lane = lane_index((classes, LANES)) % ANG
    for tile in range(COLS // LANES):
        columns = slice(tile * LANES, (tile + 1) * LANES)
        value = tile_of(
            groups, tile, lambda k: class_ref[:, k * LANES : (k + 1) * LANES]
        )
        wide = value.astype(jnp.float32)
        total = total + wide * wide
        other = pltpu.roll(value, ANG, 1)
        for rotation in range(ROTS):
            offset = ANG_STEP * rotation % ANG
            turned = value
            if offset:
                turned = pltpu.roll(jnp.where(lane < ANG - offset, value, other), offset, 1)
            rotated_ref[rotation * classes : (rotation + 1) * classes, columns] = turned
    norm_ref[...] = jnp.broadcast_to(jnp.sum(total, axis=1, keepdims=True), (classes, LANES))


def to_lanes(column, width):
    n = column.shape[0]
    row = lax.broadcasted_iota(jnp.int32, (n, width), 0)
    return jnp.sum(
        jnp.where(lane_index((n, width)) % n == row, column, 0.0), axis=0, keepdims=True
    )


def fold_lanes(row, period, combine):
    result = row[:, :LANES]
    for part in range(1, row.shape[1] // LANES):
        result = combine(result, row[:, part * LANES : (part + 1) * LANES])
    step = LANES // 2
    while step >= period:
        result = combine(result, pltpu.roll(result, step, 1))
        step //= 2
    return result


def to_column(row):
    n = row.shape[1]
    diagonal = lax.broadcasted_iota(jnp.int32, (n, n), 0) == lane_index((n, n))
    return jnp.sum(jnp.where(diagonal, row, 0.0), axis=1, keepdims=True)


def pack_kernel(
    groups, particle_hbm, index_hbm, prior_hbm, group_hbm, class_hbm, scale_hbm, rows_hbm,
    packed_ref, class_ref, scale_ref, rows_ref, particle_ref, index_ref, prior_ref, group_ref, sems,
):
    particles, candidates = index_ref.shape
    copies = [
        pltpu.make_async_copy(source, target, sems.at[i])
        for i, (source, target) in enumerate(
            [
                (index_hbm, index_ref),
                (prior_hbm, prior_ref),
                (group_hbm, group_ref),
                (particle_hbm, particle_ref),
                (class_hbm, class_ref),
                (scale_hbm, scale_ref),
                (rows_hbm, rows_ref),
            ]
        )
    ]
    for copy in copies:
        copy.start()
    for copy in copies[:3]:
        copy.wait()
    lane = lane_index((particles, META))
    index = jnp.concatenate(
        [table_row(index_ref[...].astype(jnp.float32)), jnp.zeros((particles, META - candidates), jnp.float32)],
        axis=1,
    )
    prior = to_column(prior_ref[...].astype(jnp.float32))
    group = to_column(group_ref[...].astype(jnp.float32))
    meta = jnp.where(lane == candidates, prior, jnp.where(lane == candidates + 1, group, index))
    packed_ref[:, COLS:] = meta.astype(jnp.bfloat16)
    copies[3].wait()
    for tile in range(COLS // LANES):
        packed_ref[:, tile * LANES : (tile + 1) * LANES] = tile_of(
            groups, tile, lambda k: particle_ref[:, k * LANES : (k + 1) * LANES]
        )
    for copy in copies[4:]:
        copy.wait()


def match_block(segments, block_ref, table_ref, scale_ref, rotated_ref, shifted_ref):
    particles = block_ref.shape[0]
    candidates = shifted_ref.shape[0] // particles
    meta = block_ref[:, COLS : COLS + META].astype(jnp.float32)
    index = meta[:, :candidates].astype(jnp.int32)
    lane = lane_index((particles, LANES))
    hot = jnp.concatenate(
        [
            jnp.where(index[:, t : t + 1] == lane, 1.0, 0.0).astype(jnp.bfloat16)
            for t in range(candidates)
        ],
        axis=0,
    )
    hot = jnp.concatenate([hot, hot], axis=1)
    groups = scale_ref.shape[1]
    group = meta[:, candidates + 1 : candidates + 2].astype(jnp.int32)
    scale_column = jnp.sum(
        jnp.where(group == lane_index((particles, groups)), scale_ref[...], 0.0),
        axis=1,
        keepdims=True,
    )
    scale = to_lanes(scale_column, LANES)
    prior = to_lanes(meta[:, candidates : candidates + 1], LANES)
    for real_start, imag_start, width in segments:
        real_columns = slice(real_start, real_start + width)
        imag_columns = slice(imag_start, imag_start + width)
        cosine = jnp.dot(hot, table_ref[:, real_columns], preferred_element_type=jnp.float32)
        sine = jnp.dot(hot, table_ref[:, imag_columns], preferred_element_type=jnp.float32)
        real = block_ref[:, real_columns].astype(jnp.float32)
        imag = block_ref[:, imag_columns].astype(jnp.float32)
        for t in range(candidates):
            part = slice(t * particles, (t + 1) * particles)
            c, s = cosine[part], sine[part]
            shifted_ref[part, real_columns] = (real * c - imag * s).astype(jnp.bfloat16)
            shifted_ref[part, imag_columns] = (real * s + imag * c).astype(jnp.bfloat16)
    product = lax.dot_general(
        rotated_ref[...],
        shifted_ref[...],
        (((1,), (1,)), ((), ())),
        preferred_element_type=jnp.float32,
    )
    return product, scale, prior


def soften_block(product, scale, prior, norm_ref, particles, rows, out):
    repeat = rows // LANES
    norm = jnp.concatenate([norm_ref[...]] * repeat, axis=1)
    scale = jnp.concatenate([scale] * repeat, axis=1)
    prior = jnp.concatenate([prior] * repeat, axis=1)
    half_square = 0.5 * scale * scale
    scores = []
    highest = None
    for rotation in range(ROTS):
        distance = jnp.abs(rotation - prior)
        score = (
            scale * product(rotation)
            - half_square * norm
            - ROT_PRIOR * (distance * distance)
        )
        scores.append(score)
        peak = jnp.max(score, axis=0, keepdims=True)
        highest = peak if highest is None else jnp.maximum(highest, peak)
    highest = fold_lanes(highest, particles, jnp.maximum)
    wide = jnp.concatenate([highest] * repeat, axis=1)
    total = None
    for rotation in range(ROTS):
        value = jnp.exp(scores[rotation] - wide)
        out(rotation, value)
        added = jnp.sum(value, axis=0, keepdims=True)
        total = added if total is None else total + added
    total = fold_lanes(total, particles, jnp.add)
    return highest, total


def score_blocks(
    count, segments, pending, chunks, last, blocks, table_ref, scale_ref, rotated_ref, norm_ref,
    shifted_ref, exp_ref, stats_ref,
):
    classes = norm_ref.shape[0]
    rows = exp_ref.shape[1] // count
    particles = blocks[0].shape[0]

    def soften(block, product):
        part = slice(block * rows, (block + 1) * rows)

        def out(rotation, value):
            exp_ref[rotation * classes : (rotation + 1) * classes, part] = value

        scale = stats_ref[2 * count + block : 2 * count + block + 1, :]
        prior = stats_ref[3 * count + block : 3 * count + block + 1, :]
        highest, total = soften_block(product, scale, prior, norm_ref, particles, rows, out)
        stats_ref[2 * block : 2 * block + 1, :] = highest
        stats_ref[2 * block + 1 : 2 * block + 2, :] = total

    for block in pending:
        part = slice(block * rows, (block + 1) * rows)
        soften(block, lambda rotation: exp_ref[rotation * classes : (rotation + 1) * classes, part])
    for block, block_ref in zip(chunks, blocks):
        part = slice(block * rows, (block + 1) * rows)
        product, scale, prior = match_block(
            segments, block_ref, table_ref, scale_ref, rotated_ref, shifted_ref.at[part, :]
        )
        stats_ref[2 * count + block : 2 * count + block + 1, :] = scale
        stats_ref[3 * count + block : 3 * count + block + 1, :] = prior
        if block != chunks[-1] or last:
            soften(block, lambda rotation: product[rotation * classes : (rotation + 1) * classes])
        else:
            exp_ref[0 : ROTS * classes, part] = product


def first_kernel(count, groups, segments, chunks, *refs):
    blocks, refs = refs[: len(chunks)], refs[len(chunks) :]
    class_ref, rows_ref, scale_ref = refs[:3]
    shifted_ref, exp_ref, stats_ref, rotated_ref, norm_ref, table_ref = refs[3:]
    build_table(segments, rows_ref, table_ref)
    rotate_classes(groups, class_ref, rotated_ref, norm_ref)
    stats_ref[...] = jnp.zeros_like(stats_ref)
    score_blocks(
        count, segments, [], chunks, False, blocks, table_ref, scale_ref, rotated_ref, norm_ref,
        shifted_ref, exp_ref, stats_ref,
    )


def rest_kernel(count, segments, pending, chunks, last, *refs):
    blocks, refs = refs[: len(chunks)], refs[len(chunks) :]
    table_ref, scale_ref, rotated_ref, norm_ref, before_ref = refs[:5]
    shifted_ref, exp_ref, stats_ref = refs[7:]
    stats_ref[...] = before_ref[...]
    score_blocks(
        count, segments, pending, chunks, last, blocks, table_ref, scale_ref, rotated_ref, norm_ref,
        shifted_ref, exp_ref, stats_ref,
    )


def merged(mine, other, block, distance):
    twin = block ^ distance
    high, other_high = mine[2 * block : 2 * block + 1, :], other[2 * twin : 2 * twin + 1, :]
    top = jnp.maximum(high, other_high)
    total = mine[2 * block + 1 : 2 * block + 2, :] * jnp.exp(high - top)
    return top, total + other[2 * twin + 1 : 2 * twin + 2, :] * jnp.exp(other_high - top)


def merge_kernel(count, distance, mine, other, out_ref):
    out_ref[...] = jnp.zeros_like(out_ref)
    for block in range(count):
        top, total = merged(mine, other, block, distance)
        out_ref[2 * block : 2 * block + 1, :] = top
        out_ref[2 * block + 1 : 2 * block + 2, :] = total


def weigh(count, stats_ref, mine, other, exp_ref, weight_ref):
    rows = exp_ref.shape[1] // count
    repeat = rows // LANES
    classes = weight_ref.shape[0] // ROTS
    mass = jnp.zeros((classes, rows), jnp.float32)
    for block in range(count):
        top, total = merged(mine, other, block, count // 2)
        factor = jnp.exp(stats_ref[2 * block : 2 * block + 1, :] - top) / total
        scale = stats_ref[2 * count + block : 2 * count + block + 1, :]
        factor = jnp.concatenate([factor * scale] * repeat, axis=1)
        scale = jnp.concatenate([scale] * repeat, axis=1)
        part = slice(block * rows, (block + 1) * rows)
        turned = None
        for rotation in range(ROTS):
            rotated = slice(rotation * classes, (rotation + 1) * classes)
            weight = exp_ref[rotated, part] * factor
            turned = weight if turned is None else turned + weight
            weight_ref[rotated, part] = weight.astype(jnp.bfloat16)
        mass = mass + turned * scale
    return jnp.broadcast_to(jnp.sum(mass, axis=1, keepdims=True), (classes, LANES))


def window_sums(weight_ref, shifted_ref, start, wide):
    classes = weight_ref.shape[0] // ROTS
    product = jnp.dot(
        weight_ref[...], shifted_ref[:, pl.ds(start, wide)], preferred_element_type=jnp.float32
    )
    lane = lane_index((classes, LANES)) % ANG
    tiles = []
    for part in range(0, wide, LANES):
        inside = product[:classes, part : part + LANES]
        wrapped = None
        for rotation in range(1, ROTS):
            offset = ANG_STEP * rotation % ANG
            turned = pltpu.roll(
                product[rotation * classes : (rotation + 1) * classes, part : part + LANES],
                LANES - offset,
                1,
            )
            within = lane < ANG - offset
            inside = inside + jnp.where(within, turned, 0.0)
            over = jnp.where(within, 0.0, turned)
            wrapped = over if wrapped is None else wrapped + over
        tiles.append(inside + pltpu.roll(wrapped, ANG, 1))
    return tiles


def block_sums(doms, width, main, distance, weight_ref, shifted_ref):
    classes = weight_ref.shape[0] // ROTS
    padded = -(-(width + 3) // LANES) * LANES
    place = lax.axis_index("dom") ^ distance
    first = place * (main or width)
    shifts = [0] if main else sorted({width * dom % LANES for dom in range(doms)})
    span = main or -(-(shifts[-1] + width) // LANES) * LANES
    base = first // LANES * LANES
    tiles = []
    for start in range(0, span, 2 * LANES):
        tiles += window_sums(
            weight_ref,
            shifted_ref,
            pl.multiple_of(base + start, LANES),
            min(2 * LANES, span - start),
        )
    if main:
        start = pl.multiple_of(doms * main + place * ANG // LANES * LANES, LANES)
        (tail,) = window_sums(weight_ref, shifted_ref, start, LANES)
        tiles.append(jnp.where(place % 2 == 1, pltpu.roll(tail, ANG, 1), tail))
    total = jnp.concatenate(tiles, axis=1)
    aligned = total
    for shift in shifts:
        if shift:
            aligned = jnp.where(first - base == shift, pltpu.roll(total, span - shift, 1), aligned)
    return pad_columns(aligned, padded)


def store_block(width, value, mass, out_ref):
    high = mass.astype(jnp.bfloat16).astype(jnp.float32)
    middle = (mass - high).astype(jnp.bfloat16).astype(jnp.float32)
    low = (mass - high - middle).astype(jnp.bfloat16).astype(jnp.float32)
    lane = lane_index(value.shape)
    tail = jnp.where(
        lane == width, high, jnp.where(lane == width + 1, middle, jnp.where(lane == width + 2, low, 0.0))
    )
    value = jnp.where(lane < width, value, tail)
    out_ref[...] = value[:, : out_ref.shape[1]].astype(out_ref.dtype)


def pad_columns(value, padded):
    if value.shape[1] < padded:
        added = jnp.zeros((value.shape[0], padded - value.shape[1]), value.dtype)
        return jnp.concatenate([value, added], axis=1)
    return value[:, :padded]


def received_mass(width, ref):
    base = width // LANES * LANES
    tail = ref[:, base:].astype(jnp.float32)
    lane = base + lane_index(tail.shape)
    tail = jnp.where((lane >= width) & (lane < width + 3), tail, 0.0)
    return jnp.sum(tail, axis=1, keepdims=True)


def first_sums_kernel(count, doms, width, main, blocks, *refs):
    stats_ref, mine, other, exp_ref, shifted_ref, weight_ref, mass_ref = refs[:7]
    mass = weigh(count, stats_ref, mine, other, exp_ref, weight_ref)
    mass_ref[...] = mass
    for block, out_ref in zip(blocks, refs[7:]):
        value = block_sums(doms, width, main, block, weight_ref, shifted_ref)
        store_block(width, value, mass[:, :1], out_ref)


def rest_sums_kernel(doms, width, main, blocks, weight_ref, shifted_ref, mass_ref, *refs):
    for block, out_ref in zip(blocks, refs[-len(blocks) :]):
        value = block_sums(doms, width, main, block, weight_ref, shifted_ref)
        store_block(width, value, mass_ref[:, :1], out_ref)


def add_kernel(width, *refs):
    out_ref = refs[-1]
    padded = -(-out_ref.shape[1] // LANES) * LANES
    total, mass = None, None
    for ref in refs[:-1]:
        value = pad_columns(ref[...].astype(jnp.float32), padded)
        total = value if total is None else total + value
        tail = received_mass(width, ref)
        mass = tail if mass is None else mass + tail
    store_block(width, total, mass, out_ref)


def final_kernel(width, own_ref, *refs):
    received, sums_ref, weights_ref = refs[:-2], refs[-2], refs[-1]
    total, mass = None, None
    for ref in (own_ref, *received):
        value = ref[:, :width].astype(jnp.float32)
        total = value if total is None else total + value
        tail = received_mass(width, ref)
        mass = tail if mass is None else mass + tail
    sums_ref[...] = total
    weights_ref[...] = to_lanes(mass, total.shape[0])


def call(kernel, shapes, scratch, flops, moved, *args, smem=(), hbm=(), chip=(), pinned=True, aliases=None):
    vmem = pl.BlockSpec(memory_space=pltpu.VMEM)
    scalar = pl.BlockSpec(memory_space=pltpu.SMEM)
    place = pl.BlockSpec(memory_space=pltpu.HBM)
    args = [
        pltpu.with_memory_space_constraint(a, pltpu.HBM) if i in hbm
        else pltpu.with_memory_space_constraint(a, pltpu.VMEM) if i in chip
        else a
        for i, a in enumerate(args)
    ]
    return pl.pallas_call(
        kernel,
        out_shape=[pltpu.VMEM(s.shape, s.dtype) if pinned else s for s in shapes],
        in_specs=[scalar if i in smem else place if i in hbm else vmem for i in range(len(args))],
        out_specs=[vmem] * len(shapes),
        scratch_shapes=scratch,
        input_output_aliases=aliases or {},
        compiler_params=pltpu.CompilerParams(vmem_limit_bytes=VMEM_LIMIT),
        cost_estimate=pl.CostEstimate(flops=flops, bytes_accessed=moved, transcendentals=0),
    )(*args)


def body(particle_spectra, class_spectra, shift_index, prior_rotation, particle_group, group_scale):
    count = lax.axis_size("cls")
    doms = lax.axis_size("dom")
    particles, candidates = shift_index.shape
    classes = class_spectra.shape[0]
    rows = particles * candidates
    width = COLS // doms
    padded = -(-(width + 3) // LANES) * LANES
    growth = (padded - width - 3) // (doms - 1)
    f32, bf16 = jnp.float32, jnp.bfloat16
    shape = jax.ShapeDtypeStruct

    groups, segments, main = column_layout(doms)
    phases = jnp.asarray(phase_rows(groups))
    packed, classes_on_chip, scales, phases_on_chip = call(
        functools.partial(pack_kernel, groups),
        [
            shape((particles, COLS + META), bf16),
            shape(class_spectra.shape, bf16),
            shape((1, group_scale.shape[0]), f32),
            shape(phases.shape, f32),
        ],
        [
            pltpu.VMEM((particles, COLS), bf16),
            pltpu.VMEM((particles, candidates), jnp.int32),
            pltpu.VMEM((1, particles), jnp.int32),
            pltpu.VMEM((1, particles), jnp.int32),
            pltpu.SemaphoreType.DMA((7,)),
        ],
        particles * COLS,
        4 * particles * COLS,
        particle_spectra, shift_index, prior_rotation[None, :], particle_group[None, :],
        class_spectra, group_scale[None, :], phases,
        hbm=(0, 1, 2, 3, 4, 5, 6),
    )
    chunks = {0: packed, 1: exchange(packed, "cls", 1)}
    for b in range(2, count, 2):
        chunks[b] = exchange(packed, "cls", b)
    stat_rows = -(-4 * count // 8) * 8
    work = 2 * rows * COLS * (ROTS * classes + 256)
    stats_shape = shape((stat_rows, LANES), f32)
    shifted_shape = shape((count * rows, COLS), bf16)
    exp_shape = shape((ROTS * classes, count * rows), f32)
    near = [0, 1]
    shifted, exps, stats, rotated, norm, table = call(
        functools.partial(first_kernel, count, groups, segments, near),
        [
            shifted_shape,
            exp_shape,
            stats_shape,
            shape((ROTS * classes, COLS), bf16),
            shape((classes, LANES), f32),
            shape((2 * LANES, COLS), bf16),
        ],
        [],
        work * len(near),
        4 * len(near) * rows * COLS,
        *[chunks[b] for b in near], classes_on_chip, phases_on_chip, scales,
    )
    for b in range(2, count, 2):
        arrived, stats = lax.optimization_barrier((chunks[b], stats))
        chunks[b + 1] = exchange(arrived, "cls", 1)
    evens, odds = list(range(2, count, 2)), list(range(3, count, 2))
    for pending, far in ((near[-1:], evens), (evens[-1:], odds)):
        shifted, exps, stats = call(
            functools.partial(rest_kernel, count, segments, pending, far, far is odds),
            [shifted_shape, exp_shape, stats_shape],
            [],
            work * len(far),
            4 * len(far) * rows * COLS,
            *[chunks[b] for b in far], table, scales, rotated, norm, stats, shifted, exps,
            aliases={len(far) + 5: 0, len(far) + 6: 1},
            chip=(len(far) + 5, len(far) + 6),
        )
    mine, distance = stats, 1
    other = exchange(mine, "cls", distance)
    while 2 * distance < count:
        (mine,) = call(
            functools.partial(merge_kernel, count, distance),
            [shape((-(-2 * count // 8) * 8, LANES), f32)],
            [],
            1024,
            1024,
            mine, other,
        )
        distance *= 2
        other = exchange(mine, "cls", distance)
    low_bit = lambda b: b & -b
    early = list(range(doms - 1, 1, -2))
    order = early + [1] + sorted(range(2, doms, 2), key=lambda b: (low_bit(b), -b))
    extents = {b: width + 3 + (doms - 1 - place) * growth for place, b in enumerate(order)}
    late = [1] + list(range(2, doms, 2))
    weights, mass, *made = call(
        functools.partial(first_sums_kernel, count, doms, width, main, early),
        [
            shape((ROTS * classes, count * rows), bf16),
            shape((classes, LANES), f32),
        ]
        + [shape((classes, extents[b]), bf16) for b in early],
        [],
        2 * count * rows * COLS * ROTS * classes // doms,
        4 * count * rows * width,
        stats, mine, other, exps, shifted,
        chip=(3, 4),
    )
    incoming = {b: [] for b in range(doms)}
    for b, block in zip(early, made):
        incoming[b ^ 1].append(exchange(block, "dom", 1))
    rest = call(
        functools.partial(rest_sums_kernel, doms, width, main, late),
        [
            shape((classes, extents.get(b, width + 3)), bf16 if b == 1 else f32) for b in late
        ],
        [],
        1024,
        1024,
        weights, shifted, mass, *made,
        chip=(1,),
    )
    blocks = dict(zip(late, rest))
    incoming[0].append(exchange(blocks[1], "dom", 1))
    for b in order[len(early) + 1 :]:
        (block,) = call(
            functools.partial(add_kernel, width),
            [shape((classes, extents[b]), bf16)],
            [],
            1024,
            1024,
            blocks[b], *incoming[b],
        )
        incoming[b ^ low_bit(b)].append(exchange(block, "dom", low_bit(b)))
    (own,) = call(
        functools.partial(rest_sums_kernel, doms, width, main, [0]),
        [shape((classes, width + 3), f32)],
        [],
        1024,
        1024,
        weights, shifted, mass, block,
        chip=(1,),
    )
    received = incoming[0]
    class_sums, class_weights = call(
        functools.partial(final_kernel, width),
        [shape((classes, width), f32), shape((1, classes), f32)],
        [],
        doms * classes * padded,
        4 * doms * classes * padded,
        own, *received,
        pinned=False,
    )
    return class_sums, class_weights.reshape(classes)


def solution(mesh):
    placed = (
        P(("groups", "dom", "cls"), None),
        P(("groups", "cls"), None),
        P(("groups", "dom", "cls"), None),
        P(("groups", "dom", "cls")),
        P(("groups", "dom", "cls")),
        P("groups"),
    )
    return jax.shard_map(
        body,
        mesh=mesh,
        in_specs=placed,
        out_specs=(P(("groups", "cls"), "dom"), P(("groups", "cls"))),
        check_vma=False,
    )
```

```python
import functools
import math

import jax
import jax.numpy as jnp
import numpy as np
from jax import lax
from jax.experimental import pallas as pl
from jax.experimental.pallas import tpu as pltpu
from jax.sharding import PartitionSpec as P

CYCLES = 18
ANG = 64
IMG = 64
ANG_STEP = 1
ROTS = 8
SHIFT_R = 5
SHIFTW = 11
HALF = CYCLES * ANG
COLS = 2 * HALF
LANES = 128
SUB = 8
META = LANES
ROT_PRIOR = 0.5
VMEM_LIMIT = 20 * 1024 * 1024


def column_layout(doms):
    width = COLS // doms
    main = width - ANG
    half = doms // 2
    if width % ANG or main <= 0 or main % LANES or half * ANG % LANES:
        step = 3 * LANES
        segments = [(start, HALF + start, step) for start in range(0, HALF, step)]
        return list(range(COLS // ANG)), segments, 0
    per = width // ANG
    groups = [per * dom + group for dom in range(doms) for group in range(per - 1)]
    groups += [per * dom + per - 1 for dom in range(doms)]
    segments = [(dom * main, (half + dom) * main, main) for dom in range(half)]
    segments.append((doms * main, doms * main + half * ANG, half * ANG))
    return groups, segments, main


def tile_of(groups, tile, read):
    low, high = groups[2 * tile], groups[2 * tile + 1]
    if low % 2 == 0 and high == low + 1:
        return read(low // 2)
    first, second = read(low // 2), read(high // 2)
    first = pltpu.roll(first, ANG, 1) if low % 2 else first
    second = second if high % 2 else pltpu.roll(second, ANG, 1)
    return jnp.where(lane_index(first.shape) < ANG, first, second)


def phase_rows(groups):
    angles = np.arange(ANG) * (2.0 * math.pi / ANG)
    radius = np.arange(CYCLES) + 1.0
    fx = (radius[:, None] * np.cos(angles)[None, :]).reshape(-1)
    fy = (radius[:, None] * np.sin(angles)[None, :]).reshape(-1)
    offsets = np.arange(SHIFTW) - SHIFT_R
    unit = 2.0 * math.pi / IMG
    along_x = unit * offsets[:, None] * fx[None, :]
    along_y = unit * offsets[:, None] * fy[None, :]
    both = (along_x[SUB:, None, :] + along_y[None, SUB:, :]).reshape(-1, HALF)
    values = np.zeros((40, COLS), np.float32)
    for start, phase in ((0, along_x), (11, along_y), (22, both)):
        values[start : start + len(phase)] = np.concatenate([np.cos(phase), np.sin(phase)], axis=1)
    columns = np.concatenate([np.arange(ANG) + ANG * group for group in groups])
    return values[:, columns]


def build_table(segments, rows_ref, table_ref):
    for real_start, imag_start, width in segments:
        real = slice(real_start, real_start + width)
        imag = slice(imag_start, imag_start + width)

        def product(block, row):
            c, s = rows_ref[block : block + SUB, real], rows_ref[block : block + SUB, imag]
            d, t = rows_ref[row : row + 1, real], rows_ref[row : row + 1, imag]
            return c * d - s * t, s * d + c * t

        blocks = [product(0, 11 + y) for y in range(SHIFTW)]
        blocks += [product(11, x) for x in range(SUB, SHIFTW)]
        blocks += [
            (rows_ref[row : row + SUB, real], rows_ref[row : row + SUB, imag])
            for row in (22, 22 + SUB)
        ]
        for pair in range(0, len(blocks), 2):
            for part, columns in ((0, real), (1, imag)):
                value = jnp.concatenate([blocks[pair][part], blocks[pair + 1][part]], axis=0)
                high = value.astype(jnp.bfloat16)
                low = (value - high.astype(jnp.float32)).astype(jnp.bfloat16)
                row = pair * SUB
                table_ref[row : row + 2 * SUB, columns] = high
                table_ref[LANES + row : LANES + row + 2 * SUB, columns] = low


def table_row(index):
    y = jnp.floor((index + 0.5) * (1.0 / SHIFTW))
    x = index - SHIFTW * y
    near = SUB * y + x
    side = SUB * (SHIFTW + x - SUB) + y
    corner = SUB * (2 * SHIFTW - SUB) + (SHIFTW - SUB) * (x - SUB) + (y - SUB)
    return jnp.where(x < SUB, near, jnp.where(y < SUB, side, corner))


def exchange(array, axis, distance):
    return lax.ppermute(array, axis, [(i, i ^ distance) for i in range(lax.axis_size(axis))])


def lane_index(shape):
    return lax.broadcasted_iota(jnp.int32, shape, len(shape) - 1)


def rotate_classes(groups, class_ref, rotated_ref, norm_ref):
    classes = class_ref.shape[0]
    total = jnp.zeros((classes, LANES), jnp.float32)
    lane = lane_index((classes, LANES)) % ANG
    for tile in range(COLS // LANES):
        columns = slice(tile * LANES, (tile + 1) * LANES)
        value = tile_of(
            groups, tile, lambda k: class_ref[:, k * LANES : (k + 1) * LANES]
        )
        wide = value.astype(jnp.float32)
        total = total + wide * wide
        other = pltpu.roll(value, ANG, 1)
        for rotation in range(ROTS):
            offset = ANG_STEP * rotation % ANG
            turned = value
            if offset:
                turned = pltpu.roll(jnp.where(lane < ANG - offset, value, other), offset, 1)
            rotated_ref[rotation * classes : (rotation + 1) * classes, columns] = turned
    norm_ref[...] = jnp.broadcast_to(jnp.sum(total, axis=1, keepdims=True), (classes, LANES))


def to_lanes(column, width):
    n = column.shape[0]
    row = lax.broadcasted_iota(jnp.int32, (n, width), 0)
    return jnp.sum(
        jnp.where(lane_index((n, width)) % n == row, column, 0.0), axis=0, keepdims=True
    )


def fold_lanes(row, period, combine):
    result = row[:, :LANES]
    for part in range(1, row.shape[1] // LANES):
        result = combine(result, row[:, part * LANES : (part + 1) * LANES])
    step = LANES // 2
    while step >= period:
        result = combine(result, pltpu.roll(result, step, 1))
        step //= 2
    return result


def to_column(row):
    n = row.shape[1]
    diagonal = lax.broadcasted_iota(jnp.int32, (n, n), 0) == lane_index((n, n))
    return jnp.sum(jnp.where(diagonal, row, 0.0), axis=1, keepdims=True)


def pack_kernel(
    groups, particle_hbm, index_hbm, prior_hbm, group_hbm, class_hbm, scale_hbm, rows_hbm,
    packed_ref, class_ref, scale_ref, rows_ref, particle_ref, index_ref, prior_ref, group_ref, sems,
):
    particles, candidates = index_ref.shape
    copies = [
        pltpu.make_async_copy(source, target, sems.at[i])
        for i, (source, target) in enumerate(
            [
                (index_hbm, index_ref),
                (prior_hbm, prior_ref),
                (group_hbm, group_ref),
                (particle_hbm, particle_ref),
                (class_hbm, class_ref),
                (scale_hbm, scale_ref),
                (rows_hbm, rows_ref),
            ]
        )
    ]
    for copy in copies:
        copy.start()
    for copy in copies[:3]:
        copy.wait()
    lane = lane_index((particles, META))
    index = jnp.concatenate(
        [table_row(index_ref[...].astype(jnp.float32)), jnp.zeros((particles, META - candidates), jnp.float32)],
        axis=1,
    )
    prior = to_column(prior_ref[...].astype(jnp.float32))
    group = to_column(group_ref[...].astype(jnp.float32))
    meta = jnp.where(lane == candidates, prior, jnp.where(lane == candidates + 1, group, index))
    packed_ref[:, COLS:] = meta.astype(jnp.bfloat16)
    copies[3].wait()
    for tile in range(COLS // LANES):
        packed_ref[:, tile * LANES : (tile + 1) * LANES] = tile_of(
            groups, tile, lambda k: particle_ref[:, k * LANES : (k + 1) * LANES]
        )
    for copy in copies[4:]:
        copy.wait()


def match_block(segments, block_ref, table_ref, scale_ref, rotated_ref, shifted_ref):
    particles = block_ref.shape[0]
    candidates = shifted_ref.shape[0] // particles
    meta = block_ref[:, COLS : COLS + META].astype(jnp.float32)
    index = meta[:, :candidates].astype(jnp.int32)
    lane = lane_index((particles, LANES))
    hot = jnp.concatenate(
        [
            jnp.where(index[:, t : t + 1] == lane, 1.0, 0.0).astype(jnp.bfloat16)
            for t in range(candidates)
        ],
        axis=0,
    )
    hot = jnp.concatenate([hot, hot], axis=1)
    groups = scale_ref.shape[1]
    group = meta[:, candidates + 1 : candidates + 2].astype(jnp.int32)
    scale_column = jnp.sum(
        jnp.where(group == lane_index((particles, groups)), scale_ref[...], 0.0),
        axis=1,
        keepdims=True,
    )
    scale = to_lanes(scale_column, LANES)
    prior = to_lanes(meta[:, candidates : candidates + 1], LANES)
    for real_start, imag_start, width in segments:
        real_columns = slice(real_start, real_start + width)
        imag_columns = slice(imag_start, imag_start + width)
        cosine = jnp.dot(hot, table_ref[:, real_columns], preferred_element_type=jnp.float32)
        sine = jnp.dot(hot, table_ref[:, imag_columns], preferred_element_type=jnp.float32)
        real = block_ref[:, real_columns].astype(jnp.float32)
        imag = block_ref[:, imag_columns].astype(jnp.float32)
        for t in range(candidates):
            part = slice(t * particles, (t + 1) * particles)
            c, s = cosine[part], sine[part]
            shifted_ref[part, real_columns] = (real * c - imag * s).astype(jnp.bfloat16)
            shifted_ref[part, imag_columns] = (real * s + imag * c).astype(jnp.bfloat16)
    product = lax.dot_general(
        rotated_ref[...],
        shifted_ref[...],
        (((1,), (1,)), ((), ())),
        preferred_element_type=jnp.float32,
    )
    return product, scale, prior


def soften_block(product, scale, prior, norm_ref, particles, rows, out):
    repeat = rows // LANES
    norm = jnp.concatenate([norm_ref[...]] * repeat, axis=1)
    scale = jnp.concatenate([scale] * repeat, axis=1)
    prior = jnp.concatenate([prior] * repeat, axis=1)
    half_square = 0.5 * scale * scale
    scores = []
    highest = None
    for rotation in range(ROTS):
        distance = jnp.abs(rotation - prior)
        score = (
            scale * product(rotation)
            - half_square * norm
            - ROT_PRIOR * (distance * distance)
        )
        scores.append(score)
        peak = jnp.max(score, axis=0, keepdims=True)
        highest = peak if highest is None else jnp.maximum(highest, peak)
    highest = fold_lanes(highest, particles, jnp.maximum)
    wide = jnp.concatenate([highest] * repeat, axis=1)
    total = None
    for rotation in range(ROTS):
        value = jnp.exp(scores[rotation] - wide)
        out(rotation, value)
        added = jnp.sum(value, axis=0, keepdims=True)
        total = added if total is None else total + added
    total = fold_lanes(total, particles, jnp.add)
    return highest, total


def score_blocks(
    count, segments, pending, chunks, last, blocks, table_ref, scale_ref, rotated_ref, norm_ref,
    shifted_ref, exp_ref, stats_ref,
):
    classes = norm_ref.shape[0]
    rows = exp_ref.shape[1] // count
    particles = blocks[0].shape[0]

    def soften(block, product):
        part = slice(block * rows, (block + 1) * rows)

        def out(rotation, value):
            exp_ref[rotation * classes : (rotation + 1) * classes, part] = value

        scale = stats_ref[2 * count + block : 2 * count + block + 1, :]
        prior = stats_ref[3 * count + block : 3 * count + block + 1, :]
        highest, total = soften_block(product, scale, prior, norm_ref, particles, rows, out)
        stats_ref[2 * block : 2 * block + 1, :] = highest
        stats_ref[2 * block + 1 : 2 * block + 2, :] = total

    for block in pending:
        part = slice(block * rows, (block + 1) * rows)
        soften(block, lambda rotation: exp_ref[rotation * classes : (rotation + 1) * classes, part])
    for block, block_ref in zip(chunks, blocks):
        part = slice(block * rows, (block + 1) * rows)
        product, scale, prior = match_block(
            segments, block_ref, table_ref, scale_ref, rotated_ref, shifted_ref.at[part, :]
        )
        stats_ref[2 * count + block : 2 * count + block + 1, :] = scale
        stats_ref[3 * count + block : 3 * count + block + 1, :] = prior
        if block != chunks[-1] or last:
            soften(block, lambda rotation: product[rotation * classes : (rotation + 1) * classes])
        else:
            exp_ref[0 : ROTS * classes, part] = product


def first_kernel(count, groups, segments, chunks, *refs):
    blocks, refs = refs[: len(chunks)], refs[len(chunks) :]
    class_ref, rows_ref, scale_ref = refs[:3]
    shifted_ref, exp_ref, stats_ref, rotated_ref, norm_ref, table_ref = refs[3:]
    build_table(segments, rows_ref, table_ref)
    rotate_classes(groups, class_ref, rotated_ref, norm_ref)
    stats_ref[...] = jnp.zeros_like(stats_ref)
    score_blocks(
        count, segments, [], chunks, False, blocks, table_ref, scale_ref, rotated_ref, norm_ref,
        shifted_ref, exp_ref, stats_ref,
    )


def rest_kernel(count, segments, pending, chunks, last, *refs):
    blocks, refs = refs[: len(chunks)], refs[len(chunks) :]
    table_ref, scale_ref, rotated_ref, norm_ref, before_ref = refs[:5]
    shifted_ref, exp_ref, stats_ref = refs[7:]
    stats_ref[...] = before_ref[...]
    score_blocks(
        count, segments, pending, chunks, last, blocks, table_ref, scale_ref, rotated_ref, norm_ref,
        shifted_ref, exp_ref, stats_ref,
    )


def merged(mine, other, block, distance):
    twin = block ^ distance
    high, other_high = mine[2 * block : 2 * block + 1, :], other[2 * twin : 2 * twin + 1, :]
    top = jnp.maximum(high, other_high)
    total = mine[2 * block + 1 : 2 * block + 2, :] * jnp.exp(high - top)
    return top, total + other[2 * twin + 1 : 2 * twin + 2, :] * jnp.exp(other_high - top)


def merge_kernel(count, distance, mine, other, out_ref):
    out_ref[...] = jnp.zeros_like(out_ref)
    for block in range(count):
        top, total = merged(mine, other, block, distance)
        out_ref[2 * block : 2 * block + 1, :] = top
        out_ref[2 * block + 1 : 2 * block + 2, :] = total


def weigh(count, stats_ref, mine, other, exp_ref, weight_ref):
    rows = exp_ref.shape[1] // count
    repeat = rows // LANES
    classes = weight_ref.shape[0] // ROTS
    mass = jnp.zeros((classes, rows), jnp.float32)
    for block in range(count):
        top, total = merged(mine, other, block, count // 2)
        factor = jnp.exp(stats_ref[2 * block : 2 * block + 1, :] - top) / total
        scale = stats_ref[2 * count + block : 2 * count + block + 1, :]
        factor = jnp.concatenate([factor * scale] * repeat, axis=1)
        scale = jnp.concatenate([scale] * repeat, axis=1)
        part = slice(block * rows, (block + 1) * rows)
        turned = None
        for rotation in range(ROTS):
            rotated = slice(rotation * classes, (rotation + 1) * classes)
            weight = exp_ref[rotated, part] * factor
            turned = weight if turned is None else turned + weight
            weight_ref[rotated, part] = weight.astype(jnp.bfloat16)
        mass = mass + turned * scale
    return jnp.broadcast_to(jnp.sum(mass, axis=1, keepdims=True), (classes, LANES))


def window_sums(weight_ref, shifted_ref, start, wide):
    classes = weight_ref.shape[0] // ROTS
    product = jnp.dot(
        weight_ref[...], shifted_ref[:, pl.ds(start, wide)], preferred_element_type=jnp.float32
    )
    lane = lane_index((classes, LANES)) % ANG
    tiles = []
    for part in range(0, wide, LANES):
        inside = product[:classes, part : part + LANES]
        wrapped = None
        for rotation in range(1, ROTS):
            offset = ANG_STEP * rotation % ANG
            turned = pltpu.roll(
                product[rotation * classes : (rotation + 1) * classes, part : part + LANES],
                LANES - offset,
                1,
            )
            within = lane < ANG - offset
            inside = inside + jnp.where(within, turned, 0.0)
            over = jnp.where(within, 0.0, turned)
            wrapped = over if wrapped is None else wrapped + over
        tiles.append(inside + pltpu.roll(wrapped, ANG, 1))
    return tiles


def block_sums(doms, width, main, distance, weight_ref, shifted_ref, tails_ref):
    classes = weight_ref.shape[0] // ROTS
    padded = -(-(width + 3) // LANES) * LANES
    place = lax.axis_index("dom") ^ distance
    first = place * (main or width)
    shifts = [0] if main else sorted({width * dom % LANES for dom in range(doms)})
    span = main or -(-(shifts[-1] + width) // LANES) * LANES
    base = first // LANES * LANES
    tiles = []
    for start in range(0, span, 2 * LANES):
        tiles += window_sums(
            weight_ref,
            shifted_ref,
            pl.multiple_of(base + start, LANES),
            min(2 * LANES, span - start),
        )
    if main:
        tail = None
        for dom in range(doms):
            part = dom * ANG // LANES * LANES
            piece = tails_ref[:, part : part + LANES]
            piece = pltpu.roll(piece, ANG, 1) if dom % 2 else piece
            tail = piece if tail is None else jnp.where(place == dom, piece, tail)
        tiles.append(tail)
    total = jnp.concatenate(tiles, axis=1)
    aligned = total
    for shift in shifts:
        if shift:
            aligned = jnp.where(first - base == shift, pltpu.roll(total, span - shift, 1), aligned)
    return pad_columns(aligned, padded)


def store_block(width, value, mass, out_ref):
    high = mass.astype(jnp.bfloat16).astype(jnp.float32)
    middle = (mass - high).astype(jnp.bfloat16).astype(jnp.float32)
    low = (mass - high - middle).astype(jnp.bfloat16).astype(jnp.float32)
    lane = lane_index(value.shape)
    tail = jnp.where(
        lane == width, high, jnp.where(lane == width + 1, middle, jnp.where(lane == width + 2, low, 0.0))
    )
    value = jnp.where(lane < width, value, tail)
    out_ref[...] = value[:, : out_ref.shape[1]].astype(out_ref.dtype)


def pad_columns(value, padded):
    if value.shape[1] < padded:
        added = jnp.zeros((value.shape[0], padded - value.shape[1]), value.dtype)
        return jnp.concatenate([value, added], axis=1)
    return value[:, :padded]


def received_mass(width, ref):
    base = width // LANES * LANES
    tail = ref[:, base:].astype(jnp.float32)
    lane = base + lane_index(tail.shape)
    tail = jnp.where((lane >= width) & (lane < width + 3), tail, 0.0)
    return jnp.sum(tail, axis=1, keepdims=True)


def first_sums_kernel(count, doms, width, main, blocks, *refs):
    stats_ref, mine, other, exp_ref, shifted_ref, weight_ref, mass_ref, tails_ref = refs[:8]
    mass = weigh(count, stats_ref, mine, other, exp_ref, weight_ref)
    mass_ref[...] = mass
    tails_ref[...] = jnp.zeros_like(tails_ref)
    for start in range(0, doms * ANG if main else 0, 2 * LANES):
        tiles = window_sums(weight_ref, shifted_ref, doms * main + start, 2 * LANES)
        tails_ref[:, start : start + 2 * LANES] = jnp.concatenate(tiles, axis=1)
    for block, out_ref in zip(blocks, refs[8:]):
        value = block_sums(doms, width, main, block, weight_ref, shifted_ref, tails_ref)
        store_block(width, value, mass[:, :1], out_ref)


def rest_sums_kernel(doms, width, main, blocks, weight_ref, shifted_ref, mass_ref, tails_ref, *refs):
    for block, out_ref in zip(blocks, refs[-len(blocks) :]):
        value = block_sums(doms, width, main, block, weight_ref, shifted_ref, tails_ref)
        store_block(width, value, mass_ref[:, :1], out_ref)


def add_kernel(width, *refs):
    out_ref = refs[-1]
    padded = -(-out_ref.shape[1] // LANES) * LANES
    total, mass = None, None
    for ref in refs[:-1]:
        value = pad_columns(ref[...].astype(jnp.float32), padded)
        total = value if total is None else total + value
        tail = received_mass(width, ref)
        mass = tail if mass is None else mass + tail
    store_block(width, total, mass, out_ref)


def final_kernel(width, own_ref, *refs):
    received, sums_ref, weights_ref = refs[:-2], refs[-2], refs[-1]
    total, mass = None, None
    for ref in (own_ref, *received):
        value = ref[:, :width].astype(jnp.float32)
        total = value if total is None else total + value
        tail = received_mass(width, ref)
        mass = tail if mass is None else mass + tail
    sums_ref[...] = total
    weights_ref[...] = to_lanes(mass, total.shape[0])


def call(kernel, shapes, scratch, flops, moved, *args, smem=(), hbm=(), chip=(), pinned=True, aliases=None):
    vmem = pl.BlockSpec(memory_space=pltpu.VMEM)
    scalar = pl.BlockSpec(memory_space=pltpu.SMEM)
    place = pl.BlockSpec(memory_space=pltpu.HBM)
    args = [
        pltpu.with_memory_space_constraint(a, pltpu.HBM) if i in hbm
        else pltpu.with_memory_space_constraint(a, pltpu.VMEM) if i in chip
        else a
        for i, a in enumerate(args)
    ]
    return pl.pallas_call(
        kernel,
        out_shape=[pltpu.VMEM(s.shape, s.dtype) if pinned else s for s in shapes],
        in_specs=[scalar if i in smem else place if i in hbm else vmem for i in range(len(args))],
        out_specs=[vmem] * len(shapes),
        scratch_shapes=scratch,
        input_output_aliases=aliases or {},
        compiler_params=pltpu.CompilerParams(vmem_limit_bytes=VMEM_LIMIT),
        cost_estimate=pl.CostEstimate(flops=flops, bytes_accessed=moved, transcendentals=0),
    )(*args)


def body(particle_spectra, class_spectra, shift_index, prior_rotation, particle_group, group_scale):
    count = lax.axis_size("cls")
    doms = lax.axis_size("dom")
    particles, candidates = shift_index.shape
    classes = class_spectra.shape[0]
    rows = particles * candidates
    width = COLS // doms
    padded = -(-(width + 3) // LANES) * LANES
    growth = (padded - width - 3) // (doms - 1)
    f32, bf16 = jnp.float32, jnp.bfloat16
    shape = jax.ShapeDtypeStruct

    groups, segments, main = column_layout(doms)
    phases = jnp.asarray(phase_rows(groups))
    packed, classes_on_chip, scales, phases_on_chip = call(
        functools.partial(pack_kernel, groups),
        [
            shape((particles, COLS + META), bf16),
            shape(class_spectra.shape, bf16),
            shape((1, group_scale.shape[0]), f32),
            shape(phases.shape, f32),
        ],
        [
            pltpu.VMEM((particles, COLS), bf16),
            pltpu.VMEM((particles, candidates), jnp.int32),
            pltpu.VMEM((1, particles), jnp.int32),
            pltpu.VMEM((1, particles), jnp.int32),
            pltpu.SemaphoreType.DMA((7,)),
        ],
        particles * COLS,
        4 * particles * COLS,
        particle_spectra, shift_index, prior_rotation[None, :], particle_group[None, :],
        class_spectra, group_scale[None, :], phases,
        hbm=(0, 1, 2, 3, 4, 5, 6),
    )
    chunks = {0: packed, 1: exchange(packed, "cls", 1)}
    for b in range(2, count, 2):
        chunks[b] = exchange(packed, "cls", b)
    stat_rows = -(-4 * count // 8) * 8
    work = 2 * rows * COLS * (ROTS * classes + 256)
    stats_shape = shape((stat_rows, LANES), f32)
    shifted_shape = shape((count * rows, COLS), bf16)
    exp_shape = shape((ROTS * classes, count * rows), f32)
    near = [0, 1]
    shifted, exps, stats, rotated, norm, table = call(
        functools.partial(first_kernel, count, groups, segments, near),
        [
            shifted_shape,
            exp_shape,
            stats_shape,
            shape((ROTS * classes, COLS), bf16),
            shape((classes, LANES), f32),
            shape((2 * LANES, COLS), bf16),
        ],
        [],
        work * len(near),
        4 * len(near) * rows * COLS,
        *[chunks[b] for b in near], classes_on_chip, phases_on_chip, scales,
    )
    for b in range(2, count, 2):
        arrived, stats = lax.optimization_barrier((chunks[b], stats))
        chunks[b + 1] = exchange(arrived, "cls", 1)
    evens, odds = list(range(2, count, 2)), list(range(3, count, 2))
    for pending, far in ((near[-1:], evens), (evens[-1:], odds)):
        shifted, exps, stats = call(
            functools.partial(rest_kernel, count, segments, pending, far, far is odds),
            [shifted_shape, exp_shape, stats_shape],
            [],
            work * len(far),
            4 * len(far) * rows * COLS,
            *[chunks[b] for b in far], table, scales, rotated, norm, stats, shifted, exps,
            aliases={len(far) + 5: 0, len(far) + 6: 1},
            chip=(len(far) + 5, len(far) + 6),
        )
    mine, distance = stats, 1
    other = exchange(mine, "cls", distance)
    while 2 * distance < count:
        (mine,) = call(
            functools.partial(merge_kernel, count, distance),
            [shape((-(-2 * count // 8) * 8, LANES), f32)],
            [],
            1024,
            1024,
            mine, other,
        )
        distance *= 2
        other = exchange(mine, "cls", distance)
    low_bit = lambda b: b & -b
    early = list(range(doms - 1, 1, -2))
    order = early + [1] + sorted(range(2, doms, 2), key=lambda b: (low_bit(b), -b))
    extents = {b: width + 3 + (doms - 1 - place) * growth for place, b in enumerate(order)}
    late = [1] + list(range(2, doms, 2))
    weights, mass, tails, *made = call(
        functools.partial(first_sums_kernel, count, doms, width, main, early),
        [
            shape((ROTS * classes, count * rows), bf16),
            shape((classes, LANES), f32),
            shape((classes, doms * ANG if main else LANES), f32),
        ]
        + [shape((classes, extents[b]), bf16) for b in early],
        [],
        2 * count * rows * COLS * ROTS * classes // doms,
        4 * count * rows * width,
        stats, mine, other, exps, shifted,
        chip=(3, 4),
    )
    incoming = {b: [] for b in range(doms)}
    for b, block in zip(early, made):
        incoming[b ^ 1].append(exchange(block, "dom", 1))
    rest = call(
        functools.partial(rest_sums_kernel, doms, width, main, late),
        [
            shape((classes, extents.get(b, width + 3)), bf16 if b == 1 else f32) for b in late
        ],
        [],
        1024,
        1024,
        weights, shifted, mass, tails, *made,
        chip=(1,),
    )
    blocks = dict(zip(late, rest))
    incoming[0].append(exchange(blocks[1], "dom", 1))
    for b in order[len(early) + 1 :]:
        (block,) = call(
            functools.partial(add_kernel, width),
            [shape((classes, extents[b]), bf16)],
            [],
            1024,
            1024,
            blocks[b], *incoming[b],
        )
        incoming[b ^ low_bit(b)].append(exchange(block, "dom", low_bit(b)))
    (own,) = call(
        functools.partial(rest_sums_kernel, doms, width, main, [0]),
        [shape((classes, width + 3), f32)],
        [],
        1024,
        1024,
        weights, shifted, mass, tails, block,
        chip=(1,),
    )
    received = incoming[0]
    class_sums, class_weights = call(
        functools.partial(final_kernel, width),
        [shape((classes, width), f32), shape((1, classes), f32)],
        [],
        doms * classes * padded,
        4 * doms * classes * padded,
        own, *received,
        pinned=False,
    )
    return class_sums, class_weights.reshape(classes)


def solution(mesh):
    placed = (
        P(("groups", "dom", "cls"), None),
        P(("groups", "cls"), None),
        P(("groups", "dom", "cls"), None),
        P(("groups", "dom", "cls")),
        P(("groups", "dom", "cls")),
        P("groups"),
    )
    return jax.shard_map(
        body,
        mesh=mesh,
        in_specs=placed,
        out_specs=(P(("groups", "cls"), "dom"), P(("groups", "cls"))),
        check_vma=False,
    )
```
